32 devices in a mesh: groups: 2 (over y), gx: 4 (over z), gy: 2 (over x), gz: 2 (over core).
Axes of the slice: x: 2, y: 2, z: 4, core: 2. Of those that a mesh axis runs over, the one named last changes fastest.
Arguments:
- concentration: float32 [32, 480, 256], P(('groups', 'gx'), 'gy', 'gz'), parts along dimension 0, may hold values from 0.03 to 0.87
- damage: float32 [32, 480, 256], P(('groups', 'gx'), 'gy', 'gz'), parts along dimension 0, may hold values from 0 to 0.4
- labels: int32 [32, 480, 256], P(('groups', 'gx'), 'gy', 'gz'), parts along dimension 0, may hold values from 0 to 2, as said below
- w_first: bfloat16 [27, 16, 4], replicated, may hold values from -0.625 to 0.625
- b_first: float32 [16], replicated, may hold values from -3 to 3
- w_second: bfloat16 [27, 16, 16], replicated, may hold values from -0.3125 to 0.3125
- b_second: float32 [16], replicated, may hold values from -3 to 3
- w_third: bfloat16 [27, 1, 16], replicated, may hold values from -0.3125 to 0.3125
- b_third: float32 [1], replicated, may hold values from -3 to 3
Outputs:
- lithium_fraction: float32 [32, 480, 256], P(('groups', 'gx'), 'gy', 'gz'), parts along dimension 0
- damage_field: float32 [32, 480, 256], P(('groups', 'gx'), 'gy', 'gz'), parts along dimension 0
- flux_rate: float32 [32, 480, 256], P(('groups', 'gx'), 'gy', 'gz'), parts along dimension 0
- crack_score: float32 [8, 120, 64], P(('groups', 'gx'), 'gy', 'gz'), parts along dimension 0
The draws below stay inside these ranges and needn't reach their ends.
There are 2 independent parts, one for each index of `groups`. The reference program is written for one: setup_inputs(seed, part) draws one part's arguments, and reference() takes and returns one part's arrays. A program takes and returns all parts, laid end to end along the dimension named above; an argument that names none is the same for every part. Nothing has to cross between parts.
Inputs may be any that keep to these rules, and one draw needn't show every extreme that they name: `labels`: 0 marks active particle, 1 binder and carbon, 2 pore.
All inputs are finite; a program needn't handle non-finite values.
Results may differ from the reference program's by a relative error of at most 0.0029.
Values may be sent and summed in bfloat16 or wider, within the bound.
No kernel may reach another device: no remote copies, remote signals or barrier semaphores. Data moves between devices by JAX's collectives and lax.ppermute only.
A program may use at most 64 MiB of HBM per device.

```python
import jax
import jax.numpy as jnp

STEPS = 2
CIN = 4
CH = 16
NX = 16
NY = 480
NZ = 256


def draw_concentration(key, part):
    rows = (jnp.arange(NX, dtype=jnp.float32) + 0.5) / NX
    trend = 0.15 + 0.6 * rows
    noise = jax.random.uniform(key, (NX, NY, NZ), jnp.float32, -0.12, 0.12)
    return (trend[:, None, None] + noise).astype(jnp.float32)


def draw_labels(key, part):
    scores = jax.random.randint(key, (NX, NY, NZ), 0, 20)
    return jnp.where(scores < 12, 0, jnp.where(scores < 16, 1, 2)).astype(jnp.int32)


def shard_levels(stream_key, dims, shards, smallest, top_value):
    loudness = 1.0
    for position, blocks in shards:
        heights = jax.random.uniform(jax.random.fold_in(jax.random.fold_in(stream_key, 6), position), (blocks,), jnp.float32, smallest / len(shards), top_value / len(shards))
        loudness = loudness * jnp.repeat(jnp.exp(heights), dims[position] // blocks).reshape((-1,) + (1,) * (len(dims) - 1 - position))
    return loudness


def gaussian(stream_key, shape, width, bound, kind=jnp.bfloat16):
    entries = jax.random.normal(stream_key, shape, jnp.float32) * width
    return jnp.minimum(jnp.maximum(entries, -bound), bound).astype(kind)


def setup_inputs(seed: int = 0, part: int = 0) -> dict:
    keys = jax.random.split(jax.random.key(seed), 10)
    part_splits = jax.random.split(jax.random.fold_in(keys[9], part), 10)
    concentration = draw_concentration(jax.random.fold_in(jax.random.fold_in(keys[9], part), 71), part)
    damage = jnp.clip(0.4 * jax.random.uniform(part_splits[1], (NX, NY, NZ), jnp.float32) ** shard_levels(part_splits[1], (NX, NY, NZ), ((0, 4), (1, 2), (2, 2)), -0.2, 0.2), 0.0, 0.4)
    labels = draw_labels(jax.random.fold_in(jax.random.fold_in(keys[9], part), 71), part)
    w_first = gaussian(keys[3], (27, CH, CIN), (27 * CIN) ** -0.5, 0.625)
    b_first = gaussian(keys[4], (CH,), 0.5, 3.0, jnp.float32)
    w_second = gaussian(keys[5], (27, CH, CH), (27 * CH) ** -0.5, 0.3125)
    b_second = gaussian(keys[6], (CH,), 0.5, 3.0, jnp.float32)
    w_third = gaussian(keys[7], (27, 1, CH), (27 * CH) ** -0.5, 0.3125)
    b_third = gaussian(keys[8], (1,), 0.5, 3.0, jnp.float32)
    return dict(concentration=concentration, damage=damage, labels=labels, w_first=w_first, b_first=b_first, w_second=w_second, b_second=b_second, w_third=w_third, b_third=b_third)


GRADIENT_ENERGY = 1.0
WELL_HEIGHT = 1.0
STRAIN_COUPLING = 4.0
TIME_STEP = 0.01
DAMAGE_RATE = 0.8
ENERGY_CRITICAL = 0.02

def phase_factor(labels):
    return jnp.where(labels == 0, 1.0, jnp.where(labels == 1, 0.3, 0.05)).astype(jnp.float32)

def shifted(padded):
    return (padded[..., 2:, 1:-1, 1:-1], padded[..., :-2, 1:-1, 1:-1], padded[..., 1:-1, 2:, 1:-1], padded[..., 1:-1, :-2, 1:-1], padded[..., 1:-1, 1:-1, 2:], padded[..., 1:-1, 1:-1, :-2])

def inner_part(field):
    return field[..., 1:-1, 1:-1, 1:-1]

def potential(fraction_pad, mobility_pad, mean_c):
    fraction = inner_part(fraction_pad)
    mobility = inner_part(mobility_pad)
    summed = jnp.zeros_like(fraction)
    for beside in shifted(fraction_pad):
        summed = summed + (beside - fraction)
    well = 2.0 * WELL_HEIGHT * fraction * (1.0 - fraction) * (1.0 - 2.0 * fraction)
    return well - GRADIENT_ENERGY * summed + STRAIN_COUPLING * mobility * (fraction - mean_c)

def divergence(chemical_pad, mobility_pad):
    chemical = inner_part(chemical_pad)
    mobility = inner_part(mobility_pad)
    summed = jnp.zeros_like(chemical)
    for beside, near_mob in zip(shifted(chemical_pad), shifted(mobility_pad)):
        summed = summed + 0.5 * (near_mob + mobility) * (beside - chemical)
    return summed

def wear_down(amplitude, fraction, mobility, mean_c):
    energy = 0.5 * STRAIN_COUPLING * mobility * (fraction - mean_c) * (fraction - mean_c)
    return amplitude * (1.0 - DAMAGE_RATE * jnp.maximum(energy - ENERGY_CRITICAL, 0.0))

def pool_four(field):
    size_x, size_y, size_z = field.shape
    return field.reshape(size_x // 4, 4, size_y // 4, 4, size_z // 4, 4).mean(axis=(1, 3, 5))

def conv_layer(activation, weight, bias_term):
    padded = jnp.pad(activation, ((0, 0), (1, 1), (1, 1), (1, 1)))
    size_x, size_y, size_z = activation.shape[1:]
    summed = jnp.zeros((weight.shape[1], size_x, size_y, size_z), jnp.float32)
    weights_wide = weight.astype(jnp.float32)
    for offset_x in range(3):
        for offset_y in range(3):
            for offset_z in range(3):
                slot = 9 * offset_x + 3 * offset_y + offset_z
                window = padded[:, offset_x:offset_x + size_x, offset_y:offset_y + size_y, offset_z:offset_z + size_z]
                summed = summed + jnp.einsum('oc,cxyz->oxyz', weights_wide[slot], window.astype(jnp.float32))
    return summed + bias_term[:, None, None, None]

def reference(concentration, damage, labels, w_first, b_first, w_second, b_second, w_third, b_third):
    factor = phase_factor(labels)
    root_factor = jnp.sqrt(factor)
    fraction = concentration
    amplitude = root_factor * (1.0 - damage)
    flux_sum = jnp.zeros_like(fraction)
    for step_index in range(STEPS):
        mobility = amplitude * amplitude
        mean_c = jnp.sum(mobility * fraction) / jnp.sum(mobility)
        mobility_pad = jnp.pad(mobility, 1, mode='wrap')
        chemical = potential(jnp.pad(fraction, 1, mode='wrap'), mobility_pad, mean_c)
        flux_sum = divergence(jnp.pad(chemical, 1, mode='wrap'), mobility_pad)
        amplitude = wear_down(amplitude, fraction, mobility, mean_c)
        fraction = fraction + TIME_STEP * flux_sum
    damage_field = 1.0 - amplitude / root_factor
    pooled = jnp.stack([pool_four(fraction), pool_four(damage_field), pool_four(amplitude * amplitude), pool_four(factor)]).astype(jnp.bfloat16)
    first_maps = jax.nn.gelu(conv_layer(pooled, w_first, b_first)).astype(jnp.bfloat16)
    second_maps = jax.nn.gelu(conv_layer(first_maps, w_second, b_second)).astype(jnp.bfloat16)
    crack_score = conv_layer(second_maps, w_third, b_third)[0]
    return (fraction, damage_field, flux_sum, crack_score)
```

```python
import jax
import jax.numpy as jnp
import numpy as np
from jax import lax
from jax.experimental import pallas as pl
from jax.experimental.pallas import tpu as pltpu
from jax.sharding import PartitionSpec as P

F32 = jnp.float32
WELL_HEIGHT = 1.0
STRAIN_COUPLING = 4.0
TIME_STEP = 0.01
DAMAGE_RATE = 0.8
ENERGY_CRITICAL = 0.02

OFF = 16
A_LOW, A_SPAN = 0.0, 1.0
B_LOW, B_SPAN = -1.1, 3.1


def to_code(x, low, span):
    v = (x - low) * (65535.0 / span) - 32768.0
    v = jnp.clip(jnp.round(v), -32768.0, 32767.0)
    return v.astype(jnp.int32).astype(jnp.int16)


def from_code(q, low, span):
    return (q.astype(jnp.int32).astype(F32) + 32768.0) * (span / 65535.0) + low


def call(kernel, outs, *args):
    return pl.pallas_call(
        kernel,
        out_shape=[jax.ShapeDtypeStruct(s, t) for s, t in outs],
        compiler_params=pltpu.CompilerParams(vmem_limit_bytes=48 * 1024 * 1024),
    )(*args)


def chunks(start, stop, size):
    return [(r, min(size, stop - r)) for r in range(start, stop, size)]


def by_label(labels, values):
    return jnp.where(labels == 0, values[0], jnp.where(labels == 1, values[1], values[2])).astype(F32)


FACTORS = (1.0, 0.3, 0.05)
ROOTS = tuple(float(np.sqrt(np.float32(v))) for v in FACTORS)


def fold(x):
    return x.reshape(x.shape[0] // 8, 8, x.shape[1]).sum(0)


def first_kernel(c_ref, d_ref, l_ref, amp_ref, lo_ref, hi_ref, sum_ref):
    nx, ny, nz = c_ref.shape
    top = jnp.zeros((8, nz), F32)
    bottom = jnp.zeros((8, nz), F32)
    for x in range(nx):
        for r, n in chunks(0, ny, 48):
            f = c_ref[x, r:r + n, :]
            a = by_label(l_ref[x, r:r + n, :], ROOTS) * (1.0 - d_ref[x, r:r + n, :])
            amp_ref[x, r:r + n, :] = a
            m = a * a
            top = top + fold(m * f)
            bottom = bottom + fold(m)
            if x < 2:
                lo_ref[x, r:r + n, :] = to_code(f, A_LOW, A_SPAN)
            if x >= nx - 2:
                hi_ref[nx - 1 - x, r:r + n, :] = to_code(f, A_LOW, A_SPAN)
            if x == 0:
                lo_ref[2, r:r + n, :] = to_code(a, A_LOW, A_SPAN)
            if x == nx - 1:
                hi_ref[2, r:r + n, :] = to_code(a, A_LOW, A_SPAN)
    sum_ref[0:8, :] = top
    sum_ref[8:16, :] = bottom


def edge_rows(f_ref, amp_ref, lo_ref, hi_ref, s_ref, out_ref, low, span):
    nx, ny, nz = f_ref.shape
    low_rows = [from_code(r[0, 0:16, :], low, span)[0:1] for r in (lo_ref, hi_ref)]
    high_rows = [from_code(r[0, ny - 16:ny, :], low, span)[15:16] for r in (lo_ref, hi_ref)]
    for side, first, second, beside in ((0, 0, 1, low_rows), (1, ny - 1, ny - 2, high_rows)):
        for x in range(nx):
            out_ref[side, 2 * x:2 * x + 1, :] = f_ref[x, first:first + 1, :]
            out_ref[side, 2 * x + 1:2 * x + 2, :] = f_ref[x, second:second + 1, :]
            if amp_ref is not None:
                out_ref[side, 10 + x:11 + x, :] = amp_ref[x, first:first + 1, :]
        out_ref[side, 8:9, :] = beside[0]
        out_ref[side, 9:10, :] = beside[1]
        out_ref[side, 16:32, :] = s_ref[...]


def edge_rows_a(f_ref, amp_ref, lo_ref, hi_ref, s_ref, out_ref):
    edge_rows(f_ref, amp_ref, lo_ref, hi_ref, s_ref, out_ref, A_LOW, A_SPAN)


def edge_rows_b(f_ref, lo_ref, hi_ref, s_ref, out_ref):
    edge_rows(f_ref, None, lo_ref, hi_ref, s_ref, out_ref, B_LOW, B_SPAN)


def assemble(f_ref, amp_ref, lo_ref, hi_ref, yr_ref, s_ref, pad_ref, apad_ref, zp_ref, low, span, add):
    nx, ny, nz = f_ref.shape
    end = OFF + ny
    lane = lax.broadcasted_iota(jnp.int32, (1, nz), 1)
    outer = (lane < 16) | (lane >= nz - 16)

    def pack(f, a):
        return f if a is None else jnp.where(outer, f, pltpu.roll(a, nz // 2, 1))

    for p, ref in ((0, lo_ref), (nx + 3, hi_ref)):
        for r, n in chunks(0, ny, 48):
            pad_ref[p, OFF + r:OFF + r + n, :] = from_code(ref[1, r:r + n, :], low, span)
    for p, ref in ((1, lo_ref), (nx + 2, hi_ref)):
        for r, n in chunks(0, ny, 48):
            f = from_code(ref[0, r:r + n, :], low, span)
            pad_ref[p, OFF + r:OFF + r + n, :] = f
            if amp_ref is not None:
                apad_ref[p - 1, OFF + r:OFF + r + n, :] = from_code(ref[2, r:r + n, :], low, span)
            zp_ref[p - 1, OFF + r:OFF + r + n, :] = f
    for p, k in ((1, 8), (nx + 2, 9)):
        pad_ref[p, OFF - 1:OFF, :] = yr_ref[1, k:k + 1, :]
        pad_ref[p, end:end + 1, :] = yr_ref[0, k:k + 1, :]
    for x in range(nx):
        for r, n in chunks(0, ny, 48):
            f = f_ref[x, r:r + n, :]
            a = None
            if amp_ref is not None:
                a = amp_ref[x, r:r + n, :]
                apad_ref[x + 1, OFF + r:OFF + r + n, :] = a
            pad_ref[x + 2, OFF + r:OFF + r + n, :] = f
            zp_ref[x + 1, OFF + r:OFF + r + n, :] = pack(f, a)
        for side, near, far in ((1, OFF - 1, OFF - 2), (0, end, end + 1)):
            f = yr_ref[side, 2 * x:2 * x + 1, :]
            pad_ref[x + 2, near:near + 1, :] = f
            pad_ref[x + 2, far:far + 1, :] = yr_ref[side, 2 * x + 1:2 * x + 2, :]
            if amp_ref is not None:
                apad_ref[x + 1, near:near + 1, :] = yr_ref[side, 10 + x:11 + x, :]
            zp_ref[x + 1, near:near + 1, :] = f
    s = s_ref[...]
    if add:
        s = s + yr_ref[0, 16:32, :]
    zp_ref[0, 0:16, :] = s
    pad_ref[0, 0:16, :] = s


def assemble_a(add):
    def kernel(f_ref, amp_ref, lo_ref, hi_ref, yr_ref, s_ref, pad_ref, apad_ref, zp_ref):
        assemble(f_ref, amp_ref, lo_ref, hi_ref, yr_ref, s_ref, pad_ref, apad_ref, zp_ref, A_LOW, A_SPAN, add)
    return kernel


def assemble_b(add):
    def kernel(f_ref, lo_ref, hi_ref, yr_ref, s_ref, pad_ref, zp_ref):
        assemble(f_ref, None, lo_ref, hi_ref, yr_ref, s_ref, pad_ref, None, zp_ref, B_LOW, B_SPAN, add)
    return kernel


def weighted_mean(pad_ref, zr_ref, add):
    s = pad_ref[0, 0:16, :]
    if add:
        s = s + zr_ref[0, 0:16, :]
    return jnp.sum(s[0:8], keepdims=True) / jnp.sum(s[8:16], keepdims=True)


def chem_of(f, m, around, mean):
    well = 2.0 * WELL_HEIGHT * f * (1.0 - f) * (1.0 - 2.0 * f)
    return well + 6.0 * f - around + STRAIN_COUPLING * m * (f - mean)


def worn(a, m, f, mean):
    e = f - mean
    energy = 0.5 * STRAIN_COUPLING * m * e * e
    return a * (1.0 - DAMAGE_RATE * jnp.maximum(energy - ENERGY_CRITICAL, 0.0))


class Geometry:
    def __init__(self, nx, ny, nz):
        self.nx, self.ny, self.nz = nx, ny, nz
        self.lane = lax.broadcasted_iota(jnp.int32, (1, nz), 1)
        self.first = self.lane == 0
        self.last = self.lane == nz - 1

    def before(self, own, other):
        return pltpu.roll(jnp.where(self.last, other, own), 1, 1)

    def after(self, own, other):
        return pltpu.roll(jnp.where(self.first, other, own), self.nz - 1, 1)


def chemistry(g, pad_ref, mob_ref, mobe_ref, zr_ref, chem_ref, cheme_ref, mean):
    nx, ny = g.nx, g.ny
    for p in range(nx + 2):
        inside = 1 <= p <= nx
        rows = chunks(OFF - 8, OFF + ny + 8, 32) if inside else chunks(OFF, OFF + ny, 48)
        for r, n in rows:
            f = pad_ref[p + 1, r:r + n, :]
            e = zr_ref[p, r:r + n, :]
            around = (pad_ref[p, r:r + n, :] + pad_ref[p + 2, r:r + n, :]
                      + pad_ref[p + 1, r - 1:r - 1 + n, :] + pad_ref[p + 1, r + 1:r + 1 + n, :]
                      + g.before(f, e) + g.after(f, e))
            chem_ref[p, r:r + n, :] = chem_of(f, mob_ref[p, r:r + n, :], around, mean)
        if inside:
            for r, n in chunks(OFF, OFF + ny, 48):
                f = pad_ref[p + 1, r:r + n, :]
                e = zr_ref[p, r:r + n, :]
                around = (zr_ref[p - 1, r:r + n, :] + zr_ref[p + 1, r:r + n, :]
                          + zr_ref[p, r - 1:r - 1 + n, :] + zr_ref[p, r + 1:r + 1 + n, :]
                          + g.before(e, f) + g.after(e, f))
                cheme_ref[p - 1, r - OFF:r - OFF + n, :] = chem_of(
                    e, mobe_ref[p - 1, r - OFF:r - OFF + n, :], around, mean)


def flux_of(g, x, r, n, mob_ref, mobe_ref, chem_ref, cheme_ref):
    p = x + 1
    m = mob_ref[p, r:r + n, :]
    q = chem_ref[p, r:r + n, :]
    me = mobe_ref[x, r - OFF:r - OFF + n, :]
    qe = cheme_ref[x, r - OFF:r - OFF + n, :]
    total = None
    for nm, nq in (
        (mob_ref[p - 1, r:r + n, :], chem_ref[p - 1, r:r + n, :]),
        (mob_ref[p + 1, r:r + n, :], chem_ref[p + 1, r:r + n, :]),
        (mob_ref[p, r - 1:r - 1 + n, :], chem_ref[p, r - 1:r - 1 + n, :]),
        (mob_ref[p, r + 1:r + 1 + n, :], chem_ref[p, r + 1:r + 1 + n, :]),
        (g.before(m, me), g.before(q, qe)),
        (g.after(m, me), g.after(q, qe)),
    ):
        term = (nm + m) * (nq - q)
        total = term if total is None else total + term
    return m, 0.5 * total


def step_a(add):
    def kernel(pad_ref, apad_ref, zr_ref, f2_ref, a2_ref, ae2_ref, lo_ref, hi_ref, sum_ref,
               mob_ref, mobe_ref, chem_ref, cheme_ref):
        nx, ny, nz = f2_ref.shape
        g = Geometry(nx, ny, nz)
        mean = weighted_mean(pad_ref, zr_ref, add)
        for p in range(nx + 2):
            inside = 1 <= p <= nx
            rows = chunks(OFF - 8, OFF + ny + 8, 32) if inside else chunks(OFF, OFF + ny, 48)
            for r, n in rows:
                a = apad_ref[p, r:r + n, :]
                m = a * a
                mob_ref[p, r:r + n, :] = m
                a2_ref[p, r:r + n, :] = worn(a, m, pad_ref[p + 1, r:r + n, :], mean)
            if inside:
                for r, n in chunks(OFF, OFF + ny, 48):
                    e = zr_ref[p, r:r + n, :]
                    a = pltpu.roll(e, nz // 2, 1)
                    m = a * a
                    mobe_ref[p - 1, r - OFF:r - OFF + n, :] = m
                    ae2_ref[p - 1, r - OFF:r - OFF + n, :] = worn(a, m, e, mean)
        chemistry(g, pad_ref, mob_ref, mobe_ref, zr_ref, chem_ref, cheme_ref, mean)
        top = jnp.zeros((8, nz), F32)
        bottom = jnp.zeros((8, nz), F32)
        for x in range(nx):
            for r, n in chunks(OFF, OFF + ny, 48):
                _, flux = flux_of(g, x, r, n, mob_ref, mobe_ref, chem_ref, cheme_ref)
                f = pad_ref[x + 2, r:r + n, :] + TIME_STEP * flux
                s = slice(r - OFF, r - OFF + n)
                f2_ref[x, s, :] = f
                a = a2_ref[x + 1, r:r + n, :]
                m = a * a
                top = top + fold(m * f)
                bottom = bottom + fold(m)
                if x < 2:
                    lo_ref[x, s, :] = to_code(f, B_LOW, B_SPAN)
                if x >= nx - 2:
                    hi_ref[nx - 1 - x, s, :] = to_code(f, B_LOW, B_SPAN)
        sum_ref[0:8, :] = top
        sum_ref[8:16, :] = bottom
    return kernel


def step_b(add):
    def kernel(pad_ref, a2_ref, ae2_ref, zr_ref, l_ref, f3_ref, dmg_ref, flux_ref, pool_ref,
               mob_ref, mobe_ref, chem_ref, cheme_ref, pool_scr):
        nx, ny, nz = f3_ref.shape
        g = Geometry(nx, ny, nz)
        mean = weighted_mean(pad_ref, zr_ref, add)
        for p in range(nx + 2):
            inside = 1 <= p <= nx
            rows = chunks(OFF - 8, OFF + ny + 8, 32) if inside else chunks(OFF, OFF + ny, 48)
            for r, n in rows:
                a = a2_ref[p, r:r + n, :]
                mob_ref[p, r:r + n, :] = a * a
            if inside:
                for r, n in chunks(0, ny, 48):
                    a = ae2_ref[p - 1, r:r + n, :]
                    mobe_ref[p - 1, r:r + n, :] = a * a
        chemistry(g, pad_ref, mob_ref, mobe_ref, zr_ref, chem_ref, cheme_ref, mean)
        for r, n in chunks(OFF, OFF + ny, 48):
            s = slice(r - OFF, r - OFF + n)
            pooled = [None] * 4
            for x in range(nx):
                m, flux = flux_of(g, x, r, n, mob_ref, mobe_ref, chem_ref, cheme_ref)
                f0 = pad_ref[x + 2, r:r + n, :]
                f = f0 + TIME_STEP * flux
                a = worn(a2_ref[x + 1, r:r + n, :], m, f0, mean)
                labels = l_ref[x, s, :]
                k = by_label(labels, FACTORS)
                dmg = 1.0 - a * by_label(labels, tuple(1.0 / v for v in ROOTS))
                f3_ref[x, s, :] = f
                dmg_ref[x, s, :] = dmg
                flux_ref[x, s, :] = flux
                for i, v in enumerate((f, dmg, a * a, k)):
                    pooled[i] = v if pooled[i] is None else pooled[i] + v
            for i in range(4):
                pool_scr[i, s, :] = pooled[i]
        py, pz = ny // 4, nz // 4
        zin = lax.broadcasted_iota(jnp.int32, (nz, 4 * pz), 0)
        out = lax.broadcasted_iota(jnp.int32, (nz, 4 * pz), 1)
        total = jnp.zeros((py, 4 * pz), F32)
        for i in range(4):
            rows = (pool_scr[i, pl.ds(0, py, stride=4), :] + pool_scr[i, pl.ds(1, py, stride=4), :]
                    + pool_scr[i, pl.ds(2, py, stride=4), :] + pool_scr[i, pl.ds(3, py, stride=4), :])
            pick = jnp.where((zin // 4 == out // 4) & (out % 4 == i), 1.0 / 64.0, 0.0).astype(F32)
            total = total + jnp.dot(rows, pick, precision=lax.Precision.HIGHEST, preferred_element_type=F32)
        pool_ref[0:py, :] = total.astype(jnp.bfloat16)
    return kernel


def ring(axis, shift):
    count = lax.axis_size(axis)
    return [(i, (i + shift) % count) for i in range(count)]


def pair_sum(s, axis):
    count = lax.axis_size(axis)
    if count & (count - 1):
        return lax.psum(s, axis)
    bit = 1
    while bit < count:
        s = s + lax.ppermute(s, axis, [(i, i ^ bit) for i in range(count)])
        bit *= 2
    return s


def both_sides(pay, axis):
    if lax.axis_size(axis) == 2:
        return lax.ppermute(pay, axis, ring(axis, 1))
    return jnp.stack([lax.ppermute(pay[0], axis, ring(axis, -1)), lax.ppermute(pay[1], axis, ring(axis, 1))])


def z_neighbour(pay, axis):
    if lax.axis_size(axis) == 2:
        return lax.ppermute(pay, axis, ring(axis, 1))
    above = lax.ppermute(pay, axis, ring(axis, -1))
    below = lax.ppermute(pay, axis, ring(axis, 1))
    lane = lax.broadcasted_iota(jnp.int32, pay.shape, pay.ndim - 1)
    quarter = pay.shape[-1] // 4
    return jnp.where((lane < quarter) | ((lane >= 2 * quarter) & (lane < 3 * quarter)), above, below)


def reduce_ahead(s):
    for axis in ("gx",) + tuple(a for a in ("gy", "gz") if lax.axis_size(a) != 2):
        s = pair_sum(s, axis)
    return s


def body(concentration, damage, labels, w_first, b_first, w_second, b_second, w_third, b_third):
    nx, ny, nz = concentration.shape
    rows = ny + 2 * OFF
    plane = (ny, nz)
    ride_y = lax.axis_size("gy") == 2
    ride_z = lax.axis_size("gz") == 2
    i16 = jnp.int16
    scratch = [
        pltpu.VMEM((nx + 2, rows, nz), F32), pltpu.VMEM((nx,) + plane, F32),
        pltpu.VMEM((nx + 2, rows, nz), F32), pltpu.VMEM((nx,) + plane, F32),
    ]

    def heavy(kernel, outs, extra, *args):
        return pl.pallas_call(
            kernel,
            out_shape=[jax.ShapeDtypeStruct(s, t) for s, t in outs],
            scratch_shapes=scratch + extra,
            compiler_params=pltpu.CompilerParams(vmem_limit_bytes=48 * 1024 * 1024),
        )(*args)

    amp, lo, hi, sums = call(
        first_kernel,
        [((nx,) + plane, F32), ((3,) + plane, i16), ((3,) + plane, i16), ((16, nz), F32)],
        concentration, damage, labels)
    from_lo = lax.ppermute(hi, "gx", ring("gx", 1))
    from_hi = lax.ppermute(lo, "gx", ring("gx", -1))
    sums = reduce_ahead(sums)
    (ypay,) = call(edge_rows_a, [((2, 32, nz), F32)], concentration, amp, from_lo, from_hi, sums)
    yr = both_sides(ypay, "gy")
    pad, apad, zpay = call(
        assemble_a(ride_y),
        [((nx + 4, rows, nz), F32), ((nx + 2, rows, nz), F32), ((nx + 2, rows, nz), F32)],
        concentration, amp, from_lo, from_hi, yr, sums)
    zr = z_neighbour(zpay, "gz")
    f2, a2, ae2, lo, hi, sums = heavy(
        step_a(ride_z),
        [((nx,) + plane, F32), ((nx + 2, rows, nz), F32), ((nx,) + plane, F32),
         ((2,) + plane, i16), ((2,) + plane, i16), ((16, nz), F32)],
        [], pad, apad, zr)

    from_lo = lax.ppermute(hi, "gx", ring("gx", 1))
    from_hi = lax.ppermute(lo, "gx", ring("gx", -1))
    sums = reduce_ahead(sums)
    (ypay,) = call(edge_rows_b, [((2, 32, nz), F32)], f2, from_lo, from_hi, sums)
    yr = both_sides(ypay, "gy")
    pad, zpay = call(
        assemble_b(ride_y),
        [((nx + 4, rows, nz), F32), ((nx + 2, rows, nz), F32)],
        f2, from_lo, from_hi, yr, sums)
    zr = z_neighbour(zpay, "gz")
    fraction, damage_field, flux_sum, pooled = heavy(
        step_b(ride_z),
        [((nx,) + plane, F32), ((nx,) + plane, F32), ((nx,) + plane, F32), ((ny // 4 + 4, nz), jnp.bfloat16)],
        [pltpu.VMEM((4,) + plane, F32)],
        pad, a2, ae2, zr, labels)
    crack_score = detector(pooled, w_first, b_first, w_second, b_second, w_third, b_third, ny // 4, nz // 4)
    return (fraction, damage_field, flux_sum, crack_score)


def extended(block, sides, width):
    for axis, dim in sides:
        count = lax.axis_size(axis)
        forward = [(i, i + 1) for i in range(count - 1)]
        backward = [(target, source) for source, target in forward]
        low = lax.ppermute(
            lax.slice_in_dim(block, block.shape[dim] - width, None, axis=dim), axis, forward)
        high = lax.ppermute(lax.slice_in_dim(block, 0, width, axis=dim), axis, backward)
        block = jnp.concatenate([low, block, high], axis=dim)
    return block


def apply_conv(padded, weight, bias_term):
    size_x = padded.shape[1] - 2
    size_y = padded.shape[2] - 2
    size_z = padded.shape[3] - 2
    pieces = []
    for i in range(3):
        for j in range(3):
            for l in range(3):
                pieces.append(padded[:, i:i + size_x, j:j + size_y, l:l + size_z])
    columns = jnp.stack(pieces)
    summed = jnp.einsum("koc,kcxyz->oxyz", weight, columns, preferred_element_type=F32)
    return summed + bias_term[:, None, None, None]


def detector(pooled, w_first, b_first, w_second, b_second, w_third, b_third, py, pz):
    maps = pooled[:py].reshape(py, pz, 4).transpose(2, 0, 1)[:, None]

    def slab_layer(activation, weight, bias_term):
        return apply_conv(extended(activation, (("gx", 1), ("gy", 2), ("gz", 3)), 1), weight, bias_term)

    maps = jax.nn.gelu(slab_layer(maps, w_first, b_first)).astype(jnp.bfloat16)
    maps = jax.nn.gelu(slab_layer(maps, w_second, b_second)).astype(jnp.bfloat16)
    return slab_layer(maps, w_third, b_third)[0]


def solution(mesh):
    slab = P(("groups", "gx"), "gy", "gz")
    return jax.shard_map(
        body,
        mesh=mesh,
        in_specs=(slab, slab, slab, P(), P(), P(), P(), P(), P()),
        out_specs=(slab, slab, slab, slab),
        check_vma=False,
    )
```

```python
import jax
import jax.numpy as jnp
import numpy as np
from jax import lax
from jax.experimental import pallas as pl
from jax.experimental.pallas import tpu as pltpu
from jax.sharding import PartitionSpec as P

F32 = jnp.float32
WELL_HEIGHT = 1.0
STRAIN_COUPLING = 4.0
TIME_STEP = 0.01
DAMAGE_RATE = 0.8
ENERGY_CRITICAL = 0.02

OFF = 16
A_LOW, A_SPAN = 0.0, 1.0
B_LOW, B_SPAN = -1.1, 3.1


def to_code(x, low, span):
    v = (x - low) * (65535.0 / span) - 32768.0
    v = jnp.clip(jnp.round(v), -32768.0, 32767.0)
    return v.astype(jnp.int32).astype(jnp.int16)


def from_code(q, low, span):
    return (q.astype(jnp.int32).astype(F32) + 32768.0) * (span / 65535.0) + low


def call(kernel, outs, *args):
    return pl.pallas_call(
        kernel,
        out_shape=[jax.ShapeDtypeStruct(s, t) for s, t in outs],
        compiler_params=pltpu.CompilerParams(vmem_limit_bytes=48 * 1024 * 1024),
    )(*args)


def chunks(start, stop, size):
    return [(r, min(size, stop - r)) for r in range(start, stop, size)]


def by_label(labels, values):
    return jnp.where(labels == 0, values[0], jnp.where(labels == 1, values[1], values[2])).astype(F32)


FACTORS = (1.0, 0.3, 0.05)
ROOTS = tuple(float(np.sqrt(np.float32(v))) for v in FACTORS)


def fold(x):
    return x.reshape(x.shape[0] // 8, 8, x.shape[1]).sum(0)


def first_kernel(c_ref, d_ref, l_ref, amp_ref, lo_ref, hi_ref, sum_ref):
    nx, ny, nz = c_ref.shape
    top = jnp.zeros((8, nz), F32)
    bottom = jnp.zeros((8, nz), F32)
    for x in range(nx):
        for r, n in chunks(0, ny, 48):
            f = c_ref[x, r:r + n, :]
            a = by_label(l_ref[x, r:r + n, :], ROOTS) * (1.0 - d_ref[x, r:r + n, :])
            amp_ref[x, r:r + n, :] = a
            m = a * a
            top = top + fold(m * f)
            bottom = bottom + fold(m)
            if x < 2:
                lo_ref[x, r:r + n, :] = to_code(f, A_LOW, A_SPAN)
            if x >= nx - 2:
                hi_ref[nx - 1 - x, r:r + n, :] = to_code(f, A_LOW, A_SPAN)
            if x == 0:
                lo_ref[2, r:r + n, :] = to_code(a, A_LOW, A_SPAN)
            if x == nx - 1:
                hi_ref[2, r:r + n, :] = to_code(a, A_LOW, A_SPAN)
    sum_ref[0:8, :] = top
    sum_ref[8:16, :] = bottom


def edge_rows(f_ref, amp_ref, lo_ref, hi_ref, s_ref, out_ref, low, span):
    nx, ny, nz = f_ref.shape
    low_rows = [from_code(r[0, 0:16, :], low, span)[0:1] for r in (lo_ref, hi_ref)]
    high_rows = [from_code(r[0, ny - 16:ny, :], low, span)[15:16] for r in (lo_ref, hi_ref)]
    for side, first, second, beside in ((0, 0, 1, low_rows), (1, ny - 1, ny - 2, high_rows)):
        for x in range(nx):
            out_ref[side, 2 * x:2 * x + 1, :] = f_ref[x, first:first + 1, :]
            out_ref[side, 2 * x + 1:2 * x + 2, :] = f_ref[x, second:second + 1, :]
            if amp_ref is not None:
                out_ref[side, 10 + x:11 + x, :] = amp_ref[x, first:first + 1, :]
        out_ref[side, 8:9, :] = beside[0]
        out_ref[side, 9:10, :] = beside[1]
        out_ref[side, 16:32, :] = s_ref[...]


def edge_rows_a(f_ref, amp_ref, lo_ref, hi_ref, s_ref, out_ref):
    edge_rows(f_ref, amp_ref, lo_ref, hi_ref, s_ref, out_ref, A_LOW, A_SPAN)


def edge_rows_b(f_ref, lo_ref, hi_ref, s_ref, out_ref):
    edge_rows(f_ref, None, lo_ref, hi_ref, s_ref, out_ref, B_LOW, B_SPAN)


def assemble(f_ref, amp_ref, lo_ref, hi_ref, yr_ref, s_ref, pad_ref, apad_ref, zp_ref, low, span, add):
    nx, ny, nz = f_ref.shape
    end = OFF + ny
    lane = lax.broadcasted_iota(jnp.int32, (1, nz), 1)
    outer = (lane < 16) | (lane >= nz - 16)

    def pack(f, a):
        return f if a is None else jnp.where(outer, f, pltpu.roll(a, nz // 2, 1))

    for p, ref in ((0, lo_ref), (nx + 3, hi_ref)):
        for r, n in chunks(0, ny, 48):
            pad_ref[p, OFF + r:OFF + r + n, :] = from_code(ref[1, r:r + n, :], low, span)
    for p, ref in ((1, lo_ref), (nx + 2, hi_ref)):
        for r, n in chunks(0, ny, 48):
            f = from_code(ref[0, r:r + n, :], low, span)
            pad_ref[p, OFF + r:OFF + r + n, :] = f
            if amp_ref is not None:
                apad_ref[p - 1, OFF + r:OFF + r + n, :] = from_code(ref[2, r:r + n, :], low, span)
            zp_ref[p - 1, OFF + r:OFF + r + n, :] = f
    for p, k in ((1, 8), (nx + 2, 9)):
        pad_ref[p, OFF - 1:OFF, :] = yr_ref[1, k:k + 1, :]
        pad_ref[p, end:end + 1, :] = yr_ref[0, k:k + 1, :]
    for x in range(nx):
        for r, n in chunks(0, ny, 48):
            f = f_ref[x, r:r + n, :]
            a = None
            if amp_ref is not None:
                a = amp_ref[x, r:r + n, :]
                apad_ref[x + 1, OFF + r:OFF + r + n, :] = a
            pad_ref[x + 2, OFF + r:OFF + r + n, :] = f
            zp_ref[x + 1, OFF + r:OFF + r + n, :] = pack(f, a)
        for side, near, far in ((1, OFF - 1, OFF - 2), (0, end, end + 1)):
            f = yr_ref[side, 2 * x:2 * x + 1, :]
            pad_ref[x + 2, near:near + 1, :] = f
            pad_ref[x + 2, far:far + 1, :] = yr_ref[side, 2 * x + 1:2 * x + 2, :]
            if amp_ref is not None:
                apad_ref[x + 1, near:near + 1, :] = yr_ref[side, 10 + x:11 + x, :]
            zp_ref[x + 1, near:near + 1, :] = f
    s = s_ref[...]
    if add:
        s = s + yr_ref[0, 16:32, :]
    zp_ref[0, 0:16, :] = s
    pad_ref[0, 0:16, :] = s


def assemble_a(add):
    def kernel(f_ref, amp_ref, lo_ref, hi_ref, yr_ref, s_ref, pad_ref, apad_ref, zp_ref):
        assemble(f_ref, amp_ref, lo_ref, hi_ref, yr_ref, s_ref, pad_ref, apad_ref, zp_ref, A_LOW, A_SPAN, add)
    return kernel


def assemble_b(add):
    def kernel(f_ref, lo_ref, hi_ref, yr_ref, s_ref, pad_ref, zp_ref):
        assemble(f_ref, None, lo_ref, hi_ref, yr_ref, s_ref, pad_ref, None, zp_ref, B_LOW, B_SPAN, add)
    return kernel


def weighted_mean(pad_ref, zr_ref, add):
    s = pad_ref[0, 0:16, :]
    if add:
        s = s + zr_ref[0, 0:16, :]
    return jnp.sum(s[0:8], keepdims=True) / jnp.sum(s[8:16], keepdims=True)


def chem_of(f, m, around, mean):
    well = 2.0 * WELL_HEIGHT * f * (1.0 - f) * (1.0 - 2.0 * f)
    return well + 6.0 * f - around + STRAIN_COUPLING * m * (f - mean)


def worn(a, m, f, mean):
    e = f - mean
    energy = 0.5 * STRAIN_COUPLING * m * e * e
    return a * (1.0 - DAMAGE_RATE * jnp.maximum(energy - ENERGY_CRITICAL, 0.0))


class Geometry:
    def __init__(self, nx, ny, nz):
        self.nx, self.ny, self.nz = nx, ny, nz
        self.lane = lax.broadcasted_iota(jnp.int32, (1, nz), 1)
        self.first = self.lane == 0
        self.last = self.lane == nz - 1

    def before(self, own, other):
        return pltpu.roll(jnp.where(self.last, other, own), 1, 1)

    def after(self, own, other):
        return pltpu.roll(jnp.where(self.first, other, own), self.nz - 1, 1)


def chemistry(g, pad_ref, mob_ref, mobe_ref, zr_ref, chem_ref, cheme_ref, mean):
    nx, ny = g.nx, g.ny
    for p in range(nx + 2):
        inside = 1 <= p <= nx
        rows = chunks(OFF - 8, OFF + ny + 8, 32) if inside else chunks(OFF, OFF + ny, 48)
        for r, n in rows:
            f = pad_ref[p + 1, r:r + n, :]
            e = zr_ref[p, r:r + n, :]
            around = (pad_ref[p, r:r + n, :] + pad_ref[p + 2, r:r + n, :]
                      + pad_ref[p + 1, r - 1:r - 1 + n, :] + pad_ref[p + 1, r + 1:r + 1 + n, :]
                      + g.before(f, e) + g.after(f, e))
            chem_ref[p, r:r + n, :] = chem_of(f, mob_ref[p, r:r + n, :], around, mean)
        if inside:
            for r, n in chunks(OFF, OFF + ny, 48):
                f = pad_ref[p + 1, r:r + n, :]
                e = zr_ref[p, r:r + n, :]
                around = (zr_ref[p - 1, r:r + n, :] + zr_ref[p + 1, r:r + n, :]
                          + zr_ref[p, r - 1:r - 1 + n, :] + zr_ref[p, r + 1:r + 1 + n, :]
                          + g.before(e, f) + g.after(e, f))
                cheme_ref[p - 1, r - OFF:r - OFF + n, :] = chem_of(
                    e, mobe_ref[p - 1, r - OFF:r - OFF + n, :], around, mean)


def flux_of(g, x, r, n, mob_ref, mobe_ref, chem_ref, cheme_ref):
    p = x + 1
    m = mob_ref[p, r:r + n, :]
    q = chem_ref[p, r:r + n, :]
    me = mobe_ref[x, r - OFF:r - OFF + n, :]
    qe = cheme_ref[x, r - OFF:r - OFF + n, :]
    total = None
    for nm, nq in (
        (mob_ref[p - 1, r:r + n, :], chem_ref[p - 1, r:r + n, :]),
        (mob_ref[p + 1, r:r + n, :], chem_ref[p + 1, r:r + n, :]),
        (mob_ref[p, r - 1:r - 1 + n, :], chem_ref[p, r - 1:r - 1 + n, :]),
        (mob_ref[p, r + 1:r + 1 + n, :], chem_ref[p, r + 1:r + 1 + n, :]),
        (g.before(m, me), g.before(q, qe)),
        (g.after(m, me), g.after(q, qe)),
    ):
        term = (nm + m) * (nq - q)
        total = term if total is None else total + term
    return m, 0.5 * total


def step_a(add):
    def kernel(pad_ref, apad_ref, zr_ref, f2_ref, a2_ref, ae2_ref, lo_ref, hi_ref, sum_ref,
               mob_ref, mobe_ref, chem_ref, cheme_ref):
        nx, ny, nz = f2_ref.shape
        g = Geometry(nx, ny, nz)
        mean = weighted_mean(pad_ref, zr_ref, add)
        for p in range(nx + 2):
            inside = 1 <= p <= nx
            rows = chunks(OFF - 8, OFF + ny + 8, 32) if inside else chunks(OFF, OFF + ny, 48)
            for r, n in rows:
                a = apad_ref[p, r:r + n, :]
                m = a * a
                mob_ref[p, r:r + n, :] = m
                a2_ref[p, r:r + n, :] = worn(a, m, pad_ref[p + 1, r:r + n, :], mean)
            if inside:
                for r, n in chunks(OFF, OFF + ny, 48):
                    e = zr_ref[p, r:r + n, :]
                    a = pltpu.roll(e, nz // 2, 1)
                    m = a * a
                    mobe_ref[p - 1, r - OFF:r - OFF + n, :] = m
                    ae2_ref[p - 1, r - OFF:r - OFF + n, :] = worn(a, m, e, mean)
        chemistry(g, pad_ref, mob_ref, mobe_ref, zr_ref, chem_ref, cheme_ref, mean)
        top = jnp.zeros((8, nz), F32)
        bottom = jnp.zeros((8, nz), F32)
        for x in range(nx):
            for r, n in chunks(OFF, OFF + ny, 48):
                _, flux = flux_of(g, x, r, n, mob_ref, mobe_ref, chem_ref, cheme_ref)
                f = pad_ref[x + 2, r:r + n, :] + TIME_STEP * flux
                s = slice(r - OFF, r - OFF + n)
                f2_ref[x, s, :] = f
                a = a2_ref[x + 1, r:r + n, :]
                m = a * a
                top = top + fold(m * f)
                bottom = bottom + fold(m)
                if x < 2:
                    lo_ref[x, s, :] = to_code(f, B_LOW, B_SPAN)
                if x >= nx - 2:
                    hi_ref[nx - 1 - x, s, :] = to_code(f, B_LOW, B_SPAN)
        sum_ref[0:8, :] = top
        sum_ref[8:16, :] = bottom
    return kernel


def step_b(add):
    def kernel(pad_ref, a2_ref, ae2_ref, zr_ref, l_ref, f3_ref, dmg_ref, flux_ref, pool_ref, edge_ref,
               mob_ref, mobe_ref, chem_ref, cheme_ref, pool_scr):
        nx, ny, nz = f3_ref.shape
        g = Geometry(nx, ny, nz)
        mean = weighted_mean(pad_ref, zr_ref, add)
        for p in range(nx + 2):
            inside = 1 <= p <= nx
            rows = chunks(OFF - 8, OFF + ny + 8, 32) if inside else chunks(OFF, OFF + ny, 48)
            for r, n in rows:
                a = a2_ref[p, r:r + n, :]
                mob_ref[p, r:r + n, :] = a * a
            if inside:
                for r, n in chunks(0, ny, 48):
                    a = ae2_ref[p - 1, r:r + n, :]
                    mobe_ref[p - 1, r:r + n, :] = a * a
        chemistry(g, pad_ref, mob_ref, mobe_ref, zr_ref, chem_ref, cheme_ref, mean)
        for r, n in chunks(OFF, OFF + ny, 48):
            s = slice(r - OFF, r - OFF + n)
            pooled = [None] * 4
            for x in range(nx):
                m, flux = flux_of(g, x, r, n, mob_ref, mobe_ref, chem_ref, cheme_ref)
                f0 = pad_ref[x + 2, r:r + n, :]
                f = f0 + TIME_STEP * flux
                a = worn(a2_ref[x + 1, r:r + n, :], m, f0, mean)
                labels = l_ref[x, s, :]
                k = by_label(labels, FACTORS)
                dmg = 1.0 - a * by_label(labels, tuple(1.0 / v for v in ROOTS))
                f3_ref[x, s, :] = f
                dmg_ref[x, s, :] = dmg
                flux_ref[x, s, :] = flux
                for i, v in enumerate((f, dmg, a * a, k)):
                    pooled[i] = v if pooled[i] is None else pooled[i] + v
            for i in range(4):
                pool_scr[i, s, :] = pooled[i]
        py, pz = ny // 4, nz // 4
        zin = lax.broadcasted_iota(jnp.int32, (nz, 4 * pz), 0)
        out = lax.broadcasted_iota(jnp.int32, (nz, 4 * pz), 1)
        total = jnp.zeros((py, 4 * pz), F32)
        for i in range(4):
            rows = (pool_scr[i, pl.ds(0, py, stride=4), :] + pool_scr[i, pl.ds(1, py, stride=4), :]
                    + pool_scr[i, pl.ds(2, py, stride=4), :] + pool_scr[i, pl.ds(3, py, stride=4), :])
            pick = jnp.where((zin // 4 == out // 4) & (out % 4 == i), 1.0 / 64.0, 0.0).astype(F32)
            total = total + jnp.dot(rows, pick, precision=lax.Precision.HIGHEST, preferred_element_type=F32)
        pool_ref[...] = total.astype(BF16)
        blank = jnp.zeros((13, 4 * pz), F32)
        edge_ref[0] = jnp.concatenate([total[0:3], blank]).astype(BF16)
        edge_ref[1] = jnp.concatenate([total[py - 3:py], blank]).astype(BF16)
    return kernel


def ring(axis, shift):
    count = lax.axis_size(axis)
    return [(i, (i + shift) % count) for i in range(count)]


def pair_sum(s, axis):
    count = lax.axis_size(axis)
    if count & (count - 1):
        return lax.psum(s, axis)
    bit = 1
    while bit < count:
        s = s + lax.ppermute(s, axis, [(i, i ^ bit) for i in range(count)])
        bit *= 2
    return s


def both_sides(pay, axis):
    if lax.axis_size(axis) == 2:
        return lax.ppermute(pay, axis, ring(axis, 1))
    return jnp.stack([lax.ppermute(pay[0], axis, ring(axis, -1)), lax.ppermute(pay[1], axis, ring(axis, 1))])


def z_neighbour(pay, axis, packed=True):
    if lax.axis_size(axis) == 2:
        return lax.ppermute(pay, axis, ring(axis, 1))
    above = lax.ppermute(pay, axis, ring(axis, -1))
    below = lax.ppermute(pay, axis, ring(axis, 1))
    lane = lax.broadcasted_iota(jnp.int32, pay.shape, pay.ndim - 1)
    part = pay.shape[-1] // (4 if packed else 2)
    return jnp.where(lane // part % 2 == 0, above, below)


def reduce_ahead(s):
    for axis in ("gx",) + tuple(a for a in ("gy", "gz") if lax.axis_size(a) != 2):
        s = pair_sum(s, axis)
    return s


def body(concentration, damage, labels, w_first, b_first, w_second, b_second, w_third, b_third):
    nx, ny, nz = concentration.shape
    rows = ny + 2 * OFF
    plane = (ny, nz)
    ride_y = lax.axis_size("gy") == 2
    ride_z = lax.axis_size("gz") == 2
    i16 = jnp.int16
    scratch = [
        pltpu.VMEM((nx + 2, rows, nz), F32), pltpu.VMEM((nx,) + plane, F32),
        pltpu.VMEM((nx + 2, rows, nz), F32), pltpu.VMEM((nx,) + plane, F32),
    ]

    def heavy(kernel, outs, extra, *args):
        return pl.pallas_call(
            kernel,
            out_shape=[jax.ShapeDtypeStruct(s, t) for s, t in outs],
            scratch_shapes=scratch + extra,
            compiler_params=pltpu.CompilerParams(vmem_limit_bytes=48 * 1024 * 1024),
        )(*args)

    amp, lo, hi, sums = call(
        first_kernel,
        [((nx,) + plane, F32), ((3,) + plane, i16), ((3,) + plane, i16), ((16, nz), F32)],
        concentration, damage, labels)
    from_lo = lax.ppermute(hi, "gx", ring("gx", 1))
    from_hi = lax.ppermute(lo, "gx", ring("gx", -1))
    sums = reduce_ahead(sums)
    (ypay,) = call(edge_rows_a, [((2, 32, nz), F32)], concentration, amp, from_lo, from_hi, sums)
    yr = both_sides(ypay, "gy")
    pad, apad, zpay = call(
        assemble_a(ride_y),
        [((nx + 4, rows, nz), F32), ((nx + 2, rows, nz), F32), ((nx + 2, rows, nz), F32)],
        concentration, amp, from_lo, from_hi, yr, sums)
    zr = z_neighbour(zpay, "gz")
    f2, a2, ae2, lo, hi, sums = heavy(
        step_a(ride_z),
        [((nx,) + plane, F32), ((nx + 2, rows, nz), F32), ((nx,) + plane, F32),
         ((2,) + plane, i16), ((2,) + plane, i16), ((16, nz), F32)],
        [], pad, apad, zr)

    from_lo = lax.ppermute(hi, "gx", ring("gx", 1))
    from_hi = lax.ppermute(lo, "gx", ring("gx", -1))
    sums = reduce_ahead(sums)
    (ypay,) = call(edge_rows_b, [((2, 32, nz), F32)], f2, from_lo, from_hi, sums)
    yr = both_sides(ypay, "gy")
    pad, zpay = call(
        assemble_b(ride_y),
        [((nx + 4, rows, nz), F32), ((nx + 2, rows, nz), F32)],
        f2, from_lo, from_hi, yr, sums)
    zr = z_neighbour(zpay, "gz")
    fraction, damage_field, flux_sum, pooled, edge = heavy(
        step_b(ride_z),
        [((nx,) + plane, F32), ((nx,) + plane, F32), ((nx,) + plane, F32), ((ny // 4, nz), BF16), ((2, 16, nz), BF16)],
        [pltpu.VMEM((4,) + plane, F32)],
        pad, a2, ae2, zr, labels)
    ids = jnp.stack([lax.axis_index(a) for a in ("gx", "gy", "gz")])
    crack_score = detector(pooled, edge, ids, w_first, b_first, w_second, b_second, w_third, b_third, ny // 4, nz // 4)
    return (fraction, damage_field, flux_sum, crack_score)


CH = 16
CIN = 4
TOP = 8
BF16 = jnp.bfloat16


def iota(shape, dim):
    return lax.broadcasted_iota(jnp.int32, shape, dim)


def lanes_for(n):
    return -(-n // 128) * 128


def one_hot(mask):
    return jnp.where(mask, 1.0, 0.0).astype(BF16)


def mm(a, b):
    return jnp.dot(a, b, preferred_element_type=F32)


def mm_nt(a, b):
    return lax.dot_general(a, b, (((1,), (1,)), ((), ())), preferred_element_type=F32)


def weight_kernel(w1_ref, w2_ref, w3_ref, b1_ref, b2_ref, t1_ref, t2_ref, t3_ref, bias_ref):
    k1 = t1_ref.shape[1] // 3
    n1 = t1_ref.shape[2]
    pz = k1 // (2 * CIN)
    spread = one_hot(iota((CH, n1), 1) % CH == iota((CH, n1), 0))
    pick_c = one_hot(iota((k1, CIN), 0) % CIN == iota((k1, CIN), 1))
    slot = iota((k1, n1), 0) // CIN
    z_in = jnp.where(slot < pz + pz // 2, slot, slot - 2 * pz)
    offset1 = z_in - iota((k1, n1), 1) // CH + 3
    k2 = t2_ref.shape[1] // 3
    n2 = t2_ref.shape[2]
    pick_o = one_hot(iota((k2, CH), 0) % CH == iota((k2, CH), 1))
    offset2 = iota((k2, n2), 0) // CH - iota((k2, n2), 1) // CH
    k3 = t3_ref.shape[1]
    n3 = t3_ref.shape[2]
    pick_3 = one_hot(iota((k3, CH), 0) % CH == iota((k3, CH), 1))
    offset3 = iota((k3, n3), 0) // CH - iota((k3, n3), 1) % pz
    part3 = iota((k3, n3), 1) // pz
    for i in range(3):
        for j in range(3):
            one = jnp.zeros((k1, n1), F32)
            two = jnp.zeros((k2, n2), F32)
            for l in range(3):
                tap = 9 * i + 3 * j + l
                wide = mm(mm_nt(pick_c, w1_ref[tap]).astype(BF16), spread)
                one = jnp.where(offset1 == l, wide, one)
                wide = mm(mm_nt(pick_o, w2_ref[tap]).astype(BF16), spread[:, :n2])
                two = jnp.where(offset2 == l, wide, two)
            t1_ref[i, j * k1:(j + 1) * k1, :] = one.astype(BF16)
            t2_ref[i, j * k2:(j + 1) * k2, :] = two.astype(BF16)
        three = jnp.zeros((k3, n3), F32)
        for j in range(3):
            for l in range(3):
                tap = 9 * i + 3 * j + l
                column = mm_nt(pick_3, jnp.broadcast_to(w3_ref[tap], (CH, CH)))[:, 0:1]
                three = jnp.where((offset3 == l) & (part3 == j), column, three)
        t3_ref[i] = three.astype(BF16)
    wide = spread.astype(F32)
    for k, ref in ((0, b1_ref), (1, b2_ref)):
        bias_ref[k:k + 1, :] = jnp.dot(ref[...], wide, precision=lax.Precision.HIGHEST, preferred_element_type=F32)


def gelu(x):
    return 0.5 * x * (1.0 + jnp.tanh(0.7978845608028654 * (x + 0.044715 * (x * x * x))))


def plane_kernel(py, y_count):
    def kernel(ids_ref, pool_ref, yr_ref, out_ref, scr_ref):
        iy = ids_ref[1]
        scr_ref[...] = jnp.zeros(scr_ref.shape, F32)
        scr_ref[TOP:TOP + py, :] = pool_ref[0:py, :].astype(F32)
        below = yr_ref[1].astype(F32)[0:3]
        above = yr_ref[0].astype(F32)[0:3]
        scr_ref[TOP - 3:TOP, :] = jnp.where(iy > 0, below, 0.0)
        scr_ref[TOP + py:TOP + py + 3, :] = jnp.where(iy < y_count - 1, above, 0.0)
        out_ref[...] = scr_ref[...].astype(BF16)
    return kernel


def conv_kernel(py, counts, shifts):
    x_count, y_count, z_count = counts
    n = len(shifts)

    def kernel(*refs):
        ids_ref, b3_ref = refs[:2]
        own = refs[2:3 + n]
        other = refs[3 + n:4 + 2 * n]
        t1_ref, t2_ref, t3_ref, bias_ref, out_ref = refs[4 + 2 * n:9 + 2 * n]
        in_ref, lhs1_ref, act1_ref, lhs2_ref, act2_ref, tail_ref = refs[9 + 2 * n:]
        ix, iy, iz = ids_ref[0], ids_ref[1], ids_ref[2]
        half = own[0].shape[1]
        pz = half // CIN
        rows = py + 4
        z_row = iota((1, half), 1) // CIN
        z_ok = ((z_row < pz // 2) & (iz < z_count - 1)) | ((z_row >= pz // 2) & (iz > 0))
        for w in range(7):
            o = w - 3
            k = 0 if o == 0 else 1 + shifts.index((-o) % x_count) if (-o) % x_count in shifts else None
            if k is None:
                in_ref[w] = jnp.zeros(in_ref.shape[1:], F32)
                continue
            inside = (ix + o >= 0) & (ix + o < x_count)
            in_ref[w, :, 0:half] = jnp.where(inside, own[k][...].astype(F32), 0.0)
            in_ref[w, :, half:] = jnp.where(z_ok & inside, other[k][...].astype(F32), 0.0)
        k1 = 2 * half
        for w in range(7):
            for j in range(3):
                start = TOP - 3 + j
                lhs1_ref[w, :, j * k1:(j + 1) * k1] = in_ref[w, start:start + rows, :].astype(BF16)
        out = None
        for i in range(3):
            part = mm(lhs1_ref[i:i + 5].reshape(5 * rows, 3 * k1), t1_ref[i])
            out = part if out is None else out + part
        width = out.shape[1]
        y = iota((rows, width), 0) - 2
        z = iota((rows, width), 1) // CH - 2
        ok = (z < pz + 2) & ((y >= 0) | (iy > 0)) & ((y < py) | (iy < y_count - 1))
        ok = ok & ((z >= 0) | (iz > 0)) & ((z < pz) | (iz < z_count - 1))
        for p in range(5):
            a = gelu(out[p * rows:(p + 1) * rows] + bias_ref[0:1, :])
            good = ok & (ix + p - 2 >= 0) & (ix + p - 2 < x_count)
            act1_ref[p, 0:rows, 0:width] = jnp.where(good, a, 0.0)
            act1_ref[p, rows:, 0:width] = jnp.zeros((act1_ref.shape[1] - rows, width), F32)
            act1_ref[p, :, width:] = jnp.zeros((act1_ref.shape[1], act1_ref.shape[2] - width), F32)
        blocks = lhs2_ref.shape[1]
        for p in range(5):
            for j in range(3):
                a = act1_ref[p, j:j + rows, :].astype(BF16)
                for b in range(blocks):
                    lhs2_ref[p, b, :, j * 256:(j + 1) * 256] = a[:, b * 128:b * 128 + 256]
        out = None
        for i in range(3):
            part = mm(lhs2_ref[i:i + 3].reshape(3 * blocks * rows, 768), t2_ref[i])
            out = part if out is None else out + part
        for b in range(blocks):
            y = iota((rows, 128), 0) - 1
            z = (iota((rows, 128), 1) + b * 128) // CH - 1
            ok = (z < pz + 1) & (y <= py) & ((y >= 0) | (iy > 0)) & ((y < py) | (iy < y_count - 1))
            ok = ok & ((z >= 0) | (iz > 0)) & ((z < pz) | (iz < z_count - 1))
            for p in range(3):
                s = (p * blocks + b) * rows
                a = gelu(out[s:s + rows] + bias_ref[1:2, 0:128])
                good = ok & (ix + p - 1 >= 0) & (ix + p - 1 < x_count)
                act2_ref[p, :, b * 128:(b + 1) * 128] = jnp.where(good, a, 0.0).astype(BF16)
        out = None
        for i in range(3):
            part = mm(act2_ref[i], t3_ref[i])
            out = part if out is None else out + part
        tail_ref[0:rows, :] = out
        score = tail_ref[0:py, :]
        for j in (1, 2):
            score = score + pltpu.roll(tail_ref[j:j + py, :], 128 - j * pz, 1)
        out_ref[0] = score[:, 0:pz] + b3_ref[0]
    return kernel


def detector(pooled, edge, ids, w_first, b_first, w_second, b_second, w_third, b_third, py, pz):
    vmem = pl.BlockSpec(memory_space=pltpu.VMEM)
    smem = pl.BlockSpec(memory_space=pltpu.SMEM)
    limit = pltpu.CompilerParams(vmem_limit_bytes=48 * 1024 * 1024)
    counts = tuple(lax.axis_size(a) for a in ("gx", "gy", "gz"))
    half = pooled.shape[1]
    assert half == 128 and pz * CIN == half and pz * 3 <= 128
    rows = py + 4
    width = lanes_for((pz + 4) * CH)
    blocks = width // 128
    t1, t2, t3, bias = call(
        weight_kernel,
        [((3, 6 * half, width), BF16), ((3, 768, 128), BF16), ((3, width, 128), BF16), ((8, width), F32)],
        w_first, w_second, w_third, b_first[None], b_second[None])
    yr = both_sides(edge, "gy")
    tall = -(-(TOP + py + 3) // 16) * 16
    plane = pl.pallas_call(
        plane_kernel(py, counts[1]),
        in_specs=[smem, vmem, vmem],
        out_shape=jax.ShapeDtypeStruct((tall, half), BF16),
        scratch_shapes=[pltpu.VMEM((tall, half), F32)],
        compiler_params=limit,
    )(ids, pooled, yr)
    shifts = []
    for s in (1, -1, 2, -2, 3, -3):
        if s % counts[0] and s % counts[0] not in shifts:
            shifts.append(s % counts[0])
    own = [plane] + [lax.ppermute(plane, "gx", ring("gx", s)) for s in shifts]
    other = [z_neighbour(v, "gz", False) for v in own]
    (score,) = pl.pallas_call(
        conv_kernel(py, counts, shifts),
        in_specs=[smem, smem] + [vmem] * (2 * len(own) + 4),
        out_shape=[jax.ShapeDtypeStruct((1, py, pz), F32)],
        scratch_shapes=[
            pltpu.VMEM((7, tall, 2 * half), F32),
            pltpu.VMEM((7, rows, 6 * half), BF16),
            pltpu.VMEM((5, rows + 8, width + 128), F32),
            pltpu.VMEM((5, blocks, rows, 768), BF16),
            pltpu.VMEM((3, rows, width), BF16),
            pltpu.VMEM((rows + 8, 128), F32),
        ],
        compiler_params=limit,
    )(ids, b_third, *own, *other, t1, t2, t3, bias)
    return score


def solution(mesh):
    slab = P(("groups", "gx"), "gy", "gz")
    return jax.shard_map(
        body,
        mesh=mesh,
        in_specs=(slab, slab, slab, P(), P(), P(), P(), P(), P()),
        out_specs=(slab, slab, slab, slab),
        check_vma=False,
    )
```

```python
import jax
import jax.numpy as jnp
import numpy as np
from jax import lax
from jax.experimental import pallas as pl
from jax.experimental.pallas import tpu as pltpu
from jax.sharding import PartitionSpec as P

F32 = jnp.float32
BF16 = jnp.bfloat16
I16 = jnp.int16
WELL_HEIGHT = 1.0
STRAIN_COUPLING = 4.0
TIME_STEP = 0.01
DAMAGE_RATE = 0.8
ENERGY_CRITICAL = 0.02

OFF = 16
A_CODE = (0.0, 1.0)
B_CODE = (-1.1, 3.1)
SUM_LOW, SUM_SPAN = -1280.0, 4096.0

VMEM = pl.BlockSpec(memory_space=pltpu.VMEM)
SMEM = pl.BlockSpec(memory_space=pltpu.SMEM)
HBM = pl.BlockSpec(memory_space=pltpu.HBM)


def to_code(x, code):
    low, span = code
    v = (x - low) * (65535.0 / span) - 32768.0
    return jnp.clip(jnp.round(v), -32768.0, 32767.0).astype(jnp.int32).astype(I16)


def from_code(q, code):
    low, span = code
    return q.astype(jnp.int32).astype(F32) * (span / 65535.0) + (low + 32768.0 * span / 65535.0)


def sum_digits(s):
    v = (s[0:2] - SUM_LOW) * (65536.0 / SUM_SPAN)
    high = jnp.floor(v)
    low = jnp.minimum(jnp.floor((v - high) * 65536.0), 65535.0)
    rows = jnp.concatenate([high, low, jnp.full((12, s.shape[1]), 32768.0, F32)]) - 32768.0
    return rows.astype(jnp.int32).astype(I16)


def from_digits(tile):
    v = tile.astype(jnp.int32).astype(F32) + 32768.0
    return (v[0:2] + v[2:4] * (1.0 / 65536.0)) * (SUM_SPAN / 65536.0) + SUM_LOW


def by_label(labels, values):
    return jnp.where(labels == 0, values[0], jnp.where(labels == 1, values[1], values[2])).astype(F32)


FACTORS = (1.0, 0.3, 0.05)
ROOTS = tuple(float(np.sqrt(np.float32(v))) for v in FACTORS)


def call(kernel, outs, *args, in_specs=None, out_specs=None, scratch=(), mib=16):
    return pl.pallas_call(
        kernel,
        in_specs=in_specs or [VMEM] * len(args),
        out_specs=out_specs or [VMEM] * len(outs),
        out_shape=[jax.ShapeDtypeStruct(s, t) for s, t in outs],
        scratch_shapes=scratch,
        compiler_params=pltpu.CompilerParams(vmem_limit_bytes=mib * 1024 * 1024),
    )(*args)


def chunks(start, stop, size):
    return [(r, min(size, stop - r)) for r in range(start, stop, size)]


def fold(x):
    return x.reshape(x.shape[0] // 8, 8, x.shape[1]).sum(0)


def to_rows(top, bottom):
    return jnp.concatenate([jnp.sum(top, 0, keepdims=True), jnp.sum(bottom, 0, keepdims=True),
                            jnp.zeros((6, top.shape[1]), F32)])


def first_kernel(c_hbm, d_hbm, l_hbm, f_ref, amp_ref, lo1_ref, hi1_ref, lo2_ref, hi2_ref, sum_ref,
                 d_ref, l_ref, sems):
    nx, ny, nz = f_ref.shape
    order = [0, nx - 1] + list(range(1, nx - 1))
    copies = []
    for x in order:
        copies.append([pltpu.make_async_copy(src.at[x], dst.at[x], sems.at[k, x])
                       for k, (src, dst) in enumerate(((c_hbm, f_ref), (d_hbm, d_ref), (l_hbm, l_ref)))])
        for c in copies[-1]:
            c.start()
    top = jnp.zeros((8, nz), F32)
    bottom = jnp.zeros((8, nz), F32)
    for k, x in enumerate(order):
        for c in copies[k]:
            c.wait()
        for r, n in chunks(0, ny, 48):
            f = f_ref[x, r:r + n, :]
            a = by_label(l_ref[x, r:r + n, :], ROOTS) * (1.0 - d_ref[x, r:r + n, :])
            amp_ref[x, r:r + n, :] = a
            m = a * a
            top = top + fold(m * f)
            bottom = bottom + fold(m)
            for near, far, first, second in ((0, 1, lo1_ref, lo2_ref), (nx - 1, nx - 2, hi1_ref, hi2_ref)):
                if x == near:
                    first[r:r + n, :] = to_code(f, A_CODE)
                    second[1, r:r + n, :] = to_code(a, A_CODE)
                if x == far:
                    second[0, r:r + n, :] = to_code(f, A_CODE)
    s = to_rows(top, bottom)
    sum_ref[...] = s
    lo1_ref[ny:ny + 16, :] = sum_digits(s)
    hi1_ref[ny:ny + 16, :] = sum_digits(s)


def edge_rows(code, ride_x, with_amp):
    def kernel(*refs):
        f_ref = refs[0]
        amp_ref = refs[1] if with_amp else None
        lo_ref, hi_ref, s_ref, far_ref = refs[1 + with_amp:5 + with_amp]
        out_ref = refs[-1]
        nx, ny, nz = f_ref.shape
        low_rows = [from_code(r[0:16, :], code)[0:1] for r in (lo_ref, hi_ref)]
        high_rows = [from_code(r[ny - 16:ny, :], code)[15:16] for r in (lo_ref, hi_ref)]
        s = s_ref[...]
        if ride_x:
            s = s + far_ref[...]
        for side, first, second, beside in ((0, 0, 1, low_rows), (1, ny - 1, ny - 2, high_rows)):
            for x in range(nx):
                out_ref[side, 2 * x:2 * x + 1, :] = f_ref[x, first:first + 1, :]
                out_ref[side, 2 * x + 1:2 * x + 2, :] = f_ref[x, second:second + 1, :]
                if amp_ref is not None:
                    out_ref[side, 10 + x:11 + x, :] = amp_ref[x, first:first + 1, :]
            out_ref[side, 8:9, :] = beside[0]
            out_ref[side, 9:10, :] = beside[1]
            out_ref[side, 16:24, :] = s
            if ride_x:
                out_ref[side, 16:18, :] = (s[0:2] + from_digits(lo_ref[ny:ny + 16, :])
                                           + from_digits(hi_ref[ny:ny + 16, :]))
    return kernel


def assemble(code, ride_y, with_amp):
    def kernel(*refs):
        f_ref = refs[0]
        amp_ref = refs[1] if with_amp else None
        lo_ref, hi_ref, yr_ref, yp_ref, pad_ref = refs[1 + with_amp:6 + with_amp]
        apad_ref = refs[7] if with_amp else None
        zp_ref = refs[-1]
        nx, ny, nz = f_ref.shape
        end = OFF + ny
        lane = lax.broadcasted_iota(jnp.int32, (1, nz), 1)
        outer = (lane < 16) | (lane >= nz - 16)
        for p, ref in ((0, lo_ref), (nx + 1, hi_ref)):
            for r, n in chunks(0, ny, 48):
                f = from_code(ref[r:r + n, :], code)
                pad_ref[p, OFF + r:OFF + r + n, :] = f
                zp_ref[p, OFF + r:OFF + r + n, :] = f
        for p, k in ((0, 8), (nx + 1, 9)):
            pad_ref[p, OFF - 1:OFF, :] = yr_ref[1, k:k + 1, :]
            pad_ref[p, end:end + 1, :] = yr_ref[0, k:k + 1, :]
        for x in range(nx):
            for r, n in chunks(0, ny, 48):
                f = f_ref[x, r:r + n, :]
                pad_ref[x + 1, OFF + r:OFF + r + n, :] = f
                if amp_ref is not None:
                    a = amp_ref[x, r:r + n, :]
                    apad_ref[x, OFF + r:OFF + r + n, :] = a
                    f = jnp.where(outer, f, pltpu.roll(a, nz // 2, 1))
                zp_ref[x + 1, OFF + r:OFF + r + n, :] = f
            for side, near, far in ((1, OFF - 1, OFF - 2), (0, end, end + 1)):
                f = yr_ref[side, 2 * x:2 * x + 1, :]
                pad_ref[x + 1, near:near + 1, :] = f
                pad_ref[x + 1, far:far + 1, :] = yr_ref[side, 2 * x + 1:2 * x + 2, :]
                if amp_ref is not None:
                    apad_ref[x, near:near + 1, :] = yr_ref[side, 10 + x:11 + x, :]
                zp_ref[x + 1, near:near + 1, :] = f
        s = yp_ref[0, 16:24, :]
        if ride_y:
            s = s + yr_ref[0, 16:24, :]
        zp_ref[0, 0:8, :] = s
        pad_ref[0, 0:8, :] = s
    return kernel


def weighted_mean(pad_ref, zr_ref, ride_z):
    s = pad_ref[0, 0:8, :]
    if ride_z:
        s = s + zr_ref[0, 0:8, :]
    return jnp.sum(s[0:1], keepdims=True) / jnp.sum(s[1:2], keepdims=True)


def worn(a, m, f, mean):
    e = f - mean
    energy = 0.5 * STRAIN_COUPLING * m * e * e
    return a * (1.0 - DAMAGE_RATE * jnp.maximum(energy - ENERGY_CRITICAL, 0.0))


class Geometry:
    def __init__(self, nx, ny, nz):
        self.nx, self.ny, self.nz = nx, ny, nz
        self.lane = lax.broadcasted_iota(jnp.int32, (1, nz), 1)
        self.first = self.lane == 0
        self.last = self.lane == nz - 1

    def before(self, own, other):
        return pltpu.roll(jnp.where(self.last, other, own), 1, 1)

    def after(self, own, other):
        return pltpu.roll(jnp.where(self.first, other, own), self.nz - 1, 1)


def chem_of(f, m, around, mean):
    well = 2.0 * WELL_HEIGHT * f * (1.0 - f) * (1.0 - 2.0 * f)
    return well + 6.0 * f - around + STRAIN_COUPLING * m * (f - mean)


def chemistry(g, pad_ref, lo2_ref, hi2_ref, code, mob_ref, mobe_ref, zr_ref, chem_ref, cheme_ref, mean):
    nx, ny = g.nx, g.ny

    def plane(p, r, n):
        if p < 0:
            return from_code(lo2_ref[0, r - OFF:r - OFF + n, :], code)
        if p > nx + 1:
            return from_code(hi2_ref[0, r - OFF:r - OFF + n, :], code)
        return pad_ref[p, r:r + n, :]

    for p in range(nx + 2):
        inside = 1 <= p <= nx
        rows = chunks(OFF - 8, OFF + ny + 8, 32) if inside else chunks(OFF, OFF + ny, 48)
        for r, n in rows:
            f = pad_ref[p, r:r + n, :]
            e = zr_ref[p, r:r + n, :]
            around = (plane(p - 1, r, n) + plane(p + 1, r, n)
                      + pad_ref[p, r - 1:r - 1 + n, :] + pad_ref[p, r + 1:r + 1 + n, :]
                      + g.before(f, e) + g.after(f, e))
            chem_ref[p, r:r + n, :] = chem_of(f, mob_ref[p, r:r + n, :], around, mean)
        if inside:
            for r, n in chunks(OFF, OFF + ny, 48):
                f = pad_ref[p, r:r + n, :]
                e = zr_ref[p, r:r + n, :]
                around = (zr_ref[p - 1, r:r + n, :] + zr_ref[p + 1, r:r + n, :]
                          + zr_ref[p, r - 1:r - 1 + n, :] + zr_ref[p, r + 1:r + 1 + n, :]
                          + g.before(e, f) + g.after(e, f))
                cheme_ref[p - 1, r - OFF:r - OFF + n, :] = chem_of(
                    e, mobe_ref[p - 1, r - OFF:r - OFF + n, :], around, mean)


def flux_of(g, x, r, n, mob_ref, mobe_ref, chem_ref, cheme_ref):
    p = x + 1
    m = mob_ref[p, r:r + n, :]
    q = chem_ref[p, r:r + n, :]
    me = mobe_ref[x, r - OFF:r - OFF + n, :]
    qe = cheme_ref[x, r - OFF:r - OFF + n, :]
    total = None
    for nm, nq in (
        (mob_ref[p - 1, r:r + n, :], chem_ref[p - 1, r:r + n, :]),
        (mob_ref[p + 1, r:r + n, :], chem_ref[p + 1, r:r + n, :]),
        (mob_ref[p, r - 1:r - 1 + n, :], chem_ref[p, r - 1:r - 1 + n, :]),
        (mob_ref[p, r + 1:r + 1 + n, :], chem_ref[p, r + 1:r + 1 + n, :]),
        (g.before(m, me), g.before(q, qe)),
        (g.after(m, me), g.after(q, qe)),
    ):
        term = (nm + m) * (nq - q)
        total = term if total is None else total + term
    return m, 0.5 * total


def step_a(ride_z):
    def kernel(pad_ref, apad_ref, lo2_ref, hi2_ref, zr_ref,
               f2_ref, a2_ref, ae2_ref, lo1_out, hi1_out, lo2_out, hi2_out, sum_ref,
               mob_ref, mobe_ref, chem_ref, cheme_ref):
        nx, ny, nz = f2_ref.shape
        g = Geometry(nx, ny, nz)
        mean = weighted_mean(pad_ref, zr_ref, ride_z)
        for p in range(nx + 2):
            inside = 1 <= p <= nx
            rows = chunks(OFF - 8, OFF + ny + 8, 32) if inside else chunks(OFF, OFF + ny, 48)
            for r, n in rows:
                if inside:
                    a = apad_ref[p - 1, r:r + n, :]
                else:
                    a = from_code((lo2_ref if p == 0 else hi2_ref)[1, r - OFF:r - OFF + n, :], A_CODE)
                m = a * a
                mob_ref[p, r:r + n, :] = m
                a2_ref[p, r:r + n, :] = worn(a, m, pad_ref[p, r:r + n, :], mean)
            if inside:
                for r, n in chunks(OFF, OFF + ny, 48):
                    e = zr_ref[p, r:r + n, :]
                    a = pltpu.roll(e, nz // 2, 1)
                    m = a * a
                    mobe_ref[p - 1, r - OFF:r - OFF + n, :] = m
                    ae2_ref[p - 1, r - OFF:r - OFF + n, :] = worn(a, m, e, mean)
        chemistry(g, pad_ref, lo2_ref, hi2_ref, A_CODE, mob_ref, mobe_ref, zr_ref, chem_ref, cheme_ref, mean)
        top = jnp.zeros((8, nz), F32)
        bottom = jnp.zeros((8, nz), F32)
        for x in range(nx):
            for r, n in chunks(OFF, OFF + ny, 48):
                _, flux = flux_of(g, x, r, n, mob_ref, mobe_ref, chem_ref, cheme_ref)
                f = pad_ref[x + 1, r:r + n, :] + TIME_STEP * flux
                s = slice(r - OFF, r - OFF + n)
                f2_ref[x, s, :] = f
                a = a2_ref[x + 1, r:r + n, :]
                m = a * a
                top = top + fold(m * f)
                bottom = bottom + fold(m)
                for near, far, first, second in ((0, 1, lo1_out, lo2_out), (nx - 1, nx - 2, hi1_out, hi2_out)):
                    if x == near:
                        first[s, :] = to_code(f, B_CODE)
                    if x == far:
                        second[0, s, :] = to_code(f, B_CODE)
        s = to_rows(top, bottom)
        sum_ref[...] = s
        lo1_out[ny:ny + 16, :] = sum_digits(s)
        hi1_out[ny:ny + 16, :] = sum_digits(s)
    return kernel


def step_b(ride_z):
    def kernel(pad_ref, a2_ref, ae2_ref, lo2_ref, hi2_ref, zr_ref, l_hbm,
               f3_hbm, dmg_hbm, flux_hbm, pool_ref, edge_ref,
               mob_ref, mobe_ref, chem_ref, cheme_ref, pool_scr, l_ref, f3_ref, dmg_ref, flux_ref, l_sem, sems):
        nx, ny, nz = f3_ref.shape
        labels_in = pltpu.make_async_copy(l_hbm, l_ref, l_sem)
        labels_in.start()
        g = Geometry(nx, ny, nz)
        mean = weighted_mean(pad_ref, zr_ref, ride_z)
        for p in range(nx + 2):
            inside = 1 <= p <= nx
            rows = chunks(OFF - 8, OFF + ny + 8, 32) if inside else chunks(OFF, OFF + ny, 48)
            for r, n in rows:
                a = a2_ref[p, r:r + n, :]
                mob_ref[p, r:r + n, :] = a * a
            if inside:
                for r, n in chunks(0, ny, 48):
                    a = ae2_ref[p - 1, r:r + n, :]
                    mobe_ref[p - 1, r:r + n, :] = a * a
        chemistry(g, pad_ref, lo2_ref, hi2_ref, B_CODE, mob_ref, mobe_ref, zr_ref, chem_ref, cheme_ref, mean)
        labels_in.wait()
        copies = []
        for k, (r, n) in enumerate(chunks(OFF, OFF + ny, 48)):
            s = slice(r - OFF, r - OFF + n)
            pooled = [None] * 4
            for x in range(nx):
                m, flux = flux_of(g, x, r, n, mob_ref, mobe_ref, chem_ref, cheme_ref)
                f0 = pad_ref[x + 1, r:r + n, :]
                f = f0 + TIME_STEP * flux
                a = worn(a2_ref[x + 1, r:r + n, :], m, f0, mean)
                labels = l_ref[x, s, :]
                factor = by_label(labels, FACTORS)
                dmg = 1.0 - a * by_label(labels, tuple(1.0 / v for v in ROOTS))
                f3_ref[x, s, :] = f
                dmg_ref[x, s, :] = dmg
                flux_ref[x, s, :] = flux
                for i, v in enumerate((f, dmg, a * a, factor)):
                    pooled[i] = v if pooled[i] is None else pooled[i] + v
            for i in range(4):
                pool_scr[i, s, :] = pooled[i]
            for i, (src, dst) in enumerate(((f3_ref, f3_hbm), (dmg_ref, dmg_hbm), (flux_ref, flux_hbm))):
                copies.append(pltpu.make_async_copy(src.at[:, s, :], dst.at[:, s, :], sems.at[i, k]))
                copies[-1].start()
        py, pz = ny // 4, nz // 4
        zin = lax.broadcasted_iota(jnp.int32, (nz, 4 * pz), 0)
        out = lax.broadcasted_iota(jnp.int32, (nz, 4 * pz), 1)
        total = jnp.zeros((py, 4 * pz), F32)
        for i in range(4):
            rows = (pool_scr[i, pl.ds(0, py, stride=4), :] + pool_scr[i, pl.ds(1, py, stride=4), :]
                    + pool_scr[i, pl.ds(2, py, stride=4), :] + pool_scr[i, pl.ds(3, py, stride=4), :])
            pick = jnp.where((zin // 4 == out // 4) & (out % 4 == i), 1.0 / 64.0, 0.0).astype(F32)
            total = total + jnp.dot(rows, pick, precision=lax.Precision.HIGHEST, preferred_element_type=F32)
        pool_ref[...] = total.astype(BF16)
        blank = jnp.zeros((13, 4 * pz), F32)
        edge_ref[0] = jnp.concatenate([total[0:3], blank]).astype(BF16)
        edge_ref[1] = jnp.concatenate([total[py - 3:py], blank]).astype(BF16)
        for c in copies:
            c.wait()
    return kernel


def ring(axis, shift):
    count = lax.axis_size(axis)
    return [(i, (i + shift) % count) for i in range(count)]


def pair_sum(s, axis):
    count = lax.axis_size(axis)
    if count & (count - 1):
        return lax.psum(s, axis)
    bit = 1
    while bit < count:
        s = s + lax.ppermute(s, axis, [(i, i ^ bit) for i in range(count)])
        bit *= 2
    return s


def both_sides(pay, axis):
    if lax.axis_size(axis) == 2:
        return lax.ppermute(pay, axis, ring(axis, 1))
    return jnp.stack([lax.ppermute(pay[0], axis, ring(axis, -1)), lax.ppermute(pay[1], axis, ring(axis, 1))])


def z_neighbour(pay, axis, packed=True):
    if lax.axis_size(axis) == 2:
        return lax.ppermute(pay, axis, ring(axis, 1))
    above = lax.ppermute(pay, axis, ring(axis, -1))
    below = lax.ppermute(pay, axis, ring(axis, 1))
    lane = lax.broadcasted_iota(jnp.int32, pay.shape, pay.ndim - 1)
    part = pay.shape[-1] // (4 if packed else 2)
    return jnp.where(lane // part % 2 == 0, above, below)


def x_sides(lo, hi):
    return lax.ppermute(hi, "gx", ring("gx", 1)), lax.ppermute(lo, "gx", ring("gx", -1))


def body(concentration, damage, labels, w_first, b_first, w_second, b_second, w_third, b_third):
    nx, ny, nz = concentration.shape
    rows = ny + 2 * OFF
    block = (nx, ny, nz)
    padded = (nx + 2, rows, nz)
    ride_x = lax.axis_size("gx") == 4
    ride_y = lax.axis_size("gy") == 2
    ride_z = lax.axis_size("gz") == 2
    scratch = [pltpu.VMEM(padded, F32), pltpu.VMEM(block, F32), pltpu.VMEM(padded, F32), pltpu.VMEM(block, F32)]

    def start(sums):
        if ride_x:
            far = lax.ppermute(sums, "gx", ring("gx", 2))
        else:
            sums = far = pair_sum(sums, "gx")
        for axis, ride in (("gy", ride_y), ("gz", ride_z)):
            if not ride:
                assert not ride_x
                sums = far = pair_sum(sums, axis)
        return sums, far

    f, amp, lo1, hi1, lo2, hi2, sums = call(
        first_kernel,
        [(block, F32), (block, F32), ((ny + 16, nz), I16), ((ny + 16, nz), I16),
         ((2, ny, nz), I16), ((2, ny, nz), I16), ((8, nz), F32)],
        concentration, damage, labels,
        in_specs=[HBM] * 3,
        scratch=[pltpu.VMEM(block, F32), pltpu.VMEM(block, jnp.int32), pltpu.SemaphoreType.DMA((3, nx))])
    matrices = weight_matrices(w_first, b_first, w_second, b_second, w_third, nz, nz // 4)
    sums, far = start(sums)
    lo1, hi1 = x_sides(lo1, hi1)
    lo2, hi2 = x_sides(lo2, hi2)
    (ypay,) = call(edge_rows(A_CODE, ride_x, True), [((2, 24, nz), F32)], f, amp, lo1, hi1, sums, far, matrices[-1])
    yr = both_sides(ypay, "gy")
    pad, apad, zpay = call(
        assemble(A_CODE, ride_y, True), [(padded, F32), ((nx, rows, nz), F32), (padded, F32)],
        f, amp, lo1, hi1, yr, ypay)
    zr = z_neighbour(zpay, "gz")
    f2, a2, ae2, lo1, hi1, lo2, hi2, sums = call(
        step_a(ride_z),
        [(block, F32), (padded, F32), (block, F32), ((ny + 16, nz), I16), ((ny + 16, nz), I16),
         ((1, ny, nz), I16), ((1, ny, nz), I16), ((8, nz), F32)],
        pad, apad, lo2, hi2, zr, scratch=scratch)

    sums, far = start(sums)
    lo1, hi1 = x_sides(lo1, hi1)
    lo2, hi2 = x_sides(lo2, hi2)
    (ypay,) = call(edge_rows(B_CODE, ride_x, False), [((2, 24, nz), F32)], f2, lo1, hi1, sums, far)
    yr = both_sides(ypay, "gy")
    pad, zpay = call(assemble(B_CODE, ride_y, False), [(padded, F32), (padded, F32)], f2, lo1, hi1, yr, ypay)
    zr = z_neighbour(zpay, "gz")
    fraction, damage_field, flux_sum, pooled, edge = call(
        step_b(ride_z),
        [(block, F32), (block, F32), (block, F32), ((ny // 4, nz), BF16), ((2, 16, nz), BF16)],
        pad, a2, ae2, lo2, hi2, zr, labels,
        in_specs=[VMEM] * 6 + [HBM], out_specs=[HBM] * 3 + [VMEM] * 2,
        scratch=scratch + [
            pltpu.VMEM((4, ny, nz), F32), pltpu.VMEM(block, jnp.int32),
            pltpu.VMEM(block, F32), pltpu.VMEM(block, F32), pltpu.VMEM(block, F32),
            pltpu.SemaphoreType.DMA, pltpu.SemaphoreType.DMA((3, len(chunks(OFF, OFF + ny, 48))))])
    ids = jnp.stack([lax.axis_index(a) for a in ("gx", "gy", "gz")])
    crack_score = detector(pooled, edge, ids, matrices, b_third, ny // 4, nz // 4)
    return (fraction, damage_field, flux_sum, crack_score)


CH = 16
CIN = 4
TOP = 8


def iota(shape, dim):
    return lax.broadcasted_iota(jnp.int32, shape, dim)


def lanes_for(n):
    return -(-n // 128) * 128


def one_hot(mask):
    return jnp.where(mask, 1.0, 0.0).astype(BF16)


def mm(a, b):
    return jnp.dot(a, b, preferred_element_type=F32)


def weight_kernel(w1_ref, w2_ref, w3_ref, b1_ref, b2_ref, t1_ref, t2_ref, t3_ref, bias_ref):
    k1 = t1_ref.shape[1] // 3
    n1 = t1_ref.shape[2]
    pz = k1 // (2 * CIN)
    spread = one_hot(iota((CH, 128), 1) % CH == iota((CH, 128), 0))
    tile1 = mm(w1_ref[...], spread)
    tile2 = mm(w2_ref[...], spread)
    tile3 = mm(w3_ref[...], one_hot(iota((3, 128), 1) // pz == iota((3, 128), 0)))
    step1 = iota((16, 128), 0) // CIN - iota((16, 128), 1) // CH
    step2 = -(iota((16, 128), 1) // CH)
    step3 = -(iota((16, 128), 1) % pz)

    def tile(source, base, stride, step, shift):
        out = jnp.zeros((16, 128), F32)
        for l in range(3):
            k = base + stride * l
            out = jnp.where(step + shift == l, source[16 * k:16 * k + 16], out)
        return out.astype(BF16)

    zero = jnp.zeros((16, 128), BF16)
    for i in range(3):
        for j in range(3):
            tap = 9 * i + 3 * j
            known = {}
            for rb in range(k1 // 16):
                z_in = rb * 16 // CIN
                z_in = z_in if z_in < pz + pz // 2 else z_in - 2 * pz
                for cb in range(n1 // 128):
                    shift = z_in - cb * 8 + 3
                    near = -4 < shift < 10
                    if near and shift not in known:
                        known[shift] = tile(tile1, tap, 1, step1, shift)
                    t1_ref[i, j * k1 + rb * 16:j * k1 + rb * 16 + 16, cb * 128:(cb + 1) * 128] = (
                        known[shift] if near else zero)
            for rb in range(16):
                t2_ref[i, j * 256 + rb * 16:j * 256 + rb * 16 + 16, :] = (
                    tile(tile2, tap, 1, step2, rb) if rb < 10 else zero)
        for rb in range(t3_ref.shape[1] // 16):
            t3_ref[i, rb * 16:rb * 16 + 16, :] = tile(tile3, 3 * i, 1, step3, rb) if rb < pz + 2 else zero
    wide = one_hot(iota((CH, n1), 1) % CH == iota((CH, n1), 0)).astype(F32)
    for k, ref in ((0, b1_ref), (1, b2_ref)):
        bias_ref[k:k + 1, :] = jnp.dot(ref[...], wide, precision=lax.Precision.HIGHEST, preferred_element_type=F32)


def weight_matrices(w_first, b_first, w_second, b_second, w_third, half, pz):
    width = lanes_for((pz + 4) * CH)
    rows1 = jnp.tile(jnp.swapaxes(w_first, 1, 2), (1, 16 // CIN, 1)).reshape(27 * 16, CH)
    rows2 = jnp.swapaxes(w_second, 1, 2).reshape(27 * CH, CH)
    rows3 = w_third.reshape(3, 3, 3, CH).transpose(0, 2, 3, 1).reshape(9 * CH, 3)
    return call(
        weight_kernel,
        [((3, 6 * half, width), BF16), ((3, 768, 128), BF16), ((3, width, 128), BF16), ((8, width), F32)],
        rows1, rows2, rows3, b_first[None], b_second[None])


def gelu(x):
    return 0.5 * x * (1.0 + jnp.tanh(0.7978845608028654 * (x + 0.044715 * (x * x * x))))


def plane_kernel(py, y_count):
    def kernel(ids_ref, pool_ref, yr_ref, out_ref, scr_ref):
        iy = ids_ref[1]
        scr_ref[...] = jnp.zeros(scr_ref.shape, F32)
        scr_ref[TOP:TOP + py, :] = pool_ref[0:py, :].astype(F32)
        below = yr_ref[1].astype(F32)[0:3]
        above = yr_ref[0].astype(F32)[0:3]
        scr_ref[TOP - 3:TOP, :] = jnp.where(iy > 0, below, 0.0)
        scr_ref[TOP + py:TOP + py + 3, :] = jnp.where(iy < y_count - 1, above, 0.0)
        out_ref[...] = scr_ref[...].astype(BF16)
    return kernel


def conv_kernel(py, counts, shifts):
    x_count, y_count, z_count = counts
    n = len(shifts)

    def kernel(*refs):
        ids_ref, b3_ref = refs[:2]
        own = refs[2:3 + n]
        other = refs[3 + n:4 + 2 * n]
        t1_ref, t2_ref, t3_ref, bias_ref, out_ref = refs[4 + 2 * n:9 + 2 * n]
        in_ref, lhs1_ref, act1_ref, lhs2_ref, act2_ref, tail_ref = refs[9 + 2 * n:]
        ix, iy, iz = ids_ref[0], ids_ref[1], ids_ref[2]
        half = own[0].shape[1]
        pz = half // CIN
        rows = py + 4
        z_row = iota((1, half), 1) // CIN
        z_ok = ((z_row < pz // 2) & (iz < z_count - 1)) | ((z_row >= pz // 2) & (iz > 0))
        for w in range(7):
            o = w - 3
            k = 0 if o == 0 else 1 + shifts.index((-o) % x_count) if (-o) % x_count in shifts else None
            if k is None:
                in_ref[w] = jnp.zeros(in_ref.shape[1:], F32)
                continue
            inside = (ix + o >= 0) & (ix + o < x_count)
            in_ref[w, :, 0:half] = jnp.where(inside, own[k][...].astype(F32), 0.0)
            in_ref[w, :, half:] = jnp.where(z_ok & inside, other[k][...].astype(F32), 0.0)
        k1 = 2 * half
        for w in range(7):
            for j in range(3):
                start = TOP - 3 + j
                lhs1_ref[w, :, j * k1:(j + 1) * k1] = in_ref[w, start:start + rows, :].astype(BF16)
        out = None
        for i in range(3):
            part = mm(lhs1_ref[i:i + 5].reshape(5 * rows, 3 * k1), t1_ref[i])
            out = part if out is None else out + part
        width = out.shape[1]
        y = iota((rows, width), 0) - 2
        z = iota((rows, width), 1) // CH - 2
        ok = (z < pz + 2) & ((y >= 0) | (iy > 0)) & ((y < py) | (iy < y_count - 1))
        ok = ok & ((z >= 0) | (iz > 0)) & ((z < pz) | (iz < z_count - 1))
        for p in range(5):
            a = gelu(out[p * rows:(p + 1) * rows] + bias_ref[0:1, :])
            good = ok & (ix + p - 2 >= 0) & (ix + p - 2 < x_count)
            act1_ref[p, 0:rows, 0:width] = jnp.where(good, a, 0.0)
            act1_ref[p, rows:, 0:width] = jnp.zeros((act1_ref.shape[1] - rows, width), F32)
            act1_ref[p, :, width:] = jnp.zeros((act1_ref.shape[1], act1_ref.shape[2] - width), F32)
        blocks = lhs2_ref.shape[1]
        for p in range(5):
            for j in range(3):
                a = act1_ref[p, j:j + rows, :].astype(BF16)
                for b in range(blocks):
                    lhs2_ref[p, b, :, j * 256:(j + 1) * 256] = a[:, b * 128:b * 128 + 256]
        out = None
        for i in range(3):
            part = mm(lhs2_ref[i:i + 3].reshape(3 * blocks * rows, 768), t2_ref[i])
            out = part if out is None else out + part
        for b in range(blocks):
            y = iota((rows, 128), 0) - 1
            z = (iota((rows, 128), 1) + b * 128) // CH - 1
            ok = (z < pz + 1) & (y <= py) & ((y >= 0) | (iy > 0)) & ((y < py) | (iy < y_count - 1))
            ok = ok & ((z >= 0) | (iz > 0)) & ((z < pz) | (iz < z_count - 1))
            for p in range(3):
                s = (p * blocks + b) * rows
                a = gelu(out[s:s + rows] + bias_ref[1:2, 0:128])
                good = ok & (ix + p - 1 >= 0) & (ix + p - 1 < x_count)
                act2_ref[p, :, b * 128:(b + 1) * 128] = jnp.where(good, a, 0.0).astype(BF16)
        out = None
        for i in range(3):
            part = mm(act2_ref[i], t3_ref[i])
            out = part if out is None else out + part
        tail_ref[0:rows, :] = out
        score = tail_ref[0:py, :]
        for j in (1, 2):
            score = score + pltpu.roll(tail_ref[j:j + py, :], 128 - j * pz, 1)
        out_ref[0] = jnp.transpose(score)[0:pz, :] + b3_ref[0]
    return kernel


def detector(pooled, edge, ids, matrices, b_third, py, pz):
    counts = tuple(lax.axis_size(a) for a in ("gx", "gy", "gz"))
    half = pooled.shape[1]
    assert half == 128 and pz * CIN == half and pz * 3 <= 128
    rows = py + 4
    width = lanes_for((pz + 4) * CH)
    blocks = width // 128
    yr = both_sides(edge, "gy")
    tall = -(-(TOP + py + 3) // 16) * 16
    (plane,) = call(
        plane_kernel(py, counts[1]), [((tall, half), BF16)], ids, pooled, yr,
        in_specs=[SMEM, VMEM, VMEM], scratch=[pltpu.VMEM((tall, half), F32)])
    shifts = []
    for s in (1, -1, 2, -2, 3, -3):
        if s % counts[0] and s % counts[0] not in shifts:
            shifts.append(s % counts[0])
    own = [plane] + [lax.ppermute(plane, "gx", ring("gx", s)) for s in shifts]
    other = [z_neighbour(v, "gz", False) for v in own]
    args = (ids, b_third, *own, *other, *matrices)
    (score,) = call(
        conv_kernel(py, counts, shifts), [((1, pz, py), F32)], *args,
        in_specs=[SMEM] * 2 + [VMEM] * (len(args) - 2),
        scratch=[
            pltpu.VMEM((7, tall, 2 * half), F32),
            pltpu.VMEM((7, rows, 6 * half), BF16),
            pltpu.VMEM((5, rows + 8, width + 128), F32),
            pltpu.VMEM((5, blocks, rows, 768), BF16),
            pltpu.VMEM((3, rows, width), BF16),
            pltpu.VMEM((rows + 8, 128), F32),
        ], mib=24)
    return jnp.swapaxes(score, 1, 2)


def solution(mesh):
    slab = P(("groups", "gx"), "gy", "gz")
    return jax.shard_map(
        body,
        mesh=mesh,
        in_specs=(slab, slab, slab, P(), P(), P(), P(), P(), P()),
        out_specs=(slab, slab, slab, slab),
        check_vma=False,
    )
```

```python
import jax
import jax.numpy as jnp
import numpy as np
from jax import lax
from jax.experimental import pallas as pl
from jax.experimental.pallas import tpu as pltpu
from jax.sharding import PartitionSpec as P

F32 = jnp.float32
BF16 = jnp.bfloat16
I16 = jnp.int16
WELL_HEIGHT = 1.0
STRAIN_COUPLING = 4.0
TIME_STEP = 0.01
DAMAGE_RATE = 0.8
ENERGY_CRITICAL = 0.02

OFF = 16
A_CODE = (0.0, 1.0)
B_CODE = (-1.1, 3.1)
SUM_LOW, SUM_SPAN = -1280.0, 4096.0

VMEM = pl.BlockSpec(memory_space=pltpu.VMEM)
SMEM = pl.BlockSpec(memory_space=pltpu.SMEM)
HBM = pl.BlockSpec(memory_space=pltpu.HBM)


def to_code(x, code):
    low, span = code
    v = (x - low) * (65535.0 / span) - 32768.0
    return jnp.clip(jnp.round(v), -32768.0, 32767.0).astype(jnp.int32).astype(I16)


def from_code(q, code):
    low, span = code
    return q.astype(jnp.int32).astype(F32) * (span / 65535.0) + (low + 32768.0 * span / 65535.0)


def sum_digits(s):
    v = (s[0:2] - SUM_LOW) * (65536.0 / SUM_SPAN)
    high = jnp.floor(v)
    low = jnp.minimum(jnp.floor((v - high) * 65536.0), 65535.0)
    rows = jnp.concatenate([high, low, jnp.full((12, s.shape[1]), 32768.0, F32)]) - 32768.0
    return rows.astype(jnp.int32).astype(I16)


def from_digits(tile):
    v = tile.astype(jnp.int32).astype(F32) + 32768.0
    return (v[0:2] + v[2:4] * (1.0 / 65536.0)) * (SUM_SPAN / 65536.0) + SUM_LOW


def by_label(labels, values):
    return jnp.where(labels == 0, values[0], jnp.where(labels == 1, values[1], values[2])).astype(F32)


FACTORS = (1.0, 0.3, 0.05)
ROOTS = tuple(float(np.sqrt(np.float32(v))) for v in FACTORS)


def call(kernel, outs, *args, in_specs=None, out_specs=None, scratch=(), mib=16):
    return pl.pallas_call(
        kernel,
        in_specs=in_specs or [VMEM] * len(args),
        out_specs=out_specs or [VMEM] * len(outs),
        out_shape=[jax.ShapeDtypeStruct(s, t) for s, t in outs],
        scratch_shapes=scratch,
        compiler_params=pltpu.CompilerParams(vmem_limit_bytes=mib * 1024 * 1024),
    )(*args)


def chunks(start, stop, size):
    return [(r, min(size, stop - r)) for r in range(start, stop, size)]


def fold(x):
    return x.reshape(x.shape[0] // 8, 8, x.shape[1]).sum(0)


def to_rows(top, bottom):
    return jnp.concatenate([jnp.sum(top, 0, keepdims=True), jnp.sum(bottom, 0, keepdims=True),
                            jnp.zeros((6, top.shape[1]), F32)])


def first_kernel(c_hbm, d_hbm, l_hbm, f_ref, amp_ref, lo_ref, hi_ref, sum_ref, d_ref, l_ref, sems):
    nx, ny, nz = f_ref.shape
    order = [0, nx - 1] + list(range(1, nx - 1))
    copies = []
    for x in order:
        copies.append([pltpu.make_async_copy(src.at[x], dst.at[x], sems.at[k, x])
                       for k, (src, dst) in enumerate(((c_hbm, f_ref), (d_hbm, d_ref), (l_hbm, l_ref)))])
        for c in copies[-1]:
            c.start()
    top = jnp.zeros((8, nz), F32)
    bottom = jnp.zeros((8, nz), F32)
    for k, x in enumerate(order):
        for c in copies[k]:
            c.wait()
        for r, n in chunks(0, ny, 48):
            f = f_ref[x, r:r + n, :]
            a = by_label(l_ref[x, r:r + n, :], ROOTS) * (1.0 - d_ref[x, r:r + n, :])
            amp_ref[x, r:r + n, :] = a
            m = a * a
            top = top + fold(m * f)
            bottom = bottom + fold(m)
            for near, far, out in ((0, 1, lo_ref), (nx - 1, nx - 2, hi_ref)):
                if x == near:
                    out[r:r + n, :] = to_code(f, A_CODE)
                    out[2 * ny + r:2 * ny + r + n, :] = to_code(a, A_CODE)
                if x == far:
                    out[ny + r:ny + r + n, :] = to_code(f, A_CODE)
    s = to_rows(top, bottom)
    sum_ref[...] = s
    lo_ref[3 * ny:3 * ny + 16, :] = sum_digits(s)
    hi_ref[3 * ny:3 * ny + 16, :] = sum_digits(s)


def edge_rows(code, ride_x, with_amp):
    def kernel(*refs):
        f_ref = refs[0]
        amp_ref = refs[1] if with_amp else None
        lo_ref, hi_ref, s_ref, far_ref = refs[1 + with_amp:5 + with_amp]
        out_ref = refs[-1]
        nx, ny, nz = f_ref.shape
        low_rows = [from_code(r[0:16, :], code)[0:1] for r in (lo_ref, hi_ref)]
        high_rows = [from_code(r[ny - 16:ny, :], code)[15:16] for r in (lo_ref, hi_ref)]
        s = s_ref[...]
        if ride_x:
            s = s + far_ref[...]
        for side, first, second, beside in ((0, 0, 1, low_rows), (1, ny - 1, ny - 2, high_rows)):
            for x in range(nx):
                out_ref[side, 2 * x:2 * x + 1, :] = f_ref[x, first:first + 1, :]
                out_ref[side, 2 * x + 1:2 * x + 2, :] = f_ref[x, second:second + 1, :]
                if amp_ref is not None:
                    out_ref[side, 10 + x:11 + x, :] = amp_ref[x, first:first + 1, :]
            out_ref[side, 8:9, :] = beside[0]
            out_ref[side, 9:10, :] = beside[1]
            out_ref[side, 16:24, :] = s
            if ride_x:
                out_ref[side, 16:18, :] = (s[0:2] + from_digits(lo_ref[lo_ref.shape[0] - 16:, :])
                                           + from_digits(hi_ref[hi_ref.shape[0] - 16:, :]))
    return kernel


def group(lane, j, nz, first, count):
    return (lane - (32 * j + first)) % nz < count


def pack_z(code, ride_y, with_amp):
    def kernel(*refs):
        f_ref = refs[0]
        amp_ref = refs[1] if with_amp else None
        lo_ref, hi_ref, yr_ref, yp_ref, out_ref = refs[1 + with_amp:]
        nx, ny, nz = f_ref.shape
        end = OFF + ny
        lane = lax.broadcasted_iota(jnp.int32, (1, nz), 1)
        for k in range(out_ref.shape[0]):
            planes = [p for p in range(4 * k, 4 * k + 4) if p < nx + 2]

            def packed(f_of, a_of, ps):
                out = None
                for p in ps:
                    j = p % 4
                    f = f_of(p)
                    f = pltpu.roll(f, 32 * j, 1) if j else f
                    out = f if out is None else jnp.where(group(lane, j, nz, -2, 4), f, out)
                    a = a_of(p)
                    if a is not None:
                        out = jnp.where(group(lane, j, nz, 15, 2), pltpu.roll(a, 32 * j + 16, 1), out)
                return out

            for r, n in chunks(0, ny, 48):
                def f_of(p):
                    if p == 0:
                        return from_code(lo_ref[r:r + n, :], code)
                    if p == nx + 1:
                        return from_code(hi_ref[r:r + n, :], code)
                    return f_ref[p - 1, r:r + n, :]

                def a_of(p):
                    return amp_ref[p - 1, r:r + n, :] if with_amp and 1 <= p <= nx else None

                out_ref[k, OFF + r:OFF + r + n, :] = packed(f_of, a_of, planes)
            inner = [p for p in planes if 1 <= p <= nx]
            if inner:
                for side, near in ((1, OFF - 1), (0, end)):
                    out_ref[k, near:near + 1, :] = packed(
                        lambda p: yr_ref[side, 2 * (p - 1):2 * (p - 1) + 1, :], lambda p: None, inner)
        s = yp_ref[0, 16:24, :]
        out_ref[0, 0:8, :] = s + yr_ref[0, 16:24, :] if ride_y else s
    return kernel


def fill(code, f_ref, lo_ref, hi_ref, yr_ref, zr_ref, pad_ref, ze_ref):
    nx, ny, nz = f_ref.shape
    end = OFF + ny
    for near, far, ref in ((1, 0, lo_ref), (nx + 2, nx + 3, hi_ref)):
        for r, n in chunks(0, ny, 48):
            pad_ref[near, OFF + r:OFF + r + n, :] = from_code(ref[r:r + n, :], code)
            pad_ref[far, OFF + r:OFF + r + n, :] = from_code(ref[ny + r:ny + r + n, :], code)
    for p, k in ((1, 8), (nx + 2, 9)):
        pad_ref[p, OFF - 1:OFF, :] = yr_ref[1, k:k + 1, :]
        pad_ref[p, end:end + 1, :] = yr_ref[0, k:k + 1, :]
    for x in range(nx):
        for r, n in chunks(0, ny, 48):
            pad_ref[x + 2, OFF + r:OFF + r + n, :] = f_ref[x, r:r + n, :]
        for side, near, far in ((1, OFF - 1, OFF - 2), (0, end, end + 1)):
            pad_ref[x + 2, near:near + 1, :] = yr_ref[side, 2 * x:2 * x + 1, :]
            pad_ref[x + 2, far:far + 1, :] = yr_ref[side, 2 * x + 1:2 * x + 2, :]
    for p in range(nx + 2):
        for r, n in chunks(OFF - 8, OFF + ny + 8, 32):
            e = zr_ref[p // 4, r:r + n, :]
            ze_ref[p, r:r + n, :] = pltpu.roll(e, nz - 32 * (p % 4), 1) if p % 4 else e


def weighted_mean(yp_ref, yr_ref, zr_ref, ride_y, ride_z):
    s = yp_ref[0, 16:24, :]
    if ride_y:
        s = s + yr_ref[0, 16:24, :]
    if ride_z:
        s = s + zr_ref[0, 0:8, :]
    return jnp.sum(s[0:1], keepdims=True) / jnp.sum(s[1:2], keepdims=True)


def worn(a, m, f, mean):
    e = f - mean
    energy = 0.5 * STRAIN_COUPLING * m * e * e
    return a * (1.0 - DAMAGE_RATE * jnp.maximum(energy - ENERGY_CRITICAL, 0.0))


class Geometry:
    def __init__(self, nx, ny, nz):
        self.nx, self.ny, self.nz = nx, ny, nz
        self.lane = lax.broadcasted_iota(jnp.int32, (1, nz), 1)
        self.first = self.lane == 0
        self.last = self.lane == nz - 1

    def before(self, own, other):
        return pltpu.roll(jnp.where(self.last, other, own), 1, 1)

    def after(self, own, other):
        return pltpu.roll(jnp.where(self.first, other, own), self.nz - 1, 1)


def chem_of(f, m, around, mean):
    well = 2.0 * WELL_HEIGHT * f * (1.0 - f) * (1.0 - 2.0 * f)
    return well + 6.0 * f - around + STRAIN_COUPLING * m * (f - mean)


def chemistry(g, pad_ref, mob_ref, mobe_ref, ze_ref, chem_ref, cheme_ref, mean):
    nx, ny = g.nx, g.ny
    for p in range(nx + 2):
        inside = 1 <= p <= nx
        rows = chunks(OFF - 8, OFF + ny + 8, 32) if inside else chunks(OFF, OFF + ny, 48)
        for r, n in rows:
            f = pad_ref[p + 1, r:r + n, :]
            e = ze_ref[p, r:r + n, :]
            around = (pad_ref[p, r:r + n, :] + pad_ref[p + 2, r:r + n, :]
                      + pad_ref[p + 1, r - 1:r - 1 + n, :] + pad_ref[p + 1, r + 1:r + 1 + n, :]
                      + g.before(f, e) + g.after(f, e))
            chem_ref[p, r:r + n, :] = chem_of(f, mob_ref[p, r:r + n, :], around, mean)
        if inside:
            for r, n in chunks(OFF, OFF + ny, 48):
                f = pad_ref[p + 1, r:r + n, :]
                e = ze_ref[p, r:r + n, :]
                around = (ze_ref[p - 1, r:r + n, :] + ze_ref[p + 1, r:r + n, :]
                          + ze_ref[p, r - 1:r - 1 + n, :] + ze_ref[p, r + 1:r + 1 + n, :]
                          + g.before(e, f) + g.after(e, f))
                cheme_ref[p - 1, r - OFF:r - OFF + n, :] = chem_of(
                    e, mobe_ref[p - 1, r - OFF:r - OFF + n, :], around, mean)


def flux_of(g, x, r, n, mob_ref, mobe_ref, chem_ref, cheme_ref):
    p = x + 1
    m = mob_ref[p, r:r + n, :]
    q = chem_ref[p, r:r + n, :]
    me = mobe_ref[x, r - OFF:r - OFF + n, :]
    qe = cheme_ref[x, r - OFF:r - OFF + n, :]
    total = None
    for nm, nq in (
        (mob_ref[p - 1, r:r + n, :], chem_ref[p - 1, r:r + n, :]),
        (mob_ref[p + 1, r:r + n, :], chem_ref[p + 1, r:r + n, :]),
        (mob_ref[p, r - 1:r - 1 + n, :], chem_ref[p, r - 1:r - 1 + n, :]),
        (mob_ref[p, r + 1:r + 1 + n, :], chem_ref[p, r + 1:r + 1 + n, :]),
        (g.before(m, me), g.before(q, qe)),
        (g.after(m, me), g.after(q, qe)),
    ):
        term = (nm + m) * (nq - q)
        total = term if total is None else total + term
    return m, 0.5 * total


def pack_edges(values, lane, nz):
    out = values[0]
    for x, v in enumerate(values[1:], 1):
        out = jnp.where(group(lane, x, nz, -1, 2), pltpu.roll(v, 32 * x, 1), out)
    return out


def step_a(ride_y, ride_z):
    def kernel(f_ref, amp_ref, lo_ref, hi_ref, yr_ref, zr_ref, yp_ref,
               f2_ref, a2_ref, ae2_ref, lo_out, hi_out, sum_ref,
               pad_ref, ze_ref, mob_ref, mobe_ref, chem_ref, cheme_ref):
        nx, ny, nz = f2_ref.shape
        end = OFF + ny
        g = Geometry(nx, ny, nz)
        mean = weighted_mean(yp_ref, yr_ref, zr_ref, ride_y, ride_z)
        fill(A_CODE, f_ref, lo_ref, hi_ref, yr_ref, zr_ref, pad_ref, ze_ref)

        def wear(p, r, n, a):
            m = a * a
            mob_ref[p, r:r + n, :] = m
            a2_ref[p, r:r + n, :] = worn(a, m, pad_ref[p + 1, r:r + n, :], mean)

        for r, n in chunks(0, ny, 48):
            wear(0, OFF + r, n, from_code(lo_ref[2 * ny + r:2 * ny + r + n, :], A_CODE))
            wear(nx + 1, OFF + r, n, from_code(hi_ref[2 * ny + r:2 * ny + r + n, :], A_CODE))
            edges = []
            for x in range(nx):
                wear(x + 1, OFF + r, n, amp_ref[x, r:r + n, :])
                p = x + 1
                a = pltpu.roll(zr_ref[p // 4, OFF + r:OFF + r + n, :], nz - 32 * (p % 4) - 16, 1)
                m = a * a
                mobe_ref[x, r:r + n, :] = m
                edges.append(worn(a, m, ze_ref[p, OFF + r:OFF + r + n, :], mean))
            ae2_ref[r:r + n, :] = pack_edges(edges, g.lane, nz)
        for x in range(nx):
            wear(x + 1, OFF - 1, 1, yr_ref[1, 10 + x:11 + x, :])
            wear(x + 1, end, 1, yr_ref[0, 10 + x:11 + x, :])
        chemistry(g, pad_ref, mob_ref, mobe_ref, ze_ref, chem_ref, cheme_ref, mean)
        top = jnp.zeros((8, nz), F32)
        bottom = jnp.zeros((8, nz), F32)
        for x in range(nx):
            for r, n in chunks(OFF, end, 48):
                _, flux = flux_of(g, x, r, n, mob_ref, mobe_ref, chem_ref, cheme_ref)
                f = pad_ref[x + 2, r:r + n, :] + TIME_STEP * flux
                s = slice(r - OFF, r - OFF + n)
                f2_ref[x, s, :] = f
                a = a2_ref[x + 1, r:r + n, :]
                m = a * a
                top = top + fold(m * f)
                bottom = bottom + fold(m)
                for near, far, out in ((0, 1, lo_out), (nx - 1, nx - 2, hi_out)):
                    if x == near:
                        out[s, :] = to_code(f, B_CODE)
                    if x == far:
                        out[r - OFF + ny:r - OFF + ny + n, :] = to_code(f, B_CODE)
        s = to_rows(top, bottom)
        sum_ref[...] = s
        lo_out[2 * ny:2 * ny + 16, :] = sum_digits(s)
        hi_out[2 * ny:2 * ny + 16, :] = sum_digits(s)
    return kernel


def step_b(ride_y, ride_z):
    def kernel(f_ref, a2_ref, ae2_ref, lo_ref, hi_ref, yr_ref, zr_ref, yp_ref, l_hbm,
               f3_hbm, dmg_hbm, flux_hbm, pool_ref, edge_ref,
               pad_ref, ze_ref, mob_ref, mobe_ref, chem_ref, cheme_ref,
               pool_scr, l_ref, f3_ref, dmg_ref, flux_ref, l_sem, sems):
        nx, ny, nz = f3_ref.shape
        labels_in = pltpu.make_async_copy(l_hbm, l_ref, l_sem)
        labels_in.start()
        g = Geometry(nx, ny, nz)
        mean = weighted_mean(yp_ref, yr_ref, zr_ref, ride_y, ride_z)
        fill(B_CODE, f_ref, lo_ref, hi_ref, yr_ref, zr_ref, pad_ref, ze_ref)
        for p in range(nx + 2):
            inside = 1 <= p <= nx
            for r, n in chunks(OFF - 8, OFF + ny + 8, 32) if inside else chunks(OFF, OFF + ny, 48):
                a = a2_ref[p, r:r + n, :]
                mob_ref[p, r:r + n, :] = a * a
        for r, n in chunks(0, ny, 48):
            a = ae2_ref[r:r + n, :]
            a = a * a
            for x in range(nx):
                mobe_ref[x, r:r + n, :] = pltpu.roll(a, nz - 32 * x, 1) if x else a
        chemistry(g, pad_ref, mob_ref, mobe_ref, ze_ref, chem_ref, cheme_ref, mean)
        labels_in.wait()
        copies = []
        for k, (r, n) in enumerate(chunks(OFF, OFF + ny, 48)):
            s = slice(r - OFF, r - OFF + n)
            pooled = [None] * 4
            for x in range(nx):
                m, flux = flux_of(g, x, r, n, mob_ref, mobe_ref, chem_ref, cheme_ref)
                f0 = pad_ref[x + 2, r:r + n, :]
                f = f0 + TIME_STEP * flux
                a = worn(a2_ref[x + 1, r:r + n, :], m, f0, mean)
                labels = l_ref[x, s, :]
                factor = by_label(labels, FACTORS)
                dmg = 1.0 - a * by_label(labels, tuple(1.0 / v for v in ROOTS))
                f3_ref[x, s, :] = f
                dmg_ref[x, s, :] = dmg
                flux_ref[x, s, :] = flux
                for i, v in enumerate((f, dmg, a * a, factor)):
                    pooled[i] = v if pooled[i] is None else pooled[i] + v
            for i in range(4):
                pool_scr[i, s, :] = pooled[i]
            for i, (src, dst) in enumerate(((f3_ref, f3_hbm), (dmg_ref, dmg_hbm), (flux_ref, flux_hbm))):
                copies.append(pltpu.make_async_copy(src.at[:, s, :], dst.at[:, s, :], sems.at[i, k]))
                copies[-1].start()
        py, pz = ny // 4, nz // 4
        zin = lax.broadcasted_iota(jnp.int32, (nz, 4 * pz), 0)
        out = lax.broadcasted_iota(jnp.int32, (nz, 4 * pz), 1)
        total = jnp.zeros((py, 4 * pz), F32)
        for i in range(4):
            rows = (pool_scr[i, pl.ds(0, py, stride=4), :] + pool_scr[i, pl.ds(1, py, stride=4), :]
                    + pool_scr[i, pl.ds(2, py, stride=4), :] + pool_scr[i, pl.ds(3, py, stride=4), :])
            pick = jnp.where((zin // 4 == out // 4) & (out % 4 == i), 1.0 / 64.0, 0.0).astype(F32)
            total = total + jnp.dot(rows, pick, precision=lax.Precision.HIGHEST, preferred_element_type=F32)
        pool_ref[...] = total.astype(BF16)
        blank = jnp.zeros((13, 4 * pz), F32)
        edge_ref[0] = jnp.concatenate([total[0:3], blank]).astype(BF16)
        edge_ref[1] = jnp.concatenate([total[py - 3:py], blank]).astype(BF16)
        for c in copies:
            c.wait()
    return kernel


def ring(axis, shift):
    count = lax.axis_size(axis)
    return [(i, (i + shift) % count) for i in range(count)]


def pair_sum(s, axis):
    count = lax.axis_size(axis)
    if count & (count - 1):
        return lax.psum(s, axis)
    bit = 1
    while bit < count:
        s = s + lax.ppermute(s, axis, [(i, i ^ bit) for i in range(count)])
        bit *= 2
    return s


def both_sides(pay, axis):
    if lax.axis_size(axis) == 2:
        return lax.ppermute(pay, axis, ring(axis, 1))
    return jnp.stack([lax.ppermute(pay[0], axis, ring(axis, -1)), lax.ppermute(pay[1], axis, ring(axis, 1))])


def z_neighbour(pay, axis, packed=True):
    if lax.axis_size(axis) == 2:
        return lax.ppermute(pay, axis, ring(axis, 1))
    above = lax.ppermute(pay, axis, ring(axis, -1))
    below = lax.ppermute(pay, axis, ring(axis, 1))
    lane = lax.broadcasted_iota(jnp.int32, pay.shape, pay.ndim - 1)
    if packed:
        low = (lane % 32 < 8) | (lane % 32 == 16)
    else:
        low = lane < pay.shape[-1] // 2
    return jnp.where(low, above, below)


def x_sides(lo, hi):
    return lax.ppermute(hi, "gx", ring("gx", 1)), lax.ppermute(lo, "gx", ring("gx", -1))


def body(concentration, damage, labels, w_first, b_first, w_second, b_second, w_third, b_third):
    nx, ny, nz = concentration.shape
    rows = ny + 2 * OFF
    block = (nx, ny, nz)
    padded = (nx + 2, rows, nz)
    ride_x = lax.axis_size("gx") == 4
    ride_y = lax.axis_size("gy") == 2
    ride_z = lax.axis_size("gz") == 2
    packed = (-(-(nx + 2) // 4), rows, nz)
    assert nz == 128
    scratch = [pltpu.VMEM((nx + 4, rows, nz), F32), pltpu.VMEM(padded, F32), pltpu.VMEM(padded, F32),
               pltpu.VMEM(block, F32), pltpu.VMEM(padded, F32), pltpu.VMEM(block, F32)]

    def start(sums):
        if ride_x:
            return sums, lax.ppermute(sums, "gx", ring("gx", 2))
        sums = pair_sum(sums, "gx")
        for axis, ride in (("gy", ride_y), ("gz", ride_z)):
            if not ride:
                sums = pair_sum(sums, axis)
        return sums, sums

    concentration, damage, labels = (
        pltpu.with_memory_space_constraint(v, pltpu.HBM) for v in (concentration, damage, labels))
    tall = 3 * ny + 16
    f, amp, lo, hi, sums = call(
        first_kernel,
        [(block, F32), (block, F32), ((tall, nz), I16), ((tall, nz), I16), ((8, nz), F32)],
        concentration, damage, labels,
        in_specs=[HBM] * 3,
        scratch=[pltpu.VMEM(block, F32), pltpu.VMEM(block, jnp.int32), pltpu.SemaphoreType.DMA((3, nx))])
    *matrices, order = weight_matrices(w_first, b_first, w_second, b_second, w_third, nz, nz // 4)
    sums, far = start(sums)
    lo, hi = x_sides(lo, hi)
    (ypay,) = call(edge_rows(A_CODE, ride_x, True), [((2, 24, nz), F32)], f, amp, lo, hi, sums, far, order)
    yr = both_sides(ypay, "gy")
    (zpay,) = call(pack_z(A_CODE, ride_y, True), [(packed, F32)], f, amp, lo, hi, yr, ypay)
    zr = z_neighbour(zpay, "gz")
    tall = 2 * ny + 16
    f, a2, ae2, lo, hi, sums = call(
        step_a(ride_y, ride_z),
        [(block, F32), (padded, F32), ((ny, nz), F32), ((tall, nz), I16), ((tall, nz), I16), ((8, nz), F32)],
        f, amp, lo, hi, yr, zr, ypay, scratch=scratch)

    sums, far = start(sums)
    lo, hi = x_sides(lo, hi)
    (ypay,) = call(edge_rows(B_CODE, ride_x, False), [((2, 24, nz), F32)], f, lo, hi, sums, far)
    yr = both_sides(ypay, "gy")
    (zpay,) = call(pack_z(B_CODE, ride_y, False), [(packed, F32)], f, lo, hi, yr, ypay)
    zr = z_neighbour(zpay, "gz")
    fraction, damage_field, flux_sum, pooled, edge = call(
        step_b(ride_y, ride_z),
        [(block, F32), (block, F32), (block, F32), ((ny // 4, nz), BF16), ((2, 16, nz), BF16)],
        f, a2, ae2, lo, hi, yr, zr, ypay, labels,
        in_specs=[VMEM] * 8 + [HBM], out_specs=[HBM] * 3 + [VMEM] * 2,
        scratch=scratch + [
            pltpu.VMEM((4, ny, nz), F32), pltpu.VMEM(block, jnp.int32),
            pltpu.VMEM(block, F32), pltpu.VMEM(block, F32), pltpu.VMEM(block, F32),
            pltpu.SemaphoreType.DMA, pltpu.SemaphoreType.DMA((3, len(chunks(OFF, OFF + ny, 48))))])
    ids = jnp.stack([lax.axis_index(a) for a in ("gx", "gy", "gz")])
    crack_score = detector(pooled, edge, ids, matrices, b_third, ny // 4, nz // 4)
    return (fraction, damage_field, flux_sum, crack_score)


CH = 16
CIN = 4
TOP = 8


def iota(shape, dim):
    return lax.broadcasted_iota(jnp.int32, shape, dim)


def lanes_for(n):
    return -(-n // 128) * 128


def one_hot(mask):
    return jnp.where(mask, 1.0, 0.0).astype(BF16)


def mm(a, b):
    return jnp.dot(a, b, preferred_element_type=F32)


def tile_shift(rb, cb, pz):
    z_in = rb * 16 // CIN
    z_in = z_in if z_in < pz + pz // 2 else z_in - 2 * pz
    return z_in - cb * 8 + 3


SHIFTS = tuple(k for k in range(-3, 10) if k % (16 // CIN) == 3)


def weight_kernel(w1_ref, w2_ref, w3_ref, b1_ref, b2_ref, d1_hbm, t2_hbm, t3_hbm, bias_hbm, order_ref,
                  d1_ref, t2_ref, t3_ref, bias_ref, sems):
    n1 = bias_ref.shape[1]
    pz = n1 // CH // 8 * 8 - 8
    spread = one_hot(iota((CH, 128), 1) % CH == iota((CH, 128), 0))
    tile1 = mm(w1_ref[...], spread)
    tile2 = mm(w2_ref[...], spread)
    tile3 = mm(w3_ref[...], one_hot(iota((3, 128), 1) // pz == iota((3, 128), 0)))
    step1 = iota((16, 128), 0) // CIN - iota((16, 128), 1) // CH
    step2 = -(iota((16, 128), 1) // CH)
    step3 = -(iota((16, 128), 1) % pz)

    def tile(source, base, stride, step, shift):
        out = jnp.zeros((16, 128), F32)
        for l in range(3):
            k = base + stride * l
            out = jnp.where(step + shift == l, source[16 * k:16 * k + 16], out)
        return out.astype(BF16)

    zero = jnp.zeros((16, 128), BF16)
    bias_ref[...] = jnp.zeros(bias_ref.shape, F32)
    for i in range(3):
        for j in range(3):
            tap = 9 * i + 3 * j
            for k, shift in enumerate(SHIFTS):
                d1_ref[3 * i + j, k] = tile(tile1, tap, 1, step1, shift)
            for rb in range(16):
                t2_ref[i, j * 256 + rb * 16:j * 256 + rb * 16 + 16, :] = (
                    tile(tile2, tap, 1, step2, rb) if rb < 10 else zero)
        for rb in range(t3_ref.shape[1] // 16):
            t3_ref[i, rb * 16:rb * 16 + 16, :] = tile(tile3, 3 * i, 1, step3, rb) if rb < pz + 2 else zero
    wide = one_hot(iota((CH, n1), 1) % CH == iota((CH, n1), 0)).astype(F32)
    for k, ref in ((0, b1_ref), (1, b2_ref)):
        bias_ref[k:k + 1, :] = jnp.dot(ref[...], wide, precision=lax.Precision.HIGHEST, preferred_element_type=F32)
    order_ref[...] = jnp.zeros(order_ref.shape, F32)
    copies = [pltpu.make_async_copy(src, dst, sems.at[k]) for k, (src, dst) in enumerate(
        ((d1_ref, d1_hbm), (t2_ref, t2_hbm), (t3_ref, t3_hbm), (bias_ref, bias_hbm)))]
    for c in copies:
        c.start()
    for c in copies:
        c.wait()


def weight_matrices(w_first, b_first, w_second, b_second, w_third, half, pz):
    width = lanes_for((pz + 4) * CH)
    rows1 = jnp.tile(jnp.swapaxes(w_first, 1, 2), (1, 16 // CIN, 1)).reshape(27 * 16, CH)
    rows2 = jnp.swapaxes(w_second, 1, 2).reshape(27 * CH, CH)
    rows3 = w_third.reshape(3, 3, 3, CH).transpose(0, 2, 3, 1).reshape(9 * CH, 3)
    outs = [((9, len(SHIFTS), 16, 128), BF16), ((3, 768, 128), BF16), ((3, width, 128), BF16), ((8, width), F32)]
    return call(
        weight_kernel, outs + [((8, 128), F32)], rows1, rows2, rows3, b_first[None], b_second[None],
        out_specs=[HBM] * 4 + [VMEM],
        scratch=[pltpu.VMEM(*v) for v in outs] + [pltpu.SemaphoreType.DMA((4,))])


def gelu(x):
    return 0.5 * x * (1.0 + jnp.tanh(0.7978845608028654 * (x + 0.044715 * (x * x * x))))


def plane_kernel(py, y_count):
    def kernel(ids_ref, pool_ref, yr_ref, out_ref, scr_ref):
        iy = ids_ref[1]
        scr_ref[...] = jnp.zeros(scr_ref.shape, F32)
        scr_ref[TOP:TOP + py, :] = pool_ref[0:py, :].astype(F32)
        below = yr_ref[1].astype(F32)[0:3]
        above = yr_ref[0].astype(F32)[0:3]
        scr_ref[TOP - 3:TOP, :] = jnp.where(iy > 0, below, 0.0)
        scr_ref[TOP + py:TOP + py + 3, :] = jnp.where(iy < y_count - 1, above, 0.0)
        out_ref[...] = scr_ref[...].astype(BF16)
    return kernel


def conv_kernel(py, counts, shifts):
    x_count, y_count, z_count = counts
    n = len(shifts)

    def kernel(*refs):
        ids_ref, b3_ref = refs[:2]
        own = refs[2:3 + n]
        other = refs[3 + n:4 + 2 * n]
        hbm = refs[4 + 2 * n:8 + 2 * n]
        out_ref = refs[8 + 2 * n]
        (in_ref, lhs1_ref, act1_ref, lhs2_ref, act2_ref, tail_ref, t1_ref,
         d1_ref, t2_ref, t3_ref, bias_ref, sems) = refs[9 + 2 * n:]
        loads = [pltpu.make_async_copy(src, dst, sems.at[k])
                 for k, (src, dst) in enumerate(zip(hbm, (d1_ref, t2_ref, t3_ref, bias_ref)))]
        for c in loads:
            c.start()
        ix, iy, iz = ids_ref[0], ids_ref[1], ids_ref[2]
        half = own[0].shape[1]
        pz = half // CIN
        rows = py + 4
        z_row = iota((1, half), 1) // CIN
        z_ok = ((z_row < pz // 2) & (iz < z_count - 1)) | ((z_row >= pz // 2) & (iz > 0))
        for w in range(7):
            o = w - 3
            k = 0 if o == 0 else 1 + shifts.index((-o) % x_count) if (-o) % x_count in shifts else None
            if k is None:
                in_ref[w] = jnp.zeros(in_ref.shape[1:], F32)
                continue
            inside = (ix + o >= 0) & (ix + o < x_count)
            in_ref[w, :, 0:half] = jnp.where(inside, own[k][...].astype(F32), 0.0)
            in_ref[w, :, half:] = jnp.where(z_ok & inside, other[k][...].astype(F32), 0.0)
        k1 = 2 * half
        for w in range(7):
            for j in range(3):
                start = TOP - 3 + j
                lhs1_ref[w, :, j * k1:(j + 1) * k1] = in_ref[w, start:start + rows, :].astype(BF16)
        loads[0].wait()
        loads[3].wait()
        zero = jnp.zeros((16, 128), BF16)
        for i in range(3):
            for j in range(3):
                for rb in range(k1 // 16):
                    for cb in range(t1_ref.shape[2] // 128):
                        shift = tile_shift(rb, cb, pz)
                        t1_ref[i, j * k1 + rb * 16:j * k1 + rb * 16 + 16, cb * 128:(cb + 1) * 128] = (
                            d1_ref[3 * i + j, SHIFTS.index(shift)] if shift in SHIFTS else zero)
        out = None
        for i in range(3):
            part = mm(lhs1_ref[i:i + 5].reshape(5 * rows, 3 * k1), t1_ref[i])
            out = part if out is None else out + part
        width = out.shape[1]
        y = iota((rows, width), 0) - 2
        z = iota((rows, width), 1) // CH - 2
        ok = (z < pz + 2) & ((y >= 0) | (iy > 0)) & ((y < py) | (iy < y_count - 1))
        ok = ok & ((z >= 0) | (iz > 0)) & ((z < pz) | (iz < z_count - 1))
        for p in range(5):
            a = gelu(out[p * rows:(p + 1) * rows] + bias_ref[0:1, :])
            good = ok & (ix + p - 2 >= 0) & (ix + p - 2 < x_count)
            act1_ref[p, 0:rows, 0:width] = jnp.where(good, a, 0.0)
            act1_ref[p, rows:, 0:width] = jnp.zeros((act1_ref.shape[1] - rows, width), F32)
            act1_ref[p, :, width:] = jnp.zeros((act1_ref.shape[1], act1_ref.shape[2] - width), F32)
        loads[1].wait()
        blocks = lhs2_ref.shape[1]
        for p in range(5):
            for j in range(3):
                a = act1_ref[p, j:j + rows, :].astype(BF16)
                for b in range(blocks):
                    lhs2_ref[p, b, :, j * 256:(j + 1) * 256] = a[:, b * 128:b * 128 + 256]
        out = None
        for i in range(3):
            part = mm(lhs2_ref[i:i + 3].reshape(3 * blocks * rows, 768), t2_ref[i])
            out = part if out is None else out + part
        for b in range(blocks):
            y = iota((rows, 128), 0) - 1
            z = (iota((rows, 128), 1) + b * 128) // CH - 1
            ok = (z < pz + 1) & (y <= py) & ((y >= 0) | (iy > 0)) & ((y < py) | (iy < y_count - 1))
            ok = ok & ((z >= 0) | (iz > 0)) & ((z < pz) | (iz < z_count - 1))
            for p in range(3):
                s = (p * blocks + b) * rows
                a = gelu(out[s:s + rows] + bias_ref[1:2, 0:128])
                good = ok & (ix + p - 1 >= 0) & (ix + p - 1 < x_count)
                act2_ref[p, :, b * 128:(b + 1) * 128] = jnp.where(good, a, 0.0).astype(BF16)
        loads[2].wait()
        out = None
        for i in range(3):
            part = mm(act2_ref[i], t3_ref[i])
            out = part if out is None else out + part
        tail_ref[0:rows, :] = out
        score = tail_ref[0:py, :]
        for j in (1, 2):
            score = score + pltpu.roll(tail_ref[j:j + py, :], 128 - j * pz, 1)
        out_ref[0] = jnp.transpose(score)[0:pz, :] + b3_ref[0]
    return kernel


def detector(pooled, edge, ids, matrices, b_third, py, pz):
    counts = tuple(lax.axis_size(a) for a in ("gx", "gy", "gz"))
    half = pooled.shape[1]
    assert half == 128 and pz * CIN == half and pz * 3 <= 128
    rows = py + 4
    width = lanes_for((pz + 4) * CH)
    blocks = width // 128
    yr = both_sides(edge, "gy")
    tall = -(-(TOP + py + 3) // 16) * 16
    (plane,) = call(
        plane_kernel(py, counts[1]), [((tall, half), BF16)], ids, pooled, yr,
        in_specs=[SMEM, VMEM, VMEM], scratch=[pltpu.VMEM((tall, half), F32)])
    shifts = []
    for s in (1, -1, 2, -2, 3, -3):
        if s % counts[0] and s % counts[0] not in shifts:
            shifts.append(s % counts[0])
    own = [plane] + [lax.ppermute(plane, "gx", ring("gx", s)) for s in shifts]
    other = [z_neighbour(v, "gz", False) for v in own]
    args = (ids, b_third, *own, *other, *(pltpu.with_memory_space_constraint(v, pltpu.HBM) for v in matrices))
    (score,) = call(
        conv_kernel(py, counts, shifts), [((1, pz, py), F32)], *args,
        in_specs=[SMEM] * 2 + [VMEM] * (len(args) - 6) + [HBM] * 4,
        scratch=[
            pltpu.VMEM((7, tall, 2 * half), F32),
            pltpu.VMEM((7, rows, 6 * half), BF16),
            pltpu.VMEM((5, rows + 8, width + 128), F32),
            pltpu.VMEM((5, blocks, rows, 768), BF16),
            pltpu.VMEM((3, rows, width), BF16),
            pltpu.VMEM((rows + 8, 128), F32),
            pltpu.VMEM((3, 6 * half, width), BF16),
        ] + [pltpu.VMEM(v.shape, v.dtype) for v in matrices] + [pltpu.SemaphoreType.DMA((4,))], mib=32)
    return jnp.swapaxes(score, 1, 2)


def solution(mesh):
    slab = P(("groups", "gx"), "gy", "gz")
    return jax.shard_map(
        body,
        mesh=mesh,
        in_specs=(slab, slab, slab, P(), P(), P(), P(), P(), P()),
        out_specs=(slab, slab, slab, slab),
        check_vma=False,
    )
```

```python
import jax
import jax.numpy as jnp
import numpy as np
from jax import lax
from jax.experimental import pallas as pl
from jax.experimental.pallas import tpu as pltpu
from jax.sharding import PartitionSpec as P

F32 = jnp.float32
BF16 = jnp.bfloat16
I16 = jnp.int16
WELL_HEIGHT = 1.0
STRAIN_COUPLING = 4.0
TIME_STEP = 0.01
DAMAGE_RATE = 0.8
ENERGY_CRITICAL = 0.02

OFF = 16
A_CODE = (0.0, 1.0)
B_CODE = (-1.1, 3.1)
SUM_LOW, SUM_SPAN = -1280.0, 4096.0

VMEM = pl.BlockSpec(memory_space=pltpu.VMEM)
SMEM = pl.BlockSpec(memory_space=pltpu.SMEM)
HBM = pl.BlockSpec(memory_space=pltpu.HBM)


def to_code(x, code):
    low, span = code
    v = (x - low) * (65535.0 / span) - 32768.0
    return jnp.clip(jnp.round(v), -32768.0, 32767.0).astype(jnp.int32).astype(I16)


def from_code(q, code):
    low, span = code
    return q.astype(jnp.int32).astype(F32) * (span / 65535.0) + (low + 32768.0 * span / 65535.0)


def sum_digits(s):
    v = (s[0:2] - SUM_LOW) * (65536.0 / SUM_SPAN)
    high = jnp.floor(v)
    low = jnp.minimum(jnp.floor((v - high) * 65536.0), 65535.0)
    rows = jnp.concatenate([high, low, jnp.full((12, s.shape[1]), 32768.0, F32)]) - 32768.0
    return rows.astype(jnp.int32).astype(I16)


def from_digits(tile):
    v = tile.astype(jnp.int32).astype(F32) + 32768.0
    return (v[0:2] + v[2:4] * (1.0 / 65536.0)) * (SUM_SPAN / 65536.0) + SUM_LOW


def by_label(labels, values):
    return jnp.where(labels == 0, values[0], jnp.where(labels == 1, values[1], values[2])).astype(F32)


FACTORS = (1.0, 0.3, 0.05)
ROOTS = tuple(float(np.sqrt(np.float32(v))) for v in FACTORS)


def call(kernel, outs, *args, in_specs=None, out_specs=None, scratch=(), mib=16):
    return pl.pallas_call(
        kernel,
        in_specs=in_specs or [VMEM] * len(args),
        out_specs=out_specs or [VMEM] * len(outs),
        out_shape=[jax.ShapeDtypeStruct(s, t) for s, t in outs],
        scratch_shapes=scratch,
        compiler_params=pltpu.CompilerParams(vmem_limit_bytes=mib * 1024 * 1024),
    )(*args)


def chunks(start, stop, size):
    return [(r, min(size, stop - r)) for r in range(start, stop, size)]


def fold(x):
    return x.reshape(x.shape[0] // 8, 8, x.shape[1]).sum(0)


def to_rows(top, bottom):
    return jnp.concatenate([jnp.sum(top, 0, keepdims=True), jnp.sum(bottom, 0, keepdims=True),
                            jnp.zeros((6, top.shape[1]), F32)])


def first_kernel(c_hbm, d_hbm, l_hbm, f_ref, amp_ref, lo_ref, hi_ref, sum_ref, d_ref, l_ref, sems):
    nx, ny, nz = f_ref.shape
    order = [0, nx - 1] + list(range(1, nx - 1))
    copies = []
    for x in order:
        copies.append([pltpu.make_async_copy(src.at[x], dst.at[x], sems.at[k, x])
                       for k, (src, dst) in enumerate(((c_hbm, f_ref), (d_hbm, d_ref), (l_hbm, l_ref)))])
        for c in copies[-1]:
            c.start()
    top = jnp.zeros((8, nz), F32)
    bottom = jnp.zeros((8, nz), F32)
    for k, x in enumerate(order):
        for c in copies[k]:
            c.wait()
        for r, n in chunks(0, ny, 48):
            f = f_ref[x, r:r + n, :]
            a = by_label(l_ref[x, r:r + n, :], ROOTS) * (1.0 - d_ref[x, r:r + n, :])
            amp_ref[x, r:r + n, :] = a
            m = a * a
            top = top + fold(m * f)
            bottom = bottom + fold(m)
            for near, far, out in ((0, 1, lo_ref), (nx - 1, nx - 2, hi_ref)):
                if x == near:
                    out[r:r + n, :] = to_code(f, A_CODE)
                    out[2 * ny + r:2 * ny + r + n, :] = to_code(a, A_CODE)
                if x == far:
                    out[ny + r:ny + r + n, :] = to_code(f, A_CODE)
    s = to_rows(top, bottom)
    sum_ref[...] = s
    lo_ref[3 * ny:3 * ny + 16, :] = sum_digits(s)
    hi_ref[3 * ny:3 * ny + 16, :] = sum_digits(s)


def edge_rows(code, ride_x, with_amp):
    def kernel(*refs):
        f_ref = refs[0]
        amp_ref = refs[1] if with_amp else None
        lo_ref, hi_ref, s_ref, far_ref = refs[1 + with_amp:5 + with_amp]
        out_ref = refs[-1]
        nx, ny, nz = f_ref.shape
        low_rows = [from_code(r[0:16, :], code)[0:1] for r in (lo_ref, hi_ref)]
        high_rows = [from_code(r[ny - 16:ny, :], code)[15:16] for r in (lo_ref, hi_ref)]
        s = s_ref[...]
        if ride_x:
            s = s + far_ref[...]
        for side, first, second, beside in ((0, 0, 1, low_rows), (1, ny - 1, ny - 2, high_rows)):
            for x in range(nx):
                out_ref[side, 2 * x:2 * x + 1, :] = f_ref[x, first:first + 1, :]
                out_ref[side, 2 * x + 1:2 * x + 2, :] = f_ref[x, second:second + 1, :]
                if amp_ref is not None:
                    out_ref[side, 10 + x:11 + x, :] = amp_ref[x, first:first + 1, :]
            out_ref[side, 8:9, :] = beside[0]
            out_ref[side, 9:10, :] = beside[1]
            out_ref[side, 16:24, :] = s
            if ride_x:
                out_ref[side, 16:18, :] = (s[0:2] + from_digits(lo_ref[lo_ref.shape[0] - 16:, :])
                                           + from_digits(hi_ref[hi_ref.shape[0] - 16:, :]))
    return kernel


def group(lane, j, nz, first, count):
    return (lane - (32 * j + first)) % nz < count


def pack_z(code, ride_y, with_amp):
    def kernel(*refs):
        f_ref = refs[0]
        amp_ref = refs[1] if with_amp else None
        lo_ref, hi_ref, yr_ref, yp_ref, out_ref = refs[1 + with_amp:]
        nx, ny, nz = f_ref.shape
        end = OFF + ny
        lane = lax.broadcasted_iota(jnp.int32, (1, nz), 1)
        for k in range(out_ref.shape[0]):
            planes = [p for p in range(4 * k, 4 * k + 4) if p < nx + 2]

            def packed(f_of, a_of, ps):
                out = None
                for p in ps:
                    j = p % 4
                    f = f_of(p)
                    f = pltpu.roll(f, 32 * j, 1) if j else f
                    out = f if out is None else jnp.where(group(lane, j, nz, -2, 4), f, out)
                    a = a_of(p)
                    if a is not None:
                        out = jnp.where(group(lane, j, nz, 15, 2), pltpu.roll(a, 32 * j + 16, 1), out)
                return out

            for r, n in chunks(0, ny, 48):
                def f_of(p):
                    if p == 0:
                        return from_code(lo_ref[r:r + n, :], code)
                    if p == nx + 1:
                        return from_code(hi_ref[r:r + n, :], code)
                    return f_ref[p - 1, r:r + n, :]

                def a_of(p):
                    return amp_ref[p - 1, r:r + n, :] if with_amp and 1 <= p <= nx else None

                out_ref[k, OFF + r:OFF + r + n, :] = packed(f_of, a_of, planes)
            inner = [p for p in planes if 1 <= p <= nx]
            if inner:
                for side, near in ((1, OFF - 1), (0, end)):
                    out_ref[k, near:near + 1, :] = packed(
                        lambda p: yr_ref[side, 2 * (p - 1):2 * (p - 1) + 1, :], lambda p: None, inner)
        s = yp_ref[0, 16:24, :]
        out_ref[0, 0:8, :] = s + yr_ref[0, 16:24, :] if ride_y else s
    return kernel


def fill(code, f_ref, lo_ref, hi_ref, yr_ref, zr_ref, pad_ref, ze_ref):
    nx, ny, nz = f_ref.shape
    end = OFF + ny
    for near, far, ref in ((1, 0, lo_ref), (nx + 2, nx + 3, hi_ref)):
        for r, n in chunks(0, ny, 48):
            pad_ref[near, OFF + r:OFF + r + n, :] = from_code(ref[r:r + n, :], code)
            pad_ref[far, OFF + r:OFF + r + n, :] = from_code(ref[ny + r:ny + r + n, :], code)
    for p, k in ((1, 8), (nx + 2, 9)):
        pad_ref[p, OFF - 1:OFF, :] = yr_ref[1, k:k + 1, :]
        pad_ref[p, end:end + 1, :] = yr_ref[0, k:k + 1, :]
    for x in range(nx):
        for r, n in chunks(0, ny, 48):
            pad_ref[x + 2, OFF + r:OFF + r + n, :] = f_ref[x, r:r + n, :]
        for side, near, far in ((1, OFF - 1, OFF - 2), (0, end, end + 1)):
            pad_ref[x + 2, near:near + 1, :] = yr_ref[side, 2 * x:2 * x + 1, :]
            pad_ref[x + 2, far:far + 1, :] = yr_ref[side, 2 * x + 1:2 * x + 2, :]
    for p in range(nx + 2):
        for r, n in chunks(OFF - 8, OFF + ny + 8, 32):
            e = zr_ref[p // 4, r:r + n, :]
            ze_ref[p, r:r + n, :] = pltpu.roll(e, nz - 32 * (p % 4), 1) if p % 4 else e


def weighted_mean(yp_ref, yr_ref, zr_ref, ride_y, ride_z):
    s = yp_ref[0, 16:24, :]
    if ride_y:
        s = s + yr_ref[0, 16:24, :]
    if ride_z:
        s = s + zr_ref[0, 0:8, :]
    return jnp.sum(s[0:1], keepdims=True) / jnp.sum(s[1:2], keepdims=True)


def worn(a, m, f, mean):
    e = f - mean
    energy = 0.5 * STRAIN_COUPLING * m * e * e
    return a * (1.0 - DAMAGE_RATE * jnp.maximum(energy - ENERGY_CRITICAL, 0.0))


class Geometry:
    def __init__(self, nx, ny, nz):
        self.nx, self.ny, self.nz = nx, ny, nz
        self.lane = lax.broadcasted_iota(jnp.int32, (1, nz), 1)
        self.first = self.lane == 0
        self.last = self.lane == nz - 1

    def before(self, own, other):
        return pltpu.roll(jnp.where(self.last, other, own), 1, 1)

    def after(self, own, other):
        return pltpu.roll(jnp.where(self.first, other, own), self.nz - 1, 1)


def chem_of(f, m, around, mean):
    well = 2.0 * WELL_HEIGHT * f * (1.0 - f) * (1.0 - 2.0 * f)
    return well + 6.0 * f - around + STRAIN_COUPLING * m * (f - mean)


def chemistry(g, pad_ref, mob_ref, mobe_ref, ze_ref, chem_ref, cheme_ref, mean):
    nx, ny = g.nx, g.ny
    for p in range(nx + 2):
        inside = 1 <= p <= nx
        rows = chunks(OFF - 8, OFF + ny + 8, 32) if inside else chunks(OFF, OFF + ny, 48)
        for r, n in rows:
            f = pad_ref[p + 1, r:r + n, :]
            e = ze_ref[p, r:r + n, :]
            around = (pad_ref[p, r:r + n, :] + pad_ref[p + 2, r:r + n, :]
                      + pad_ref[p + 1, r - 1:r - 1 + n, :] + pad_ref[p + 1, r + 1:r + 1 + n, :]
                      + g.before(f, e) + g.after(f, e))
            chem_ref[p, r:r + n, :] = chem_of(f, mob_ref[p, r:r + n, :], around, mean)
        if inside:
            for r, n in chunks(OFF, OFF + ny, 48):
                f = pad_ref[p + 1, r:r + n, :]
                e = ze_ref[p, r:r + n, :]
                around = (ze_ref[p - 1, r:r + n, :] + ze_ref[p + 1, r:r + n, :]
                          + ze_ref[p, r - 1:r - 1 + n, :] + ze_ref[p, r + 1:r + 1 + n, :]
                          + g.before(e, f) + g.after(e, f))
                cheme_ref[p - 1, r - OFF:r - OFF + n, :] = chem_of(
                    e, mobe_ref[p - 1, r - OFF:r - OFF + n, :], around, mean)


def flux_of(g, x, r, n, mob_ref, mobe_ref, chem_ref, cheme_ref):
    p = x + 1
    m = mob_ref[p, r:r + n, :]
    q = chem_ref[p, r:r + n, :]
    me = mobe_ref[x, r - OFF:r - OFF + n, :]
    qe = cheme_ref[x, r - OFF:r - OFF + n, :]
    total = None
    for nm, nq in (
        (mob_ref[p - 1, r:r + n, :], chem_ref[p - 1, r:r + n, :]),
        (mob_ref[p + 1, r:r + n, :], chem_ref[p + 1, r:r + n, :]),
        (mob_ref[p, r - 1:r - 1 + n, :], chem_ref[p, r - 1:r - 1 + n, :]),
        (mob_ref[p, r + 1:r + 1 + n, :], chem_ref[p, r + 1:r + 1 + n, :]),
        (g.before(m, me), g.before(q, qe)),
        (g.after(m, me), g.after(q, qe)),
    ):
        term = (nm + m) * (nq - q)
        total = term if total is None else total + term
    return m, 0.5 * total


def pack_edges(values, lane, nz):
    out = values[0]
    for x, v in enumerate(values[1:], 1):
        out = jnp.where(group(lane, x, nz, -1, 2), pltpu.roll(v, 32 * x, 1), out)
    return out


def step_a(ride_y, ride_z):
    def kernel(f_ref, amp_ref, lo_ref, hi_ref, yr_ref, zr_ref, yp_ref,
               f2_ref, a2_ref, ae2_ref, lo_out, hi_out, sum_ref,
               pad_ref, ze_ref, mob_ref, mobe_ref, chem_ref, cheme_ref):
        nx, ny, nz = f2_ref.shape
        end = OFF + ny
        g = Geometry(nx, ny, nz)
        mean = weighted_mean(yp_ref, yr_ref, zr_ref, ride_y, ride_z)
        fill(A_CODE, f_ref, lo_ref, hi_ref, yr_ref, zr_ref, pad_ref, ze_ref)

        def wear(p, r, n, a):
            m = a * a
            mob_ref[p, r:r + n, :] = m
            a2_ref[p, r:r + n, :] = worn(a, m, pad_ref[p + 1, r:r + n, :], mean)

        for r, n in chunks(0, ny, 48):
            wear(0, OFF + r, n, from_code(lo_ref[2 * ny + r:2 * ny + r + n, :], A_CODE))
            wear(nx + 1, OFF + r, n, from_code(hi_ref[2 * ny + r:2 * ny + r + n, :], A_CODE))
            edges = []
            for x in range(nx):
                wear(x + 1, OFF + r, n, amp_ref[x, r:r + n, :])
                p = x + 1
                a = pltpu.roll(zr_ref[p // 4, OFF + r:OFF + r + n, :], nz - 32 * (p % 4) - 16, 1)
                m = a * a
                mobe_ref[x, r:r + n, :] = m
                edges.append(worn(a, m, ze_ref[p, OFF + r:OFF + r + n, :], mean))
            ae2_ref[r:r + n, :] = pack_edges(edges, g.lane, nz)
        for x in range(nx):
            wear(x + 1, OFF - 1, 1, yr_ref[1, 10 + x:11 + x, :])
            wear(x + 1, end, 1, yr_ref[0, 10 + x:11 + x, :])
        chemistry(g, pad_ref, mob_ref, mobe_ref, ze_ref, chem_ref, cheme_ref, mean)
        top = jnp.zeros((8, nz), F32)
        bottom = jnp.zeros((8, nz), F32)
        for x in range(nx):
            for r, n in chunks(OFF, end, 48):
                _, flux = flux_of(g, x, r, n, mob_ref, mobe_ref, chem_ref, cheme_ref)
                f = pad_ref[x + 2, r:r + n, :] + TIME_STEP * flux
                s = slice(r - OFF, r - OFF + n)
                f2_ref[x, s, :] = f
                a = a2_ref[x + 1, r:r + n, :]
                m = a * a
                top = top + fold(m * f)
                bottom = bottom + fold(m)
                for near, far, out in ((0, 1, lo_out), (nx - 1, nx - 2, hi_out)):
                    if x == near:
                        out[s, :] = to_code(f, B_CODE)
                    if x == far:
                        out[r - OFF + ny:r - OFF + ny + n, :] = to_code(f, B_CODE)
        s = to_rows(top, bottom)
        sum_ref[...] = s
        lo_out[2 * ny:2 * ny + 16, :] = sum_digits(s)
        hi_out[2 * ny:2 * ny + 16, :] = sum_digits(s)
    return kernel


def step_b(ride_y, ride_z):
    def kernel(f_ref, a2_ref, ae2_ref, lo_ref, hi_ref, yr_ref, zr_ref, yp_ref, l_hbm,
               f3_hbm, dmg_hbm, flux_hbm, pool_ref, edge_ref,
               pad_ref, ze_ref, mob_ref, mobe_ref, chem_ref, cheme_ref,
               pool_scr, l_ref, f3_ref, dmg_ref, flux_ref, l_sem, sems):
        nx, ny, nz = f3_ref.shape
        labels_in = pltpu.make_async_copy(l_hbm, l_ref, l_sem)
        labels_in.start()
        g = Geometry(nx, ny, nz)
        mean = weighted_mean(yp_ref, yr_ref, zr_ref, ride_y, ride_z)
        fill(B_CODE, f_ref, lo_ref, hi_ref, yr_ref, zr_ref, pad_ref, ze_ref)
        for p in range(nx + 2):
            inside = 1 <= p <= nx
            for r, n in chunks(OFF - 8, OFF + ny + 8, 32) if inside else chunks(OFF, OFF + ny, 48):
                a = a2_ref[p, r:r + n, :]
                mob_ref[p, r:r + n, :] = a * a
        for r, n in chunks(0, ny, 48):
            a = ae2_ref[r:r + n, :]
            a = a * a
            for x in range(nx):
                mobe_ref[x, r:r + n, :] = pltpu.roll(a, nz - 32 * x, 1) if x else a
        chemistry(g, pad_ref, mob_ref, mobe_ref, ze_ref, chem_ref, cheme_ref, mean)
        labels_in.wait()
        copies = []
        for k, (r, n) in enumerate(chunks(OFF, OFF + ny, 48)):
            s = slice(r - OFF, r - OFF + n)
            pooled = [None] * 4
            for x in range(nx):
                m, flux = flux_of(g, x, r, n, mob_ref, mobe_ref, chem_ref, cheme_ref)
                f0 = pad_ref[x + 2, r:r + n, :]
                f = f0 + TIME_STEP * flux
                a = worn(a2_ref[x + 1, r:r + n, :], m, f0, mean)
                labels = l_ref[x, s, :]
                factor = by_label(labels, FACTORS)
                dmg = 1.0 - a * by_label(labels, tuple(1.0 / v for v in ROOTS))
                f3_ref[x, s, :] = f
                dmg_ref[x, s, :] = dmg
                flux_ref[x, s, :] = flux
                for i, v in enumerate((f, dmg, a * a, factor)):
                    pooled[i] = v if pooled[i] is None else pooled[i] + v
            for i in range(4):
                pool_scr[i, s, :] = pooled[i]
            for i, (src, dst) in enumerate(((f3_ref, f3_hbm), (dmg_ref, dmg_hbm), (flux_ref, flux_hbm))):
                copies.append(pltpu.make_async_copy(src.at[:, s, :], dst.at[:, s, :], sems.at[i, k]))
                copies[-1].start()
        py, pz = ny // 4, nz // 4
        zin = lax.broadcasted_iota(jnp.int32, (nz, 4 * pz), 0)
        out = lax.broadcasted_iota(jnp.int32, (nz, 4 * pz), 1)
        total = jnp.zeros((py, 4 * pz), F32)
        for i in range(4):
            rows = (pool_scr[i, pl.ds(0, py, stride=4), :] + pool_scr[i, pl.ds(1, py, stride=4), :]
                    + pool_scr[i, pl.ds(2, py, stride=4), :] + pool_scr[i, pl.ds(3, py, stride=4), :])
            pick = jnp.where((zin // 4 == out // 4) & (out % 4 == i), 1.0 / 64.0, 0.0).astype(F32)
            total = total + jnp.dot(rows, pick, precision=lax.Precision.HIGHEST, preferred_element_type=F32)
        pool_ref[...] = total.astype(BF16)
        blank = jnp.zeros((13, 4 * pz), F32)
        edge_ref[0] = jnp.concatenate([total[0:3], blank]).astype(BF16)
        edge_ref[1] = jnp.concatenate([total[py - 3:py], blank]).astype(BF16)
        for c in copies:
            c.wait()
    return kernel


def ring(axis, shift):
    count = lax.axis_size(axis)
    return [(i, (i + shift) % count) for i in range(count)]


def pair_sum(s, axis):
    count = lax.axis_size(axis)
    if count & (count - 1):
        return lax.psum(s, axis)
    bit = 1
    while bit < count:
        s = s + lax.ppermute(s, axis, [(i, i ^ bit) for i in range(count)])
        bit *= 2
    return s


def both_sides(pay, axis):
    if lax.axis_size(axis) == 2:
        return lax.ppermute(pay, axis, ring(axis, 1))
    return jnp.stack([lax.ppermute(pay[0], axis, ring(axis, -1)), lax.ppermute(pay[1], axis, ring(axis, 1))])


def z_neighbour(pay, axis, packed=True):
    if lax.axis_size(axis) == 2:
        return lax.ppermute(pay, axis, ring(axis, 1))
    above = lax.ppermute(pay, axis, ring(axis, -1))
    below = lax.ppermute(pay, axis, ring(axis, 1))
    lane = lax.broadcasted_iota(jnp.int32, pay.shape, pay.ndim - 1)
    if packed:
        low = (lane % 32 < 8) | (lane % 32 == 16)
    else:
        low = lane < pay.shape[-1] // 2
    return jnp.where(low, above, below)


def x_sides(lo, hi):
    return lax.ppermute(hi, "gx", ring("gx", 1)), lax.ppermute(lo, "gx", ring("gx", -1))


def body(concentration, damage, labels, w_first, b_first, w_second, b_second, w_third, b_third):
    nx, ny, nz = concentration.shape
    rows = ny + 2 * OFF
    block = (nx, ny, nz)
    padded = (nx + 2, rows, nz)
    ride_x = lax.axis_size("gx") == 4
    ride_y = lax.axis_size("gy") == 2
    ride_z = lax.axis_size("gz") == 2
    packed = (-(-(nx + 2) // 4), rows, nz)
    assert nz == 128
    scratch = [pltpu.VMEM((nx + 4, rows, nz), F32), pltpu.VMEM(padded, F32), pltpu.VMEM(padded, F32),
               pltpu.VMEM(block, F32), pltpu.VMEM(padded, F32), pltpu.VMEM(block, F32)]

    def start(sums):
        if ride_x:
            return sums, lax.ppermute(sums, "gx", ring("gx", 2))
        sums = pair_sum(sums, "gx")
        for axis, ride in (("gy", ride_y), ("gz", ride_z)):
            if not ride:
                sums = pair_sum(sums, axis)
        return sums, sums

    concentration, damage, labels = (
        pltpu.with_memory_space_constraint(v, pltpu.HBM) for v in (concentration, damage, labels))
    tall = 3 * ny + 16
    f, amp, lo, hi, sums = call(
        first_kernel,
        [(block, F32), (block, F32), ((tall, nz), I16), ((tall, nz), I16), ((8, nz), F32)],
        concentration, damage, labels,
        in_specs=[HBM] * 3,
        scratch=[pltpu.VMEM(block, F32), pltpu.VMEM(block, jnp.int32), pltpu.SemaphoreType.DMA((3, nx))])
    *matrices, order = weight_matrices(w_first, b_first, w_second, b_second, w_third, nz, nz // 4)
    sums, far = start(sums)
    lo, hi = x_sides(lo, hi)
    (ypay,) = call(edge_rows(A_CODE, ride_x, True), [((2, 24, nz), F32)], f, amp, lo, hi, sums, far, order)
    yr = both_sides(ypay, "gy")
    (zpay,) = call(pack_z(A_CODE, ride_y, True), [(packed, F32)], f, amp, lo, hi, yr, ypay)
    zr = z_neighbour(zpay, "gz")
    tall = 2 * ny + 16
    f, a2, ae2, lo, hi, sums = call(
        step_a(ride_y, ride_z),
        [(block, F32), (padded, F32), ((ny, nz), F32), ((tall, nz), I16), ((tall, nz), I16), ((8, nz), F32)],
        f, amp, lo, hi, yr, zr, ypay, scratch=scratch)

    sums, far = start(sums)
    lo, hi = x_sides(lo, hi)
    (ypay,) = call(edge_rows(B_CODE, ride_x, False), [((2, 24, nz), F32)], f, lo, hi, sums, far)
    yr = both_sides(ypay, "gy")
    (zpay,) = call(pack_z(B_CODE, ride_y, False), [(packed, F32)], f, lo, hi, yr, ypay)
    zr = z_neighbour(zpay, "gz")
    fraction, damage_field, flux_sum, pooled, edge = call(
        step_b(ride_y, ride_z),
        [(block, F32), (block, F32), (block, F32), ((ny // 4, nz), BF16), ((2, 16, nz), BF16)],
        f, a2, ae2, lo, hi, yr, zr, ypay, labels,
        in_specs=[VMEM] * 8 + [HBM], out_specs=[HBM] * 3 + [VMEM] * 2,
        scratch=scratch + [
            pltpu.VMEM((4, ny, nz), F32), pltpu.VMEM(block, jnp.int32),
            pltpu.VMEM(block, F32), pltpu.VMEM(block, F32), pltpu.VMEM(block, F32),
            pltpu.SemaphoreType.DMA, pltpu.SemaphoreType.DMA((3, len(chunks(OFF, OFF + ny, 48))))])
    ids = jnp.stack([lax.axis_index(a) for a in ("gx", "gy", "gz")])
    crack_score = detector(pooled, edge, ids, matrices, b_third, ny // 4, nz // 4)
    return (fraction, damage_field, flux_sum, crack_score)


CH = 16
CIN = 4
TOP = 8


def iota(shape, dim):
    return lax.broadcasted_iota(jnp.int32, shape, dim)


def lanes_for(n):
    return -(-n // 128) * 128


def one_hot(mask):
    return jnp.where(mask, 1.0, 0.0).astype(BF16)


def mm(a, b):
    return jnp.dot(a, b, preferred_element_type=F32)


def tile_shift(rb, cb, pz):
    z_in = rb * 16 // CIN
    z_in = z_in if z_in < pz + pz // 2 else z_in - 2 * pz
    return z_in - cb * 8 + 3


SHIFTS = tuple(k for k in range(-3, 10) if k % (16 // CIN) == 3)


def weight_kernel(w1_ref, w2_ref, w3_ref, b1_ref, b2_ref, t1_hbm, t2_hbm, t3_hbm, bias_hbm, order_ref,
                  t1_ref, t2_ref, t3_ref, bias_ref, sems):
    n1 = bias_ref.shape[1]
    k1 = t1_ref.shape[1] // 3
    pz = k1 // (2 * CIN)
    spread = one_hot(iota((CH, 128), 1) % CH == iota((CH, 128), 0))
    tile1 = mm(w1_ref[...], spread)
    tile2 = mm(w2_ref[...], spread)
    tile3 = mm(w3_ref[...], one_hot(iota((3, 128), 1) // pz == iota((3, 128), 0)))
    step1 = iota((16, 128), 0) // CIN - iota((16, 128), 1) // CH
    step2 = -(iota((16, 128), 1) // CH)
    step3 = -(iota((16, 128), 1) % pz)

    def tile(source, base, stride, step, shift):
        out = jnp.zeros((16, 128), F32)
        for l in range(3):
            k = base + stride * l
            out = jnp.where(step + shift == l, source[16 * k:16 * k + 16], out)
        return out.astype(BF16)

    zero = jnp.zeros((16, 128), BF16)
    bias_ref[...] = jnp.zeros(bias_ref.shape, F32)
    for i in range(3):
        for j in range(3):
            tap = 9 * i + 3 * j
            known = {k: tile(tile1, tap, 1, step1, k) for k in SHIFTS}
            for rb in range(k1 // 16):
                for cb in range(n1 // 128):
                    t1_ref[i, j * k1 + rb * 16:j * k1 + rb * 16 + 16, cb * 128:(cb + 1) * 128] = known.get(
                        tile_shift(rb, cb, pz), zero)
            for rb in range(16):
                t2_ref[i, j * 256 + rb * 16:j * 256 + rb * 16 + 16, :] = (
                    tile(tile2, tap, 1, step2, rb) if rb < 10 else zero)
        for rb in range(t3_ref.shape[1] // 16):
            t3_ref[i, rb * 16:rb * 16 + 16, :] = tile(tile3, 3 * i, 1, step3, rb) if rb < pz + 2 else zero
    wide = one_hot(iota((CH, n1), 1) % CH == iota((CH, n1), 0)).astype(F32)
    for k, ref in ((0, b1_ref), (1, b2_ref)):
        bias_ref[k:k + 1, :] = jnp.dot(ref[...], wide, precision=lax.Precision.HIGHEST, preferred_element_type=F32)
    order_ref[...] = jnp.zeros(order_ref.shape, F32)
    copies = [pltpu.make_async_copy(src, dst, sems.at[k]) for k, (src, dst) in enumerate(
        ((t1_ref, t1_hbm), (t2_ref, t2_hbm), (t3_ref, t3_hbm), (bias_ref, bias_hbm)))]
    for c in copies:
        c.start()
    for c in copies:
        c.wait()


def weight_matrices(w_first, b_first, w_second, b_second, w_third, half, pz):
    width = lanes_for((pz + 4) * CH)
    rows1 = jnp.tile(jnp.swapaxes(w_first, 1, 2), (1, 16 // CIN, 1)).reshape(27 * 16, CH)
    rows2 = jnp.swapaxes(w_second, 1, 2).reshape(27 * CH, CH)
    rows3 = w_third.reshape(3, 3, 3, CH).transpose(0, 2, 3, 1).reshape(9 * CH, 3)
    outs = [((3, 6 * half, width), BF16), ((3, 768, 128), BF16), ((3, width, 128), BF16), ((8, width), F32)]
    return pl.pallas_call(
        weight_kernel,
        in_specs=[VMEM] * 5,
        out_specs=[HBM] * 4 + [VMEM],
        out_shape=[pltpu.HBM(*v) for v in outs] + [jax.ShapeDtypeStruct((8, 128), F32)],
        scratch_shapes=[pltpu.VMEM(*v) for v in outs] + [pltpu.SemaphoreType.DMA((4,))],
        compiler_params=pltpu.CompilerParams(vmem_limit_bytes=16 * 1024 * 1024),
    )(rows1, rows2, rows3, b_first[None], b_second[None])


def gelu(x):
    return 0.5 * x * (1.0 + jnp.tanh(0.7978845608028654 * (x + 0.044715 * (x * x * x))))


def plane_kernel(py, y_count):
    def kernel(ids_ref, pool_ref, yr_ref, out_ref, scr_ref):
        iy = ids_ref[1]
        scr_ref[...] = jnp.zeros(scr_ref.shape, F32)
        scr_ref[TOP:TOP + py, :] = pool_ref[0:py, :].astype(F32)
        below = yr_ref[1].astype(F32)[0:3]
        above = yr_ref[0].astype(F32)[0:3]
        scr_ref[TOP - 3:TOP, :] = jnp.where(iy > 0, below, 0.0)
        scr_ref[TOP + py:TOP + py + 3, :] = jnp.where(iy < y_count - 1, above, 0.0)
        out_ref[...] = scr_ref[...].astype(BF16)
    return kernel


def conv_kernel(py, counts, shifts):
    x_count, y_count, z_count = counts
    n = len(shifts)

    def kernel(*refs):
        ids_ref, b3_ref = refs[:2]
        own = refs[2:3 + n]
        other = refs[3 + n:4 + 2 * n]
        t1_ref, t2_ref, t3_ref, bias_ref, out_ref = refs[4 + 2 * n:9 + 2 * n]
        in_ref, lhs1_ref, act1_ref, lhs2_ref, act2_ref, tail_ref = refs[9 + 2 * n:]
        ix, iy, iz = ids_ref[0], ids_ref[1], ids_ref[2]
        half = own[0].shape[1]
        pz = half // CIN
        rows = py + 4
        z_row = iota((1, half), 1) // CIN
        z_ok = ((z_row < pz // 2) & (iz < z_count - 1)) | ((z_row >= pz // 2) & (iz > 0))
        for w in range(7):
            o = w - 3
            k = 0 if o == 0 else 1 + shifts.index((-o) % x_count) if (-o) % x_count in shifts else None
            if k is None:
                in_ref[w] = jnp.zeros(in_ref.shape[1:], F32)
                continue
            inside = (ix + o >= 0) & (ix + o < x_count)
            in_ref[w, :, 0:half] = jnp.where(inside, own[k][...].astype(F32), 0.0)
            in_ref[w, :, half:] = jnp.where(z_ok & inside, other[k][...].astype(F32), 0.0)
        k1 = 2 * half
        for w in range(7):
            for j in range(3):
                start = TOP - 3 + j
                lhs1_ref[w, :, j * k1:(j + 1) * k1] = in_ref[w, start:start + rows, :].astype(BF16)
        out = None
        for i in range(3):
            part = mm(lhs1_ref[i:i + 5].reshape(5 * rows, 3 * k1), t1_ref[i])
            out = part if out is None else out + part
        width = out.shape[1]
        y = iota((rows, width), 0) - 2
        z = iota((rows, width), 1) // CH - 2
        ok = (z < pz + 2) & ((y >= 0) | (iy > 0)) & ((y < py) | (iy < y_count - 1))
        ok = ok & ((z >= 0) | (iz > 0)) & ((z < pz) | (iz < z_count - 1))
        for p in range(5):
            a = gelu(out[p * rows:(p + 1) * rows] + bias_ref[0:1, :])
            good = ok & (ix + p - 2 >= 0) & (ix + p - 2 < x_count)
            act1_ref[p, 0:rows, 0:width] = jnp.where(good, a, 0.0)
            act1_ref[p, rows:, 0:width] = jnp.zeros((act1_ref.shape[1] - rows, width), F32)
            act1_ref[p, :, width:] = jnp.zeros((act1_ref.shape[1], act1_ref.shape[2] - width), F32)
        blocks = lhs2_ref.shape[1]
        for p in range(5):
            for j in range(3):
                a = act1_ref[p, j:j + rows, :].astype(BF16)
                for b in range(blocks):
                    lhs2_ref[p, b, :, j * 256:(j + 1) * 256] = a[:, b * 128:b * 128 + 256]
        out = None
        for i in range(3):
            part = mm(lhs2_ref[i:i + 3].reshape(3 * blocks * rows, 768), t2_ref[i])
            out = part if out is None else out + part
        for b in range(blocks):
            y = iota((rows, 128), 0) - 1
            z = (iota((rows, 128), 1) + b * 128) // CH - 1
            ok = (z < pz + 1) & (y <= py) & ((y >= 0) | (iy > 0)) & ((y < py) | (iy < y_count - 1))
            ok = ok & ((z >= 0) | (iz > 0)) & ((z < pz) | (iz < z_count - 1))
            for p in range(3):
                s = (p * blocks + b) * rows
                a = gelu(out[s:s + rows] + bias_ref[1:2, 0:128])
                good = ok & (ix + p - 1 >= 0) & (ix + p - 1 < x_count)
                act2_ref[p, :, b * 128:(b + 1) * 128] = jnp.where(good, a, 0.0).astype(BF16)
        out = None
        for i in range(3):
            part = mm(act2_ref[i], t3_ref[i])
            out = part if out is None else out + part
        tail_ref[0:rows, :] = out
        score = tail_ref[0:py, :]
        for j in (1, 2):
            score = score + pltpu.roll(tail_ref[j:j + py, :], 128 - j * pz, 1)
        out_ref[0] = jnp.transpose(score)[0:pz, :] + b3_ref[0]
    return kernel


def detector(pooled, edge, ids, matrices, b_third, py, pz):
    counts = tuple(lax.axis_size(a) for a in ("gx", "gy", "gz"))
    half = pooled.shape[1]
    assert half == 128 and pz * CIN == half and pz * 3 <= 128
    rows = py + 4
    width = lanes_for((pz + 4) * CH)
    blocks = width // 128
    yr = both_sides(edge, "gy")
    tall = -(-(TOP + py + 3) // 16) * 16
    (plane,) = call(
        plane_kernel(py, counts[1]), [((tall, half), BF16)], ids, pooled, yr,
        in_specs=[SMEM, VMEM, VMEM], scratch=[pltpu.VMEM((tall, half), F32)])
    shifts = []
    for s in (1, -1, 2, -2, 3, -3):
        if s % counts[0] and s % counts[0] not in shifts:
            shifts.append(s % counts[0])
    own = [plane] + [lax.ppermute(plane, "gx", ring("gx", s)) for s in shifts]
    other = [z_neighbour(v, "gz", False) for v in own]
    args = (ids, b_third, *own, *other, *matrices)
    (score,) = call(
        conv_kernel(py, counts, shifts), [((1, pz, py), F32)], *args,
        in_specs=[SMEM] * 2 + [VMEM] * (len(args) - 2),
        scratch=[
            pltpu.VMEM((7, tall, 2 * half), F32),
            pltpu.VMEM((7, rows, 6 * half), BF16),
            pltpu.VMEM((5, rows + 8, width + 128), F32),
            pltpu.VMEM((5, blocks, rows, 768), BF16),
            pltpu.VMEM((3, rows, width), BF16),
            pltpu.VMEM((rows + 8, 128), F32),
        ], mib=32)
    return jnp.swapaxes(score, 1, 2)


def solution(mesh):
    slab = P(("groups", "gx"), "gy", "gz")
    return jax.shard_map(
        body,
        mesh=mesh,
        in_specs=(slab, slab, slab, P(), P(), P(), P(), P(), P()),
        out_specs=(slab, slab, slab, slab),
        check_vma=False,
    )
```

```python
import jax
import jax.numpy as jnp
import numpy as np
from jax import lax
from jax.experimental import pallas as pl
from jax.experimental.pallas import tpu as pltpu
from jax.sharding import PartitionSpec as P

F32 = jnp.float32
BF16 = jnp.bfloat16
I16 = jnp.int16
WELL_HEIGHT = 1.0
STRAIN_COUPLING = 4.0
TIME_STEP = 0.01
DAMAGE_RATE = 0.8
ENERGY_CRITICAL = 0.02

OFF = 16
A_CODE = (0.0, 1.0)
B_CODE = (-1.1, 3.1)
SUM_LOW, SUM_SPAN = -1280.0, 4096.0

VMEM = pl.BlockSpec(memory_space=pltpu.VMEM)
SMEM = pl.BlockSpec(memory_space=pltpu.SMEM)
HBM = pl.BlockSpec(memory_space=pltpu.HBM)


def to_code(x, code):
    low, span = code
    v = (x - low) * (65535.0 / span) - 32768.0
    return jnp.clip(jnp.round(v), -32768.0, 32767.0).astype(jnp.int32).astype(I16)


def from_code(q, code):
    low, span = code
    return q.astype(jnp.int32).astype(F32) * (span / 65535.0) + (low + 32768.0 * span / 65535.0)


def sum_digits(s):
    v = (s[0:2] - SUM_LOW) * (65536.0 / SUM_SPAN)
    high = jnp.floor(v)
    low = jnp.minimum(jnp.floor((v - high) * 65536.0), 65535.0)
    rows = jnp.concatenate([high, low, jnp.full((12, s.shape[1]), 32768.0, F32)]) - 32768.0
    return rows.astype(jnp.int32).astype(I16)


def from_digits(tile):
    v = tile.astype(jnp.int32).astype(F32) + 32768.0
    return (v[0:2] + v[2:4] * (1.0 / 65536.0)) * (SUM_SPAN / 65536.0) + SUM_LOW


def by_label(labels, values):
    return jnp.where(labels == 0, values[0], jnp.where(labels == 1, values[1], values[2])).astype(F32)


FACTORS = (1.0, 0.3, 0.05)
ROOTS = tuple(float(np.sqrt(np.float32(v))) for v in FACTORS)


def call(kernel, outs, *args, in_specs=None, out_specs=None, scratch=(), mib=16):
    return pl.pallas_call(
        kernel,
        in_specs=in_specs or [VMEM] * len(args),
        out_specs=out_specs or [VMEM] * len(outs),
        out_shape=[jax.ShapeDtypeStruct(s, t) for s, t in outs],
        scratch_shapes=scratch,
        compiler_params=pltpu.CompilerParams(vmem_limit_bytes=mib * 1024 * 1024),
    )(*args)


def chunks(start, stop, size):
    return [(r, min(size, stop - r)) for r in range(start, stop, size)]


def fold(x):
    return x.reshape(x.shape[0] // 8, 8, x.shape[1]).sum(0)


def to_rows(top, bottom):
    return jnp.concatenate([jnp.sum(top, 0, keepdims=True), jnp.sum(bottom, 0, keepdims=True),
                            jnp.zeros((6, top.shape[1]), F32)])


def first_kernel(c_hbm, d_hbm, l_hbm, f_ref, amp_ref, lo_ref, hi_ref, sum_ref, d_ref, l_ref, sems):
    nx, ny, nz = f_ref.shape
    order = [0, nx - 1] + list(range(1, nx - 1))
    copies = []
    for x in order:
        copies.append([pltpu.make_async_copy(src.at[x], dst.at[x], sems.at[k, x])
                       for k, (src, dst) in enumerate(((c_hbm, f_ref), (d_hbm, d_ref), (l_hbm, l_ref)))])
        for c in copies[-1]:
            c.start()
    top = jnp.zeros((8, nz), F32)
    bottom = jnp.zeros((8, nz), F32)
    for k, x in enumerate(order):
        for c in copies[k]:
            c.wait()
        for r, n in chunks(0, ny, 48):
            f = f_ref[x, r:r + n, :]
            a = by_label(l_ref[x, r:r + n, :], ROOTS) * (1.0 - d_ref[x, r:r + n, :])
            amp_ref[x, r:r + n, :] = a
            m = a * a
            top = top + fold(m * f)
            bottom = bottom + fold(m)
            for near, far, out in ((0, 1, lo_ref), (nx - 1, nx - 2, hi_ref)):
                if x == near:
                    out[r:r + n, :] = to_code(f, A_CODE)
                    out[2 * ny + r:2 * ny + r + n, :] = to_code(a, A_CODE)
                if x == far:
                    out[ny + r:ny + r + n, :] = to_code(f, A_CODE)
    s = to_rows(top, bottom)
    sum_ref[...] = s
    lo_ref[3 * ny:3 * ny + 16, :] = sum_digits(s)
    hi_ref[3 * ny:3 * ny + 16, :] = sum_digits(s)


def edge_rows(code, ride_x, with_amp):
    def kernel(*refs):
        f_ref = refs[0]
        amp_ref = refs[1] if with_amp else None
        lo_ref, hi_ref, s_ref, far_ref = refs[1 + with_amp:5 + with_amp]
        out_ref = refs[-1]
        nx, ny, nz = f_ref.shape
        low_rows = [from_code(r[0:16, :], code)[0:1] for r in (lo_ref, hi_ref)]
        high_rows = [from_code(r[ny - 16:ny, :], code)[15:16] for r in (lo_ref, hi_ref)]
        s = s_ref[...]
        if ride_x:
            s = s + far_ref[...]
        for side, first, second, beside in ((0, 0, 1, low_rows), (1, ny - 1, ny - 2, high_rows)):
            for x in range(nx):
                out_ref[side, 2 * x:2 * x + 1, :] = f_ref[x, first:first + 1, :]
                out_ref[side, 2 * x + 1:2 * x + 2, :] = f_ref[x, second:second + 1, :]
                if amp_ref is not None:
                    out_ref[side, 10 + x:11 + x, :] = amp_ref[x, first:first + 1, :]
            out_ref[side, 8:9, :] = beside[0]
            out_ref[side, 9:10, :] = beside[1]
            out_ref[side, 16:24, :] = s
            if ride_x:
                out_ref[side, 16:18, :] = (s[0:2] + from_digits(lo_ref[lo_ref.shape[0] - 16:, :])
                                           + from_digits(hi_ref[hi_ref.shape[0] - 16:, :]))
    return kernel


def group(lane, j, nz, first, count):
    return (lane - (32 * j + first)) % nz < count


def pack_z(code, ride_y, with_amp):
    def kernel(*refs):
        f_ref = refs[0]
        amp_ref = refs[1] if with_amp else None
        lo_ref, hi_ref, yr_ref, yp_ref, out_ref = refs[1 + with_amp:]
        nx, ny, nz = f_ref.shape
        end = OFF + ny
        lane = lax.broadcasted_iota(jnp.int32, (1, nz), 1)
        for k in range(out_ref.shape[0]):
            planes = [p for p in range(4 * k, 4 * k + 4) if p < nx + 2]

            def packed(f_of, a_of, ps):
                out = None
                for p in ps:
                    j = p % 4
                    f = f_of(p)
                    f = pltpu.roll(f, 32 * j, 1) if j else f
                    out = f if out is None else jnp.where(group(lane, j, nz, -2, 4), f, out)
                    a = a_of(p)
                    if a is not None:
                        out = jnp.where(group(lane, j, nz, 15, 2), pltpu.roll(a, 32 * j + 16, 1), out)
                return out

            for r, n in chunks(0, ny, 48):
                def f_of(p):
                    if p == 0:
                        return from_code(lo_ref[r:r + n, :], code)
                    if p == nx + 1:
                        return from_code(hi_ref[r:r + n, :], code)
                    return f_ref[p - 1, r:r + n, :]

                def a_of(p):
                    return amp_ref[p - 1, r:r + n, :] if with_amp and 1 <= p <= nx else None

                out_ref[k, OFF + r:OFF + r + n, :] = packed(f_of, a_of, planes)
            inner = [p for p in planes if 1 <= p <= nx]
            if inner:
                for side, near in ((1, OFF - 1), (0, end)):
                    out_ref[k, near:near + 1, :] = packed(
                        lambda p: yr_ref[side, 2 * (p - 1):2 * (p - 1) + 1, :], lambda p: None, inner)
        s = yp_ref[0, 16:24, :]
        out_ref[0, 0:8, :] = s + yr_ref[0, 16:24, :] if ride_y else s
    return kernel


def fill(code, f_ref, lo_ref, hi_ref, yr_ref, zr_ref, pad_ref, ze_ref):
    nx, ny, nz = f_ref.shape
    end = OFF + ny
    for near, far, ref in ((1, 0, lo_ref), (nx + 2, nx + 3, hi_ref)):
        for r, n in chunks(0, ny, 48):
            pad_ref[near, OFF + r:OFF + r + n, :] = from_code(ref[r:r + n, :], code)
            pad_ref[far, OFF + r:OFF + r + n, :] = from_code(ref[ny + r:ny + r + n, :], code)
    for p, k in ((1, 8), (nx + 2, 9)):
        pad_ref[p, OFF - 1:OFF, :] = yr_ref[1, k:k + 1, :]
        pad_ref[p, end:end + 1, :] = yr_ref[0, k:k + 1, :]
    for x in range(nx):
        for r, n in chunks(0, ny, 48):
            pad_ref[x + 2, OFF + r:OFF + r + n, :] = f_ref[x, r:r + n, :]
        for side, near, far in ((1, OFF - 1, OFF - 2), (0, end, end + 1)):
            pad_ref[x + 2, near:near + 1, :] = yr_ref[side, 2 * x:2 * x + 1, :]
            pad_ref[x + 2, far:far + 1, :] = yr_ref[side, 2 * x + 1:2 * x + 2, :]
    for p in range(nx + 2):
        for r, n in chunks(OFF - 8, OFF + ny + 8, 32):
            e = zr_ref[p // 4, r:r + n, :]
            ze_ref[p, r:r + n, :] = pltpu.roll(e, nz - 32 * (p % 4), 1) if p % 4 else e


def weighted_mean(yp_ref, yr_ref, zr_ref, ride_y, ride_z):
    s = yp_ref[0, 16:24, :]
    if ride_y:
        s = s + yr_ref[0, 16:24, :]
    if ride_z:
        s = s + zr_ref[0, 0:8, :]
    return jnp.sum(s[0:1], keepdims=True) / jnp.sum(s[1:2], keepdims=True)


def worn(a, m, f, mean):
    e = f - mean
    energy = 0.5 * STRAIN_COUPLING * m * e * e
    return a * (1.0 - DAMAGE_RATE * jnp.maximum(energy - ENERGY_CRITICAL, 0.0))


class Geometry:
    def __init__(self, nx, ny, nz):
        self.nx, self.ny, self.nz = nx, ny, nz
        self.lane = lax.broadcasted_iota(jnp.int32, (1, nz), 1)
        self.first = self.lane == 0
        self.last = self.lane == nz - 1

    def before(self, own, other):
        return pltpu.roll(jnp.where(self.last, other, own), 1, 1)

    def after(self, own, other):
        return pltpu.roll(jnp.where(self.first, other, own), self.nz - 1, 1)


def chem_of(f, m, around, mean):
    well = 2.0 * WELL_HEIGHT * f * (1.0 - f) * (1.0 - 2.0 * f)
    return well + 6.0 * f - around + STRAIN_COUPLING * m * (f - mean)


def chemistry(g, pad_ref, mob_ref, mobe_ref, ze_ref, chem_ref, cheme_ref, mean):
    nx, ny = g.nx, g.ny
    for p in range(nx + 2):
        inside = 1 <= p <= nx
        rows = chunks(OFF - 8, OFF + ny + 8, 32) if inside else chunks(OFF, OFF + ny, 48)
        for r, n in rows:
            f = pad_ref[p + 1, r:r + n, :]
            e = ze_ref[p, r:r + n, :]
            around = (pad_ref[p, r:r + n, :] + pad_ref[p + 2, r:r + n, :]
                      + pad_ref[p + 1, r - 1:r - 1 + n, :] + pad_ref[p + 1, r + 1:r + 1 + n, :]
                      + g.before(f, e) + g.after(f, e))
            chem_ref[p, r:r + n, :] = chem_of(f, mob_ref[p, r:r + n, :], around, mean)
        if inside:
            for r, n in chunks(OFF, OFF + ny, 48):
                f = pad_ref[p + 1, r:r + n, :]
                e = ze_ref[p, r:r + n, :]
                around = (ze_ref[p - 1, r:r + n, :] + ze_ref[p + 1, r:r + n, :]
                          + ze_ref[p, r - 1:r - 1 + n, :] + ze_ref[p, r + 1:r + 1 + n, :]
                          + g.before(e, f) + g.after(e, f))
                cheme_ref[p - 1, r - OFF:r - OFF + n, :] = chem_of(
                    e, mobe_ref[p - 1, r - OFF:r - OFF + n, :], around, mean)


def flux_of(g, x, r, n, mob_ref, mobe_ref, chem_ref, cheme_ref):
    p = x + 1
    m = mob_ref[p, r:r + n, :]
    q = chem_ref[p, r:r + n, :]
    me = mobe_ref[x, r - OFF:r - OFF + n, :]
    qe = cheme_ref[x, r - OFF:r - OFF + n, :]
    total = None
    for nm, nq in (
        (mob_ref[p - 1, r:r + n, :], chem_ref[p - 1, r:r + n, :]),
        (mob_ref[p + 1, r:r + n, :], chem_ref[p + 1, r:r + n, :]),
        (mob_ref[p, r - 1:r - 1 + n, :], chem_ref[p, r - 1:r - 1 + n, :]),
        (mob_ref[p, r + 1:r + 1 + n, :], chem_ref[p, r + 1:r + 1 + n, :]),
        (g.before(m, me), g.before(q, qe)),
        (g.after(m, me), g.after(q, qe)),
    ):
        term = (nm + m) * (nq - q)
        total = term if total is None else total + term
    return m, 0.5 * total


def pack_edges(values, lane, nz):
    out = values[0]
    for x, v in enumerate(values[1:], 1):
        out = jnp.where(group(lane, x, nz, -1, 2), pltpu.roll(v, 32 * x, 1), out)
    return out


def step_a(ride_y, ride_z):
    def kernel(f_ref, amp_ref, lo_ref, hi_ref, yr_ref, zr_ref, yp_ref,
               f2_ref, a2_ref, ae2_ref, lo_out, hi_out, sum_ref,
               pad_ref, ze_ref, mob_ref, mobe_ref, chem_ref, cheme_ref):
        nx, ny, nz = f2_ref.shape
        end = OFF + ny
        g = Geometry(nx, ny, nz)
        mean = weighted_mean(yp_ref, yr_ref, zr_ref, ride_y, ride_z)
        fill(A_CODE, f_ref, lo_ref, hi_ref, yr_ref, zr_ref, pad_ref, ze_ref)

        def wear(p, r, n, a):
            m = a * a
            mob_ref[p, r:r + n, :] = m
            a2_ref[p, r:r + n, :] = worn(a, m, pad_ref[p + 1, r:r + n, :], mean)

        for r, n in chunks(0, ny, 48):
            wear(0, OFF + r, n, from_code(lo_ref[2 * ny + r:2 * ny + r + n, :], A_CODE))
            wear(nx + 1, OFF + r, n, from_code(hi_ref[2 * ny + r:2 * ny + r + n, :], A_CODE))
            edges = []
            for x in range(nx):
                wear(x + 1, OFF + r, n, amp_ref[x, r:r + n, :])
                p = x + 1
                a = pltpu.roll(zr_ref[p // 4, OFF + r:OFF + r + n, :], nz - 32 * (p % 4) - 16, 1)
                m = a * a
                mobe_ref[x, r:r + n, :] = m
                edges.append(worn(a, m, ze_ref[p, OFF + r:OFF + r + n, :], mean))
            ae2_ref[r:r + n, :] = pack_edges(edges, g.lane, nz)
        for x in range(nx):
            wear(x + 1, OFF - 1, 1, yr_ref[1, 10 + x:11 + x, :])
            wear(x + 1, end, 1, yr_ref[0, 10 + x:11 + x, :])
        chemistry(g, pad_ref, mob_ref, mobe_ref, ze_ref, chem_ref, cheme_ref, mean)
        top = jnp.zeros((8, nz), F32)
        bottom = jnp.zeros((8, nz), F32)
        for x in range(nx):
            for r, n in chunks(OFF, end, 48):
                _, flux = flux_of(g, x, r, n, mob_ref, mobe_ref, chem_ref, cheme_ref)
                f = pad_ref[x + 2, r:r + n, :] + TIME_STEP * flux
                s = slice(r - OFF, r - OFF + n)
                f2_ref[x, s, :] = f
                a = a2_ref[x + 1, r:r + n, :]
                m = a * a
                top = top + fold(m * f)
                bottom = bottom + fold(m)
                for near, far, out in ((0, 1, lo_out), (nx - 1, nx - 2, hi_out)):
                    if x == near:
                        out[s, :] = to_code(f, B_CODE)
                    if x == far:
                        out[r - OFF + ny:r - OFF + ny + n, :] = to_code(f, B_CODE)
        s = to_rows(top, bottom)
        sum_ref[...] = s
        lo_out[2 * ny:2 * ny + 16, :] = sum_digits(s)
        hi_out[2 * ny:2 * ny + 16, :] = sum_digits(s)
    return kernel


def step_b(ride_y, ride_z):
    def kernel(f_ref, a2_ref, ae2_ref, lo_ref, hi_ref, yr_ref, zr_ref, yp_ref, l_hbm,
               f3_hbm, dmg_hbm, flux_hbm, pool_ref, edge_ref,
               pad_ref, ze_ref, mob_ref, mobe_ref, chem_ref, cheme_ref,
               pool_scr, l_ref, f3_ref, dmg_ref, flux_ref, l_sem, sems):
        nx, ny, nz = f3_ref.shape
        labels_in = pltpu.make_async_copy(l_hbm, l_ref, l_sem)
        labels_in.start()
        g = Geometry(nx, ny, nz)
        mean = weighted_mean(yp_ref, yr_ref, zr_ref, ride_y, ride_z)
        fill(B_CODE, f_ref, lo_ref, hi_ref, yr_ref, zr_ref, pad_ref, ze_ref)
        for p in range(nx + 2):
            inside = 1 <= p <= nx
            for r, n in chunks(OFF - 8, OFF + ny + 8, 32) if inside else chunks(OFF, OFF + ny, 48):
                a = a2_ref[p, r:r + n, :]
                mob_ref[p, r:r + n, :] = a * a
        for r, n in chunks(0, ny, 48):
            a = ae2_ref[r:r + n, :]
            a = a * a
            for x in range(nx):
                mobe_ref[x, r:r + n, :] = pltpu.roll(a, nz - 32 * x, 1) if x else a
        chemistry(g, pad_ref, mob_ref, mobe_ref, ze_ref, chem_ref, cheme_ref, mean)
        labels_in.wait()
        copies = []
        for k, (r, n) in enumerate(chunks(OFF, OFF + ny, 48)):
            s = slice(r - OFF, r - OFF + n)
            pooled = [None] * 4
            for x in range(nx):
                m, flux = flux_of(g, x, r, n, mob_ref, mobe_ref, chem_ref, cheme_ref)
                f0 = pad_ref[x + 2, r:r + n, :]
                f = f0 + TIME_STEP * flux
                a = worn(a2_ref[x + 1, r:r + n, :], m, f0, mean)
                labels = l_ref[x, s, :]
                factor = by_label(labels, FACTORS)
                dmg = 1.0 - a * by_label(labels, tuple(1.0 / v for v in ROOTS))
                f3_ref[x, s, :] = f
                dmg_ref[x, s, :] = dmg
                flux_ref[x, s, :] = flux
                for i, v in enumerate((f, dmg, a * a, factor)):
                    pooled[i] = v if pooled[i] is None else pooled[i] + v
            for i in range(4):
                pool_scr[i, s, :] = pooled[i]
            for i, (src, dst) in enumerate(((f3_ref, f3_hbm), (dmg_ref, dmg_hbm), (flux_ref, flux_hbm))):
                copies.append(pltpu.make_async_copy(src.at[:, s, :], dst.at[:, s, :], sems.at[i, k]))
                copies[-1].start()
        py, pz = ny // 4, nz // 4
        zin = lax.broadcasted_iota(jnp.int32, (nz, 4 * pz), 0)
        out = lax.broadcasted_iota(jnp.int32, (nz, 4 * pz), 1)
        total = jnp.zeros((py, 4 * pz), F32)
        for i in range(4):
            rows = (pool_scr[i, pl.ds(0, py, stride=4), :] + pool_scr[i, pl.ds(1, py, stride=4), :]
                    + pool_scr[i, pl.ds(2, py, stride=4), :] + pool_scr[i, pl.ds(3, py, stride=4), :])
            pick = jnp.where((zin // 4 == out // 4) & (out % 4 == i), 1.0 / 64.0, 0.0).astype(F32)
            total = total + jnp.dot(rows, pick, precision=lax.Precision.HIGHEST, preferred_element_type=F32)
        pool_ref[...] = total.astype(BF16)
        blank = jnp.zeros((13, 4 * pz), F32)
        edge_ref[0] = jnp.concatenate([total[0:3], blank]).astype(BF16)
        edge_ref[1] = jnp.concatenate([total[py - 3:py], blank]).astype(BF16)
        for c in copies:
            c.wait()
    return kernel


def ring(axis, shift):
    count = lax.axis_size(axis)
    return [(i, (i + shift) % count) for i in range(count)]


def pair_sum(s, axis):
    count = lax.axis_size(axis)
    if count & (count - 1):
        return lax.psum(s, axis)
    bit = 1
    while bit < count:
        s = s + lax.ppermute(s, axis, [(i, i ^ bit) for i in range(count)])
        bit *= 2
    return s


def both_sides(pay, axis):
    if lax.axis_size(axis) == 2:
        return lax.ppermute(pay, axis, ring(axis, 1))
    return jnp.stack([lax.ppermute(pay[0], axis, ring(axis, -1)), lax.ppermute(pay[1], axis, ring(axis, 1))])


def z_neighbour(pay, axis, packed=True):
    if lax.axis_size(axis) == 2:
        return lax.ppermute(pay, axis, ring(axis, 1))
    above = lax.ppermute(pay, axis, ring(axis, -1))
    below = lax.ppermute(pay, axis, ring(axis, 1))
    lane = lax.broadcasted_iota(jnp.int32, pay.shape, pay.ndim - 1)
    if packed:
        low = (lane % 32 < 8) | (lane % 32 == 16)
    else:
        low = lane < pay.shape[-1] // 2
    return jnp.where(low, above, below)


def x_sides(lo, hi):
    return lax.ppermute(hi, "gx", ring("gx", 1)), lax.ppermute(lo, "gx", ring("gx", -1))


def body(concentration, damage, labels, w_first, b_first, w_second, b_second, w_third, b_third):
    nx, ny, nz = concentration.shape
    rows = ny + 2 * OFF
    block = (nx, ny, nz)
    padded = (nx + 2, rows, nz)
    ride_x = lax.axis_size("gx") == 4
    ride_y = lax.axis_size("gy") == 2
    ride_z = lax.axis_size("gz") == 2
    packed = (-(-(nx + 2) // 4), rows, nz)
    assert nz == 128
    scratch = [pltpu.VMEM((nx + 4, rows, nz), F32), pltpu.VMEM(padded, F32), pltpu.VMEM(padded, F32),
               pltpu.VMEM(block, F32), pltpu.VMEM(padded, F32), pltpu.VMEM(block, F32)]

    def start(sums):
        if ride_x:
            return sums, lax.ppermute(sums, "gx", ring("gx", 2))
        sums = pair_sum(sums, "gx")
        for axis, ride in (("gy", ride_y), ("gz", ride_z)):
            if not ride:
                sums = pair_sum(sums, axis)
        return sums, sums

    concentration, damage, labels = (
        pltpu.with_memory_space_constraint(v, pltpu.HBM) for v in (concentration, damage, labels))
    tall = 3 * ny + 16
    f, amp, lo, hi, sums = call(
        first_kernel,
        [(block, F32), (block, F32), ((tall, nz), I16), ((tall, nz), I16), ((8, nz), F32)],
        concentration, damage, labels,
        in_specs=[HBM] * 3,
        scratch=[pltpu.VMEM(block, F32), pltpu.VMEM(block, jnp.int32), pltpu.SemaphoreType.DMA((3, nx))])
    weights = weight_rows(w_first, w_second, w_third)
    sums, far = start(sums)
    lo, hi = x_sides(lo, hi)
    (ypay,) = call(edge_rows(A_CODE, ride_x, True), [((2, 24, nz), F32)], f, amp, lo, hi, sums, far, *weights)
    yr = both_sides(ypay, "gy")
    (zpay,) = call(pack_z(A_CODE, ride_y, True), [(packed, F32)], f, amp, lo, hi, yr, ypay)
    zr = z_neighbour(zpay, "gz")
    tall = 2 * ny + 16
    f, a2, ae2, lo, hi, sums = call(
        step_a(ride_y, ride_z),
        [(block, F32), (padded, F32), ((ny, nz), F32), ((tall, nz), I16), ((tall, nz), I16), ((8, nz), F32)],
        f, amp, lo, hi, yr, zr, ypay, scratch=scratch)

    sums, far = start(sums)
    lo, hi = x_sides(lo, hi)
    (ypay,) = call(edge_rows(B_CODE, ride_x, False), [((2, 24, nz), F32)], f, lo, hi, sums, far)
    yr = both_sides(ypay, "gy")
    (zpay,) = call(pack_z(B_CODE, ride_y, False), [(packed, F32)], f, lo, hi, yr, ypay)
    zr = z_neighbour(zpay, "gz")
    fraction, damage_field, flux_sum, pooled, edge = call(
        step_b(ride_y, ride_z),
        [(block, F32), (block, F32), (block, F32), ((ny // 4, nz), BF16), ((2, 16, nz), BF16)],
        f, a2, ae2, lo, hi, yr, zr, ypay, labels,
        in_specs=[VMEM] * 8 + [HBM], out_specs=[HBM] * 3 + [VMEM] * 2,
        scratch=scratch + [
            pltpu.VMEM((4, ny, nz), F32), pltpu.VMEM(block, jnp.int32),
            pltpu.VMEM(block, F32), pltpu.VMEM(block, F32), pltpu.VMEM(block, F32),
            pltpu.SemaphoreType.DMA, pltpu.SemaphoreType.DMA((3, len(chunks(OFF, OFF + ny, 48))))])
    ids = jnp.stack([lax.axis_index(a) for a in ("gx", "gy", "gz")])
    crack_score = detector(pooled, edge, ids, weights + (b_first[None], b_second[None]), b_third, ny // 4, nz // 4)
    return (fraction, damage_field, flux_sum, crack_score)


CH = 16
CIN = 4
TOP = 8


def iota(shape, dim):
    return lax.broadcasted_iota(jnp.int32, shape, dim)


def lanes_for(n):
    return -(-n // 128) * 128


def one_hot(mask):
    return jnp.where(mask, 1.0, 0.0).astype(BF16)


def mm(a, b):
    return jnp.dot(a, b, preferred_element_type=F32)


def tile_shift(rb, cb, pz):
    z_in = rb * 16 // CIN
    z_in = z_in if z_in < pz + pz // 2 else z_in - 2 * pz
    return z_in - cb * 8 + 3


SHIFTS = tuple(k for k in range(-3, 10) if k % (16 // CIN) == 3)


def weight_kernel(w1_ref, w2_ref, w3_ref, b1_ref, b2_ref, plane_ref, t1_ref, t2_ref, t3_ref, bias_ref):
    n1 = bias_ref.shape[1]
    k1 = t1_ref.shape[1] // 3
    pz = k1 // (2 * CIN)
    spread = one_hot(iota((CH, 128), 1) % CH == iota((CH, 128), 0))
    tile1 = mm(w1_ref[...], spread)
    tile2 = mm(w2_ref[...], spread)
    tile3 = mm(w3_ref[...], one_hot(iota((3, 128), 1) // pz == iota((3, 128), 0)))
    step1 = iota((16, 128), 0) // CIN - iota((16, 128), 1) // CH
    step2 = -(iota((16, 128), 1) // CH)
    step3 = -(iota((16, 128), 1) % pz)

    def tile(source, base, stride, step, shift):
        out = jnp.zeros((16, 128), F32)
        for l in range(3):
            k = base + stride * l
            out = jnp.where(step + shift == l, source[16 * k:16 * k + 16], out)
        return out.astype(BF16)

    zero = jnp.zeros((16, 128), BF16)
    bias_ref[...] = jnp.zeros(bias_ref.shape, F32)
    for i in range(3):
        for j in range(3):
            tap = 9 * i + 3 * j
            known = {k: tile(tile1, tap, 1, step1, k) for k in SHIFTS}
            for rb in range(k1 // 16):
                for cb in range(n1 // 128):
                    t1_ref[i, j * k1 + rb * 16:j * k1 + rb * 16 + 16, cb * 128:(cb + 1) * 128] = known.get(
                        tile_shift(rb, cb, pz), zero)
            for rb in range(16):
                t2_ref[i, j * 256 + rb * 16:j * 256 + rb * 16 + 16, :] = (
                    tile(tile2, tap, 1, step2, rb) if rb < 10 else zero)
        for rb in range(t3_ref.shape[1] // 16):
            t3_ref[i, rb * 16:rb * 16 + 16, :] = tile(tile3, 3 * i, 1, step3, rb) if rb < pz + 2 else zero
    wide = one_hot(iota((CH, n1), 1) % CH == iota((CH, n1), 0)).astype(F32)
    for k, ref in ((0, b1_ref), (1, b2_ref)):
        bias_ref[k:k + 1, :] = jnp.dot(ref[...], wide, precision=lax.Precision.HIGHEST, preferred_element_type=F32)


def weight_rows(w_first, w_second, w_third):
    return (jnp.tile(jnp.swapaxes(w_first, 1, 2), (1, 16 // CIN, 1)).reshape(27 * 16, CH),
            jnp.swapaxes(w_second, 1, 2).reshape(27 * CH, CH),
            w_third.reshape(3, 3, 3, CH).transpose(0, 2, 3, 1).reshape(9 * CH, 3))


def gelu(x):
    return 0.5 * x * (1.0 + jnp.tanh(0.7978845608028654 * (x + 0.044715 * (x * x * x))))


def plane_kernel(py, y_count):
    def kernel(ids_ref, pool_ref, yr_ref, out_ref, scr_ref):
        iy = ids_ref[1]
        scr_ref[...] = jnp.zeros(scr_ref.shape, F32)
        scr_ref[TOP:TOP + py, :] = pool_ref[0:py, :].astype(F32)
        below = yr_ref[1].astype(F32)[0:3]
        above = yr_ref[0].astype(F32)[0:3]
        scr_ref[TOP - 3:TOP, :] = jnp.where(iy > 0, below, 0.0)
        scr_ref[TOP + py:TOP + py + 3, :] = jnp.where(iy < y_count - 1, above, 0.0)
        out_ref[...] = scr_ref[...].astype(BF16)
    return kernel


def conv_kernel(py, counts, shifts):
    x_count, y_count, z_count = counts
    n = len(shifts)

    def kernel(*refs):
        ids_ref, b3_ref = refs[:2]
        own = refs[2:3 + n]
        other = refs[3 + n:4 + 2 * n]
        t1_ref, t2_ref, t3_ref, bias_ref, out_ref = refs[4 + 2 * n:9 + 2 * n]
        in_ref, lhs1_ref, act1_ref, lhs2_ref, act2_ref, tail_ref = refs[9 + 2 * n:]
        ix, iy, iz = ids_ref[0], ids_ref[1], ids_ref[2]
        half = own[0].shape[1]
        pz = half // CIN
        rows = py + 4
        z_row = iota((1, half), 1) // CIN
        z_ok = ((z_row < pz // 2) & (iz < z_count - 1)) | ((z_row >= pz // 2) & (iz > 0))
        for w in range(7):
            o = w - 3
            k = 0 if o == 0 else 1 + shifts.index((-o) % x_count) if (-o) % x_count in shifts else None
            if k is None:
                in_ref[w] = jnp.zeros(in_ref.shape[1:], F32)
                continue
            inside = (ix + o >= 0) & (ix + o < x_count)
            in_ref[w, :, 0:half] = jnp.where(inside, own[k][...].astype(F32), 0.0)
            in_ref[w, :, half:] = jnp.where(z_ok & inside, other[k][...].astype(F32), 0.0)
        k1 = 2 * half
        for w in range(7):
            for j in range(3):
                start = TOP - 3 + j
                lhs1_ref[w, :, j * k1:(j + 1) * k1] = in_ref[w, start:start + rows, :].astype(BF16)
        out = None
        for i in range(3):
            part = mm(lhs1_ref[i:i + 5].reshape(5 * rows, 3 * k1), t1_ref[i])
            out = part if out is None else out + part
        width = out.shape[1]
        y = iota((rows, width), 0) - 2
        z = iota((rows, width), 1) // CH - 2
        ok = (z < pz + 2) & ((y >= 0) | (iy > 0)) & ((y < py) | (iy < y_count - 1))
        ok = ok & ((z >= 0) | (iz > 0)) & ((z < pz) | (iz < z_count - 1))
        for p in range(5):
            a = gelu(out[p * rows:(p + 1) * rows] + bias_ref[0:1, :])
            good = ok & (ix + p - 2 >= 0) & (ix + p - 2 < x_count)
            act1_ref[p, 0:rows, 0:width] = jnp.where(good, a, 0.0)
            act1_ref[p, rows:, 0:width] = jnp.zeros((act1_ref.shape[1] - rows, width), F32)
            act1_ref[p, :, width:] = jnp.zeros((act1_ref.shape[1], act1_ref.shape[2] - width), F32)
        blocks = lhs2_ref.shape[1]
        for p in range(5):
            for j in range(3):
                a = act1_ref[p, j:j + rows, :].astype(BF16)
                for b in range(blocks):
                    lhs2_ref[p, b, :, j * 256:(j + 1) * 256] = a[:, b * 128:b * 128 + 256]
        out = None
        for i in range(3):
            part = mm(lhs2_ref[i:i + 3].reshape(3 * blocks * rows, 768), t2_ref[i])
            out = part if out is None else out + part
        for b in range(blocks):
            y = iota((rows, 128), 0) - 1
            z = (iota((rows, 128), 1) + b * 128) // CH - 1
            ok = (z < pz + 1) & (y <= py) & ((y >= 0) | (iy > 0)) & ((y < py) | (iy < y_count - 1))
            ok = ok & ((z >= 0) | (iz > 0)) & ((z < pz) | (iz < z_count - 1))
            for p in range(3):
                s = (p * blocks + b) * rows
                a = gelu(out[s:s + rows] + bias_ref[1:2, 0:128])
                good = ok & (ix + p - 1 >= 0) & (ix + p - 1 < x_count)
                act2_ref[p, :, b * 128:(b + 1) * 128] = jnp.where(good, a, 0.0).astype(BF16)
        out = None
        for i in range(3):
            part = mm(act2_ref[i], t3_ref[i])
            out = part if out is None else out + part
        tail_ref[0:rows, :] = out
        score = tail_ref[0:py, :]
        for j in (1, 2):
            score = score + pltpu.roll(tail_ref[j:j + py, :], 128 - j * pz, 1)
        out_ref[0] = jnp.transpose(score)[0:pz, :] + b3_ref[0]
    return kernel


def detector(pooled, edge, ids, weights, b_third, py, pz):
    counts = tuple(lax.axis_size(a) for a in ("gx", "gy", "gz"))
    half = pooled.shape[1]
    assert half == 128 and pz * CIN == half and pz * 3 <= 128
    rows = py + 4
    width = lanes_for((pz + 4) * CH)
    blocks = width // 128
    yr = both_sides(edge, "gy")
    tall = -(-(TOP + py + 3) // 16) * 16
    (plane,) = call(
        plane_kernel(py, counts[1]), [((tall, half), BF16)], ids, pooled, yr,
        in_specs=[SMEM, VMEM, VMEM], scratch=[pltpu.VMEM((tall, half), F32)])
    shifts = []
    for s in (1, -1, 2, -2, 3, -3):
        if s % counts[0] and s % counts[0] not in shifts:
            shifts.append(s % counts[0])
    own = [plane] + [lax.ppermute(plane, "gx", ring("gx", s)) for s in shifts]
    matrices = call(
        weight_kernel,
        [((3, 6 * half, width), BF16), ((3, 768, 128), BF16), ((3, width, 128), BF16), ((8, width), F32)],
        *weights, plane)
    own[1], *matrices = lax.optimization_barrier((own[1], *matrices))
    other = [z_neighbour(v, "gz", False) for v in own]
    args = (ids, b_third, *own, *other, *matrices)
    (score,) = call(
        conv_kernel(py, counts, shifts), [((1, pz, py), F32)], *args,
        in_specs=[SMEM] * 2 + [VMEM] * (len(args) - 2),
        scratch=[
            pltpu.VMEM((7, tall, 2 * half), F32),
            pltpu.VMEM((7, rows, 6 * half), BF16),
            pltpu.VMEM((5, rows + 8, width + 128), F32),
            pltpu.VMEM((5, blocks, rows, 768), BF16),
            pltpu.VMEM((3, rows, width), BF16),
            pltpu.VMEM((rows + 8, 128), F32),
        ], mib=32)
    return jnp.swapaxes(score, 1, 2)


def solution(mesh):
    slab = P(("groups", "gx"), "gy", "gz")
    return jax.shard_map(
        body,
        mesh=mesh,
        in_specs=(slab, slab, slab, P(), P(), P(), P(), P(), P()),
        out_specs=(slab, slab, slab, slab),
        check_vma=False,
    )
```

```python
import jax
import jax.numpy as jnp
import numpy as np
from jax import lax
from jax.experimental import pallas as pl
from jax.experimental.pallas import tpu as pltpu
from jax.sharding import PartitionSpec as P

F32 = jnp.float32
BF16 = jnp.bfloat16
I16 = jnp.int16
WELL_HEIGHT = 1.0
STRAIN_COUPLING = 4.0
TIME_STEP = 0.01
DAMAGE_RATE = 0.8
ENERGY_CRITICAL = 0.02

OFF = 16
A_CODE = (0.0, 1.0)
B_CODE = (-1.1, 3.1)
SUM_LOW, SUM_SPAN = -1280.0, 4096.0

VMEM = pl.BlockSpec(memory_space=pltpu.VMEM)
HBM = pl.BlockSpec(memory_space=pltpu.HBM)


def to_code(x, code):
    low, span = code
    v = (x - low) * (65535.0 / span) - 32768.0
    return jnp.clip(jnp.round(v), -32768.0, 32767.0).astype(jnp.int32).astype(I16)


def from_code(q, code):
    low, span = code
    return q.astype(jnp.int32).astype(F32) * (span / 65535.0) + (low + 32768.0 * span / 65535.0)


def sum_digits(s):
    v = (s[0:2] - SUM_LOW) * (65536.0 / SUM_SPAN)
    high = jnp.floor(v)
    low = jnp.minimum(jnp.floor((v - high) * 65536.0), 65535.0)
    rows = jnp.concatenate([high, low, jnp.full((12, s.shape[1]), 32768.0, F32)]) - 32768.0
    return rows.astype(jnp.int32).astype(I16)


def from_digits(tile):
    v = tile.astype(jnp.int32).astype(F32) + 32768.0
    return (v[0:2] + v[2:4] * (1.0 / 65536.0)) * (SUM_SPAN / 65536.0) + SUM_LOW


def by_label(labels, values):
    return jnp.where(labels == 0, values[0], jnp.where(labels == 1, values[1], values[2])).astype(F32)


FACTORS = (1.0, 0.3, 0.05)
ROOTS = tuple(float(np.sqrt(np.float32(v))) for v in FACTORS)


def call(kernel, outs, *args, in_specs=None, out_specs=None, scratch=(), mib=16):
    return pl.pallas_call(
        kernel,
        in_specs=in_specs or [VMEM] * len(args),
        out_specs=out_specs or [VMEM] * len(outs),
        out_shape=[jax.ShapeDtypeStruct(s, t) for s, t in outs],
        scratch_shapes=scratch,
        compiler_params=pltpu.CompilerParams(vmem_limit_bytes=mib * 1024 * 1024),
    )(*args)


def chunks(start, stop, size):
    return [(r, min(size, stop - r)) for r in range(start, stop, size)]


def fold(x):
    return x.reshape(x.shape[0] // 8, 8, x.shape[1]).sum(0)


def to_rows(top, bottom):
    return jnp.concatenate([jnp.sum(top, 0, keepdims=True), jnp.sum(bottom, 0, keepdims=True),
                            jnp.zeros((6, top.shape[1]), F32)])


def first_kernel(c_hbm, d_hbm, l_hbm, f_ref, amp_ref, lo_ref, hi_ref, sum_ref, d_ref, l_ref, sems):
    nx, ny, nz = f_ref.shape
    order = [0, nx - 1] + list(range(1, nx - 1))
    copies = []
    for x in order:
        copies.append([pltpu.make_async_copy(src.at[x], dst.at[x], sems.at[k, x])
                       for k, (src, dst) in enumerate(((c_hbm, f_ref), (d_hbm, d_ref), (l_hbm, l_ref)))])
        for c in copies[-1]:
            c.start()
    top = jnp.zeros((8, nz), F32)
    bottom = jnp.zeros((8, nz), F32)
    for k, x in enumerate(order):
        for c in copies[k]:
            c.wait()
        for r, n in chunks(0, ny, 48):
            f = f_ref[x, r:r + n, :]
            a = by_label(l_ref[x, r:r + n, :], ROOTS) * (1.0 - d_ref[x, r:r + n, :])
            amp_ref[x, r:r + n, :] = a
            m = a * a
            top = top + fold(m * f)
            bottom = bottom + fold(m)
            for near, far, out in ((0, 1, lo_ref), (nx - 1, nx - 2, hi_ref)):
                if x == near:
                    out[r:r + n, :] = to_code(f, A_CODE)
                    out[2 * ny + r:2 * ny + r + n, :] = to_code(a, A_CODE)
                if x == far:
                    out[ny + r:ny + r + n, :] = to_code(f, A_CODE)
    s = to_rows(top, bottom)
    sum_ref[...] = s
    lo_ref[3 * ny:3 * ny + 16, :] = sum_digits(s)
    hi_ref[3 * ny:3 * ny + 16, :] = sum_digits(s)


def edge_rows(code, ride_x, with_amp):
    def kernel(*refs):
        f_ref = refs[0]
        amp_ref = refs[1] if with_amp else None
        lo_ref, hi_ref, s_ref, far_ref = refs[1 + with_amp:5 + with_amp]
        out_ref = refs[-1]
        nx, ny, nz = f_ref.shape
        low_rows = [from_code(r[0:16, :], code)[0:1] for r in (lo_ref, hi_ref)]
        high_rows = [from_code(r[ny - 16:ny, :], code)[15:16] for r in (lo_ref, hi_ref)]
        s = s_ref[...]
        if ride_x:
            s = s + far_ref[...]
        for side, first, second, beside in ((0, 0, 1, low_rows), (1, ny - 1, ny - 2, high_rows)):
            for x in range(nx):
                out_ref[side, 2 * x:2 * x + 1, :] = f_ref[x, first:first + 1, :]
                out_ref[side, 2 * x + 1:2 * x + 2, :] = f_ref[x, second:second + 1, :]
                if amp_ref is not None:
                    out_ref[side, 10 + x:11 + x, :] = amp_ref[x, first:first + 1, :]
            out_ref[side, 8:9, :] = beside[0]
            out_ref[side, 9:10, :] = beside[1]
            out_ref[side, 16:24, :] = s
            if ride_x:
                out_ref[side, 16:18, :] = (s[0:2] + from_digits(lo_ref[lo_ref.shape[0] - 16:, :])
                                           + from_digits(hi_ref[hi_ref.shape[0] - 16:, :]))
    return kernel


def group(lane, j, nz, first, count):
    return (lane - (32 * j + first)) % nz < count


def pack_z(code, ride_y, with_amp):
    def kernel(*refs):
        f_ref = refs[0]
        amp_ref = refs[1] if with_amp else None
        lo_ref, hi_ref, yr_ref, yp_ref, out_ref = refs[1 + with_amp:]
        nx, ny, nz = f_ref.shape
        end = OFF + ny
        lane = lax.broadcasted_iota(jnp.int32, (1, nz), 1)
        for k in range(out_ref.shape[0]):
            planes = [p for p in range(4 * k, 4 * k + 4) if p < nx + 2]

            def packed(f_of, a_of, ps):
                out = None
                for p in ps:
                    j = p % 4
                    f = f_of(p)
                    f = pltpu.roll(f, 32 * j, 1) if j else f
                    out = f if out is None else jnp.where(group(lane, j, nz, -2, 4), f, out)
                    a = a_of(p)
                    if a is not None:
                        out = jnp.where(group(lane, j, nz, 15, 2), pltpu.roll(a, 32 * j + 16, 1), out)
                return out

            for r, n in chunks(0, ny, 48):
                def f_of(p):
                    if p == 0:
                        return from_code(lo_ref[r:r + n, :], code)
                    if p == nx + 1:
                        return from_code(hi_ref[r:r + n, :], code)
                    return f_ref[p - 1, r:r + n, :]

                def a_of(p):
                    return amp_ref[p - 1, r:r + n, :] if with_amp and 1 <= p <= nx else None

                out_ref[k, OFF + r:OFF + r + n, :] = packed(f_of, a_of, planes)
            inner = [p for p in planes if 1 <= p <= nx]
            if inner:
                for side, near in ((1, OFF - 1), (0, end)):
                    out_ref[k, near:near + 1, :] = packed(
                        lambda p: yr_ref[side, 2 * (p - 1):2 * (p - 1) + 1, :], lambda p: None, inner)
        s = yp_ref[0, 16:24, :]
        out_ref[0, 0:8, :] = s + yr_ref[0, 16:24, :] if ride_y else s
    return kernel


def spread(spans, extra, size):
    return [v for a, b in spans for v in chunks(OFF + a - extra, OFF + b + extra, size)]


def fill(code, f_ref, lo_ref, hi_ref, yr_ref, zr_ref, pad_ref, ze_ref, spans):
    nx, ny, nz = f_ref.shape
    end = OFF + ny
    wide = [v for a, b in spans for v in chunks(max(a - 16, 0), min(b + 16, ny), 48)]
    for near, far, ref in ((1, 0, lo_ref), (nx + 2, nx + 3, hi_ref)):
        for r, n in wide:
            pad_ref[near, OFF + r:OFF + r + n, :] = from_code(ref[r:r + n, :], code)
            pad_ref[far, OFF + r:OFF + r + n, :] = from_code(ref[ny + r:ny + r + n, :], code)
    for p, k in ((1, 8), (nx + 2, 9)):
        pad_ref[p, OFF - 1:OFF, :] = yr_ref[1, k:k + 1, :]
        pad_ref[p, end:end + 1, :] = yr_ref[0, k:k + 1, :]
    for x in range(nx):
        for r, n in wide:
            pad_ref[x + 2, OFF + r:OFF + r + n, :] = f_ref[x, r:r + n, :]
        for side, near, far in ((1, OFF - 1, OFF - 2), (0, end, end + 1)):
            pad_ref[x + 2, near:near + 1, :] = yr_ref[side, 2 * x:2 * x + 1, :]
            pad_ref[x + 2, far:far + 1, :] = yr_ref[side, 2 * x + 1:2 * x + 2, :]
    for p in range(nx + 2):
        for r, n in spread(spans, 8, 32):
            e = zr_ref[p // 4, r:r + n, :]
            ze_ref[p, r:r + n, :] = pltpu.roll(e, nz - 32 * (p % 4), 1) if p % 4 else e


def weighted_mean(yp_ref, yr_ref, zr_ref, ride_y, ride_z):
    s = yp_ref[0, 16:24, :]
    if ride_y:
        s = s + yr_ref[0, 16:24, :]
    if ride_z:
        s = s + zr_ref[0, 0:8, :]
    return jnp.sum(s[0:1], keepdims=True) / jnp.sum(s[1:2], keepdims=True)


def worn(a, m, f, mean):
    e = f - mean
    energy = 0.5 * STRAIN_COUPLING * m * e * e
    return a * (1.0 - DAMAGE_RATE * jnp.maximum(energy - ENERGY_CRITICAL, 0.0))


class Geometry:
    def __init__(self, nx, ny, nz):
        self.nx, self.ny, self.nz = nx, ny, nz
        self.lane = lax.broadcasted_iota(jnp.int32, (1, nz), 1)
        self.first = self.lane == 0
        self.last = self.lane == nz - 1

    def before(self, own, other):
        return pltpu.roll(jnp.where(self.last, other, own), 1, 1)

    def after(self, own, other):
        return pltpu.roll(jnp.where(self.first, other, own), self.nz - 1, 1)


def chem_of(f, m, around, mean):
    well = 2.0 * WELL_HEIGHT * f * (1.0 - f) * (1.0 - 2.0 * f)
    return well + 6.0 * f - around + STRAIN_COUPLING * m * (f - mean)


def chemistry(g, pad_ref, mob_ref, mobe_ref, ze_ref, chem_ref, cheme_ref, mean, spans):
    nx = g.nx
    for p in range(nx + 2):
        inside = 1 <= p <= nx
        rows = spread(spans, 8, 32) if inside else spread(spans, 0, 48)
        for r, n in rows:
            f = pad_ref[p + 1, r:r + n, :]
            e = ze_ref[p, r:r + n, :]
            around = (pad_ref[p, r:r + n, :] + pad_ref[p + 2, r:r + n, :]
                      + pad_ref[p + 1, r - 1:r - 1 + n, :] + pad_ref[p + 1, r + 1:r + 1 + n, :]
                      + g.before(f, e) + g.after(f, e))
            chem_ref[p, r:r + n, :] = chem_of(f, mob_ref[p, r:r + n, :], around, mean)
        if inside:
            for r, n in spread(spans, 0, 48):
                f = pad_ref[p + 1, r:r + n, :]
                e = ze_ref[p, r:r + n, :]
                around = (ze_ref[p - 1, r:r + n, :] + ze_ref[p + 1, r:r + n, :]
                          + ze_ref[p, r - 1:r - 1 + n, :] + ze_ref[p, r + 1:r + 1 + n, :]
                          + g.before(e, f) + g.after(e, f))
                cheme_ref[p - 1, r - OFF:r - OFF + n, :] = chem_of(
                    e, mobe_ref[p - 1, r - OFF:r - OFF + n, :], around, mean)


def flux_of(g, x, r, n, mob_ref, mobe_ref, chem_ref, cheme_ref):
    p = x + 1
    m = mob_ref[p, r:r + n, :]
    q = chem_ref[p, r:r + n, :]
    me = mobe_ref[x, r - OFF:r - OFF + n, :]
    qe = cheme_ref[x, r - OFF:r - OFF + n, :]
    total = None
    for nm, nq in (
        (mob_ref[p - 1, r:r + n, :], chem_ref[p - 1, r:r + n, :]),
        (mob_ref[p + 1, r:r + n, :], chem_ref[p + 1, r:r + n, :]),
        (mob_ref[p, r - 1:r - 1 + n, :], chem_ref[p, r - 1:r - 1 + n, :]),
        (mob_ref[p, r + 1:r + 1 + n, :], chem_ref[p, r + 1:r + 1 + n, :]),
        (g.before(m, me), g.before(q, qe)),
        (g.after(m, me), g.after(q, qe)),
    ):
        term = (nm + m) * (nq - q)
        total = term if total is None else total + term
    return m, 0.5 * total


def pack_edges(values, lane, nz):
    out = values[0]
    for x, v in enumerate(values[1:], 1):
        out = jnp.where(group(lane, x, nz, -1, 2), pltpu.roll(v, 32 * x, 1), out)
    return out


def step_a(ride_y, ride_z):
    def kernel(f_ref, amp_ref, lo_ref, hi_ref, yr_ref, zr_ref, yp_ref,
               f2_ref, a2_ref, ae2_ref, lo_out, hi_out, sum_ref,
               pad_ref, ze_ref, mob_ref, mobe_ref, chem_ref, cheme_ref):
        nx, ny, nz = f2_ref.shape
        end = OFF + ny
        g = Geometry(nx, ny, nz)
        mean = weighted_mean(yp_ref, yr_ref, zr_ref, ride_y, ride_z)
        fill(A_CODE, f_ref, lo_ref, hi_ref, yr_ref, zr_ref, pad_ref, ze_ref, [(0, ny)])

        def wear(p, r, n, a):
            m = a * a
            mob_ref[p, r:r + n, :] = m
            a2_ref[p, r:r + n, :] = worn(a, m, pad_ref[p + 1, r:r + n, :], mean)

        for r, n in chunks(0, ny, 48):
            wear(0, OFF + r, n, from_code(lo_ref[2 * ny + r:2 * ny + r + n, :], A_CODE))
            wear(nx + 1, OFF + r, n, from_code(hi_ref[2 * ny + r:2 * ny + r + n, :], A_CODE))
            edges = []
            for x in range(nx):
                wear(x + 1, OFF + r, n, amp_ref[x, r:r + n, :])
                p = x + 1
                a = pltpu.roll(zr_ref[p // 4, OFF + r:OFF + r + n, :], nz - 32 * (p % 4) - 16, 1)
                m = a * a
                mobe_ref[x, r:r + n, :] = m
                edges.append(worn(a, m, ze_ref[p, OFF + r:OFF + r + n, :], mean))
            ae2_ref[r:r + n, :] = pack_edges(edges, g.lane, nz)
        for x in range(nx):
            wear(x + 1, OFF - 1, 1, yr_ref[1, 10 + x:11 + x, :])
            wear(x + 1, end, 1, yr_ref[0, 10 + x:11 + x, :])
        chemistry(g, pad_ref, mob_ref, mobe_ref, ze_ref, chem_ref, cheme_ref, mean, [(0, ny)])
        top = jnp.zeros((8, nz), F32)
        bottom = jnp.zeros((8, nz), F32)
        for x in range(nx):
            for r, n in chunks(OFF, end, 48):
                _, flux = flux_of(g, x, r, n, mob_ref, mobe_ref, chem_ref, cheme_ref)
                f = pad_ref[x + 2, r:r + n, :] + TIME_STEP * flux
                s = slice(r - OFF, r - OFF + n)
                f2_ref[x, s, :] = f
                a = a2_ref[x + 1, r:r + n, :]
                m = a * a
                top = top + fold(m * f)
                bottom = bottom + fold(m)
                for near, far, out in ((0, 1, lo_out), (nx - 1, nx - 2, hi_out)):
                    if x == near:
                        out[s, :] = to_code(f, B_CODE)
                    if x == far:
                        out[r - OFF + ny:r - OFF + ny + n, :] = to_code(f, B_CODE)
        s = to_rows(top, bottom)
        sum_ref[...] = s
        lo_out[2 * ny:2 * ny + 16, :] = sum_digits(s)
        hi_out[2 * ny:2 * ny + 16, :] = sum_digits(s)
    return kernel


def potentials_b(g, mean, a2_ref, ae2_ref, others, scratch, spans):
    f_ref, lo_ref, hi_ref, yr_ref, zr_ref = others
    pad_ref, ze_ref, mob_ref, mobe_ref, chem_ref, cheme_ref = scratch
    nx, nz = g.nx, g.nz
    fill(B_CODE, f_ref, lo_ref, hi_ref, yr_ref, zr_ref, pad_ref, ze_ref, spans)
    for p in range(nx + 2):
        for r, n in spread(spans, 8, 32) if 1 <= p <= nx else spread(spans, 0, 48):
            a = a2_ref[p, r:r + n, :]
            mob_ref[p, r:r + n, :] = a * a
    for r, n in spread(spans, 0, 48):
        a = ae2_ref[r - OFF:r - OFF + n, :]
        a = a * a
        for x in range(nx):
            mobe_ref[x, r - OFF:r - OFF + n, :] = pltpu.roll(a, nz - 32 * x, 1) if x else a
    chemistry(g, pad_ref, mob_ref, mobe_ref, ze_ref, chem_ref, cheme_ref, mean, spans)


def finish_b(g, mean, x, r, n, labels, a2_ref, scratch):
    pad_ref, ze_ref, mob_ref, mobe_ref, chem_ref, cheme_ref = scratch
    m, flux = flux_of(g, x, r, n, mob_ref, mobe_ref, chem_ref, cheme_ref)
    f0 = pad_ref[x + 2, r:r + n, :]
    f = f0 + TIME_STEP * flux
    a = worn(a2_ref[x + 1, r:r + n, :], m, f0, mean)
    dmg = 1.0 - a * by_label(labels, tuple(1.0 / v for v in ROOTS))
    return flux, (f, dmg, a * a, by_label(labels, FACTORS))


def pool_rows(scr_ref, count, nz):
    zin = lax.broadcasted_iota(jnp.int32, (nz, nz), 0)
    out = lax.broadcasted_iota(jnp.int32, (nz, nz), 1)
    total = jnp.zeros((count, nz), F32)
    for i in range(4):
        rows = (scr_ref[i, pl.ds(0, count, stride=4), :] + scr_ref[i, pl.ds(1, count, stride=4), :]
                + scr_ref[i, pl.ds(2, count, stride=4), :] + scr_ref[i, pl.ds(3, count, stride=4), :])
        pick = jnp.where((zin // 4 == out // 4) & (out % 4 == i), 1.0 / 64.0, 0.0).astype(F32)
        total = total + jnp.dot(rows, pick, precision=lax.Precision.HIGHEST, preferred_element_type=F32)
    return total


def edge_b(ride_y, ride_z):
    def kernel(f_ref, a2_ref, ae2_ref, lo_ref, hi_ref, yr_ref, zr_ref, yp_ref, l_hbm, edge_ref, *rest):
        *scratch, pool_scr, l_ref, l_sem = rest
        nx, ny, nz = f_ref.shape
        spans = [(0, 16), (ny - 16, ny)]
        loads = [pltpu.make_async_copy(l_hbm.at[:, a:b, :], l_ref.at[:, 16 * k:16 * k + 16, :], l_sem.at[k])
                 for k, (a, b) in enumerate(spans)]
        for c in loads:
            c.start()
        g = Geometry(nx, ny, nz)
        mean = weighted_mean(yp_ref, yr_ref, zr_ref, ride_y, ride_z)
        potentials_b(g, mean, a2_ref, ae2_ref, (f_ref, lo_ref, hi_ref, yr_ref, zr_ref), scratch, spans)
        for c in loads:
            c.wait()
        for k, (a, b) in enumerate(spans):
            s = slice(16 * k, 16 * k + 16)
            pooled = [None] * 4
            for x in range(nx):
                _, values = finish_b(g, mean, x, OFF + a, 16, l_ref[x, s, :], a2_ref, scratch)
                pooled = [v if p is None else p + v for p, v in zip(pooled, values)]
            for i in range(4):
                pool_scr[i, s, :] = pooled[i]
        total = pool_rows(pool_scr, 8, nz)
        blank = jnp.zeros((13, nz), F32)
        edge_ref[0] = jnp.concatenate([total[0:3], blank]).astype(BF16)
        edge_ref[1] = jnp.concatenate([total[5:8], blank]).astype(BF16)
    return kernel


def step_b(ride_y, ride_z):
    def kernel(f_ref, a2_ref, ae2_ref, lo_ref, hi_ref, yr_ref, zr_ref, yp_ref, l_hbm,
               f3_hbm, dmg_hbm, flux_hbm, pool_ref, *rest):
        *scratch, pool_scr, l_ref, f3_ref, dmg_ref, flux_ref, l_sem, sems = rest
        nx, ny, nz = f_ref.shape
        labels_in = pltpu.make_async_copy(l_hbm, l_ref, l_sem)
        labels_in.start()
        g = Geometry(nx, ny, nz)
        mean = weighted_mean(yp_ref, yr_ref, zr_ref, ride_y, ride_z)
        potentials_b(g, mean, a2_ref, ae2_ref, (f_ref, lo_ref, hi_ref, yr_ref, zr_ref), scratch, [(0, ny)])
        labels_in.wait()
        copies = []
        for k, (r, n) in enumerate(chunks(OFF, OFF + ny, 48)):
            s = slice(r - OFF, r - OFF + n)
            pooled = [None] * 4
            for x in range(nx):
                flux, values = finish_b(g, mean, x, r, n, l_ref[x, s, :], a2_ref, scratch)
                f3_ref[x, s, :] = values[0]
                dmg_ref[x, s, :] = values[1]
                flux_ref[x, s, :] = flux
                pooled = [v if p is None else p + v for p, v in zip(pooled, values)]
            for i in range(4):
                pool_scr[i, s, :] = pooled[i]
            for i, (src, dst) in enumerate(((f3_ref, f3_hbm), (dmg_ref, dmg_hbm), (flux_ref, flux_hbm))):
                copies.append(pltpu.make_async_copy(src.at[:, s, :], dst.at[:, s, :], sems.at[i, k]))
                copies[-1].start()
        pool_ref[...] = pool_rows(pool_scr, ny // 4, nz).astype(BF16)
        for c in copies:
            c.wait()
    return kernel


def ring(axis, shift):
    count = lax.axis_size(axis)
    return [(i, (i + shift) % count) for i in range(count)]


def pair_sum(s, axis):
    count = lax.axis_size(axis)
    if count & (count - 1):
        return lax.psum(s, axis)
    bit = 1
    while bit < count:
        s = s + lax.ppermute(s, axis, [(i, i ^ bit) for i in range(count)])
        bit *= 2
    return s


def both_sides(pay, axis):
    if lax.axis_size(axis) == 2:
        return lax.ppermute(pay, axis, ring(axis, 1))
    return jnp.stack([lax.ppermute(pay[0], axis, ring(axis, -1)), lax.ppermute(pay[1], axis, ring(axis, 1))])


def z_neighbour(pay, axis, packed=True):
    if lax.axis_size(axis) == 2:
        return lax.ppermute(pay, axis, ring(axis, 1))
    above = lax.ppermute(pay, axis, ring(axis, -1))
    below = lax.ppermute(pay, axis, ring(axis, 1))
    lane = lax.broadcasted_iota(jnp.int32, pay.shape, pay.ndim - 1)
    if packed:
        low = (lane % 32 < 8) | (lane % 32 == 16)
    else:
        low = lane < pay.shape[-1] // 2
    return jnp.where(low, above, below)


def x_sides(lo, hi):
    return lax.ppermute(hi, "gx", ring("gx", 1)), lax.ppermute(lo, "gx", ring("gx", -1))


def body(concentration, damage, labels, w_first, b_first, w_second, b_second, w_third, b_third):
    nx, ny, nz = concentration.shape
    rows = ny + 2 * OFF
    block = (nx, ny, nz)
    padded = (nx + 2, rows, nz)
    ride_x = lax.axis_size("gx") == 4
    ride_y = lax.axis_size("gy") == 2
    ride_z = lax.axis_size("gz") == 2
    packed = (-(-(nx + 2) // 4), rows, nz)
    assert nz == 128
    scratch = [pltpu.VMEM((nx + 4, rows, nz), F32), pltpu.VMEM(padded, F32), pltpu.VMEM(padded, F32),
               pltpu.VMEM(block, F32), pltpu.VMEM(padded, F32), pltpu.VMEM(block, F32)]

    def start(sums):
        if ride_x:
            return sums, lax.ppermute(sums, "gx", ring("gx", 2))
        sums = pair_sum(sums, "gx")
        for axis, ride in (("gy", ride_y), ("gz", ride_z)):
            if not ride:
                sums = pair_sum(sums, axis)
        return sums, sums

    concentration, damage, labels = (
        pltpu.with_memory_space_constraint(v, pltpu.HBM) for v in (concentration, damage, labels))
    tall = 3 * ny + 16
    f, amp, lo, hi, sums = call(
        first_kernel,
        [(block, F32), (block, F32), ((tall, nz), I16), ((tall, nz), I16), ((8, nz), F32)],
        concentration, damage, labels,
        in_specs=[HBM] * 3,
        scratch=[pltpu.VMEM(block, F32), pltpu.VMEM(block, jnp.int32), pltpu.SemaphoreType.DMA((3, nx))])
    weights = weight_rows(w_first, w_second, w_third)
    sums, far = start(sums)
    lo, hi = x_sides(lo, hi)
    (ypay,) = call(edge_rows(A_CODE, ride_x, True), [((2, 24, nz), F32)], f, amp, lo, hi, sums, far, *weights)
    yr = both_sides(ypay, "gy")
    (zpay,) = call(pack_z(A_CODE, ride_y, True), [(packed, F32)], f, amp, lo, hi, yr, ypay)
    zr = z_neighbour(zpay, "gz")
    tall = 2 * ny + 16
    f, a2, ae2, lo, hi, sums = call(
        step_a(ride_y, ride_z),
        [(block, F32), (padded, F32), ((ny, nz), F32), ((tall, nz), I16), ((tall, nz), I16), ((8, nz), F32)],
        f, amp, lo, hi, yr, zr, ypay, scratch=scratch)

    sums, far = start(sums)
    lo, hi = x_sides(lo, hi)
    (ypay,) = call(edge_rows(B_CODE, ride_x, False), [((2, 24, nz), F32)], f, lo, hi, sums, far)
    yr = both_sides(ypay, "gy")
    (zpay,) = call(pack_z(B_CODE, ride_y, False), [(packed, F32)], f, lo, hi, yr, ypay)
    zr = z_neighbour(zpay, "gz")
    last = (f, a2, ae2, lo, hi, yr, zr, ypay, labels)
    (edge,) = call(
        edge_b(ride_y, ride_z), [((2, 16, nz), BF16)], *last, in_specs=[VMEM] * 8 + [HBM],
        scratch=scratch + [
            pltpu.VMEM((4, 32, nz), F32), pltpu.VMEM((nx, 32, nz), jnp.int32), pltpu.SemaphoreType.DMA((2,))])
    fraction, damage_field, flux_sum, pooled = call(
        step_b(ride_y, ride_z),
        [(block, F32), (block, F32), (block, F32), ((ny // 4, nz), BF16)], *last,
        in_specs=[VMEM] * 8 + [HBM], out_specs=[HBM] * 3 + [VMEM],
        scratch=scratch + [
            pltpu.VMEM((4, ny, nz), F32), pltpu.VMEM(block, jnp.int32),
            pltpu.VMEM(block, F32), pltpu.VMEM(block, F32), pltpu.VMEM(block, F32),
            pltpu.SemaphoreType.DMA, pltpu.SemaphoreType.DMA((3, len(chunks(OFF, OFF + ny, 48))))])
    ids = jnp.broadcast_to(jnp.stack([lax.axis_index(a) for a in ("gx", "gy", "gz")])[:, None], (3, nz))
    crack_score = detector(pooled, edge, ids, weights + (b_first[None], b_second[None], b_third[None]), ny // 4, nz // 4)
    return (fraction, damage_field, flux_sum, crack_score)


CH = 16
CIN = 4
TOP = 8


def iota(shape, dim):
    return lax.broadcasted_iota(jnp.int32, shape, dim)


def lanes_for(n):
    return -(-n // 128) * 128


def one_hot(mask):
    return jnp.where(mask, 1.0, 0.0).astype(BF16)


def mm(a, b):
    return jnp.dot(a, b, preferred_element_type=F32)


def tile_shift(rb, cb, pz):
    z_in = rb * 16 // CIN
    z_in = z_in if z_in < pz + pz // 2 else z_in - 2 * pz
    return z_in - cb * 8 + 3


SHIFTS = tuple(k for k in range(-3, 10) if k % (16 // CIN) == 3)


def weight_kernel(w1_ref, w2_ref, w3_ref, b1_ref, b2_ref, b3_ref, plane_ref, t1_ref, t2_ref, t3_ref, bias_ref):
    n1 = bias_ref.shape[1]
    k1 = t1_ref.shape[1] // 3
    pz = k1 // (2 * CIN)
    spread = one_hot(iota((CH, 128), 1) % CH == iota((CH, 128), 0))
    tile1 = mm(w1_ref[...], spread)
    tile2 = mm(w2_ref[...], spread)
    tile3 = mm(w3_ref[...], one_hot(iota((3, 128), 1) // pz == iota((3, 128), 0)))
    step1 = iota((16, 128), 0) // CIN - iota((16, 128), 1) // CH
    step2 = -(iota((16, 128), 1) // CH)
    step3 = -(iota((16, 128), 1) % pz)

    def tile(source, base, stride, step, shift):
        out = jnp.zeros((16, 128), F32)
        for l in range(3):
            k = base + stride * l
            out = jnp.where(step + shift == l, source[16 * k:16 * k + 16], out)
        return out.astype(BF16)

    zero = jnp.zeros((16, 128), BF16)
    bias_ref[...] = jnp.broadcast_to(b3_ref[...], bias_ref.shape)
    for i in range(3):
        for j in range(3):
            tap = 9 * i + 3 * j
            known = {k: tile(tile1, tap, 1, step1, k) for k in SHIFTS}
            for rb in range(k1 // 16):
                for cb in range(n1 // 128):
                    t1_ref[i, j * k1 + rb * 16:j * k1 + rb * 16 + 16, cb * 128:(cb + 1) * 128] = known.get(
                        tile_shift(rb, cb, pz), zero)
            for rb in range(16):
                t2_ref[i, j * 256 + rb * 16:j * 256 + rb * 16 + 16, :] = (
                    tile(tile2, tap, 1, step2, rb) if rb < 10 else zero)
        for rb in range(t3_ref.shape[1] // 16):
            t3_ref[i, rb * 16:rb * 16 + 16, :] = tile(tile3, 3 * i, 1, step3, rb) if rb < pz + 2 else zero
    wide = one_hot(iota((CH, n1), 1) % CH == iota((CH, n1), 0)).astype(F32)
    for k, ref in ((0, b1_ref), (1, b2_ref)):
        bias_ref[k:k + 1, :] = jnp.dot(ref[...], wide, precision=lax.Precision.HIGHEST, preferred_element_type=F32)


def weight_rows(w_first, w_second, w_third):
    return (jnp.tile(jnp.swapaxes(w_first, 1, 2), (1, 16 // CIN, 1)).reshape(27 * 16, CH),
            jnp.swapaxes(w_second, 1, 2).reshape(27 * CH, CH),
            w_third.reshape(3, 3, 3, CH).transpose(0, 2, 3, 1).reshape(9 * CH, 3))


def gelu(x):
    return 0.5 * x * (1.0 + jnp.tanh(0.7978845608028654 * (x + 0.044715 * (x * x * x))))


def plane_kernel(py, y_count):
    def kernel(ids_ref, pool_ref, yr_ref, out_ref, scr_ref):
        iy = ids_ref[1:2, 0:1]
        scr_ref[...] = jnp.zeros(scr_ref.shape, F32)
        scr_ref[TOP:TOP + py, :] = pool_ref[0:py, :].astype(F32)
        below = yr_ref[1].astype(F32)[0:3]
        above = yr_ref[0].astype(F32)[0:3]
        scr_ref[TOP - 3:TOP, :] = jnp.where(iy > 0, below, 0.0)
        scr_ref[TOP + py:TOP + py + 3, :] = jnp.where(iy < y_count - 1, above, 0.0)
        out_ref[...] = scr_ref[...].astype(BF16)
    return kernel


def conv_kernel(py, counts, shifts):
    x_count, y_count, z_count = counts
    n = len(shifts)

    def kernel(*refs):
        ids_ref = refs[0]
        own = refs[1:2 + n]
        other = refs[2 + n:3 + 2 * n]
        t1_ref, t2_ref, t3_ref, bias_ref, out_ref = refs[3 + 2 * n:8 + 2 * n]
        in_ref, lhs1_ref, act1_ref, lhs2_ref, act2_ref, tail_ref = refs[8 + 2 * n:]
        ix, iy, iz = ids_ref[0:1, 0:1], ids_ref[1:2, 0:1], ids_ref[2:3, 0:1]
        half = own[0].shape[1]
        pz = half // CIN
        rows = py + 4
        z_row = iota((1, half), 1) // CIN
        z_ok = ((z_row < pz // 2) & (iz < z_count - 1)) | ((z_row >= pz // 2) & (iz > 0))
        for w in range(7):
            o = w - 3
            k = 0 if o == 0 else 1 + shifts.index((-o) % x_count) if (-o) % x_count in shifts else None
            if k is None:
                in_ref[w] = jnp.zeros(in_ref.shape[1:], F32)
                continue
            inside = (ix + o >= 0) & (ix + o < x_count)
            in_ref[w, :, 0:half] = jnp.where(inside, own[k][...].astype(F32), 0.0)
            in_ref[w, :, half:] = jnp.where(z_ok & inside, other[k][...].astype(F32), 0.0)
        k1 = 2 * half
        for w in range(7):
            for j in range(3):
                start = TOP - 3 + j
                lhs1_ref[w, :, j * k1:(j + 1) * k1] = in_ref[w, start:start + rows, :].astype(BF16)
        out = None
        for i in range(3):
            part = mm(lhs1_ref[i:i + 5].reshape(5 * rows, 3 * k1), t1_ref[i])
            out = part if out is None else out + part
        width = out.shape[1]
        y = iota((rows, width), 0) - 2
        z = iota((rows, width), 1) // CH - 2
        ok = (z < pz + 2) & ((y >= 0) | (iy > 0)) & ((y < py) | (iy < y_count - 1))
        ok = ok & ((z >= 0) | (iz > 0)) & ((z < pz) | (iz < z_count - 1))
        for p in range(5):
            a = gelu(out[p * rows:(p + 1) * rows] + bias_ref[0:1, :])
            good = ok & (ix + p - 2 >= 0) & (ix + p - 2 < x_count)
            act1_ref[p, 0:rows, 0:width] = jnp.where(good, a, 0.0)
            act1_ref[p, rows:, 0:width] = jnp.zeros((act1_ref.shape[1] - rows, width), F32)
            act1_ref[p, :, width:] = jnp.zeros((act1_ref.shape[1], act1_ref.shape[2] - width), F32)
        blocks = lhs2_ref.shape[1]
        for p in range(5):
            for j in range(3):
                a = act1_ref[p, j:j + rows, :].astype(BF16)
                for b in range(blocks):
                    lhs2_ref[p, b, :, j * 256:(j + 1) * 256] = a[:, b * 128:b * 128 + 256]
        out = None
        for i in range(3):
            part = mm(lhs2_ref[i:i + 3].reshape(3 * blocks * rows, 768), t2_ref[i])
            out = part if out is None else out + part
        for b in range(blocks):
            y = iota((rows, 128), 0) - 1
            z = (iota((rows, 128), 1) + b * 128) // CH - 1
            ok = (z < pz + 1) & (y <= py) & ((y >= 0) | (iy > 0)) & ((y < py) | (iy < y_count - 1))
            ok = ok & ((z >= 0) | (iz > 0)) & ((z < pz) | (iz < z_count - 1))
            for p in range(3):
                s = (p * blocks + b) * rows
                a = gelu(out[s:s + rows] + bias_ref[1:2, 0:128])
                good = ok & (ix + p - 1 >= 0) & (ix + p - 1 < x_count)
                act2_ref[p, :, b * 128:(b + 1) * 128] = jnp.where(good, a, 0.0).astype(BF16)
        out = None
        for i in range(3):
            part = mm(act2_ref[i], t3_ref[i])
            out = part if out is None else out + part
        tail_ref[0:rows, :] = out
        score = tail_ref[0:py, :]
        for j in (1, 2):
            score = score + pltpu.roll(tail_ref[j:j + py, :], 128 - j * pz, 1)
        out_ref[0] = jnp.transpose(score)[0:pz, :] + bias_ref[2:3, 0:1]
    return kernel


def detector(pooled, edge, ids, weights, py, pz):
    counts = tuple(lax.axis_size(a) for a in ("gx", "gy", "gz"))
    half = pooled.shape[1]
    assert half == 128 and pz * CIN == half and pz * 3 <= 128
    rows = py + 4
    width = lanes_for((pz + 4) * CH)
    blocks = width // 128
    yr = both_sides(edge, "gy")
    tall = -(-(TOP + py + 3) // 16) * 16
    (plane,) = call(
        plane_kernel(py, counts[1]), [((tall, half), BF16)], ids, pooled, yr,
        scratch=[pltpu.VMEM((tall, half), F32)])
    shifts = []
    for s in (1, -1, 2, -2, 3, -3):
        if s % counts[0] and s % counts[0] not in shifts:
            shifts.append(s % counts[0])
    own = [plane] + [lax.ppermute(plane, "gx", ring("gx", s)) for s in shifts]
    matrices = call(
        weight_kernel,
        [((3, 6 * half, width), BF16), ((3, 768, 128), BF16), ((3, width, 128), BF16), ((8, width), F32)],
        *weights, plane)
    own[1], *matrices = lax.optimization_barrier((own[1], *matrices))
    other = [z_neighbour(v, "gz", False) for v in own]
    args = (ids, *own, *other, *matrices)
    (score,) = call(
        conv_kernel(py, counts, shifts), [((1, pz, py), F32)], *args,
        scratch=[
            pltpu.VMEM((7, tall, 2 * half), F32),
            pltpu.VMEM((7, rows, 6 * half), BF16),
            pltpu.VMEM((5, rows + 8, width + 128), F32),
            pltpu.VMEM((5, blocks, rows, 768), BF16),
            pltpu.VMEM((3, rows, width), BF16),
            pltpu.VMEM((rows + 8, 128), F32),
        ], mib=32)
    return jnp.swapaxes(score, 1, 2)


def solution(mesh):
    slab = P(("groups", "gx"), "gy", "gz")
    return jax.shard_map(
        body,
        mesh=mesh,
        in_specs=(slab, slab, slab, P(), P(), P(), P(), P(), P()),
        out_specs=(slab, slab, slab, slab),
        check_vma=False,
    )
```

```python
import jax
import jax.numpy as jnp
import numpy as np
from jax import lax
from jax.experimental import pallas as pl
from jax.experimental.pallas import tpu as pltpu
from jax.sharding import PartitionSpec as P

F32 = jnp.float32
BF16 = jnp.bfloat16
I16 = jnp.int16
WELL_HEIGHT = 1.0
STRAIN_COUPLING = 4.0
TIME_STEP = 0.01
DAMAGE_RATE = 0.8
ENERGY_CRITICAL = 0.02

OFF = 16
A_CODE = (0.0, 1.0)
B_CODE = (-1.1, 3.1)
SUM_LOW, SUM_SPAN = -1280.0, 4096.0

VMEM = pl.BlockSpec(memory_space=pltpu.VMEM)
HBM = pl.BlockSpec(memory_space=pltpu.HBM)


def to_code(x, code):
    low, span = code
    v = (x - low) * (65535.0 / span) - 32768.0
    return jnp.clip(jnp.round(v), -32768.0, 32767.0).astype(jnp.int32).astype(I16)


def from_code(q, code):
    low, span = code
    return q.astype(jnp.int32).astype(F32) * (span / 65535.0) + (low + 32768.0 * span / 65535.0)


def sum_digits(s):
    v = (s[0:2] - SUM_LOW) * (65536.0 / SUM_SPAN)
    high = jnp.floor(v)
    low = jnp.minimum(jnp.floor((v - high) * 65536.0), 65535.0)
    rows = jnp.concatenate([high, low, jnp.full((12, s.shape[1]), 32768.0, F32)]) - 32768.0
    return rows.astype(jnp.int32).astype(I16)


def from_digits(tile):
    v = tile.astype(jnp.int32).astype(F32) + 32768.0
    return (v[0:2] + v[2:4] * (1.0 / 65536.0)) * (SUM_SPAN / 65536.0) + SUM_LOW


def by_label(labels, values):
    return jnp.where(labels == 0, values[0], jnp.where(labels == 1, values[1], values[2])).astype(F32)


FACTORS = (1.0, 0.3, 0.05)
ROOTS = tuple(float(np.sqrt(np.float32(v))) for v in FACTORS)


def call(kernel, outs, *args, in_specs=None, out_specs=None, scratch=(), mib=16):
    return pl.pallas_call(
        kernel,
        in_specs=in_specs or [VMEM] * len(args),
        out_specs=out_specs or [VMEM] * len(outs),
        out_shape=[jax.ShapeDtypeStruct(s, t) for s, t in outs],
        scratch_shapes=scratch,
        compiler_params=pltpu.CompilerParams(vmem_limit_bytes=mib * 1024 * 1024),
    )(*args)


def chunks(start, stop, size):
    return [(r, min(size, stop - r)) for r in range(start, stop, size)]


def fold(x):
    return x.reshape(x.shape[0] // 8, 8, x.shape[1]).sum(0)


def to_rows(top, bottom):
    return jnp.concatenate([jnp.sum(top, 0, keepdims=True), jnp.sum(bottom, 0, keepdims=True),
                            jnp.zeros((6, top.shape[1]), F32)])


def first_kernel(c_hbm, d_hbm, l_hbm, f_ref, amp_ref, lo_ref, hi_ref, sum_ref, le_ref, d_ref, l_ref, sems):
    nx, ny, nz = f_ref.shape
    order = [0, nx - 1] + list(range(1, nx - 1))
    copies = []
    for x in order:
        copies.append([pltpu.make_async_copy(src.at[x], dst.at[x], sems.at[k, x])
                       for k, (src, dst) in enumerate(((c_hbm, f_ref), (d_hbm, d_ref), (l_hbm, l_ref)))])
        for c in copies[-1]:
            c.start()
    top = jnp.zeros((8, nz), F32)
    bottom = jnp.zeros((8, nz), F32)
    for k, x in enumerate(order):
        for c in copies[k]:
            c.wait()
        le_ref[x, 0:16, :] = l_ref[x, 0:16, :]
        le_ref[x, 16:32, :] = l_ref[x, ny - 16:ny, :]
        for r, n in chunks(0, ny, 48):
            f = f_ref[x, r:r + n, :]
            a = by_label(l_ref[x, r:r + n, :], ROOTS) * (1.0 - d_ref[x, r:r + n, :])
            amp_ref[x, r:r + n, :] = a
            m = a * a
            top = top + fold(m * f)
            bottom = bottom + fold(m)
            for near, far, out in ((0, 1, lo_ref), (nx - 1, nx - 2, hi_ref)):
                if x == near:
                    out[r:r + n, :] = to_code(f, A_CODE)
                    out[2 * ny + r:2 * ny + r + n, :] = to_code(a, A_CODE)
                if x == far:
                    out[ny + r:ny + r + n, :] = to_code(f, A_CODE)
    s = to_rows(top, bottom)
    sum_ref[...] = s
    lo_ref[3 * ny:3 * ny + 16, :] = sum_digits(s)
    hi_ref[3 * ny:3 * ny + 16, :] = sum_digits(s)


def edge_rows(code, ride_x, with_amp):
    def kernel(*refs):
        f_ref = refs[0]
        amp_ref = refs[1] if with_amp else None
        lo_ref, hi_ref, s_ref, far_ref = refs[1 + with_amp:5 + with_amp]
        out_ref = refs[-1]
        nx, ny, nz = f_ref.shape
        low_rows = [from_code(r[0:16, :], code)[0:1] for r in (lo_ref, hi_ref)]
        high_rows = [from_code(r[ny - 16:ny, :], code)[15:16] for r in (lo_ref, hi_ref)]
        s = s_ref[...]
        if ride_x:
            s = s + far_ref[...]
        for side, first, second, beside in ((0, 0, 1, low_rows), (1, ny - 1, ny - 2, high_rows)):
            for x in range(nx):
                out_ref[side, 2 * x:2 * x + 1, :] = f_ref[x, first:first + 1, :]
                out_ref[side, 2 * x + 1:2 * x + 2, :] = f_ref[x, second:second + 1, :]
                if amp_ref is not None:
                    out_ref[side, 10 + x:11 + x, :] = amp_ref[x, first:first + 1, :]
            out_ref[side, 8:9, :] = beside[0]
            out_ref[side, 9:10, :] = beside[1]
            out_ref[side, 16:24, :] = s
            if ride_x:
                out_ref[side, 16:18, :] = (s[0:2] + from_digits(lo_ref[lo_ref.shape[0] - 16:, :])
                                           + from_digits(hi_ref[hi_ref.shape[0] - 16:, :]))
    return kernel


def group(lane, j, nz, first, count):
    return (lane - (32 * j + first)) % nz < count


def pack_z(code, ride_y, with_amp):
    def kernel(*refs):
        f_ref = refs[0]
        amp_ref = refs[1] if with_amp else None
        lo_ref, hi_ref, yr_ref, yp_ref, out_ref = refs[1 + with_amp:]
        nx, ny, nz = f_ref.shape
        end = OFF + ny
        lane = lax.broadcasted_iota(jnp.int32, (1, nz), 1)
        for k in range(out_ref.shape[0]):
            planes = [p for p in range(4 * k, 4 * k + 4) if p < nx + 2]

            def packed(f_of, a_of, ps):
                out = None
                for p in ps:
                    j = p % 4
                    f = f_of(p)
                    f = pltpu.roll(f, 32 * j, 1) if j else f
                    out = f if out is None else jnp.where(group(lane, j, nz, -2, 4), f, out)
                    a = a_of(p)
                    if a is not None:
                        out = jnp.where(group(lane, j, nz, 15, 2), pltpu.roll(a, 32 * j + 16, 1), out)
                return out

            for r, n in chunks(0, ny, 48):
                def f_of(p):
                    if p == 0:
                        return from_code(lo_ref[r:r + n, :], code)
                    if p == nx + 1:
                        return from_code(hi_ref[r:r + n, :], code)
                    return f_ref[p - 1, r:r + n, :]

                def a_of(p):
                    return amp_ref[p - 1, r:r + n, :] if with_amp and 1 <= p <= nx else None

                out_ref[k, OFF + r:OFF + r + n, :] = packed(f_of, a_of, planes)
            inner = [p for p in planes if 1 <= p <= nx]
            if inner:
                for side, near in ((1, OFF - 1), (0, end)):
                    out_ref[k, near:near + 1, :] = packed(
                        lambda p: yr_ref[side, 2 * (p - 1):2 * (p - 1) + 1, :], lambda p: None, inner)
        s = yp_ref[0, 16:24, :]
        out_ref[0, 0:8, :] = s + yr_ref[0, 16:24, :] if ride_y else s
    return kernel


def spread(spans, extra, size):
    return [v for a, b in spans for v in chunks(OFF + a - extra, OFF + b + extra, size)]


def fill(code, f_ref, lo_ref, hi_ref, yr_ref, zr_ref, pad_ref, ec_ref, spans):
    nx, ny, nz = f_ref.shape
    end = OFF + ny
    wide = [v for a, b in spans for v in chunks(max(a - 16, 0), min(b + 16, ny), 48)]
    for near, far, ref in ((1, 0, lo_ref), (nx + 2, nx + 3, hi_ref)):
        for r, n in wide:
            pad_ref[near, OFF + r:OFF + r + n, :] = from_code(ref[r:r + n, :], code)
            pad_ref[far, OFF + r:OFF + r + n, :] = from_code(ref[ny + r:ny + r + n, :], code)
    for p, k in ((1, 8), (nx + 2, 9)):
        pad_ref[p, OFF - 1:OFF, :] = yr_ref[1, k:k + 1, :]
        pad_ref[p, end:end + 1, :] = yr_ref[0, k:k + 1, :]
    for x in range(nx):
        for r, n in wide:
            pad_ref[x + 2, OFF + r:OFF + r + n, :] = f_ref[x, r:r + n, :]
        for side, near, far in ((1, OFF - 1, OFF - 2), (0, end, end + 1)):
            pad_ref[x + 2, near:near + 1, :] = yr_ref[side, 2 * x:2 * x + 1, :]
            pad_ref[x + 2, far:far + 1, :] = yr_ref[side, 2 * x + 1:2 * x + 2, :]
    lane = lax.broadcasted_iota(jnp.int32, (1, nz), 1)
    for r, n in spread(spans, 8, 32):
        ec_ref[r:r + n, :] = regroup(zr_ref, r, n, lane, 1)


def regroup(z_ref, r, n, lane, first):
    here = z_ref[0, r:r + n, :]
    if not first:
        return here
    next_four = z_ref[1, r:r + n, :]
    return pltpu.roll(jnp.where(group(lane, 0, 128, -8, 32 * first), next_four, here), 128 - 32 * first, 1)


def weighted_mean(yp_ref, yr_ref, zr_ref, ride_y, ride_z):
    s = yp_ref[0, 16:24, :]
    if ride_y:
        s = s + yr_ref[0, 16:24, :]
    if ride_z:
        s = s + zr_ref[0, 0:8, :]
    return jnp.sum(s[0:1], keepdims=True) / jnp.sum(s[1:2], keepdims=True)


def worn(a, m, f, mean):
    e = f - mean
    loss = DAMAGE_RATE * 0.5 * STRAIN_COUPLING * (m * (e * e)) - DAMAGE_RATE * ENERGY_CRITICAL
    return a * (1.0 - jnp.maximum(loss, 0.0))


class Geometry:
    def __init__(self, nx, ny, nz):
        self.nx, self.ny, self.nz = nx, ny, nz
        self.lane = lax.broadcasted_iota(jnp.int32, (1, nz), 1)
        self.first = self.lane == 0
        self.last = self.lane == nz - 1

    def before(self, own, other):
        return pltpu.roll(jnp.where(self.last, other, own), 1, 1)

    def after(self, own, other):
        return pltpu.roll(jnp.where(self.first, other, own), self.nz - 1, 1)

    def unpack(self, packed, j):
        return pltpu.roll(packed, self.nz - 32 * j, 1) if j else packed


def chem_of(f, m, around, mean):
    w = 2.0 * WELL_HEIGHT
    return ((2.0 * w * f - 3.0 * w) * f + (w + 6.0)) * f - around + STRAIN_COUPLING * (m * (f - mean))


def chemistry(g, pad_ref, mob_ref, mobe_ref, zr_ref, zo_ref, ec_ref, chem_ref, cheme_ref, mean, spans):
    nx = g.nx
    for p in range(nx + 2):
        for r, n in spread(spans, 8, 32) if 1 <= p <= nx else spread(spans, 0, 48):
            f = pad_ref[p + 1, r:r + n, :]
            e = g.unpack(zr_ref[p // 4, r:r + n, :], p % 4)
            around = (pad_ref[p, r:r + n, :] + pad_ref[p + 2, r:r + n, :]
                      + pad_ref[p + 1, r - 1:r - 1 + n, :] + pad_ref[p + 1, r + 1:r + 1 + n, :]
                      + g.before(f, e) + g.after(f, e))
            chem_ref[p, r:r + n, :] = chem_of(f, mob_ref[p, r:r + n, :], around, mean)
    firsts, lasts = g.lane % 32 == 0, g.lane % 32 == 31
    for r, n in spread(spans, 0, 48):
        e = ec_ref[r:r + n, :]
        own = regroup(zo_ref, r, n, g.lane, 1)
        around = (regroup(zr_ref, r, n, g.lane, 0) + regroup(zr_ref, r, n, g.lane, 2)
                  + ec_ref[r - 1:r - 1 + n, :] + ec_ref[r + 1:r + 1 + n, :]
                  + pltpu.roll(jnp.where(lasts, own, e), 1, 1)
                  + pltpu.roll(jnp.where(firsts, own, e), g.nz - 1, 1))
        cheme_ref[r - OFF:r - OFF + n, :] = chem_of(e, mobe_ref[r - OFF:r - OFF + n, :], around, mean)


def flux_of(g, x, r, n, mob_ref, mobe_ref, chem_ref, cheme_ref):
    p = x + 1
    m = mob_ref[p, r:r + n, :]
    q = chem_ref[p, r:r + n, :]
    me = g.unpack(mobe_ref[r - OFF:r - OFF + n, :], x)
    qe = g.unpack(cheme_ref[r - OFF:r - OFF + n, :], x)
    total = None
    for nm, nq in (
        (mob_ref[p - 1, r:r + n, :], chem_ref[p - 1, r:r + n, :]),
        (mob_ref[p + 1, r:r + n, :], chem_ref[p + 1, r:r + n, :]),
        (mob_ref[p, r - 1:r - 1 + n, :], chem_ref[p, r - 1:r - 1 + n, :]),
        (mob_ref[p, r + 1:r + 1 + n, :], chem_ref[p, r + 1:r + 1 + n, :]),
        (g.before(m, me), g.before(q, qe)),
        (g.after(m, me), g.after(q, qe)),
    ):
        term = (nm + m) * (nq - q)
        total = term if total is None else total + term
    return m, 0.5 * total


def step_a(ride_y, ride_z):
    def kernel(f_ref, amp_ref, lo_ref, hi_ref, yr_ref, zr_ref, zo_ref, yp_ref,
               f2_ref, a2_ref, ae2_ref, lo_out, hi_out, sum_ref,
               pad_ref, ec_ref, mob_ref, mobe_ref, chem_ref, cheme_ref):
        nx, ny, nz = f2_ref.shape
        end = OFF + ny
        g = Geometry(nx, ny, nz)
        mean = weighted_mean(yp_ref, yr_ref, zr_ref, ride_y, ride_z)
        fill(A_CODE, f_ref, lo_ref, hi_ref, yr_ref, zr_ref, pad_ref, ec_ref, [(0, ny)])

        def wear(p, r, n, a):
            m = a * a
            mob_ref[p, r:r + n, :] = m
            a2_ref[p, r:r + n, :] = worn(a, m, pad_ref[p + 1, r:r + n, :], mean)

        for r, n in chunks(0, ny, 48):
            wear(0, OFF + r, n, from_code(lo_ref[2 * ny + r:2 * ny + r + n, :], A_CODE))
            wear(nx + 1, OFF + r, n, from_code(hi_ref[2 * ny + r:2 * ny + r + n, :], A_CODE))
            for x in range(nx):
                wear(x + 1, OFF + r, n, amp_ref[x, r:r + n, :])
            e = ec_ref[OFF + r:OFF + r + n, :]
            a = pltpu.roll(e, nz - 16, 1)
            m = a * a
            mobe_ref[r:r + n, :] = m
            ae2_ref[r:r + n, :] = worn(a, m, e, mean)
        for x in range(nx):
            wear(x + 1, OFF - 1, 1, yr_ref[1, 10 + x:11 + x, :])
            wear(x + 1, end, 1, yr_ref[0, 10 + x:11 + x, :])
        chemistry(g, pad_ref, mob_ref, mobe_ref, zr_ref, zo_ref, ec_ref, chem_ref, cheme_ref, mean, [(0, ny)])
        top = jnp.zeros((8, nz), F32)
        bottom = jnp.zeros((8, nz), F32)
        for x in range(nx):
            for r, n in chunks(OFF, end, 48):
                _, flux = flux_of(g, x, r, n, mob_ref, mobe_ref, chem_ref, cheme_ref)
                f = pad_ref[x + 2, r:r + n, :] + TIME_STEP * flux
                s = slice(r - OFF, r - OFF + n)
                f2_ref[x, s, :] = f
                a = a2_ref[x + 1, r:r + n, :]
                m = a * a
                top = top + fold(m * f)
                bottom = bottom + fold(m)
                for near, far, out in ((0, 1, lo_out), (nx - 1, nx - 2, hi_out)):
                    if x == near:
                        out[s, :] = to_code(f, B_CODE)
                    if x == far:
                        out[r - OFF + ny:r - OFF + ny + n, :] = to_code(f, B_CODE)
        s = to_rows(top, bottom)
        sum_ref[...] = s
        lo_out[2 * ny:2 * ny + 16, :] = sum_digits(s)
        hi_out[2 * ny:2 * ny + 16, :] = sum_digits(s)
    return kernel


def potentials_b(g, mean, a2_ref, ae2_ref, others, scratch, spans):
    f_ref, lo_ref, hi_ref, yr_ref, zr_ref, zo_ref = others
    pad_ref, ec_ref, mob_ref, mobe_ref, chem_ref, cheme_ref = scratch
    nx = g.nx
    fill(B_CODE, f_ref, lo_ref, hi_ref, yr_ref, zr_ref, pad_ref, ec_ref, spans)
    for p in range(nx + 2):
        for r, n in spread(spans, 8, 32) if 1 <= p <= nx else spread(spans, 0, 48):
            a = a2_ref[p, r:r + n, :]
            mob_ref[p, r:r + n, :] = a * a
    for r, n in spread(spans, 0, 48):
        a = ae2_ref[r - OFF:r - OFF + n, :]
        mobe_ref[r - OFF:r - OFF + n, :] = a * a
    chemistry(g, pad_ref, mob_ref, mobe_ref, zr_ref, zo_ref, ec_ref, chem_ref, cheme_ref, mean, spans)


def finish_b(g, mean, x, r, n, labels, a2_ref, scratch):
    pad_ref, ec_ref, mob_ref, mobe_ref, chem_ref, cheme_ref = scratch
    m, flux = flux_of(g, x, r, n, mob_ref, mobe_ref, chem_ref, cheme_ref)
    f0 = pad_ref[x + 2, r:r + n, :]
    f = f0 + TIME_STEP * flux
    a = worn(a2_ref[x + 1, r:r + n, :], m, f0, mean)
    dmg = 1.0 - a * by_label(labels, tuple(1.0 / v for v in ROOTS))
    return flux, (f, dmg, a * a, by_label(labels, FACTORS))


def pool_rows(scr_ref, count, nz):
    zin = lax.broadcasted_iota(jnp.int32, (nz, nz), 0)
    out = lax.broadcasted_iota(jnp.int32, (nz, nz), 1)
    total = jnp.zeros((count, nz), F32)
    for i in range(4):
        rows = (scr_ref[i, pl.ds(0, count, stride=4), :] + scr_ref[i, pl.ds(1, count, stride=4), :]
                + scr_ref[i, pl.ds(2, count, stride=4), :] + scr_ref[i, pl.ds(3, count, stride=4), :])
        pick = jnp.where((zin // 4 == out // 4) & (out % 4 == i), 1.0 / 64.0, 0.0).astype(F32)
        total = total + jnp.dot(rows, pick, precision=lax.Precision.HIGHEST, preferred_element_type=F32)
    return total


def edge_b(ride_y, ride_z):
    def kernel(f_ref, a2_ref, ae2_ref, lo_ref, hi_ref, yr_ref, zr_ref, zo_ref, yp_ref, l_ref, edge_ref, *rest):
        *scratch, pool_scr = rest
        nx, ny, nz = f_ref.shape
        spans = [(0, 16), (ny - 16, ny)]
        g = Geometry(nx, ny, nz)
        mean = weighted_mean(yp_ref, yr_ref, zr_ref, ride_y, ride_z)
        potentials_b(g, mean, a2_ref, ae2_ref, (f_ref, lo_ref, hi_ref, yr_ref, zr_ref, zo_ref), scratch, spans)
        for k, (a, b) in enumerate(spans):
            s = slice(16 * k, 16 * k + 16)
            pooled = [None] * 4
            for x in range(nx):
                _, values = finish_b(g, mean, x, OFF + a, 16, l_ref[x, s, :], a2_ref, scratch)
                pooled = [v if p is None else p + v for p, v in zip(pooled, values)]
            for i in range(4):
                pool_scr[i, s, :] = pooled[i]
        total = pool_rows(pool_scr, 8, nz)
        blank = jnp.zeros((13, nz), F32)
        edge_ref[0] = jnp.concatenate([total[0:3], blank]).astype(BF16)
        edge_ref[1] = jnp.concatenate([total[5:8], blank]).astype(BF16)
    return kernel


def step_b(ride_y, ride_z):
    def kernel(f_ref, a2_ref, ae2_ref, lo_ref, hi_ref, yr_ref, zr_ref, zo_ref, yp_ref, l_hbm,
               f3_hbm, dmg_hbm, flux_hbm, pool_ref, *rest):
        *scratch, pool_scr, l_ref, f3_ref, dmg_ref, flux_ref, l_sem, sems = rest
        nx, ny, nz = f_ref.shape
        labels_in = pltpu.make_async_copy(l_hbm, l_ref, l_sem)
        labels_in.start()
        g = Geometry(nx, ny, nz)
        mean = weighted_mean(yp_ref, yr_ref, zr_ref, ride_y, ride_z)
        potentials_b(g, mean, a2_ref, ae2_ref, (f_ref, lo_ref, hi_ref, yr_ref, zr_ref, zo_ref), scratch, [(0, ny)])
        labels_in.wait()
        copies = []
        for k, (r, n) in enumerate(chunks(OFF, OFF + ny, 48)):
            s = slice(r - OFF, r - OFF + n)
            pooled = [None] * 4
            for x in range(nx):
                flux, values = finish_b(g, mean, x, r, n, l_ref[x, s, :], a2_ref, scratch)
                f3_ref[x, s, :] = values[0]
                dmg_ref[x, s, :] = values[1]
                flux_ref[x, s, :] = flux
                pooled = [v if p is None else p + v for p, v in zip(pooled, values)]
            for i in range(4):
                pool_scr[i, s, :] = pooled[i]
            for i, (src, dst) in enumerate(((f3_ref, f3_hbm), (dmg_ref, dmg_hbm), (flux_ref, flux_hbm))):
                copies.append(pltpu.make_async_copy(src.at[:, s, :], dst.at[:, s, :], sems.at[i, k]))
                copies[-1].start()
        pool_ref[...] = pool_rows(pool_scr, ny // 4, nz).astype(BF16)
        for c in copies:
            c.wait()
    return kernel


def ring(axis, shift):
    count = lax.axis_size(axis)
    return [(i, (i + shift) % count) for i in range(count)]


def pair_sum(s, axis):
    count = lax.axis_size(axis)
    if count & (count - 1):
        return lax.psum(s, axis)
    bit = 1
    while bit < count:
        s = s + lax.ppermute(s, axis, [(i, i ^ bit) for i in range(count)])
        bit *= 2
    return s


def both_sides(pay, axis):
    if lax.axis_size(axis) == 2:
        return lax.ppermute(pay, axis, ring(axis, 1))
    return jnp.stack([lax.ppermute(pay[0], axis, ring(axis, -1)), lax.ppermute(pay[1], axis, ring(axis, 1))])


def z_neighbour(pay, axis, packed=True):
    if lax.axis_size(axis) == 2:
        return lax.ppermute(pay, axis, ring(axis, 1))
    above = lax.ppermute(pay, axis, ring(axis, -1))
    below = lax.ppermute(pay, axis, ring(axis, 1))
    lane = lax.broadcasted_iota(jnp.int32, pay.shape, pay.ndim - 1)
    if packed:
        low = (lane % 32 < 8) | (lane % 32 == 16)
    else:
        low = lane < pay.shape[-1] // 2
    return jnp.where(low, above, below)


def x_sides(lo, hi):
    return lax.ppermute(hi, "gx", ring("gx", 1)), lax.ppermute(lo, "gx", ring("gx", -1))


def body(concentration, damage, labels, w_first, b_first, w_second, b_second, w_third, b_third):
    nx, ny, nz = concentration.shape
    rows = ny + 2 * OFF
    block = (nx, ny, nz)
    padded = (nx + 2, rows, nz)
    ride_x = lax.axis_size("gx") == 4
    ride_y = lax.axis_size("gy") == 2
    ride_z = lax.axis_size("gz") == 2
    packed = (-(-(nx + 2) // 4), rows, nz)
    assert nz == 128 and nx == 4
    scratch = [pltpu.VMEM((nx + 4, rows, nz), F32), pltpu.VMEM((rows, nz), F32), pltpu.VMEM(padded, F32),
               pltpu.VMEM((ny, nz), F32), pltpu.VMEM(padded, F32), pltpu.VMEM((ny, nz), F32)]

    def start(sums):
        if ride_x:
            return sums, lax.ppermute(sums, "gx", ring("gx", 2))
        sums = pair_sum(sums, "gx")
        for axis, ride in (("gy", ride_y), ("gz", ride_z)):
            if not ride:
                sums = pair_sum(sums, axis)
        return sums, sums

    concentration, damage, labels = (
        pltpu.with_memory_space_constraint(v, pltpu.HBM) for v in (concentration, damage, labels))
    tall = 3 * ny + 16
    f, amp, lo, hi, sums, edge_labels = call(
        first_kernel,
        [(block, F32), (block, F32), ((tall, nz), I16), ((tall, nz), I16), ((8, nz), F32),
         ((nx, 32, nz), jnp.int32)],
        concentration, damage, labels,
        in_specs=[HBM] * 3,
        scratch=[pltpu.VMEM(block, F32), pltpu.VMEM(block, jnp.int32), pltpu.SemaphoreType.DMA((3, nx))])
    weights = weight_rows(w_first, w_second, w_third)
    sums, far = start(sums)
    lo, hi = x_sides(lo, hi)
    (ypay,) = call(edge_rows(A_CODE, ride_x, True), [((2, 24, nz), F32)], f, amp, lo, hi, sums, far, *weights)
    yr = both_sides(ypay, "gy")
    (zpay,) = call(pack_z(A_CODE, ride_y, True), [(packed, F32)], f, amp, lo, hi, yr, ypay)
    zr = z_neighbour(zpay, "gz")
    tall = 2 * ny + 16
    f, a2, ae2, lo, hi, sums = call(
        step_a(ride_y, ride_z),
        [(block, F32), (padded, F32), ((ny, nz), F32), ((tall, nz), I16), ((tall, nz), I16), ((8, nz), F32)],
        f, amp, lo, hi, yr, zr, zpay, ypay, scratch=scratch)

    sums, far = start(sums)
    lo, hi = x_sides(lo, hi)
    (ypay,) = call(edge_rows(B_CODE, ride_x, False), [((2, 24, nz), F32)], f, lo, hi, sums, far)
    yr = both_sides(ypay, "gy")
    (zpay,) = call(pack_z(B_CODE, ride_y, False), [(packed, F32)], f, lo, hi, yr, ypay)
    zr = z_neighbour(zpay, "gz")
    last = (f, a2, ae2, lo, hi, yr, zr, zpay, ypay)
    (edge,) = call(
        edge_b(ride_y, ride_z), [((2, 16, nz), BF16)], *last, edge_labels,
        scratch=scratch + [pltpu.VMEM((4, 32, nz), F32)])
    fraction, damage_field, flux_sum, pooled = call(
        step_b(ride_y, ride_z),
        [(block, F32), (block, F32), (block, F32), ((ny // 4, nz), BF16)], *last, labels,
        in_specs=[VMEM] * 9 + [HBM], out_specs=[HBM] * 3 + [VMEM],
        scratch=scratch + [
            pltpu.VMEM((4, ny, nz), F32), pltpu.VMEM(block, jnp.int32),
            pltpu.VMEM(block, F32), pltpu.VMEM(block, F32), pltpu.VMEM(block, F32),
            pltpu.SemaphoreType.DMA, pltpu.SemaphoreType.DMA((3, len(chunks(OFF, OFF + ny, 48))))])
    ids = jnp.broadcast_to(jnp.stack([lax.axis_index(a) for a in ("gx", "gy", "gz")])[:, None], (3, nz))
    crack_score = detector(pooled, edge, ids, weights + (b_first[None], b_second[None], b_third[None]), ny // 4, nz // 4)
    return (fraction, damage_field, flux_sum, crack_score)


CH = 16
CIN = 4
TOP = 8


def iota(shape, dim):
    return lax.broadcasted_iota(jnp.int32, shape, dim)


def lanes_for(n):
    return -(-n // 128) * 128


def one_hot(mask):
    return jnp.where(mask, 1.0, 0.0).astype(BF16)


def mm(a, b):
    return jnp.dot(a, b, preferred_element_type=F32)


def tile_shift(rb, cb, pz):
    z_in = rb * 16 // CIN
    z_in = z_in if z_in < pz + pz // 2 else z_in - 2 * pz
    return z_in - cb * 8 + 3


SHIFTS = tuple(k for k in range(-3, 10) if k % (16 // CIN) == 3)


def weight_kernel(w1_ref, w2_ref, w3_ref, b1_ref, b2_ref, b3_ref, plane_ref, t1_ref, t2_ref, t3_ref, bias_ref):
    n1 = bias_ref.shape[1]
    k1 = t1_ref.shape[1] // 3
    pz = k1 // (2 * CIN)
    spread = one_hot(iota((CH, 128), 1) % CH == iota((CH, 128), 0))
    tile1 = mm(w1_ref[...], spread)
    tile2 = mm(w2_ref[...], spread)
    tile3 = mm(w3_ref[...], one_hot(iota((3, 128), 1) // pz == iota((3, 128), 0)))
    step1 = iota((16, 128), 0) // CIN - iota((16, 128), 1) // CH
    step2 = -(iota((16, 128), 1) // CH)
    step3 = -(iota((16, 128), 1) % pz)

    def tile(source, base, stride, step, shift):
        out = jnp.zeros((16, 128), F32)
        for l in range(3):
            k = base + stride * l
            out = jnp.where(step + shift == l, source[16 * k:16 * k + 16], out)
        return out.astype(BF16)

    zero = jnp.zeros((16, 128), BF16)
    bias_ref[...] = jnp.broadcast_to(b3_ref[...], bias_ref.shape)
    for i in range(3):
        for j in range(3):
            tap = 9 * i + 3 * j
            known = {k: tile(tile1, tap, 1, step1, k) for k in SHIFTS}
            for rb in range(k1 // 16):
                for cb in range(n1 // 128):
                    t1_ref[i, j * k1 + rb * 16:j * k1 + rb * 16 + 16, cb * 128:(cb + 1) * 128] = known.get(
                        tile_shift(rb, cb, pz), zero)
            for rb in range(16):
                t2_ref[i, j * 256 + rb * 16:j * 256 + rb * 16 + 16, :] = (
                    tile(tile2, tap, 1, step2, rb) if rb < 10 else zero)
        for rb in range(t3_ref.shape[1] // 16):
            t3_ref[i, rb * 16:rb * 16 + 16, :] = tile(tile3, 3 * i, 1, step3, rb) if rb < pz + 2 else zero
    wide = one_hot(iota((CH, n1), 1) % CH == iota((CH, n1), 0)).astype(F32)
    for k, ref in ((0, b1_ref), (1, b2_ref)):
        bias_ref[k:k + 1, :] = jnp.dot(ref[...], wide, precision=lax.Precision.HIGHEST, preferred_element_type=F32)


def weight_rows(w_first, w_second, w_third):
    return (jnp.tile(jnp.swapaxes(w_first, 1, 2), (1, 16 // CIN, 1)).reshape(27 * 16, CH),
            jnp.swapaxes(w_second, 1, 2).reshape(27 * CH, CH),
            w_third.reshape(3, 3, 3, CH).transpose(0, 2, 3, 1).reshape(9 * CH, 3))


def gelu(x):
    return 0.5 * x * (1.0 + jnp.tanh(0.7978845608028654 * (x + 0.044715 * (x * x * x))))


def plane_kernel(py, y_count):
    def kernel(ids_ref, pool_ref, yr_ref, out_ref, scr_ref):
        iy = ids_ref[1:2, 0:1]
        scr_ref[...] = jnp.zeros(scr_ref.shape, F32)
        scr_ref[TOP:TOP + py, :] = pool_ref[0:py, :].astype(F32)
        below = yr_ref[1].astype(F32)[0:3]
        above = yr_ref[0].astype(F32)[0:3]
        scr_ref[TOP - 3:TOP, :] = jnp.where(iy > 0, below, 0.0)
        scr_ref[TOP + py:TOP + py + 3, :] = jnp.where(iy < y_count - 1, above, 0.0)
        out_ref[...] = scr_ref[...].astype(BF16)
    return kernel


def conv_kernel(py, counts, shifts):
    x_count, y_count, z_count = counts
    n = len(shifts)

    def kernel(*refs):
        ids_ref = refs[0]
        own = refs[1:2 + n]
        other = refs[2 + n:3 + 2 * n]
        t1_ref, t2_ref, t3_ref, bias_ref, out_ref = refs[3 + 2 * n:8 + 2 * n]
        in_ref, lhs1_ref, act1_ref, lhs2_ref, act2_ref, tail_ref = refs[8 + 2 * n:]
        ix, iy, iz = ids_ref[0:1, 0:1], ids_ref[1:2, 0:1], ids_ref[2:3, 0:1]
        half = own[0].shape[1]
        pz = half // CIN
        rows = py + 4
        z_row = iota((1, half), 1) // CIN
        z_ok = ((z_row < pz // 2) & (iz < z_count - 1)) | ((z_row >= pz // 2) & (iz > 0))
        for w in range(7):
            o = w - 3
            k = 0 if o == 0 else 1 + shifts.index((-o) % x_count) if (-o) % x_count in shifts else None
            if k is None:
                in_ref[w] = jnp.zeros(in_ref.shape[1:], F32)
                continue
            inside = (ix + o >= 0) & (ix + o < x_count)
            in_ref[w, :, 0:half] = jnp.where(inside, own[k][...].astype(F32), 0.0)
            in_ref[w, :, half:] = jnp.where(z_ok & inside, other[k][...].astype(F32), 0.0)
        k1 = 2 * half
        for w in range(7):
            for j in range(3):
                start = TOP - 3 + j
                lhs1_ref[w, :, j * k1:(j + 1) * k1] = in_ref[w, start:start + rows, :].astype(BF16)
        out = None
        for i in range(3):
            part = mm(lhs1_ref[i:i + 5].reshape(5 * rows, 3 * k1), t1_ref[i])
            out = part if out is None else out + part
        width = out.shape[1]
        y = iota((rows, width), 0) - 2
        z = iota((rows, width), 1) // CH - 2
        ok = (z < pz + 2) & ((y >= 0) | (iy > 0)) & ((y < py) | (iy < y_count - 1))
        ok = ok & ((z >= 0) | (iz > 0)) & ((z < pz) | (iz < z_count - 1))
        for p in range(5):
            a = gelu(out[p * rows:(p + 1) * rows] + bias_ref[0:1, :])
            good = ok & (ix + p - 2 >= 0) & (ix + p - 2 < x_count)
            act1_ref[p, 0:rows, 0:width] = jnp.where(good, a, 0.0)
            act1_ref[p, rows:, 0:width] = jnp.zeros((act1_ref.shape[1] - rows, width), F32)
            act1_ref[p, :, width:] = jnp.zeros((act1_ref.shape[1], act1_ref.shape[2] - width), F32)
        blocks = lhs2_ref.shape[1]
        for p in range(5):
            for j in range(3):
                a = act1_ref[p, j:j + rows, :].astype(BF16)
                for b in range(blocks):
                    lhs2_ref[p, b, :, j * 256:(j + 1) * 256] = a[:, b * 128:b * 128 + 256]
        out = None
        for i in range(3):
            part = mm(lhs2_ref[i:i + 3].reshape(3 * blocks * rows, 768), t2_ref[i])
            out = part if out is None else out + part
        for b in range(blocks):
            y = iota((rows, 128), 0) - 1
            z = (iota((rows, 128), 1) + b * 128) // CH - 1
            ok = (z < pz + 1) & (y <= py) & ((y >= 0) | (iy > 0)) & ((y < py) | (iy < y_count - 1))
            ok = ok & ((z >= 0) | (iz > 0)) & ((z < pz) | (iz < z_count - 1))
            for p in range(3):
                s = (p * blocks + b) * rows
                a = gelu(out[s:s + rows] + bias_ref[1:2, 0:128])
                good = ok & (ix + p - 1 >= 0) & (ix + p - 1 < x_count)
                act2_ref[p, :, b * 128:(b + 1) * 128] = jnp.where(good, a, 0.0).astype(BF16)
        out = None
        for i in range(3):
            part = mm(act2_ref[i], t3_ref[i])
            out = part if out is None else out + part
        tail_ref[0:rows, :] = out
        score = tail_ref[0:py, :]
        for j in (1, 2):
            score = score + pltpu.roll(tail_ref[j:j + py, :], 128 - j * pz, 1)
        out_ref[0] = jnp.transpose(score)[0:pz, :] + bias_ref[2:3, 0:1]
    return kernel


def detector(pooled, edge, ids, weights, py, pz):
    counts = tuple(lax.axis_size(a) for a in ("gx", "gy", "gz"))
    half = pooled.shape[1]
    assert half == 128 and pz * CIN == half and pz * 3 <= 128
    rows = py + 4
    width = lanes_for((pz + 4) * CH)
    blocks = width // 128
    yr = both_sides(edge, "gy")
    tall = -(-(TOP + py + 3) // 16) * 16
    (plane,) = call(
        plane_kernel(py, counts[1]), [((tall, half), BF16)], ids, pooled, yr,
        scratch=[pltpu.VMEM((tall, half), F32)])
    shifts = []
    for s in (1, -1, 2, -2, 3, -3):
        if s % counts[0] and s % counts[0] not in shifts:
            shifts.append(s % counts[0])
    own = [plane] + [lax.ppermute(plane, "gx", ring("gx", s)) for s in shifts]
    matrices = call(
        weight_kernel,
        [((3, 6 * half, width), BF16), ((3, 768, 128), BF16), ((3, width, 128), BF16), ((8, width), F32)],
        *weights, plane)
    own[1], *matrices = lax.optimization_barrier((own[1], *matrices))
    other = [z_neighbour(v, "gz", False) for v in own]
    args = (ids, *own, *other, *matrices)
    (score,) = call(
        conv_kernel(py, counts, shifts), [((1, pz, py), F32)], *args,
        scratch=[
            pltpu.VMEM((7, tall, 2 * half), F32),
            pltpu.VMEM((7, rows, 6 * half), BF16),
            pltpu.VMEM((5, rows + 8, width + 128), F32),
            pltpu.VMEM((5, blocks, rows, 768), BF16),
            pltpu.VMEM((3, rows, width), BF16),
            pltpu.VMEM((rows + 8, 128), F32),
        ], mib=32)
    return jnp.swapaxes(score, 1, 2)


def solution(mesh):
    slab = P(("groups", "gx"), "gy", "gz")
    return jax.shard_map(
        body,
        mesh=mesh,
        in_specs=(slab, slab, slab, P(), P(), P(), P(), P(), P()),
        out_specs=(slab, slab, slab, slab),
        check_vma=False,
    )
```

```python
import jax
import jax.numpy as jnp
import numpy as np
from jax import lax
from jax.experimental import pallas as pl
from jax.experimental.pallas import tpu as pltpu
from jax.sharding import PartitionSpec as P

F32 = jnp.float32
BF16 = jnp.bfloat16
I16 = jnp.int16
WELL_HEIGHT = 1.0
STRAIN_COUPLING = 4.0
TIME_STEP = 0.01
DAMAGE_RATE = 0.8
ENERGY_CRITICAL = 0.02

OFF = 16
A_CODE = (0.0, 1.0)
B_CODE = (-1.1, 3.1)
SUM_LOW, SUM_SPAN = -1280.0, 4096.0

VMEM = pl.BlockSpec(memory_space=pltpu.VMEM)
HBM = pl.BlockSpec(memory_space=pltpu.HBM)


def to_code(x, code):
    low, span = code
    v = (x - low) * (65535.0 / span) - 32768.0
    return jnp.clip(jnp.round(v), -32768.0, 32767.0).astype(jnp.int32).astype(I16)


def from_code(q, code):
    low, span = code
    return q.astype(jnp.int32).astype(F32) * (span / 65535.0) + (low + 32768.0 * span / 65535.0)


def sum_digits(s):
    v = (s[0:2] - SUM_LOW) * (65536.0 / SUM_SPAN)
    high = jnp.floor(v)
    low = jnp.minimum(jnp.floor((v - high) * 65536.0), 65535.0)
    rows = jnp.concatenate([high, low, jnp.full((12, s.shape[1]), 32768.0, F32)]) - 32768.0
    return rows.astype(jnp.int32).astype(I16)


def from_digits(tile):
    v = tile.astype(jnp.int32).astype(F32) + 32768.0
    return (v[0:2] + v[2:4] * (1.0 / 65536.0)) * (SUM_SPAN / 65536.0) + SUM_LOW


def by_label(labels, values):
    return jnp.where(labels == 0, values[0], jnp.where(labels == 1, values[1], values[2])).astype(F32)


FACTORS = (1.0, 0.3, 0.05)
ROOTS = tuple(float(np.sqrt(np.float32(v))) for v in FACTORS)


def call(kernel, outs, *args, in_specs=None, out_specs=None, scratch=(), mib=16):
    return pl.pallas_call(
        kernel,
        in_specs=in_specs or [VMEM] * len(args),
        out_specs=out_specs or [VMEM] * len(outs),
        out_shape=[jax.ShapeDtypeStruct(s, t) for s, t in outs],
        scratch_shapes=scratch,
        compiler_params=pltpu.CompilerParams(vmem_limit_bytes=mib * 1024 * 1024),
    )(*args)


def chunks(start, stop, size):
    return [(r, min(size, stop - r)) for r in range(start, stop, size)]


def fold(x):
    return x.reshape(x.shape[0] // 8, 8, x.shape[1]).sum(0)


def to_rows(top, bottom):
    return jnp.concatenate([jnp.sum(top, 0, keepdims=True), jnp.sum(bottom, 0, keepdims=True),
                            jnp.zeros((6, top.shape[1]), F32)])


def first_kernel(c_hbm, d_hbm, l_hbm, f_ref, amp_ref, lo_ref, hi_ref, sum_ref, le_ref, d_ref, l_ref, sems):
    nx, ny, nz = f_ref.shape
    order = [0, nx - 1] + list(range(1, nx - 1))
    copies = []
    for x in order:
        copies.append([pltpu.make_async_copy(src.at[x], dst.at[x], sems.at[k, x])
                       for k, (src, dst) in enumerate(((c_hbm, f_ref), (d_hbm, d_ref), (l_hbm, l_ref)))])
        for c in copies[-1]:
            c.start()
    top = jnp.zeros((8, nz), F32)
    bottom = jnp.zeros((8, nz), F32)
    for k, x in enumerate(order):
        for c in copies[k]:
            c.wait()
        le_ref[x, 0:16, :] = l_ref[x, 0:16, :]
        le_ref[x, 16:32, :] = l_ref[x, ny - 16:ny, :]
        for r, n in chunks(0, ny, 48):
            f = f_ref[x, r:r + n, :]
            a = by_label(l_ref[x, r:r + n, :], ROOTS) * (1.0 - d_ref[x, r:r + n, :])
            amp_ref[x, r:r + n, :] = a
            m = a * a
            top = top + fold(m * f)
            bottom = bottom + fold(m)
            for near, far, out in ((0, 1, lo_ref), (nx - 1, nx - 2, hi_ref)):
                if x == near:
                    out[r:r + n, :] = to_code(f, A_CODE)
                    out[2 * ny + r:2 * ny + r + n, :] = to_code(a, A_CODE)
                if x == far:
                    out[ny + r:ny + r + n, :] = to_code(f, A_CODE)
    s = to_rows(top, bottom)
    sum_ref[...] = s
    lo_ref[3 * ny:3 * ny + 16, :] = sum_digits(s)
    hi_ref[3 * ny:3 * ny + 16, :] = sum_digits(s)


def edge_rows(code, ride_x, with_amp):
    def kernel(*refs):
        f_ref = refs[0]
        amp_ref = refs[1] if with_amp else None
        lo_ref, hi_ref, s_ref, far_ref = refs[1 + with_amp:5 + with_amp]
        out_ref = refs[-1]
        nx, ny, nz = f_ref.shape
        low_rows = [from_code(r[0:16, :], code)[0:1] for r in (lo_ref, hi_ref)]
        high_rows = [from_code(r[ny - 16:ny, :], code)[15:16] for r in (lo_ref, hi_ref)]
        s = s_ref[...]
        if ride_x:
            s = s + far_ref[...]
        for side, first, second, beside in ((0, 0, 1, low_rows), (1, ny - 1, ny - 2, high_rows)):
            for x in range(nx):
                out_ref[side, 2 * x:2 * x + 1, :] = f_ref[x, first:first + 1, :]
                out_ref[side, 2 * x + 1:2 * x + 2, :] = f_ref[x, second:second + 1, :]
                if amp_ref is not None:
                    out_ref[side, 10 + x:11 + x, :] = amp_ref[x, first:first + 1, :]
            out_ref[side, 8:9, :] = beside[0]
            out_ref[side, 9:10, :] = beside[1]
            out_ref[side, 16:24, :] = s
            if ride_x:
                out_ref[side, 16:18, :] = (s[0:2] + from_digits(lo_ref[lo_ref.shape[0] - 16:, :])
                                           + from_digits(hi_ref[hi_ref.shape[0] - 16:, :]))
    return kernel


def group(lane, j, nz, first, count):
    return (lane - (32 * j + first)) % nz < count


def pack_z(code, ride_y, with_amp):
    def kernel(*refs):
        f_ref = refs[0]
        amp_ref = refs[1] if with_amp else None
        lo_ref, hi_ref, yr_ref, yp_ref, out_ref = refs[1 + with_amp:]
        nx, ny, nz = f_ref.shape
        end = OFF + ny
        lane = lax.broadcasted_iota(jnp.int32, (1, nz), 1)
        for k in range(out_ref.shape[0]):
            planes = [p for p in range(4 * k, 4 * k + 4) if p < nx + 2]

            def packed(f_of, a_of, ps):
                out = None
                for p in ps:
                    j = p % 4
                    f = f_of(p)
                    f = pltpu.roll(f, 32 * j, 1) if j else f
                    out = f if out is None else jnp.where(group(lane, j, nz, -2, 4), f, out)
                    a = a_of(p)
                    if a is not None:
                        out = jnp.where(group(lane, j, nz, 15, 2), pltpu.roll(a, 32 * j + 16, 1), out)
                return out

            for r, n in chunks(0, ny, 48):
                def f_of(p):
                    if p == 0:
                        return from_code(lo_ref[r:r + n, :], code)
                    if p == nx + 1:
                        return from_code(hi_ref[r:r + n, :], code)
                    return f_ref[p - 1, r:r + n, :]

                def a_of(p):
                    return amp_ref[p - 1, r:r + n, :] if with_amp and 1 <= p <= nx else None

                out_ref[k, OFF + r:OFF + r + n, :] = packed(f_of, a_of, planes)
            inner = [p for p in planes if 1 <= p <= nx]
            if inner:
                for side, near in ((1, OFF - 1), (0, end)):
                    out_ref[k, near:near + 1, :] = packed(
                        lambda p: yr_ref[side, 2 * (p - 1):2 * (p - 1) + 1, :], lambda p: None, inner)
        s = yp_ref[0, 16:24, :]
        out_ref[0, 0:8, :] = s + yr_ref[0, 16:24, :] if ride_y else s
    return kernel


def spread(spans, extra, size):
    return [v for a, b in spans for v in chunks(OFF + a - extra, OFF + b + extra, size)]


def fill(code, f_ref, lo_ref, hi_ref, yr_ref, zr_ref, pad_ref, ze_ref, ec_ref, spans):
    nx, ny, nz = f_ref.shape
    end = OFF + ny
    wide = [v for a, b in spans for v in chunks(max(a - 16, 0), min(b + 16, ny), 48)]
    for near, far, ref in ((1, 0, lo_ref), (nx + 2, nx + 3, hi_ref)):
        for r, n in wide:
            pad_ref[near, OFF + r:OFF + r + n, :] = from_code(ref[r:r + n, :], code)
            pad_ref[far, OFF + r:OFF + r + n, :] = from_code(ref[ny + r:ny + r + n, :], code)
    for p, k in ((1, 8), (nx + 2, 9)):
        pad_ref[p, OFF - 1:OFF, :] = yr_ref[1, k:k + 1, :]
        pad_ref[p, end:end + 1, :] = yr_ref[0, k:k + 1, :]
    for x in range(nx):
        for r, n in wide:
            pad_ref[x + 2, OFF + r:OFF + r + n, :] = f_ref[x, r:r + n, :]
        for side, near, far in ((1, OFF - 1, OFF - 2), (0, end, end + 1)):
            pad_ref[x + 2, near:near + 1, :] = yr_ref[side, 2 * x:2 * x + 1, :]
            pad_ref[x + 2, far:far + 1, :] = yr_ref[side, 2 * x + 1:2 * x + 2, :]
    lane = lax.broadcasted_iota(jnp.int32, (1, nz), 1)
    for r, n in spread(spans, 8, 32):
        ec_ref[r:r + n, :] = regroup(zr_ref, r, n, lane, 1)
        for p in range(nx + 2):
            e = zr_ref[p // 4, r:r + n, :]
            ze_ref[p, r:r + n, :] = pltpu.roll(e, nz - 32 * (p % 4), 1) if p % 4 else e


def regroup(z_ref, r, n, lane, first):
    here = z_ref[0, r:r + n, :]
    if not first:
        return here
    next_four = z_ref[1, r:r + n, :]
    return pltpu.roll(jnp.where(group(lane, 0, 128, -8, 32 * first), next_four, here), 128 - 32 * first, 1)


def weighted_mean(yp_ref, yr_ref, zr_ref, ride_y, ride_z):
    s = yp_ref[0, 16:24, :]
    if ride_y:
        s = s + yr_ref[0, 16:24, :]
    if ride_z:
        s = s + zr_ref[0, 0:8, :]
    return jnp.sum(s[0:1], keepdims=True) / jnp.sum(s[1:2], keepdims=True)


def worn(a, m, f, mean):
    e = f - mean
    loss = DAMAGE_RATE * 0.5 * STRAIN_COUPLING * (m * (e * e)) - DAMAGE_RATE * ENERGY_CRITICAL
    return a * (1.0 - jnp.maximum(loss, 0.0))


class Geometry:
    def __init__(self, nx, ny, nz):
        self.nx, self.ny, self.nz = nx, ny, nz
        self.lane = lax.broadcasted_iota(jnp.int32, (1, nz), 1)
        self.first = self.lane == 0
        self.last = self.lane == nz - 1

    def before(self, own, other):
        return pltpu.roll(jnp.where(self.last, other, own), 1, 1)

    def after(self, own, other):
        return pltpu.roll(jnp.where(self.first, other, own), self.nz - 1, 1)

    def unpack(self, packed, j):
        return pltpu.roll(packed, self.nz - 32 * j, 1) if j else packed


def chem_of(f, m, around, mean):
    w = 2.0 * WELL_HEIGHT
    return ((2.0 * w * f - 3.0 * w) * f + (w + 6.0)) * f - around + STRAIN_COUPLING * (m * (f - mean))


def chemistry(g, pad_ref, mob_ref, ae_ref, zr_ref, zo_ref, ze_ref, ec_ref, chem_ref, cheme_ref, mean, spans):
    nx = g.nx
    for p in range(nx + 2):
        for r, n in spread(spans, 8, 32) if 1 <= p <= nx else spread(spans, 0, 48):
            f = pad_ref[p + 1, r:r + n, :]
            e = ze_ref[p, r:r + n, :]
            around = (pad_ref[p, r:r + n, :] + pad_ref[p + 2, r:r + n, :]
                      + pad_ref[p + 1, r - 1:r - 1 + n, :] + pad_ref[p + 1, r + 1:r + 1 + n, :]
                      + g.before(f, e) + g.after(f, e))
            chem_ref[p, r:r + n, :] = chem_of(f, mob_ref[p, r:r + n, :], around, mean)
    firsts, lasts = g.lane % 32 == 0, g.lane % 32 == 31
    for r, n in spread(spans, 0, 48):
        e = ec_ref[r:r + n, :]
        own = regroup(zo_ref, r, n, g.lane, 1)
        around = (regroup(zr_ref, r, n, g.lane, 0) + regroup(zr_ref, r, n, g.lane, 2)
                  + ec_ref[r - 1:r - 1 + n, :] + ec_ref[r + 1:r + 1 + n, :]
                  + pltpu.roll(jnp.where(lasts, own, e), 1, 1)
                  + pltpu.roll(jnp.where(firsts, own, e), g.nz - 1, 1))
        packed = chem_of(e, ae_ref[r - OFF:r - OFF + n, :], around, mean)
        for x in range(nx):
            cheme_ref[x, r - OFF:r - OFF + n, :] = g.unpack(packed, x)


def flux_of(g, x, r, n, mob_ref, mobe_ref, chem_ref, cheme_ref):
    p = x + 1
    m = mob_ref[p, r:r + n, :]
    q = chem_ref[p, r:r + n, :]
    me = mobe_ref[x, r - OFF:r - OFF + n, :]
    qe = cheme_ref[x, r - OFF:r - OFF + n, :]
    total = None
    for nm, nq in (
        (mob_ref[p - 1, r:r + n, :], chem_ref[p - 1, r:r + n, :]),
        (mob_ref[p + 1, r:r + n, :], chem_ref[p + 1, r:r + n, :]),
        (mob_ref[p, r - 1:r - 1 + n, :], chem_ref[p, r - 1:r - 1 + n, :]),
        (mob_ref[p, r + 1:r + 1 + n, :], chem_ref[p, r + 1:r + 1 + n, :]),
        (g.before(m, me), g.before(q, qe)),
        (g.after(m, me), g.after(q, qe)),
    ):
        term = (nm + m) * (nq - q)
        total = term if total is None else total + term
    return m, 0.5 * total


def step_a(ride_y, ride_z):
    def kernel(f_ref, amp_ref, lo_ref, hi_ref, yr_ref, zr_ref, zo_ref, yp_ref,
               f2_ref, a2_ref, ae2_ref, lo_out, hi_out, sum_ref,
               pad_ref, ze_ref, ec_ref, ae_ref, mob_ref, mobe_ref, chem_ref, cheme_ref):
        nx, ny, nz = f2_ref.shape
        end = OFF + ny
        g = Geometry(nx, ny, nz)
        mean = weighted_mean(yp_ref, yr_ref, zr_ref, ride_y, ride_z)
        fill(A_CODE, f_ref, lo_ref, hi_ref, yr_ref, zr_ref, pad_ref, ze_ref, ec_ref, [(0, ny)])

        def wear(p, r, n, a):
            m = a * a
            mob_ref[p, r:r + n, :] = m
            a2_ref[p, r:r + n, :] = worn(a, m, pad_ref[p + 1, r:r + n, :], mean)

        for r, n in chunks(0, ny, 48):
            wear(0, OFF + r, n, from_code(lo_ref[2 * ny + r:2 * ny + r + n, :], A_CODE))
            wear(nx + 1, OFF + r, n, from_code(hi_ref[2 * ny + r:2 * ny + r + n, :], A_CODE))
            for x in range(nx):
                wear(x + 1, OFF + r, n, amp_ref[x, r:r + n, :])
            e = ec_ref[OFF + r:OFF + r + n, :]
            a = pltpu.roll(e, nz - 16, 1)
            m = a * a
            ae_ref[r:r + n, :] = m
            for x in range(nx):
                mobe_ref[x, r:r + n, :] = g.unpack(m, x)
            ae2_ref[r:r + n, :] = worn(a, m, e, mean)
        for x in range(nx):
            wear(x + 1, OFF - 1, 1, yr_ref[1, 10 + x:11 + x, :])
            wear(x + 1, end, 1, yr_ref[0, 10 + x:11 + x, :])
        chemistry(g, pad_ref, mob_ref, ae_ref, zr_ref, zo_ref, ze_ref, ec_ref, chem_ref, cheme_ref, mean, [(0, ny)])
        top = jnp.zeros((8, nz), F32)
        bottom = jnp.zeros((8, nz), F32)
        for x in range(nx):
            for r, n in chunks(OFF, end, 48):
                _, flux = flux_of(g, x, r, n, mob_ref, mobe_ref, chem_ref, cheme_ref)
                f = pad_ref[x + 2, r:r + n, :] + TIME_STEP * flux
                s = slice(r - OFF, r - OFF + n)
                f2_ref[x, s, :] = f
                a = a2_ref[x + 1, r:r + n, :]
                m = a * a
                top = top + fold(m * f)
                bottom = bottom + fold(m)
                for near, far, out in ((0, 1, lo_out), (nx - 1, nx - 2, hi_out)):
                    if x == near:
                        out[s, :] = to_code(f, B_CODE)
                    if x == far:
                        out[r - OFF + ny:r - OFF + ny + n, :] = to_code(f, B_CODE)
        s = to_rows(top, bottom)
        sum_ref[...] = s
        lo_out[2 * ny:2 * ny + 16, :] = sum_digits(s)
        hi_out[2 * ny:2 * ny + 16, :] = sum_digits(s)
    return kernel


def potentials_b(g, mean, a2_ref, ae2_ref, others, scratch, spans):
    f_ref, lo_ref, hi_ref, yr_ref, zr_ref, zo_ref = others
    pad_ref, ze_ref, ec_ref, ae_ref, mob_ref, mobe_ref, chem_ref, cheme_ref = scratch
    nx = g.nx
    fill(B_CODE, f_ref, lo_ref, hi_ref, yr_ref, zr_ref, pad_ref, ze_ref, ec_ref, spans)
    for p in range(nx + 2):
        for r, n in spread(spans, 8, 32) if 1 <= p <= nx else spread(spans, 0, 48):
            a = a2_ref[p, r:r + n, :]
            mob_ref[p, r:r + n, :] = a * a
    for r, n in spread(spans, 0, 48):
        a = ae2_ref[r - OFF:r - OFF + n, :]
        m = a * a
        ae_ref[r - OFF:r - OFF + n, :] = m
        for x in range(nx):
            mobe_ref[x, r - OFF:r - OFF + n, :] = g.unpack(m, x)
    chemistry(g, pad_ref, mob_ref, ae_ref, zr_ref, zo_ref, ze_ref, ec_ref, chem_ref, cheme_ref, mean, spans)


def finish_b(g, mean, x, r, n, labels, a2_ref, scratch):
    pad_ref, ze_ref, ec_ref, ae_ref, mob_ref, mobe_ref, chem_ref, cheme_ref = scratch
    m, flux = flux_of(g, x, r, n, mob_ref, mobe_ref, chem_ref, cheme_ref)
    f0 = pad_ref[x + 2, r:r + n, :]
    f = f0 + TIME_STEP * flux
    a = worn(a2_ref[x + 1, r:r + n, :], m, f0, mean)
    dmg = 1.0 - a * by_label(labels, tuple(1.0 / v for v in ROOTS))
    return flux, (f, dmg, a * a, by_label(labels, FACTORS))


def pool_rows(scr_ref, count, nz):
    zin = lax.broadcasted_iota(jnp.int32, (nz, nz), 0)
    out = lax.broadcasted_iota(jnp.int32, (nz, nz), 1)
    total = jnp.zeros((count, nz), F32)
    for i in range(4):
        rows = (scr_ref[i, pl.ds(0, count, stride=4), :] + scr_ref[i, pl.ds(1, count, stride=4), :]
                + scr_ref[i, pl.ds(2, count, stride=4), :] + scr_ref[i, pl.ds(3, count, stride=4), :])
        pick = jnp.where((zin // 4 == out // 4) & (out % 4 == i), 1.0 / 64.0, 0.0).astype(F32)
        total = total + jnp.dot(rows, pick, precision=lax.Precision.HIGHEST, preferred_element_type=F32)
    return total


def edge_b(ride_y, ride_z):
    def kernel(f_ref, a2_ref, ae2_ref, lo_ref, hi_ref, yr_ref, zr_ref, zo_ref, yp_ref, l_ref, edge_ref, *rest):
        *scratch, pool_scr = rest
        nx, ny, nz = f_ref.shape
        spans = [(0, 16), (ny - 16, ny)]
        g = Geometry(nx, ny, nz)
        mean = weighted_mean(yp_ref, yr_ref, zr_ref, ride_y, ride_z)
        potentials_b(g, mean, a2_ref, ae2_ref, (f_ref, lo_ref, hi_ref, yr_ref, zr_ref, zo_ref), scratch, spans)
        for k, (a, b) in enumerate(spans):
            s = slice(16 * k, 16 * k + 16)
            pooled = [None] * 4
            for x in range(nx):
                _, values = finish_b(g, mean, x, OFF + a, 16, l_ref[x, s, :], a2_ref, scratch)
                pooled = [v if p is None else p + v for p, v in zip(pooled, values)]
            for i in range(4):
                pool_scr[i, s, :] = pooled[i]
        total = pool_rows(pool_scr, 8, nz)
        blank = jnp.zeros((13, nz), F32)
        edge_ref[0] = jnp.concatenate([total[0:3], blank]).astype(BF16)
        edge_ref[1] = jnp.concatenate([total[5:8], blank]).astype(BF16)
    return kernel


def step_b(ride_y, ride_z):
    def kernel(f_ref, a2_ref, ae2_ref, lo_ref, hi_ref, yr_ref, zr_ref, zo_ref, yp_ref, l_hbm,
               f3_hbm, dmg_hbm, flux_hbm, pool_ref, *rest):
        *scratch, pool_scr, l_ref, f3_ref, dmg_ref, flux_ref, l_sem, sems = rest
        nx, ny, nz = f_ref.shape
        labels_in = pltpu.make_async_copy(l_hbm, l_ref, l_sem)
        labels_in.start()
        g = Geometry(nx, ny, nz)
        mean = weighted_mean(yp_ref, yr_ref, zr_ref, ride_y, ride_z)
        potentials_b(g, mean, a2_ref, ae2_ref, (f_ref, lo_ref, hi_ref, yr_ref, zr_ref, zo_ref), scratch, [(0, ny)])
        labels_in.wait()
        copies = []
        for k, (r, n) in enumerate(chunks(OFF, OFF + ny, 48)):
            s = slice(r - OFF, r - OFF + n)
            pooled = [None] * 4
            for x in range(nx):
                flux, values = finish_b(g, mean, x, r, n, l_ref[x, s, :], a2_ref, scratch)
                f3_ref[x, s, :] = values[0]
                dmg_ref[x, s, :] = values[1]
                flux_ref[x, s, :] = flux
                pooled = [v if p is None else p + v for p, v in zip(pooled, values)]
            for i in range(4):
                pool_scr[i, s, :] = pooled[i]
            for i, (src, dst) in enumerate(((f3_ref, f3_hbm), (dmg_ref, dmg_hbm), (flux_ref, flux_hbm))):
                copies.append(pltpu.make_async_copy(src.at[:, s, :], dst.at[:, s, :], sems.at[i, k]))
                copies[-1].start()
        pool_ref[...] = pool_rows(pool_scr, ny // 4, nz).astype(BF16)
        for c in copies:
            c.wait()
    return kernel


def ring(axis, shift):
    count = lax.axis_size(axis)
    return [(i, (i + shift) % count) for i in range(count)]


def pair_sum(s, axis):
    count = lax.axis_size(axis)
    if count & (count - 1):
        return lax.psum(s, axis)
    bit = 1
    while bit < count:
        s = s + lax.ppermute(s, axis, [(i, i ^ bit) for i in range(count)])
        bit *= 2
    return s


def both_sides(pay, axis):
    if lax.axis_size(axis) == 2:
        return lax.ppermute(pay, axis, ring(axis, 1))
    return jnp.stack([lax.ppermute(pay[0], axis, ring(axis, -1)), lax.ppermute(pay[1], axis, ring(axis, 1))])


def z_neighbour(pay, axis, packed=True):
    if lax.axis_size(axis) == 2:
        return lax.ppermute(pay, axis, ring(axis, 1))
    above = lax.ppermute(pay, axis, ring(axis, -1))
    below = lax.ppermute(pay, axis, ring(axis, 1))
    lane = lax.broadcasted_iota(jnp.int32, pay.shape, pay.ndim - 1)
    if packed:
        low = (lane % 32 < 8) | (lane % 32 == 16)
    else:
        low = lane < pay.shape[-1] // 2
    return jnp.where(low, above, below)


def x_sides(lo, hi):
    return lax.ppermute(hi, "gx", ring("gx", 1)), lax.ppermute(lo, "gx", ring("gx", -1))


def body(concentration, damage, labels, w_first, b_first, w_second, b_second, w_third, b_third):
    nx, ny, nz = concentration.shape
    rows = ny + 2 * OFF
    block = (nx, ny, nz)
    padded = (nx + 2, rows, nz)
    ride_x = lax.axis_size("gx") == 4
    ride_y = lax.axis_size("gy") == 2
    ride_z = lax.axis_size("gz") == 2
    packed = (-(-(nx + 2) // 4), rows, nz)
    assert nz == 128 and nx == 4
    scratch = [pltpu.VMEM((nx + 4, rows, nz), F32), pltpu.VMEM(padded, F32), pltpu.VMEM((rows, nz), F32),
               pltpu.VMEM((ny, nz), F32), pltpu.VMEM(padded, F32), pltpu.VMEM(block, F32),
               pltpu.VMEM(padded, F32), pltpu.VMEM(block, F32)]

    def start(sums):
        if ride_x:
            return sums, lax.ppermute(sums, "gx", ring("gx", 2))
        sums = pair_sum(sums, "gx")
        for axis, ride in (("gy", ride_y), ("gz", ride_z)):
            if not ride:
                sums = pair_sum(sums, axis)
        return sums, sums

    concentration, damage, labels = (
        pltpu.with_memory_space_constraint(v, pltpu.HBM) for v in (concentration, damage, labels))
    tall = 3 * ny + 16
    f, amp, lo, hi, sums, edge_labels = call(
        first_kernel,
        [(block, F32), (block, F32), ((tall, nz), I16), ((tall, nz), I16), ((8, nz), F32),
         ((nx, 32, nz), jnp.int32)],
        concentration, damage, labels,
        in_specs=[HBM] * 3,
        scratch=[pltpu.VMEM(block, F32), pltpu.VMEM(block, jnp.int32), pltpu.SemaphoreType.DMA((3, nx))])
    weights = weight_rows(w_first, w_second, w_third)
    sums, far = start(sums)
    lo, hi = x_sides(lo, hi)
    (ypay,) = call(edge_rows(A_CODE, ride_x, True), [((2, 24, nz), F32)], f, amp, lo, hi, sums, far, *weights)
    yr = both_sides(ypay, "gy")
    (zpay,) = call(pack_z(A_CODE, ride_y, True), [(packed, F32)], f, amp, lo, hi, yr, ypay)
    zr = z_neighbour(zpay, "gz")
    tall = 2 * ny + 16
    f, a2, ae2, lo, hi, sums = call(
        step_a(ride_y, ride_z),
        [(block, F32), (padded, F32), ((ny, nz), F32), ((tall, nz), I16), ((tall, nz), I16), ((8, nz), F32)],
        f, amp, lo, hi, yr, zr, zpay, ypay, scratch=scratch)

    sums, far = start(sums)
    lo, hi = x_sides(lo, hi)
    (ypay,) = call(edge_rows(B_CODE, ride_x, False), [((2, 24, nz), F32)], f, lo, hi, sums, far)
    yr = both_sides(ypay, "gy")
    (zpay,) = call(pack_z(B_CODE, ride_y, False), [(packed, F32)], f, lo, hi, yr, ypay)
    zr = z_neighbour(zpay, "gz")
    last = (f, a2, ae2, lo, hi, yr, zr, zpay, ypay)
    (edge,) = call(
        edge_b(ride_y, ride_z), [((2, 16, nz), BF16)], *last, edge_labels,
        scratch=scratch + [pltpu.VMEM((4, 32, nz), F32)])
    fraction, damage_field, flux_sum, pooled = call(
        step_b(ride_y, ride_z),
        [(block, F32), (block, F32), (block, F32), ((ny // 4, nz), BF16)], *last, labels,
        in_specs=[VMEM] * 9 + [HBM], out_specs=[HBM] * 3 + [VMEM],
        scratch=scratch + [
            pltpu.VMEM((4, ny, nz), F32), pltpu.VMEM(block, jnp.int32),
            pltpu.VMEM(block, F32), pltpu.VMEM(block, F32), pltpu.VMEM(block, F32),
            pltpu.SemaphoreType.DMA, pltpu.SemaphoreType.DMA((3, len(chunks(OFF, OFF + ny, 48))))])
    ids = jnp.broadcast_to(jnp.stack([lax.axis_index(a) for a in ("gx", "gy", "gz")])[:, None], (3, nz))
    crack_score = detector(pooled, edge, ids, weights + (b_first[None], b_second[None], b_third[None]), ny // 4, nz // 4)
    return (fraction, damage_field, flux_sum, crack_score)


CH = 16
CIN = 4
TOP = 8


def iota(shape, dim):
    return lax.broadcasted_iota(jnp.int32, shape, dim)


def lanes_for(n):
    return -(-n // 128) * 128


def one_hot(mask):
    return jnp.where(mask, 1.0, 0.0).astype(BF16)


def mm(a, b):
    return jnp.dot(a, b, preferred_element_type=F32)


def tile_shift(rb, cb, pz):
    z_in = rb * 16 // CIN
    z_in = z_in if z_in < pz + pz // 2 else z_in - 2 * pz
    return z_in - cb * 8 + 3


SHIFTS = tuple(k for k in range(-3, 10) if k % (16 // CIN) == 3)


def weight_kernel(w1_ref, w2_ref, w3_ref, b1_ref, b2_ref, b3_ref, plane_ref, t1_ref, t2_ref, t3_ref, bias_ref):
    n1 = bias_ref.shape[1]
    k1 = t1_ref.shape[1] // 3
    pz = k1 // (2 * CIN)
    spread = one_hot(iota((CH, 128), 1) % CH == iota((CH, 128), 0))
    tile1 = mm(w1_ref[...], spread)
    tile2 = mm(w2_ref[...], spread)
    tile3 = mm(w3_ref[...], one_hot(iota((3, 128), 1) // pz == iota((3, 128), 0)))
    step1 = iota((16, 128), 0) // CIN - iota((16, 128), 1) // CH
    step2 = -(iota((16, 128), 1) // CH)
    step3 = -(iota((16, 128), 1) % pz)

    def tile(source, base, stride, step, shift):
        out = jnp.zeros((16, 128), F32)
        for l in range(3):
            k = base + stride * l
            out = jnp.where(step + shift == l, source[16 * k:16 * k + 16], out)
        return out.astype(BF16)

    zero = jnp.zeros((16, 128), BF16)
    bias_ref[...] = jnp.broadcast_to(b3_ref[...], bias_ref.shape)
    for i in range(3):
        for j in range(3):
            tap = 9 * i + 3 * j
            known = {k: tile(tile1, tap, 1, step1, k) for k in SHIFTS}
            for rb in range(k1 // 16):
                for cb in range(n1 // 128):
                    t1_ref[i, j * k1 + rb * 16:j * k1 + rb * 16 + 16, cb * 128:(cb + 1) * 128] = known.get(
                        tile_shift(rb, cb, pz), zero)
            for rb in range(16):
                t2_ref[i, j * 256 + rb * 16:j * 256 + rb * 16 + 16, :] = (
                    tile(tile2, tap, 1, step2, rb) if rb < 10 else zero)
        for rb in range(t3_ref.shape[1] // 16):
            t3_ref[i, rb * 16:rb * 16 + 16, :] = tile(tile3, 3 * i, 1, step3, rb) if rb < pz + 2 else zero
    wide = one_hot(iota((CH, n1), 1) % CH == iota((CH, n1), 0)).astype(F32)
    for k, ref in ((0, b1_ref), (1, b2_ref)):
        bias_ref[k:k + 1, :] = jnp.dot(ref[...], wide, precision=lax.Precision.HIGHEST, preferred_element_type=F32)


def weight_rows(w_first, w_second, w_third):
    return (jnp.tile(jnp.swapaxes(w_first, 1, 2), (1, 16 // CIN, 1)).reshape(27 * 16, CH),
            jnp.swapaxes(w_second, 1, 2).reshape(27 * CH, CH),
            w_third.reshape(3, 3, 3, CH).transpose(0, 2, 3, 1).reshape(9 * CH, 3))


def gelu(x):
    return 0.5 * x * (1.0 + jnp.tanh(0.7978845608028654 * (x + 0.044715 * (x * x * x))))


def plane_kernel(py, y_count):
    def kernel(ids_ref, pool_ref, yr_ref, out_ref, scr_ref):
        iy = ids_ref[1:2, 0:1]
        scr_ref[...] = jnp.zeros(scr_ref.shape, F32)
        scr_ref[TOP:TOP + py, :] = pool_ref[0:py, :].astype(F32)
        below = yr_ref[1].astype(F32)[0:3]
        above = yr_ref[0].astype(F32)[0:3]
        scr_ref[TOP - 3:TOP, :] = jnp.where(iy > 0, below, 0.0)
        scr_ref[TOP + py:TOP + py + 3, :] = jnp.where(iy < y_count - 1, above, 0.0)
        out_ref[...] = scr_ref[...].astype(BF16)
    return kernel


def conv_kernel(py, counts, shifts):
    x_count, y_count, z_count = counts
    n = len(shifts)

    def kernel(*refs):
        ids_ref = refs[0]
        own = refs[1:2 + n]
        other = refs[2 + n:3 + 2 * n]
        t1_ref, t2_ref, t3_ref, bias_ref, out_ref = refs[3 + 2 * n:8 + 2 * n]
        in_ref, lhs1_ref, act1_ref, lhs2_ref, act2_ref, tail_ref = refs[8 + 2 * n:]
        ix, iy, iz = ids_ref[0:1, 0:1], ids_ref[1:2, 0:1], ids_ref[2:3, 0:1]
        half = own[0].shape[1]
        pz = half // CIN
        rows = py + 4
        z_row = iota((1, half), 1) // CIN
        z_ok = ((z_row < pz // 2) & (iz < z_count - 1)) | ((z_row >= pz // 2) & (iz > 0))
        for w in range(7):
            o = w - 3
            k = 0 if o == 0 else 1 + shifts.index((-o) % x_count) if (-o) % x_count in shifts else None
            if k is None:
                in_ref[w] = jnp.zeros(in_ref.shape[1:], F32)
                continue
            inside = (ix + o >= 0) & (ix + o < x_count)
            in_ref[w, :, 0:half] = jnp.where(inside, own[k][...].astype(F32), 0.0)
            in_ref[w, :, half:] = jnp.where(z_ok & inside, other[k][...].astype(F32), 0.0)
        k1 = 2 * half
        for w in range(7):
            for j in range(3):
                start = TOP - 3 + j
                lhs1_ref[w, :, j * k1:(j + 1) * k1] = in_ref[w, start:start + rows, :].astype(BF16)
        out = None
        for i in range(3):
            part = mm(lhs1_ref[i:i + 5].reshape(5 * rows, 3 * k1), t1_ref[i])
            out = part if out is None else out + part
        width = out.shape[1]
        y = iota((rows, width), 0) - 2
        z = iota((rows, width), 1) // CH - 2
        ok = (z < pz + 2) & ((y >= 0) | (iy > 0)) & ((y < py) | (iy < y_count - 1))
        ok = ok & ((z >= 0) | (iz > 0)) & ((z < pz) | (iz < z_count - 1))
        for p in range(5):
            a = gelu(out[p * rows:(p + 1) * rows] + bias_ref[0:1, :])
            good = ok & (ix + p - 2 >= 0) & (ix + p - 2 < x_count)
            act1_ref[p, 0:rows, 0:width] = jnp.where(good, a, 0.0)
            act1_ref[p, rows:, 0:width] = jnp.zeros((act1_ref.shape[1] - rows, width), F32)
            act1_ref[p, :, width:] = jnp.zeros((act1_ref.shape[1], act1_ref.shape[2] - width), F32)
        blocks = lhs2_ref.shape[1]
        for p in range(5):
            for j in range(3):
                a = act1_ref[p, j:j + rows, :].astype(BF16)
                for b in range(blocks):
                    lhs2_ref[p, b, :, j * 256:(j + 1) * 256] = a[:, b * 128:b * 128 + 256]
        out = None
        for i in range(3):
            part = mm(lhs2_ref[i:i + 3].reshape(3 * blocks * rows, 768), t2_ref[i])
            out = part if out is None else out + part
        for b in range(blocks):
            y = iota((rows, 128), 0) - 1
            z = (iota((rows, 128), 1) + b * 128) // CH - 1
            ok = (z < pz + 1) & (y <= py) & ((y >= 0) | (iy > 0)) & ((y < py) | (iy < y_count - 1))
            ok = ok & ((z >= 0) | (iz > 0)) & ((z < pz) | (iz < z_count - 1))
            for p in range(3):
                s = (p * blocks + b) * rows
                a = gelu(out[s:s + rows] + bias_ref[1:2, 0:128])
                good = ok & (ix + p - 1 >= 0) & (ix + p - 1 < x_count)
                act2_ref[p, :, b * 128:(b + 1) * 128] = jnp.where(good, a, 0.0).astype(BF16)
        out = None
        for i in range(3):
            part = mm(act2_ref[i], t3_ref[i])
            out = part if out is None else out + part
        tail_ref[0:rows, :] = out
        score = tail_ref[0:py, :]
        for j in (1, 2):
            score = score + pltpu.roll(tail_ref[j:j + py, :], 128 - j * pz, 1)
        out_ref[0] = jnp.transpose(score)[0:pz, :] + bias_ref[2:3, 0:1]
    return kernel


def detector(pooled, edge, ids, weights, py, pz):
    counts = tuple(lax.axis_size(a) for a in ("gx", "gy", "gz"))
    half = pooled.shape[1]
    assert half == 128 and pz * CIN == half and pz * 3 <= 128
    rows = py + 4
    width = lanes_for((pz + 4) * CH)
    blocks = width // 128
    yr = both_sides(edge, "gy")
    tall = -(-(TOP + py + 3) // 16) * 16
    (plane,) = call(
        plane_kernel(py, counts[1]), [((tall, half), BF16)], ids, pooled, yr,
        scratch=[pltpu.VMEM((tall, half), F32)])
    shifts = []
    for s in (1, -1, 2, -2, 3, -3):
        if s % counts[0] and s % counts[0] not in shifts:
            shifts.append(s % counts[0])
    own = [plane] + [lax.ppermute(plane, "gx", ring("gx", s)) for s in shifts]
    matrices = call(
        weight_kernel,
        [((3, 6 * half, width), BF16), ((3, 768, 128), BF16), ((3, width, 128), BF16), ((8, width), F32)],
        *weights, plane)
    own[1], *matrices = lax.optimization_barrier((own[1], *matrices))
    other = [z_neighbour(v, "gz", False) for v in own]
    args = (ids, *own, *other, *matrices)
    (score,) = call(
        conv_kernel(py, counts, shifts), [((1, pz, py), F32)], *args,
        scratch=[
            pltpu.VMEM((7, tall, 2 * half), F32),
            pltpu.VMEM((7, rows, 6 * half), BF16),
            pltpu.VMEM((5, rows + 8, width + 128), F32),
            pltpu.VMEM((5, blocks, rows, 768), BF16),
            pltpu.VMEM((3, rows, width), BF16),
            pltpu.VMEM((rows + 8, 128), F32),
        ], mib=32)
    return jnp.swapaxes(score, 1, 2)


def solution(mesh):
    slab = P(("groups", "gx"), "gy", "gz")
    return jax.shard_map(
        body,
        mesh=mesh,
        in_specs=(slab, slab, slab, P(), P(), P(), P(), P(), P()),
        out_specs=(slab, slab, slab, slab),
        check_vma=False,
    )
```

```python
import functools

import jax
import jax.numpy as jnp
import numpy as np
from jax import lax
from jax.experimental import pallas as pl
from jax.experimental.pallas import tpu as pltpu
from jax.sharding import PartitionSpec as P

F32 = jnp.float32
BF16 = jnp.bfloat16
I16 = jnp.int16
WELL_HEIGHT = 1.0
STRAIN_COUPLING = 4.0
TIME_STEP = 0.01
DAMAGE_RATE = 0.8
ENERGY_CRITICAL = 0.02

OFF = 16
A_CODE = (0.0, 1.0)
B_CODE = (-1.1, 3.1)
SUM_LOW, SUM_SPAN = -1280.0, 4096.0

VMEM = pl.BlockSpec(memory_space=pltpu.VMEM)
HBM = pl.BlockSpec(memory_space=pltpu.HBM)


def to_code(x, code):
    low, span = code
    v = (x - low) * (65535.0 / span) - 32768.0
    return jnp.clip(jnp.round(v), -32768.0, 32767.0).astype(jnp.int32).astype(I16)


def from_code(q, code):
    low, span = code
    return q.astype(jnp.int32).astype(F32) * (span / 65535.0) + (low + 32768.0 * span / 65535.0)


def sum_digits(s):
    v = (s[0:2] - SUM_LOW) * (65536.0 / SUM_SPAN)
    high = jnp.floor(v)
    low = jnp.minimum(jnp.floor((v - high) * 65536.0), 65535.0)
    rows = jnp.concatenate([high, low, jnp.full((12, s.shape[1]), 32768.0, F32)]) - 32768.0
    return rows.astype(jnp.int32).astype(I16)


def from_digits(tile):
    v = tile.astype(jnp.int32).astype(F32) + 32768.0
    return (v[0:2] + v[2:4] * (1.0 / 65536.0)) * (SUM_SPAN / 65536.0) + SUM_LOW


def each(count, body):
    def step(i, carry):
        body(i)
        return carry
    lax.fori_loop(0, count, step, 0)


def by_label(labels, values):
    return jnp.where(labels == 0, values[0], jnp.where(labels == 1, values[1], values[2])).astype(F32)


FACTORS = (1.0, 0.3, 0.05)
ROOTS = tuple(float(np.sqrt(np.float32(v))) for v in FACTORS)


def call(kernel, outs, *args, in_specs=None, out_specs=None, scratch=(), mib=16):
    return pl.pallas_call(
        kernel,
        in_specs=in_specs or [VMEM] * len(args),
        out_specs=out_specs or [VMEM] * len(outs),
        out_shape=[jax.ShapeDtypeStruct(s, t) for s, t in outs],
        scratch_shapes=scratch,
        compiler_params=pltpu.CompilerParams(vmem_limit_bytes=mib * 1024 * 1024),
    )(*args)


def chunks(start, stop, size):
    return [(r, min(size, stop - r)) for r in range(start, stop, size)]


def fold(x):
    return x.reshape(x.shape[0] // 8, 8, x.shape[1]).sum(0)


def to_rows(top, bottom):
    return jnp.concatenate([jnp.sum(top, 0, keepdims=True), jnp.sum(bottom, 0, keepdims=True),
                            jnp.zeros((6, top.shape[1]), F32)])


def first_kernel(c_hbm, d_hbm, l_hbm, f_ref, amp_ref, lo_ref, hi_ref, sum_ref, le_ref, d_ref, l_ref, sems):
    nx, ny, nz = f_ref.shape
    order = [0, nx - 1] + list(range(1, nx - 1))
    copies = []
    for x in order:
        copies.append([pltpu.make_async_copy(src.at[x], dst.at[x], sems.at[k, x])
                       for k, (src, dst) in enumerate(((c_hbm, f_ref), (d_hbm, d_ref), (l_hbm, l_ref)))])
        for c in copies[-1]:
            c.start()
    top = jnp.zeros((8, nz), F32)
    bottom = jnp.zeros((8, nz), F32)
    for k, x in enumerate(order):
        for c in copies[k]:
            c.wait()
        le_ref[x, 0:16, :] = l_ref[x, 0:16, :]
        le_ref[x, 16:32, :] = l_ref[x, ny - 16:ny, :]
        for r, n in chunks(0, ny, 48):
            f = f_ref[x, r:r + n, :]
            a = by_label(l_ref[x, r:r + n, :], ROOTS) * (1.0 - d_ref[x, r:r + n, :])
            amp_ref[x, r:r + n, :] = a
            m = a * a
            top = top + fold(m * f)
            bottom = bottom + fold(m)
            for near, far, out in ((0, 1, lo_ref), (nx - 1, nx - 2, hi_ref)):
                if x == near:
                    out[r:r + n, :] = to_code(f, A_CODE)
                    out[2 * ny + r:2 * ny + r + n, :] = to_code(a, A_CODE)
                if x == far:
                    out[ny + r:ny + r + n, :] = to_code(f, A_CODE)
    s = to_rows(top, bottom)
    sum_ref[...] = s
    lo_ref[3 * ny:3 * ny + 16, :] = sum_digits(s)
    hi_ref[3 * ny:3 * ny + 16, :] = sum_digits(s)


def edge_rows(code, ride_x, with_amp):
    def kernel(*refs):
        f_ref = refs[0]
        amp_ref = refs[1] if with_amp else None
        lo_ref, hi_ref, s_ref, far_ref = refs[1 + with_amp:5 + with_amp]
        out_ref = refs[-1]
        nx, ny, nz = f_ref.shape
        low_rows = [from_code(r[0:16, :], code)[0:1] for r in (lo_ref, hi_ref)]
        high_rows = [from_code(r[ny - 16:ny, :], code)[15:16] for r in (lo_ref, hi_ref)]
        s = s_ref[...]
        if ride_x:
            s = s + far_ref[...]
        for side, first, second, beside in ((0, 0, 1, low_rows), (1, ny - 1, ny - 2, high_rows)):
            for x in range(nx):
                out_ref[side, 2 * x:2 * x + 1, :] = f_ref[x, first:first + 1, :]
                out_ref[side, 2 * x + 1:2 * x + 2, :] = f_ref[x, second:second + 1, :]
                if amp_ref is not None:
                    out_ref[side, 10 + x:11 + x, :] = amp_ref[x, first:first + 1, :]
            out_ref[side, 8:9, :] = beside[0]
            out_ref[side, 9:10, :] = beside[1]
            out_ref[side, 16:24, :] = s
            if ride_x:
                out_ref[side, 16:18, :] = (s[0:2] + from_digits(lo_ref[lo_ref.shape[0] - 16:, :])
                                           + from_digits(hi_ref[hi_ref.shape[0] - 16:, :]))
    return kernel


def group(lane, j, nz, first, count):
    return (lane - (32 * j + first)) % nz < count


def pack_z(code, ride_y, with_amp):
    def kernel(*refs):
        f_ref = refs[0]
        amp_ref = refs[1] if with_amp else None
        lo_ref, hi_ref, yr_ref, yp_ref, out_ref = refs[1 + with_amp:]
        nx, ny, nz = f_ref.shape
        end = OFF + ny
        lane = lax.broadcasted_iota(jnp.int32, (1, nz), 1)
        for k in range(out_ref.shape[0]):
            planes = [p for p in range(4 * k, 4 * k + 4) if p < nx + 2]

            def packed(f_of, a_of, ps):
                out = None
                for p in ps:
                    j = p % 4
                    f = f_of(p)
                    f = pltpu.roll(f, 32 * j, 1) if j else f
                    out = f if out is None else jnp.where(group(lane, j, nz, -2, 4), f, out)
                    a = a_of(p)
                    if a is not None:
                        out = jnp.where(group(lane, j, nz, 15, 2), pltpu.roll(a, 32 * j + 16, 1), out)
                return out

            for r, n in chunks(0, ny, 48):
                def f_of(p):
                    if p == 0:
                        return from_code(lo_ref[r:r + n, :], code)
                    if p == nx + 1:
                        return from_code(hi_ref[r:r + n, :], code)
                    return f_ref[p - 1, r:r + n, :]

                def a_of(p):
                    return amp_ref[p - 1, r:r + n, :] if with_amp and 1 <= p <= nx else None

                out_ref[k, OFF + r:OFF + r + n, :] = packed(f_of, a_of, planes)
            inner = [p for p in planes if 1 <= p <= nx]
            if inner:
                for side, near in ((1, OFF - 1), (0, end)):
                    out_ref[k, near:near + 1, :] = packed(
                        lambda p: yr_ref[side, 2 * (p - 1):2 * (p - 1) + 1, :], lambda p: None, inner)
        s = yp_ref[0, 16:24, :]
        out_ref[0, 0:8, :] = s + yr_ref[0, 16:24, :] if ride_y else s
    return kernel


def spread(spans, extra, size):
    return [v for a, b in spans for v in chunks(OFF + a - extra, OFF + b + extra, size)]


def fill(code, f_ref, lo_ref, hi_ref, yr_ref, zr_ref, pad_ref, ze_ref, ec_ref, spans):
    nx, ny, nz = f_ref.shape
    end = OFF + ny
    wide = [v for a, b in spans for v in chunks(max(a - 16, 0), min(b + 16, ny), 48)]
    for near, far, ref in ((1, 0, lo_ref), (nx + 2, nx + 3, hi_ref)):
        for r, n in wide:
            pad_ref[near, OFF + r:OFF + r + n, :] = from_code(ref[r:r + n, :], code)
            pad_ref[far, OFF + r:OFF + r + n, :] = from_code(ref[ny + r:ny + r + n, :], code)
    for p, k in ((1, 8), (nx + 2, 9)):
        pad_ref[p, OFF - 1:OFF, :] = yr_ref[1, k:k + 1, :]
        pad_ref[p, end:end + 1, :] = yr_ref[0, k:k + 1, :]
    @functools.partial(each, nx)
    def _(x):
        for r, n in wide:
            pad_ref[x + 2, OFF + r:OFF + r + n, :] = f_ref[x, r:r + n, :]

    for x in range(nx):
        for side, near, far in ((1, OFF - 1, OFF - 2), (0, end, end + 1)):
            pad_ref[x + 2, near:near + 1, :] = yr_ref[side, 2 * x:2 * x + 1, :]
            pad_ref[x + 2, far:far + 1, :] = yr_ref[side, 2 * x + 1:2 * x + 2, :]
    lane = lax.broadcasted_iota(jnp.int32, (1, nz), 1)
    for r, n in spread(spans, 8, 32):
        ec_ref[r:r + n, :] = regroup(zr_ref, r, n, lane, 1)
        for p in range(nx + 2):
            e = zr_ref[p // 4, r:r + n, :]
            ze_ref[p, r:r + n, :] = pltpu.roll(e, nz - 32 * (p % 4), 1) if p % 4 else e


def regroup(z_ref, r, n, lane, first):
    here = z_ref[0, r:r + n, :]
    if not first:
        return here
    next_four = z_ref[1, r:r + n, :]
    return pltpu.roll(jnp.where(group(lane, 0, 128, -8, 32 * first), next_four, here), 128 - 32 * first, 1)


def weighted_mean(yp_ref, yr_ref, zr_ref, ride_y, ride_z):
    s = yp_ref[0, 16:24, :]
    if ride_y:
        s = s + yr_ref[0, 16:24, :]
    if ride_z:
        s = s + zr_ref[0, 0:8, :]
    return jnp.sum(s[0:1], keepdims=True) / jnp.sum(s[1:2], keepdims=True)


def worn(a, m, f, mean):
    e = f - mean
    loss = DAMAGE_RATE * 0.5 * STRAIN_COUPLING * (m * (e * e)) - DAMAGE_RATE * ENERGY_CRITICAL
    return a * (1.0 - jnp.maximum(loss, 0.0))


class Geometry:
    def __init__(self, nx, ny, nz):
        self.nx, self.ny, self.nz = nx, ny, nz
        self.lane = lax.broadcasted_iota(jnp.int32, (1, nz), 1)
        self.first = self.lane == 0
        self.last = self.lane == nz - 1

    def before(self, own, other):
        return pltpu.roll(jnp.where(self.last, other, own), 1, 1)

    def after(self, own, other):
        return pltpu.roll(jnp.where(self.first, other, own), self.nz - 1, 1)

    def unpack(self, packed, j):
        return pltpu.roll(packed, self.nz - 32 * j, 1) if j else packed


def chem_of(f, m, around, mean):
    w = 2.0 * WELL_HEIGHT
    return ((2.0 * w * f - 3.0 * w) * f + (w + 6.0)) * f - around + STRAIN_COUPLING * (m * (f - mean))


def chemistry(g, pad_ref, mob_ref, ae_ref, zr_ref, zo_ref, ze_ref, ec_ref, chem_ref, cheme_ref, mean, spans):
    nx = g.nx
    @functools.partial(each, nx + 2)
    def _(p):
        for r, n in spread(spans, 8, 32):
            f = pad_ref[p + 1, r:r + n, :]
            e = ze_ref[p, r:r + n, :]
            around = (pad_ref[p, r:r + n, :] + pad_ref[p + 2, r:r + n, :]
                      + pad_ref[p + 1, r - 1:r - 1 + n, :] + pad_ref[p + 1, r + 1:r + 1 + n, :]
                      + g.before(f, e) + g.after(f, e))
            chem_ref[p, r:r + n, :] = chem_of(f, mob_ref[p, r:r + n, :], around, mean)

    firsts, lasts = g.lane % 32 == 0, g.lane % 32 == 31
    for r, n in spread(spans, 0, 48):
        e = ec_ref[r:r + n, :]
        own = regroup(zo_ref, r, n, g.lane, 1)
        around = (regroup(zr_ref, r, n, g.lane, 0) + regroup(zr_ref, r, n, g.lane, 2)
                  + ec_ref[r - 1:r - 1 + n, :] + ec_ref[r + 1:r + 1 + n, :]
                  + pltpu.roll(jnp.where(lasts, own, e), 1, 1)
                  + pltpu.roll(jnp.where(firsts, own, e), g.nz - 1, 1))
        packed = chem_of(e, ae_ref[r - OFF:r - OFF + n, :], around, mean)
        for x in range(nx):
            cheme_ref[x, r - OFF:r - OFF + n, :] = g.unpack(packed, x)


def flux_of(g, x, r, n, mob_ref, mobe_ref, chem_ref, cheme_ref):
    p = x + 1
    m = mob_ref[p, r:r + n, :]
    q = chem_ref[p, r:r + n, :]
    me = mobe_ref[x, r - OFF:r - OFF + n, :]
    qe = cheme_ref[x, r - OFF:r - OFF + n, :]
    total = None
    for nm, nq in (
        (mob_ref[p - 1, r:r + n, :], chem_ref[p - 1, r:r + n, :]),
        (mob_ref[p + 1, r:r + n, :], chem_ref[p + 1, r:r + n, :]),
        (mob_ref[p, r - 1:r - 1 + n, :], chem_ref[p, r - 1:r - 1 + n, :]),
        (mob_ref[p, r + 1:r + 1 + n, :], chem_ref[p, r + 1:r + 1 + n, :]),
        (g.before(m, me), g.before(q, qe)),
        (g.after(m, me), g.after(q, qe)),
    ):
        term = (nm + m) * (nq - q)
        total = term if total is None else total + term
    return m, 0.5 * total


def step_a(ride_y, ride_z):
    def kernel(f_ref, amp_ref, lo_ref, hi_ref, yr_ref, zr_ref, zo_ref, yp_ref,
               f2_ref, a2_ref, ae2_ref, lo_out, hi_out, sum_ref,
               pad_ref, ze_ref, ec_ref, ae_ref, mob_ref, mobe_ref, chem_ref, cheme_ref):
        nx, ny, nz = f2_ref.shape
        end = OFF + ny
        g = Geometry(nx, ny, nz)
        mean = weighted_mean(yp_ref, yr_ref, zr_ref, ride_y, ride_z)
        fill(A_CODE, f_ref, lo_ref, hi_ref, yr_ref, zr_ref, pad_ref, ze_ref, ec_ref, [(0, ny)])

        def wear(p, r, n, a):
            m = a * a
            mob_ref[p, r:r + n, :] = m
            a2_ref[p, r:r + n, :] = worn(a, m, pad_ref[p + 1, r:r + n, :], mean)

        for r, n in chunks(0, ny, 48):
            wear(0, OFF + r, n, from_code(lo_ref[2 * ny + r:2 * ny + r + n, :], A_CODE))
            wear(nx + 1, OFF + r, n, from_code(hi_ref[2 * ny + r:2 * ny + r + n, :], A_CODE))
            e = ec_ref[OFF + r:OFF + r + n, :]
            a = pltpu.roll(e, nz - 16, 1)
            m = a * a
            ae_ref[r:r + n, :] = m
            for x in range(nx):
                mobe_ref[x, r:r + n, :] = g.unpack(m, x)
            ae2_ref[r:r + n, :] = worn(a, m, e, mean)

        @functools.partial(each, nx)
        def _(x):
            for r, n in chunks(0, ny, 48):
                wear(x + 1, OFF + r, n, amp_ref[x, r:r + n, :])

        for x in range(nx):
            wear(x + 1, OFF - 1, 1, yr_ref[1, 10 + x:11 + x, :])
            wear(x + 1, end, 1, yr_ref[0, 10 + x:11 + x, :])
        chemistry(g, pad_ref, mob_ref, ae_ref, zr_ref, zo_ref, ze_ref, ec_ref, chem_ref, cheme_ref, mean, [(0, ny)])

        def advance(x, carry):
            top, bottom = carry
            for r, n in chunks(OFF, end, 48):
                _, flux = flux_of(g, x, r, n, mob_ref, mobe_ref, chem_ref, cheme_ref)
                f = pad_ref[x + 2, r:r + n, :] + TIME_STEP * flux
                f2_ref[x, r - OFF:r - OFF + n, :] = f
                a = a2_ref[x + 1, r:r + n, :]
                m = a * a
                top = top + fold(m * f)
                bottom = bottom + fold(m)
            return top, bottom

        zero = jnp.zeros((8, nz), F32)
        top, bottom = lax.fori_loop(0, nx, advance, (zero, zero))
        for near, far, out in ((0, 1, lo_out), (nx - 1, nx - 2, hi_out)):
            for r, n in chunks(0, ny, 48):
                out[r:r + n, :] = to_code(f2_ref[near, r:r + n, :], B_CODE)
                out[ny + r:ny + r + n, :] = to_code(f2_ref[far, r:r + n, :], B_CODE)
        s = to_rows(top, bottom)
        sum_ref[...] = s
        lo_out[2 * ny:2 * ny + 16, :] = sum_digits(s)
        hi_out[2 * ny:2 * ny + 16, :] = sum_digits(s)
    return kernel


def potentials_b(g, mean, a2_ref, ae2_ref, others, scratch, spans):
    f_ref, lo_ref, hi_ref, yr_ref, zr_ref, zo_ref = others
    pad_ref, ze_ref, ec_ref, ae_ref, mob_ref, mobe_ref, chem_ref, cheme_ref = scratch
    nx = g.nx
    fill(B_CODE, f_ref, lo_ref, hi_ref, yr_ref, zr_ref, pad_ref, ze_ref, ec_ref, spans)

    @functools.partial(each, nx + 2)
    def _(p):
        for r, n in spread(spans, 8, 32):
            a = a2_ref[p, r:r + n, :]
            mob_ref[p, r:r + n, :] = a * a

    for r, n in spread(spans, 0, 48):
        a = ae2_ref[r - OFF:r - OFF + n, :]
        m = a * a
        ae_ref[r - OFF:r - OFF + n, :] = m
        for x in range(nx):
            mobe_ref[x, r - OFF:r - OFF + n, :] = g.unpack(m, x)
    chemistry(g, pad_ref, mob_ref, ae_ref, zr_ref, zo_ref, ze_ref, ec_ref, chem_ref, cheme_ref, mean, spans)


def finish_b(g, mean, x, r, n, labels, a2_ref, scratch):
    pad_ref, ze_ref, ec_ref, ae_ref, mob_ref, mobe_ref, chem_ref, cheme_ref = scratch
    m, flux = flux_of(g, x, r, n, mob_ref, mobe_ref, chem_ref, cheme_ref)
    f0 = pad_ref[x + 2, r:r + n, :]
    f = f0 + TIME_STEP * flux
    a = worn(a2_ref[x + 1, r:r + n, :], m, f0, mean)
    dmg = 1.0 - a * by_label(labels, tuple(1.0 / v for v in ROOTS))
    return flux, (f, dmg, a * a, by_label(labels, FACTORS))


def pool_rows(scr_ref, count, nz):
    zin = lax.broadcasted_iota(jnp.int32, (nz, nz), 0)
    out = lax.broadcasted_iota(jnp.int32, (nz, nz), 1)
    total = jnp.zeros((count, nz), F32)
    for i in range(4):
        rows = (scr_ref[i, pl.ds(0, count, stride=4), :] + scr_ref[i, pl.ds(1, count, stride=4), :]
                + scr_ref[i, pl.ds(2, count, stride=4), :] + scr_ref[i, pl.ds(3, count, stride=4), :])
        pick = jnp.where((zin // 4 == out // 4) & (out % 4 == i), 1.0 / 64.0, 0.0).astype(F32)
        total = total + jnp.dot(rows, pick, precision=lax.Precision.HIGHEST, preferred_element_type=F32)
    return total


def edge_b(ride_y, ride_z):
    def kernel(f_ref, a2_ref, ae2_ref, lo_ref, hi_ref, yr_ref, zr_ref, zo_ref, yp_ref, l_ref, edge_ref, *rest):
        *scratch, pool_scr = rest
        nx, ny, nz = f_ref.shape
        spans = [(0, 16), (ny - 16, ny)]
        g = Geometry(nx, ny, nz)
        mean = weighted_mean(yp_ref, yr_ref, zr_ref, ride_y, ride_z)
        potentials_b(g, mean, a2_ref, ae2_ref, (f_ref, lo_ref, hi_ref, yr_ref, zr_ref, zo_ref), scratch, spans)
        for k, (a, b) in enumerate(spans):
            s = slice(16 * k, 16 * k + 16)
            pooled = [None] * 4
            for x in range(nx):
                _, values = finish_b(g, mean, x, OFF + a, 16, l_ref[x, s, :], a2_ref, scratch)
                pooled = [v if p is None else p + v for p, v in zip(pooled, values)]
            for i in range(4):
                pool_scr[i, s, :] = pooled[i]
        total = pool_rows(pool_scr, 8, nz)
        blank = jnp.zeros((13, nz), F32)
        edge_ref[0] = jnp.concatenate([total[0:3], blank]).astype(BF16)
        edge_ref[1] = jnp.concatenate([total[5:8], blank]).astype(BF16)
    return kernel


def step_b(ride_y, ride_z):
    def kernel(f_ref, a2_ref, ae2_ref, lo_ref, hi_ref, yr_ref, zr_ref, zo_ref, yp_ref, l_hbm,
               f3_hbm, dmg_hbm, flux_hbm, pool_ref, *rest):
        *scratch, pool_scr, l_ref, f3_ref, dmg_ref, flux_ref, l_sem, sems = rest
        nx, ny, nz = f_ref.shape
        labels_in = pltpu.make_async_copy(l_hbm, l_ref, l_sem)
        labels_in.start()
        g = Geometry(nx, ny, nz)
        mean = weighted_mean(yp_ref, yr_ref, zr_ref, ride_y, ride_z)
        potentials_b(g, mean, a2_ref, ae2_ref, (f_ref, lo_ref, hi_ref, yr_ref, zr_ref, zo_ref), scratch, [(0, ny)])
        labels_in.wait()
        outs = ((f3_ref, f3_hbm), (dmg_ref, dmg_hbm), (flux_ref, flux_hbm))

        def out_copy(i, x):
            return pltpu.make_async_copy(outs[i][0].at[x], outs[i][1].at[x], sems.at[i, x])

        pool_scr[...] = jnp.zeros(pool_scr.shape, F32)

        @functools.partial(each, nx)
        def _(x):
            for r, n in chunks(OFF, OFF + ny, 48):
                s = slice(r - OFF, r - OFF + n)
                flux, values = finish_b(g, mean, x, r, n, l_ref[x, s, :], a2_ref, scratch)
                f3_ref[x, s, :] = values[0]
                dmg_ref[x, s, :] = values[1]
                flux_ref[x, s, :] = flux
                for i in range(4):
                    pool_scr[i, s, :] = pool_scr[i, s, :] + values[i]
            for i in range(3):
                out_copy(i, x).start()

        pool_ref[...] = pool_rows(pool_scr, ny // 4, nz).astype(BF16)
        for x in range(nx):
            for i in range(3):
                out_copy(i, x).wait()
    return kernel


def ring(axis, shift):
    count = lax.axis_size(axis)
    return [(i, (i + shift) % count) for i in range(count)]


def pair_sum(s, axis):
    count = lax.axis_size(axis)
    if count & (count - 1):
        return lax.psum(s, axis)
    bit = 1
    while bit < count:
        s = s + lax.ppermute(s, axis, [(i, i ^ bit) for i in range(count)])
        bit *= 2
    return s


def both_sides(pay, axis):
    if lax.axis_size(axis) == 2:
        return lax.ppermute(pay, axis, ring(axis, 1))
    return jnp.stack([lax.ppermute(pay[0], axis, ring(axis, -1)), lax.ppermute(pay[1], axis, ring(axis, 1))])


def z_neighbour(pay, axis, packed=True):
    if lax.axis_size(axis) == 2:
        return lax.ppermute(pay, axis, ring(axis, 1))
    above = lax.ppermute(pay, axis, ring(axis, -1))
    below = lax.ppermute(pay, axis, ring(axis, 1))
    lane = lax.broadcasted_iota(jnp.int32, pay.shape, pay.ndim - 1)
    if packed:
        low = (lane % 32 < 8) | (lane % 32 == 16)
    else:
        low = lane < pay.shape[-1] // 2
    return jnp.where(low, above, below)


def x_sides(lo, hi):
    return lax.ppermute(hi, "gx", ring("gx", 1)), lax.ppermute(lo, "gx", ring("gx", -1))


def body(concentration, damage, labels, w_first, b_first, w_second, b_second, w_third, b_third):
    nx, ny, nz = concentration.shape
    rows = ny + 2 * OFF
    block = (nx, ny, nz)
    padded = (nx + 2, rows, nz)
    ride_x = lax.axis_size("gx") == 4
    ride_y = lax.axis_size("gy") == 2
    ride_z = lax.axis_size("gz") == 2
    packed = (-(-(nx + 2) // 4), rows, nz)
    assert nz == 128 and nx == 4
    scratch = [pltpu.VMEM((nx + 4, rows, nz), F32), pltpu.VMEM(padded, F32), pltpu.VMEM((rows, nz), F32),
               pltpu.VMEM((ny, nz), F32), pltpu.VMEM(padded, F32), pltpu.VMEM(block, F32),
               pltpu.VMEM(padded, F32), pltpu.VMEM(block, F32)]

    def start(sums):
        if ride_x:
            return sums, lax.ppermute(sums, "gx", ring("gx", 2))
        sums = pair_sum(sums, "gx")
        for axis, ride in (("gy", ride_y), ("gz", ride_z)):
            if not ride:
                sums = pair_sum(sums, axis)
        return sums, sums

    concentration, damage, labels = (
        pltpu.with_memory_space_constraint(v, pltpu.HBM) for v in (concentration, damage, labels))
    tall = 3 * ny + 16
    f, amp, lo, hi, sums, edge_labels = call(
        first_kernel,
        [(block, F32), (block, F32), ((tall, nz), I16), ((tall, nz), I16), ((8, nz), F32),
         ((nx, 32, nz), jnp.int32)],
        concentration, damage, labels,
        in_specs=[HBM] * 3,
        scratch=[pltpu.VMEM(block, F32), pltpu.VMEM(block, jnp.int32), pltpu.SemaphoreType.DMA((3, nx))])
    weights = weight_rows(w_first, w_second, w_third)
    sums, far = start(sums)
    lo, hi = x_sides(lo, hi)
    (ypay,) = call(edge_rows(A_CODE, ride_x, True), [((2, 24, nz), F32)], f, amp, lo, hi, sums, far, *weights)
    yr = both_sides(ypay, "gy")
    (zpay,) = call(pack_z(A_CODE, ride_y, True), [(packed, F32)], f, amp, lo, hi, yr, ypay)
    zr = z_neighbour(zpay, "gz")
    tall = 2 * ny + 16
    f, a2, ae2, lo, hi, sums = call(
        step_a(ride_y, ride_z),
        [(block, F32), (padded, F32), ((ny, nz), F32), ((tall, nz), I16), ((tall, nz), I16), ((8, nz), F32)],
        f, amp, lo, hi, yr, zr, zpay, ypay, scratch=scratch)

    sums, far = start(sums)
    lo, hi = x_sides(lo, hi)
    (ypay,) = call(edge_rows(B_CODE, ride_x, False), [((2, 24, nz), F32)], f, lo, hi, sums, far)
    yr = both_sides(ypay, "gy")
    (zpay,) = call(pack_z(B_CODE, ride_y, False), [(packed, F32)], f, lo, hi, yr, ypay)
    zr = z_neighbour(zpay, "gz")
    last = (f, a2, ae2, lo, hi, yr, zr, zpay, ypay)
    (edge,) = call(
        edge_b(ride_y, ride_z), [((2, 16, nz), BF16)], *last, edge_labels,
        scratch=scratch + [pltpu.VMEM((4, 32, nz), F32)])
    fraction, damage_field, flux_sum, pooled = call(
        step_b(ride_y, ride_z),
        [(block, F32), (block, F32), (block, F32), ((ny // 4, nz), BF16)], *last, labels,
        in_specs=[VMEM] * 9 + [HBM], out_specs=[HBM] * 3 + [VMEM],
        scratch=scratch + [
            pltpu.VMEM((4, ny, nz), F32), pltpu.VMEM(block, jnp.int32),
            pltpu.VMEM(block, F32), pltpu.VMEM(block, F32), pltpu.VMEM(block, F32),
            pltpu.SemaphoreType.DMA, pltpu.SemaphoreType.DMA((3, nx))])
    ids = jnp.broadcast_to(jnp.stack([lax.axis_index(a) for a in ("gx", "gy", "gz")])[:, None], (3, nz))
    crack_score = detector(pooled, edge, ids, weights + (b_first[None], b_second[None], b_third[None]), ny // 4, nz // 4)
    return (fraction, damage_field, flux_sum, crack_score)


CH = 16
CIN = 4
TOP = 8


def iota(shape, dim):
    return lax.broadcasted_iota(jnp.int32, shape, dim)


def lanes_for(n):
    return -(-n // 128) * 128


def one_hot(mask):
    return jnp.where(mask, 1.0, 0.0).astype(BF16)


def mm(a, b):
    return jnp.dot(a, b, preferred_element_type=F32)


def tile_shift(rb, cb, pz):
    z_in = rb * 16 // CIN
    z_in = z_in if z_in < pz + pz // 2 else z_in - 2 * pz
    return z_in - cb * 8 + 3


SHIFTS = tuple(k for k in range(-3, 10) if k % (16 // CIN) == 3)


def weight_kernel(w1_ref, w2_ref, w3_ref, b1_ref, b2_ref, b3_ref, plane_ref, t1_ref, t2_ref, t3_ref, bias_ref):
    n1 = bias_ref.shape[1]
    k1 = t1_ref.shape[1] // 3
    pz = k1 // (2 * CIN)
    spread = one_hot(iota((CH, 128), 1) % CH == iota((CH, 128), 0))
    tile1 = mm(w1_ref[...], spread)
    tile2 = mm(w2_ref[...], spread)
    tile3 = mm(w3_ref[...], one_hot(iota((3, 128), 1) // pz == iota((3, 128), 0)))
    step1 = iota((16, 128), 0) // CIN - iota((16, 128), 1) // CH
    step2 = -(iota((16, 128), 1) // CH)
    step3 = -(iota((16, 128), 1) % pz)

    def tile(source, base, stride, step, shift):
        out = jnp.zeros((16, 128), F32)
        for l in range(3):
            k = base + stride * l
            out = jnp.where(step + shift == l, source[16 * k:16 * k + 16], out)
        return out.astype(BF16)

    zero = jnp.zeros((16, 128), BF16)
    bias_ref[...] = jnp.broadcast_to(b3_ref[...], bias_ref.shape)
    for i in range(3):
        for j in range(3):
            tap = 9 * i + 3 * j
            known = {k: tile(tile1, tap, 1, step1, k) for k in SHIFTS}
            for rb in range(k1 // 16):
                for cb in range(n1 // 128):
                    t1_ref[i, j * k1 + rb * 16:j * k1 + rb * 16 + 16, cb * 128:(cb + 1) * 128] = known.get(
                        tile_shift(rb, cb, pz), zero)
            for rb in range(16):
                t2_ref[i, j * 256 + rb * 16:j * 256 + rb * 16 + 16, :] = (
                    tile(tile2, tap, 1, step2, rb) if rb < 10 else zero)
        for rb in range(t3_ref.shape[1] // 16):
            t3_ref[i, rb * 16:rb * 16 + 16, :] = tile(tile3, 3 * i, 1, step3, rb) if rb < pz + 2 else zero
    wide = one_hot(iota((CH, n1), 1) % CH == iota((CH, n1), 0)).astype(F32)
    for k, ref in ((0, b1_ref), (1, b2_ref)):
        bias_ref[k:k + 1, :] = jnp.dot(ref[...], wide, precision=lax.Precision.HIGHEST, preferred_element_type=F32)


def weight_rows(w_first, w_second, w_third):
    return (jnp.tile(jnp.swapaxes(w_first, 1, 2), (1, 16 // CIN, 1)).reshape(27 * 16, CH),
            jnp.swapaxes(w_second, 1, 2).reshape(27 * CH, CH),
            w_third.reshape(3, 3, 3, CH).transpose(0, 2, 3, 1).reshape(9 * CH, 3))


def gelu(x):
    return 0.5 * x * (1.0 + jnp.tanh(0.7978845608028654 * (x + 0.044715 * (x * x * x))))


def plane_kernel(py, y_count):
    def kernel(ids_ref, pool_ref, yr_ref, out_ref, scr_ref):
        iy = ids_ref[1:2, 0:1]
        scr_ref[...] = jnp.zeros(scr_ref.shape, F32)
        scr_ref[TOP:TOP + py, :] = pool_ref[0:py, :].astype(F32)
        below = yr_ref[1].astype(F32)[0:3]
        above = yr_ref[0].astype(F32)[0:3]
        scr_ref[TOP - 3:TOP, :] = jnp.where(iy > 0, below, 0.0)
        scr_ref[TOP + py:TOP + py + 3, :] = jnp.where(iy < y_count - 1, above, 0.0)
        out_ref[...] = scr_ref[...].astype(BF16)
    return kernel


def conv_kernel(py, counts, shifts):
    x_count, y_count, z_count = counts
    n = len(shifts)

    def kernel(*refs):
        ids_ref = refs[0]
        own = refs[1:2 + n]
        other = refs[2 + n:3 + 2 * n]
        t1_ref, t2_ref, t3_ref, bias_ref, out_ref = refs[3 + 2 * n:8 + 2 * n]
        in_ref, lhs1_ref, act1_ref, lhs2_ref, act2_ref, tail_ref = refs[8 + 2 * n:]
        ix, iy, iz = ids_ref[0:1, 0:1], ids_ref[1:2, 0:1], ids_ref[2:3, 0:1]
        half = own[0].shape[1]
        pz = half // CIN
        rows = py + 4
        z_row = iota((1, half), 1) // CIN
        z_ok = ((z_row < pz // 2) & (iz < z_count - 1)) | ((z_row >= pz // 2) & (iz > 0))
        for w in range(7):
            o = w - 3
            k = 0 if o == 0 else 1 + shifts.index((-o) % x_count) if (-o) % x_count in shifts else None
            if k is None:
                in_ref[w] = jnp.zeros(in_ref.shape[1:], F32)
                continue
            inside = (ix + o >= 0) & (ix + o < x_count)
            in_ref[w, :, 0:half] = jnp.where(inside, own[k][...].astype(F32), 0.0)
            in_ref[w, :, half:] = jnp.where(z_ok & inside, other[k][...].astype(F32), 0.0)
        k1 = 2 * half
        for w in range(7):
            for j in range(3):
                start = TOP - 3 + j
                lhs1_ref[w, :, j * k1:(j + 1) * k1] = in_ref[w, start:start + rows, :].astype(BF16)
        out = None
        for i in range(3):
            part = mm(lhs1_ref[i:i + 5].reshape(5 * rows, 3 * k1), t1_ref[i])
            out = part if out is None else out + part
        width = out.shape[1]
        y = iota((rows, width), 0) - 2
        z = iota((rows, width), 1) // CH - 2
        ok = (z < pz + 2) & ((y >= 0) | (iy > 0)) & ((y < py) | (iy < y_count - 1))
        ok = ok & ((z >= 0) | (iz > 0)) & ((z < pz) | (iz < z_count - 1))
        for p in range(5):
            a = gelu(out[p * rows:(p + 1) * rows] + bias_ref[0:1, :])
            good = ok & (ix + p - 2 >= 0) & (ix + p - 2 < x_count)
            act1_ref[p, 0:rows, 0:width] = jnp.where(good, a, 0.0)
            act1_ref[p, rows:, 0:width] = jnp.zeros((act1_ref.shape[1] - rows, width), F32)
            act1_ref[p, :, width:] = jnp.zeros((act1_ref.shape[1], act1_ref.shape[2] - width), F32)
        blocks = lhs2_ref.shape[1]
        for p in range(5):
            for j in range(3):
                a = act1_ref[p, j:j + rows, :].astype(BF16)
                for b in range(blocks):
                    lhs2_ref[p, b, :, j * 256:(j + 1) * 256] = a[:, b * 128:b * 128 + 256]
        out = None
        for i in range(3):
            part = mm(lhs2_ref[i:i + 3].reshape(3 * blocks * rows, 768), t2_ref[i])
            out = part if out is None else out + part
        for b in range(blocks):
            y = iota((rows, 128), 0) - 1
            z = (iota((rows, 128), 1) + b * 128) // CH - 1
            ok = (z < pz + 1) & (y <= py) & ((y >= 0) | (iy > 0)) & ((y < py) | (iy < y_count - 1))
            ok = ok & ((z >= 0) | (iz > 0)) & ((z < pz) | (iz < z_count - 1))
            for p in range(3):
                s = (p * blocks + b) * rows
                a = gelu(out[s:s + rows] + bias_ref[1:2, 0:128])
                good = ok & (ix + p - 1 >= 0) & (ix + p - 1 < x_count)
                act2_ref[p, :, b * 128:(b + 1) * 128] = jnp.where(good, a, 0.0).astype(BF16)
        out = None
        for i in range(3):
            part = mm(act2_ref[i], t3_ref[i])
            out = part if out is None else out + part
        tail_ref[0:rows, :] = out
        score = tail_ref[0:py, :]
        for j in (1, 2):
            score = score + pltpu.roll(tail_ref[j:j + py, :], 128 - j * pz, 1)
        out_ref[0] = jnp.transpose(score)[0:pz, :] + bias_ref[2:3, 0:1]
    return kernel


def detector(pooled, edge, ids, weights, py, pz):
    counts = tuple(lax.axis_size(a) for a in ("gx", "gy", "gz"))
    half = pooled.shape[1]
    assert half == 128 and pz * CIN == half and pz * 3 <= 128
    rows = py + 4
    width = lanes_for((pz + 4) * CH)
    blocks = width // 128
    yr = both_sides(edge, "gy")
    tall = -(-(TOP + py + 3) // 16) * 16
    (plane,) = call(
        plane_kernel(py, counts[1]), [((tall, half), BF16)], ids, pooled, yr,
        scratch=[pltpu.VMEM((tall, half), F32)])
    shifts = []
    for s in (1, -1, 2, -2, 3, -3):
        if s % counts[0] and s % counts[0] not in shifts:
            shifts.append(s % counts[0])
    own = [plane] + [lax.ppermute(plane, "gx", ring("gx", s)) for s in shifts]
    matrices = call(
        weight_kernel,
        [((3, 6 * half, width), BF16), ((3, 768, 128), BF16), ((3, width, 128), BF16), ((8, width), F32)],
        *weights, plane)
    own[1], *matrices = lax.optimization_barrier((own[1], *matrices))
    other = [z_neighbour(v, "gz", False) for v in own]
    args = (ids, *own, *other, *matrices)
    (score,) = call(
        conv_kernel(py, counts, shifts), [((1, pz, py), F32)], *args,
        scratch=[
            pltpu.VMEM((7, tall, 2 * half), F32),
            pltpu.VMEM((7, rows, 6 * half), BF16),
            pltpu.VMEM((5, rows + 8, width + 128), F32),
            pltpu.VMEM((5, blocks, rows, 768), BF16),
            pltpu.VMEM((3, rows, width), BF16),
            pltpu.VMEM((rows + 8, 128), F32),
        ], mib=32)
    return jnp.swapaxes(score, 1, 2)


def solution(mesh):
    slab = P(("groups", "gx"), "gy", "gz")
    return jax.shard_map(
        body,
        mesh=mesh,
        in_specs=(slab, slab, slab, P(), P(), P(), P(), P(), P()),
        out_specs=(slab, slab, slab, slab),
        check_vma=False,
    )
```

```python
import functools

import jax
import jax.numpy as jnp
import numpy as np
from jax import lax
from jax.experimental import pallas as pl
from jax.experimental.pallas import tpu as pltpu
from jax.sharding import PartitionSpec as P

F32 = jnp.float32
BF16 = jnp.bfloat16
I16 = jnp.int16
WELL_HEIGHT = 1.0
STRAIN_COUPLING = 4.0
TIME_STEP = 0.01
DAMAGE_RATE = 0.8
ENERGY_CRITICAL = 0.02

OFF = 16
A_CODE = (0.0, 1.0)
B_CODE = (-1.1, 3.1)
SUM_LOW, SUM_SPAN = -1280.0, 4096.0

VMEM = pl.BlockSpec(memory_space=pltpu.VMEM)
HBM = pl.BlockSpec(memory_space=pltpu.HBM)


def to_code(x, code):
    low, span = code
    v = (x - low) * (65535.0 / span) - 32768.0
    return jnp.clip(jnp.round(v), -32768.0, 32767.0).astype(jnp.int32).astype(I16)


def from_code(q, code):
    low, span = code
    return q.astype(jnp.int32).astype(F32) * (span / 65535.0) + (low + 32768.0 * span / 65535.0)


def sum_digits(s):
    v = (s[0:2] - SUM_LOW) * (65536.0 / SUM_SPAN)
    high = jnp.floor(v)
    low = jnp.minimum(jnp.floor((v - high) * 65536.0), 65535.0)
    rows = jnp.concatenate([high, low, jnp.full((12, s.shape[1]), 32768.0, F32)]) - 32768.0
    return rows.astype(jnp.int32).astype(I16)


def from_digits(tile):
    v = tile.astype(jnp.int32).astype(F32) + 32768.0
    return (v[0:2] + v[2:4] * (1.0 / 65536.0)) * (SUM_SPAN / 65536.0) + SUM_LOW


def each(count, looped, body):
    def step(i, carry):
        body(i)
        return carry
    if looped:
        lax.fori_loop(0, count, step, 0)
    else:
        for i in range(count):
            body(i)


def by_label(labels, values):
    return jnp.where(labels == 0, values[0], jnp.where(labels == 1, values[1], values[2])).astype(F32)


FACTORS = (1.0, 0.3, 0.05)
ROOTS = tuple(float(np.sqrt(np.float32(v))) for v in FACTORS)


def call(kernel, outs, *args, in_specs=None, out_specs=None, scratch=(), mib=16):
    return pl.pallas_call(
        kernel,
        in_specs=in_specs or [VMEM] * len(args),
        out_specs=out_specs or [VMEM] * len(outs),
        out_shape=[jax.ShapeDtypeStruct(s, t) for s, t in outs],
        scratch_shapes=scratch,
        compiler_params=pltpu.CompilerParams(vmem_limit_bytes=mib * 1024 * 1024),
    )(*args)


def chunks(start, stop, size):
    return [(r, min(size, stop - r)) for r in range(start, stop, size)]


def fold(x):
    return x.reshape(x.shape[0] // 8, 8, x.shape[1]).sum(0)


def to_rows(top, bottom):
    return jnp.concatenate([jnp.sum(top, 0, keepdims=True), jnp.sum(bottom, 0, keepdims=True),
                            jnp.zeros((6, top.shape[1]), F32)])


def first_kernel(c_hbm, d_hbm, l_hbm, f_ref, amp_ref, lo_ref, hi_ref, sum_ref, le_ref, d_ref, l_ref, sems):
    nx, ny, nz = f_ref.shape
    order = [0, nx - 1] + list(range(1, nx - 1))
    copies = []
    for x in order:
        copies.append([pltpu.make_async_copy(src.at[x], dst.at[x], sems.at[k, x])
                       for k, (src, dst) in enumerate(((c_hbm, f_ref), (d_hbm, d_ref), (l_hbm, l_ref)))])
        for c in copies[-1]:
            c.start()
    top = jnp.zeros((8, nz), F32)
    bottom = jnp.zeros((8, nz), F32)
    for k, x in enumerate(order):
        for c in copies[k]:
            c.wait()
        le_ref[x, 0:16, :] = l_ref[x, 0:16, :]
        le_ref[x, 16:32, :] = l_ref[x, ny - 16:ny, :]
        for r, n in chunks(0, ny, 48):
            f = f_ref[x, r:r + n, :]
            a = by_label(l_ref[x, r:r + n, :], ROOTS) * (1.0 - d_ref[x, r:r + n, :])
            amp_ref[x, r:r + n, :] = a
            m = a * a
            top = top + fold(m * f)
            bottom = bottom + fold(m)
            for near, far, out in ((0, 1, lo_ref), (nx - 1, nx - 2, hi_ref)):
                if x == near:
                    out[r:r + n, :] = to_code(f, A_CODE)
                    out[2 * ny + r:2 * ny + r + n, :] = to_code(a, A_CODE)
                if x == far:
                    out[ny + r:ny + r + n, :] = to_code(f, A_CODE)
    s = to_rows(top, bottom)
    sum_ref[...] = s
    lo_ref[3 * ny:3 * ny + 16, :] = sum_digits(s)
    hi_ref[3 * ny:3 * ny + 16, :] = sum_digits(s)


def edge_rows(code, ride_x, with_amp):
    def kernel(*refs):
        f_ref = refs[0]
        amp_ref = refs[1] if with_amp else None
        lo_ref, hi_ref, s_ref, far_ref = refs[1 + with_amp:5 + with_amp]
        out_ref = refs[-1]
        nx, ny, nz = f_ref.shape
        low_rows = [from_code(r[0:16, :], code)[0:1] for r in (lo_ref, hi_ref)]
        high_rows = [from_code(r[ny - 16:ny, :], code)[15:16] for r in (lo_ref, hi_ref)]
        s = s_ref[...]
        if ride_x:
            s = s + far_ref[...]
        for side, first, second, beside in ((0, 0, 1, low_rows), (1, ny - 1, ny - 2, high_rows)):
            for x in range(nx):
                out_ref[side, 2 * x:2 * x + 1, :] = f_ref[x, first:first + 1, :]
                out_ref[side, 2 * x + 1:2 * x + 2, :] = f_ref[x, second:second + 1, :]
                if amp_ref is not None:
                    out_ref[side, 10 + x:11 + x, :] = amp_ref[x, first:first + 1, :]
            out_ref[side, 8:9, :] = beside[0]
            out_ref[side, 9:10, :] = beside[1]
            out_ref[side, 16:24, :] = s
            if ride_x:
                out_ref[side, 16:18, :] = (s[0:2] + from_digits(lo_ref[lo_ref.shape[0] - 16:, :])
                                           + from_digits(hi_ref[hi_ref.shape[0] - 16:, :]))
    return kernel


def group(lane, j, nz, first, count):
    return (lane - (32 * j + first)) % nz < count


def pack_z(code, ride_y, with_amp):
    def kernel(*refs):
        f_ref = refs[0]
        amp_ref = refs[1] if with_amp else None
        lo_ref, hi_ref, yr_ref, yp_ref, out_ref = refs[1 + with_amp:]
        nx, ny, nz = f_ref.shape
        end = OFF + ny
        lane = lax.broadcasted_iota(jnp.int32, (1, nz), 1)
        for k in range(out_ref.shape[0]):
            planes = [p for p in range(4 * k, 4 * k + 4) if p < nx + 2]

            def packed(f_of, a_of, ps):
                out = None
                for p in ps:
                    j = p % 4
                    f = f_of(p)
                    f = pltpu.roll(f, 32 * j, 1) if j else f
                    out = f if out is None else jnp.where(group(lane, j, nz, -2, 4), f, out)
                    a = a_of(p)
                    if a is not None:
                        out = jnp.where(group(lane, j, nz, 15, 2), pltpu.roll(a, 32 * j + 16, 1), out)
                return out

            for r, n in chunks(0, ny, 48):
                def f_of(p):
                    if p == 0:
                        return from_code(lo_ref[r:r + n, :], code)
                    if p == nx + 1:
                        return from_code(hi_ref[r:r + n, :], code)
                    return f_ref[p - 1, r:r + n, :]

                def a_of(p):
                    return amp_ref[p - 1, r:r + n, :] if with_amp and 1 <= p <= nx else None

                out_ref[k, OFF + r:OFF + r + n, :] = packed(f_of, a_of, planes)
            inner = [p for p in planes if 1 <= p <= nx]
            if inner:
                for side, near in ((1, OFF - 1), (0, end)):
                    out_ref[k, near:near + 1, :] = packed(
                        lambda p: yr_ref[side, 2 * (p - 1):2 * (p - 1) + 1, :], lambda p: None, inner)
        s = yp_ref[0, 16:24, :]
        out_ref[0, 0:8, :] = s + yr_ref[0, 16:24, :] if ride_y else s
    return kernel


def spread(spans, extra, size):
    return [v for a, b in spans for v in chunks(OFF + a - extra, OFF + b + extra, size)]


def fill(code, f_ref, lo_ref, hi_ref, yr_ref, zr_ref, pad_ref, ze_ref, spans):
    nx, ny, nz = f_ref.shape
    end = OFF + ny
    wide = [v for a, b in spans for v in chunks(max(a - 16, 0), min(b + 16, ny), 48)]
    for near, far, ref in ((1, 0, lo_ref), (nx + 2, nx + 3, hi_ref)):
        for r, n in wide:
            pad_ref[near, OFF + r:OFF + r + n, :] = from_code(ref[r:r + n, :], code)
            pad_ref[far, OFF + r:OFF + r + n, :] = from_code(ref[ny + r:ny + r + n, :], code)
    for p, k in ((1, 8), (nx + 2, 9)):
        pad_ref[p, OFF - 1:OFF, :] = yr_ref[1, k:k + 1, :]
        pad_ref[p, end:end + 1, :] = yr_ref[0, k:k + 1, :]
    for x in range(nx):
        for r, n in wide:
            pad_ref[x + 2, OFF + r:OFF + r + n, :] = f_ref[x, r:r + n, :]
        for side, near, far in ((1, OFF - 1, OFF - 2), (0, end, end + 1)):
            pad_ref[x + 2, near:near + 1, :] = yr_ref[side, 2 * x:2 * x + 1, :]
            pad_ref[x + 2, far:far + 1, :] = yr_ref[side, 2 * x + 1:2 * x + 2, :]
    for p in range(nx + 2):
        for r, n in spread(spans, 8, 32):
            e = zr_ref[p // 4, r:r + n, :]
            ze_ref[p, r:r + n, :] = pltpu.roll(e, nz - 32 * (p % 4), 1) if p % 4 else e


def weighted_mean(yp_ref, yr_ref, zr_ref, ride_y, ride_z):
    s = yp_ref[0, 16:24, :]
    if ride_y:
        s = s + yr_ref[0, 16:24, :]
    if ride_z:
        s = s + zr_ref[0, 0:8, :]
    return jnp.sum(s[0:1], keepdims=True) / jnp.sum(s[1:2], keepdims=True)


def worn(a, m, f, mean):
    e = f - mean
    loss = DAMAGE_RATE * 0.5 * STRAIN_COUPLING * (m * (e * e)) - DAMAGE_RATE * ENERGY_CRITICAL
    return a * (1.0 - jnp.maximum(loss, 0.0))


class Geometry:
    def __init__(self, nx, ny, nz):
        self.nx, self.ny, self.nz = nx, ny, nz
        self.lane = lax.broadcasted_iota(jnp.int32, (1, nz), 1)
        self.first = self.lane == 0
        self.last = self.lane == nz - 1

    def before(self, own, other):
        return pltpu.roll(jnp.where(self.last, other, own), 1, 1)

    def after(self, own, other):
        return pltpu.roll(jnp.where(self.first, other, own), self.nz - 1, 1)


def chem_of(f, m, around, mean):
    w = 2.0 * WELL_HEIGHT
    return ((2.0 * w * f - 3.0 * w) * f + (w + 6.0)) * f - around + STRAIN_COUPLING * (m * (f - mean))


def chemistry(g, pad_ref, mob_ref, mobe_ref, ze_ref, chem_ref, cheme_ref, mean, spans, looped=False):
    nx = g.nx

    @functools.partial(each, nx + 2, looped)
    def _(p):
        for r, n in spread(spans, 0, 48) if not looped and p in (0, nx + 1) else spread(spans, 8, 32):
            f = pad_ref[p + 1, r:r + n, :]
            e = ze_ref[p, r:r + n, :]
            around = (pad_ref[p, r:r + n, :] + pad_ref[p + 2, r:r + n, :]
                      + pad_ref[p + 1, r - 1:r - 1 + n, :] + pad_ref[p + 1, r + 1:r + 1 + n, :]
                      + g.before(f, e) + g.after(f, e))
            chem_ref[p, r:r + n, :] = chem_of(f, mob_ref[p, r:r + n, :], around, mean)

    @functools.partial(each, nx, looped)
    def _(x):
        p = x + 1
        for r, n in spread(spans, 0, 48):
            f = pad_ref[p + 1, r:r + n, :]
            e = ze_ref[p, r:r + n, :]
            around = (ze_ref[p - 1, r:r + n, :] + ze_ref[p + 1, r:r + n, :]
                      + ze_ref[p, r - 1:r - 1 + n, :] + ze_ref[p, r + 1:r + 1 + n, :]
                      + g.before(e, f) + g.after(e, f))
            cheme_ref[x, r - OFF:r - OFF + n, :] = chem_of(
                e, mobe_ref[x, r - OFF:r - OFF + n, :], around, mean)


def flux_of(g, x, r, n, mob_ref, mobe_ref, chem_ref, cheme_ref):
    p = x + 1
    m = mob_ref[p, r:r + n, :]
    q = chem_ref[p, r:r + n, :]
    me = mobe_ref[x, r - OFF:r - OFF + n, :]
    qe = cheme_ref[x, r - OFF:r - OFF + n, :]
    total = None
    for nm, nq in (
        (mob_ref[p - 1, r:r + n, :], chem_ref[p - 1, r:r + n, :]),
        (mob_ref[p + 1, r:r + n, :], chem_ref[p + 1, r:r + n, :]),
        (mob_ref[p, r - 1:r - 1 + n, :], chem_ref[p, r - 1:r - 1 + n, :]),
        (mob_ref[p, r + 1:r + 1 + n, :], chem_ref[p, r + 1:r + 1 + n, :]),
        (g.before(m, me), g.before(q, qe)),
        (g.after(m, me), g.after(q, qe)),
    ):
        term = (nm + m) * (nq - q)
        total = term if total is None else total + term
    return m, 0.5 * total


def pack_edges(values, lane, nz):
    out = values[0]
    for x, v in enumerate(values[1:], 1):
        out = jnp.where(group(lane, x, nz, -1, 2), pltpu.roll(v, 32 * x, 1), out)
    return out


def step_a(ride_y, ride_z):
    def kernel(f_ref, amp_ref, lo_ref, hi_ref, yr_ref, zr_ref, yp_ref,
               f2_ref, a2_ref, ae2_ref, lo_out, hi_out, sum_ref,
               pad_ref, ze_ref, mob_ref, mobe_ref, chem_ref, cheme_ref):
        nx, ny, nz = f2_ref.shape
        end = OFF + ny
        g = Geometry(nx, ny, nz)
        mean = weighted_mean(yp_ref, yr_ref, zr_ref, ride_y, ride_z)
        fill(A_CODE, f_ref, lo_ref, hi_ref, yr_ref, zr_ref, pad_ref, ze_ref, [(0, ny)])

        def wear(p, r, n, a):
            m = a * a
            mob_ref[p, r:r + n, :] = m
            a2_ref[p, r:r + n, :] = worn(a, m, pad_ref[p + 1, r:r + n, :], mean)

        for r, n in chunks(0, ny, 48):
            wear(0, OFF + r, n, from_code(lo_ref[2 * ny + r:2 * ny + r + n, :], A_CODE))
            wear(nx + 1, OFF + r, n, from_code(hi_ref[2 * ny + r:2 * ny + r + n, :], A_CODE))
            edges = []
            for x in range(nx):
                wear(x + 1, OFF + r, n, amp_ref[x, r:r + n, :])
                p = x + 1
                a = pltpu.roll(zr_ref[p // 4, OFF + r:OFF + r + n, :], nz - 32 * (p % 4) - 16, 1)
                m = a * a
                mobe_ref[x, r:r + n, :] = m
                edges.append(worn(a, m, ze_ref[p, OFF + r:OFF + r + n, :], mean))
            ae2_ref[r:r + n, :] = pack_edges(edges, g.lane, nz)
        for x in range(nx):
            wear(x + 1, OFF - 1, 1, yr_ref[1, 10 + x:11 + x, :])
            wear(x + 1, end, 1, yr_ref[0, 10 + x:11 + x, :])
        chemistry(g, pad_ref, mob_ref, mobe_ref, ze_ref, chem_ref, cheme_ref, mean, [(0, ny)])
        top = jnp.zeros((8, nz), F32)
        bottom = jnp.zeros((8, nz), F32)
        for x in range(nx):
            for r, n in chunks(OFF, end, 48):
                _, flux = flux_of(g, x, r, n, mob_ref, mobe_ref, chem_ref, cheme_ref)
                f = pad_ref[x + 2, r:r + n, :] + TIME_STEP * flux
                s = slice(r - OFF, r - OFF + n)
                f2_ref[x, s, :] = f
                a = a2_ref[x + 1, r:r + n, :]
                m = a * a
                top = top + fold(m * f)
                bottom = bottom + fold(m)
                for near, far, out in ((0, 1, lo_out), (nx - 1, nx - 2, hi_out)):
                    if x == near:
                        out[s, :] = to_code(f, B_CODE)
                    if x == far:
                        out[r - OFF + ny:r - OFF + ny + n, :] = to_code(f, B_CODE)
        s = to_rows(top, bottom)
        sum_ref[...] = s
        lo_out[2 * ny:2 * ny + 16, :] = sum_digits(s)
        hi_out[2 * ny:2 * ny + 16, :] = sum_digits(s)
    return kernel


def potentials_b(g, mean, a2_ref, ae2_ref, others, scratch, spans, looped):
    f_ref, lo_ref, hi_ref, yr_ref, zr_ref = others
    pad_ref, ze_ref, mob_ref, mobe_ref, chem_ref, cheme_ref = scratch
    nx, nz = g.nx, g.nz
    fill(B_CODE, f_ref, lo_ref, hi_ref, yr_ref, zr_ref, pad_ref, ze_ref, spans)

    @functools.partial(each, nx + 2, looped)
    def _(p):
        for r, n in spread(spans, 8, 32):
            a = a2_ref[p, r:r + n, :]
            mob_ref[p, r:r + n, :] = a * a

    for r, n in spread(spans, 0, 48):
        a = ae2_ref[r - OFF:r - OFF + n, :]
        a = a * a
        for x in range(nx):
            mobe_ref[x, r - OFF:r - OFF + n, :] = pltpu.roll(a, nz - 32 * x, 1) if x else a
    chemistry(g, pad_ref, mob_ref, mobe_ref, ze_ref, chem_ref, cheme_ref, mean, spans, looped)


def finish_b(g, mean, x, r, n, labels, a2_ref, scratch):
    pad_ref, ze_ref, mob_ref, mobe_ref, chem_ref, cheme_ref = scratch
    m, flux = flux_of(g, x, r, n, mob_ref, mobe_ref, chem_ref, cheme_ref)
    f0 = pad_ref[x + 2, r:r + n, :]
    f = f0 + TIME_STEP * flux
    a = worn(a2_ref[x + 1, r:r + n, :], m, f0, mean)
    dmg = 1.0 - a * by_label(labels, tuple(1.0 / v for v in ROOTS))
    return flux, (f, dmg, a * a, by_label(labels, FACTORS))


def pool_rows(scr_ref, count, nz):
    zin = lax.broadcasted_iota(jnp.int32, (nz, nz), 0)
    out = lax.broadcasted_iota(jnp.int32, (nz, nz), 1)
    total = jnp.zeros((count, nz), F32)
    for i in range(4):
        rows = (scr_ref[i, pl.ds(0, count, stride=4), :] + scr_ref[i, pl.ds(1, count, stride=4), :]
                + scr_ref[i, pl.ds(2, count, stride=4), :] + scr_ref[i, pl.ds(3, count, stride=4), :])
        pick = jnp.where((zin // 4 == out // 4) & (out % 4 == i), 1.0 / 64.0, 0.0).astype(F32)
        total = total + jnp.dot(rows, pick, precision=lax.Precision.HIGHEST, preferred_element_type=F32)
    return total


def edge_b(ride_y, ride_z):
    def kernel(f_ref, a2_ref, ae2_ref, lo_ref, hi_ref, yr_ref, zr_ref, yp_ref, l_ref, edge_ref, *rest):
        *scratch, pool_scr = rest
        nx, ny, nz = f_ref.shape
        spans = [(0, 16), (ny - 16, ny)]
        g = Geometry(nx, ny, nz)
        mean = weighted_mean(yp_ref, yr_ref, zr_ref, ride_y, ride_z)
        potentials_b(g, mean, a2_ref, ae2_ref, (f_ref, lo_ref, hi_ref, yr_ref, zr_ref), scratch, spans, False)
        for k, (a, b) in enumerate(spans):
            s = slice(16 * k, 16 * k + 16)
            pooled = [None] * 4
            for x in range(nx):
                _, values = finish_b(g, mean, x, OFF + a, 16, l_ref[x, s, :], a2_ref, scratch)
                pooled = [v if p is None else p + v for p, v in zip(pooled, values)]
            for i in range(4):
                pool_scr[i, s, :] = pooled[i]
        total = pool_rows(pool_scr, 8, nz)
        blank = jnp.zeros((13, nz), F32)
        edge_ref[0] = jnp.concatenate([total[0:3], blank]).astype(BF16)
        edge_ref[1] = jnp.concatenate([total[5:8], blank]).astype(BF16)
    return kernel


def step_b(ride_y, ride_z):
    def kernel(f_ref, a2_ref, ae2_ref, lo_ref, hi_ref, yr_ref, zr_ref, yp_ref, l_hbm,
               f3_hbm, dmg_hbm, flux_hbm, pool_ref, *rest):
        *scratch, pool_scr, l_ref, f3_ref, dmg_ref, flux_ref, l_sem, sems = rest
        nx, ny, nz = f_ref.shape
        labels_in = pltpu.make_async_copy(l_hbm, l_ref, l_sem)
        labels_in.start()
        g = Geometry(nx, ny, nz)
        mean = weighted_mean(yp_ref, yr_ref, zr_ref, ride_y, ride_z)
        potentials_b(g, mean, a2_ref, ae2_ref, (f_ref, lo_ref, hi_ref, yr_ref, zr_ref), scratch, [(0, ny)], True)
        labels_in.wait()
        outs = ((f3_ref, f3_hbm), (dmg_ref, dmg_hbm), (flux_ref, flux_hbm))

        def out_copy(i, x):
            return pltpu.make_async_copy(outs[i][0].at[x], outs[i][1].at[x], sems.at[i, x])

        pool_scr[...] = jnp.zeros(pool_scr.shape, F32)

        @functools.partial(each, nx, True)
        def _(x):
            for r, n in chunks(OFF, OFF + ny, 48):
                s = slice(r - OFF, r - OFF + n)
                flux, values = finish_b(g, mean, x, r, n, l_ref[x, s, :], a2_ref, scratch)
                f3_ref[x, s, :] = values[0]
                dmg_ref[x, s, :] = values[1]
                flux_ref[x, s, :] = flux
                for i in range(4):
                    pool_scr[i, s, :] = pool_scr[i, s, :] + values[i]
            for i in range(3):
                out_copy(i, x).start()

        pool_ref[...] = pool_rows(pool_scr, ny // 4, nz).astype(BF16)
        for x in range(nx):
            for i in range(3):
                out_copy(i, x).wait()
    return kernel


def ring(axis, shift):
    count = lax.axis_size(axis)
    return [(i, (i + shift) % count) for i in range(count)]


def pair_sum(s, axis):
    count = lax.axis_size(axis)
    if count & (count - 1):
        return lax.psum(s, axis)
    bit = 1
    while bit < count:
        s = s + lax.ppermute(s, axis, [(i, i ^ bit) for i in range(count)])
        bit *= 2
    return s


def both_sides(pay, axis):
    if lax.axis_size(axis) == 2:
        return lax.ppermute(pay, axis, ring(axis, 1))
    return jnp.stack([lax.ppermute(pay[0], axis, ring(axis, -1)), lax.ppermute(pay[1], axis, ring(axis, 1))])


def z_neighbour(pay, axis, packed=True):
    if lax.axis_size(axis) == 2:
        return lax.ppermute(pay, axis, ring(axis, 1))
    above = lax.ppermute(pay, axis, ring(axis, -1))
    below = lax.ppermute(pay, axis, ring(axis, 1))
    lane = lax.broadcasted_iota(jnp.int32, pay.shape, pay.ndim - 1)
    if packed:
        low = (lane % 32 < 8) | (lane % 32 == 16)
    else:
        low = lane < pay.shape[-1] // 2
    return jnp.where(low, above, below)


def x_sides(lo, hi):
    return lax.ppermute(hi, "gx", ring("gx", 1)), lax.ppermute(lo, "gx", ring("gx", -1))


def body(concentration, damage, labels, w_first, b_first, w_second, b_second, w_third, b_third):
    nx, ny, nz = concentration.shape
    rows = ny + 2 * OFF
    block = (nx, ny, nz)
    padded = (nx + 2, rows, nz)
    ride_x = lax.axis_size("gx") == 4
    ride_y = lax.axis_size("gy") == 2
    ride_z = lax.axis_size("gz") == 2
    packed = (-(-(nx + 2) // 4), rows, nz)
    assert nz == 128
    scratch = [pltpu.VMEM((nx + 4, rows, nz), F32), pltpu.VMEM(padded, F32), pltpu.VMEM(padded, F32),
               pltpu.VMEM(block, F32), pltpu.VMEM(padded, F32), pltpu.VMEM(block, F32)]

    def start(sums):
        if ride_x:
            return sums, lax.ppermute(sums, "gx", ring("gx", 2))
        sums = pair_sum(sums, "gx")
        for axis, ride in (("gy", ride_y), ("gz", ride_z)):
            if not ride:
                sums = pair_sum(sums, axis)
        return sums, sums

    concentration, damage, labels = (
        pltpu.with_memory_space_constraint(v, pltpu.HBM) for v in (concentration, damage, labels))
    tall = 3 * ny + 16
    f, amp, lo, hi, sums, edge_labels = call(
        first_kernel,
        [(block, F32), (block, F32), ((tall, nz), I16), ((tall, nz), I16), ((8, nz), F32),
         ((nx, 32, nz), jnp.int32)],
        concentration, damage, labels,
        in_specs=[HBM] * 3,
        scratch=[pltpu.VMEM(block, F32), pltpu.VMEM(block, jnp.int32), pltpu.SemaphoreType.DMA((3, nx))])
    weights = weight_rows(w_first, w_second, w_third)
    sums, far = start(sums)
    lo, hi = x_sides(lo, hi)
    (ypay,) = call(edge_rows(A_CODE, ride_x, True), [((2, 24, nz), F32)], f, amp, lo, hi, sums, far, *weights)
    yr = both_sides(ypay, "gy")
    (zpay,) = call(pack_z(A_CODE, ride_y, True), [(packed, F32)], f, amp, lo, hi, yr, ypay)
    zr = z_neighbour(zpay, "gz")
    tall = 2 * ny + 16
    f, a2, ae2, lo, hi, sums = call(
        step_a(ride_y, ride_z),
        [(block, F32), (padded, F32), ((ny, nz), F32), ((tall, nz), I16), ((tall, nz), I16), ((8, nz), F32)],
        f, amp, lo, hi, yr, zr, ypay, scratch=scratch)

    sums, far = start(sums)
    lo, hi = x_sides(lo, hi)
    (ypay,) = call(edge_rows(B_CODE, ride_x, False), [((2, 24, nz), F32)], f, lo, hi, sums, far)
    yr = both_sides(ypay, "gy")
    (zpay,) = call(pack_z(B_CODE, ride_y, False), [(packed, F32)], f, lo, hi, yr, ypay)
    zr = z_neighbour(zpay, "gz")
    last = (f, a2, ae2, lo, hi, yr, zr, ypay)
    (edge,) = call(
        edge_b(ride_y, ride_z), [((2, 16, nz), BF16)], *last, edge_labels,
        scratch=scratch + [pltpu.VMEM((4, 32, nz), F32)])
    fraction, damage_field, flux_sum, pooled = call(
        step_b(ride_y, ride_z),
        [(block, F32), (block, F32), (block, F32), ((ny // 4, nz), BF16)], *last, labels,
        in_specs=[VMEM] * 8 + [HBM], out_specs=[HBM] * 3 + [VMEM],
        scratch=scratch + [
            pltpu.VMEM((4, ny, nz), F32), pltpu.VMEM(block, jnp.int32),
            pltpu.VMEM(block, F32), pltpu.VMEM(block, F32), pltpu.VMEM(block, F32),
            pltpu.SemaphoreType.DMA, pltpu.SemaphoreType.DMA((3, nx))])
    ids = jnp.broadcast_to(jnp.stack([lax.axis_index(a) for a in ("gx", "gy", "gz")])[:, None], (3, nz))
    crack_score = detector(pooled, edge, ids, weights + (b_first[None], b_second[None], b_third[None]), ny // 4, nz // 4)
    return (fraction, damage_field, flux_sum, crack_score)


CH = 16
CIN = 4
TOP = 8


def iota(shape, dim):
    return lax.broadcasted_iota(jnp.int32, shape, dim)


def lanes_for(n):
    return -(-n // 128) * 128


def one_hot(mask):
    return jnp.where(mask, 1.0, 0.0).astype(BF16)


def mm(a, b):
    return jnp.dot(a, b, preferred_element_type=F32)


def tile_shift(rb, cb, pz):
    z_in = rb * 16 // CIN
    z_in = z_in if z_in < pz + pz // 2 else z_in - 2 * pz
    return z_in - cb * 8 + 3


SHIFTS = tuple(k for k in range(-3, 10) if k % (16 // CIN) == 3)


def weight_kernel(w1_ref, w2_ref, w3_ref, b1_ref, b2_ref, b3_ref, plane_ref, t1_ref, t2_ref, t3_ref, bias_ref):
    n1 = bias_ref.shape[1]
    k1 = t1_ref.shape[1] // 3
    pz = k1 // (2 * CIN)
    spread = one_hot(iota((CH, 128), 1) % CH == iota((CH, 128), 0))
    tile1 = mm(w1_ref[...], spread)
    tile2 = mm(w2_ref[...], spread)
    tile3 = mm(w3_ref[...], one_hot(iota((3, 128), 1) // pz == iota((3, 128), 0)))
    step1 = iota((16, 128), 0) // CIN - iota((16, 128), 1) // CH
    step2 = -(iota((16, 128), 1) // CH)
    step3 = -(iota((16, 128), 1) % pz)

    def tile(source, base, stride, step, shift):
        out = jnp.zeros((16, 128), F32)
        for l in range(3):
            k = base + stride * l
            out = jnp.where(step + shift == l, source[16 * k:16 * k + 16], out)
        return out.astype(BF16)

    zero = jnp.zeros((16, 128), BF16)
    bias_ref[...] = jnp.broadcast_to(b3_ref[...], bias_ref.shape)
    for i in range(3):
        for j in range(3):
            tap = 9 * i + 3 * j
            known = {k: tile(tile1, tap, 1, step1, k) for k in SHIFTS}
            for rb in range(k1 // 16):
                for cb in range(n1 // 128):
                    t1_ref[i, j * k1 + rb * 16:j * k1 + rb * 16 + 16, cb * 128:(cb + 1) * 128] = known.get(
                        tile_shift(rb, cb, pz), zero)
            for rb in range(16):
                t2_ref[i, j * 256 + rb * 16:j * 256 + rb * 16 + 16, :] = (
                    tile(tile2, tap, 1, step2, rb) if rb < 10 else zero)
        for rb in range(t3_ref.shape[1] // 16):
            t3_ref[i, rb * 16:rb * 16 + 16, :] = tile(tile3, 3 * i, 1, step3, rb) if rb < pz + 2 else zero
    wide = one_hot(iota((CH, n1), 1) % CH == iota((CH, n1), 0)).astype(F32)
    for k, ref in ((0, b1_ref), (1, b2_ref)):
        bias_ref[k:k + 1, :] = jnp.dot(ref[...], wide, precision=lax.Precision.HIGHEST, preferred_element_type=F32)


def weight_rows(w_first, w_second, w_third):
    return (jnp.tile(jnp.swapaxes(w_first, 1, 2), (1, 16 // CIN, 1)).reshape(27 * 16, CH),
            jnp.swapaxes(w_second, 1, 2).reshape(27 * CH, CH),
            w_third.reshape(3, 3, 3, CH).transpose(0, 2, 3, 1).reshape(9 * CH, 3))


def gelu(x):
    return 0.5 * x * (1.0 + jnp.tanh(0.7978845608028654 * (x + 0.044715 * (x * x * x))))


def plane_kernel(py, y_count):
    def kernel(ids_ref, pool_ref, yr_ref, out_ref, scr_ref):
        iy = ids_ref[1:2, 0:1]
        scr_ref[...] = jnp.zeros(scr_ref.shape, F32)
        scr_ref[TOP:TOP + py, :] = pool_ref[0:py, :].astype(F32)
        below = yr_ref[1].astype(F32)[0:3]
        above = yr_ref[0].astype(F32)[0:3]
        scr_ref[TOP - 3:TOP, :] = jnp.where(iy > 0, below, 0.0)
        scr_ref[TOP + py:TOP + py + 3, :] = jnp.where(iy < y_count - 1, above, 0.0)
        out_ref[...] = scr_ref[...].astype(BF16)
    return kernel


def conv_kernel(py, counts, shifts):
    x_count, y_count, z_count = counts
    n = len(shifts)

    def kernel(*refs):
        ids_ref = refs[0]
        own = refs[1:2 + n]
        other = refs[2 + n:3 + 2 * n]
        t1_ref, t2_ref, t3_ref, bias_ref, out_ref = refs[3 + 2 * n:8 + 2 * n]
        in_ref, lhs1_ref, act1_ref, lhs2_ref, act2_ref, tail_ref = refs[8 + 2 * n:]
        ix, iy, iz = ids_ref[0:1, 0:1], ids_ref[1:2, 0:1], ids_ref[2:3, 0:1]
        half = own[0].shape[1]
        pz = half // CIN
        rows = py + 4
        z_row = iota((1, half), 1) // CIN
        z_ok = ((z_row < pz // 2) & (iz < z_count - 1)) | ((z_row >= pz // 2) & (iz > 0))
        for w in range(7):
            o = w - 3
            k = 0 if o == 0 else 1 + shifts.index((-o) % x_count) if (-o) % x_count in shifts else None
            if k is None:
                in_ref[w] = jnp.zeros(in_ref.shape[1:], F32)
                continue
            inside = (ix + o >= 0) & (ix + o < x_count)
            in_ref[w, :, 0:half] = jnp.where(inside, own[k][...].astype(F32), 0.0)
            in_ref[w, :, half:] = jnp.where(z_ok & inside, other[k][...].astype(F32), 0.0)
        k1 = 2 * half
        for w in range(7):
            for j in range(3):
                start = TOP - 3 + j
                lhs1_ref[w, :, j * k1:(j + 1) * k1] = in_ref[w, start:start + rows, :].astype(BF16)
        out = None
        for i in range(3):
            part = mm(lhs1_ref[i:i + 5].reshape(5 * rows, 3 * k1), t1_ref[i])
            out = part if out is None else out + part
        width = out.shape[1]
        y = iota((rows, width), 0) - 2
        z = iota((rows, width), 1) // CH - 2
        ok = (z < pz + 2) & ((y >= 0) | (iy > 0)) & ((y < py) | (iy < y_count - 1))
        ok = ok & ((z >= 0) | (iz > 0)) & ((z < pz) | (iz < z_count - 1))
        for p in range(5):
            a = gelu(out[p * rows:(p + 1) * rows] + bias_ref[0:1, :])
            good = ok & (ix + p - 2 >= 0) & (ix + p - 2 < x_count)
            act1_ref[p, 0:rows, 0:width] = jnp.where(good, a, 0.0)
            act1_ref[p, rows:, 0:width] = jnp.zeros((act1_ref.shape[1] - rows, width), F32)
            act1_ref[p, :, width:] = jnp.zeros((act1_ref.shape[1], act1_ref.shape[2] - width), F32)
        blocks = lhs2_ref.shape[1]
        for p in range(5):
            for j in range(3):
                a = act1_ref[p, j:j + rows, :].astype(BF16)
                for b in range(blocks):
                    lhs2_ref[p, b, :, j * 256:(j + 1) * 256] = a[:, b * 128:b * 128 + 256]
        out = None
        for i in range(3):
            part = mm(lhs2_ref[i:i + 3].reshape(3 * blocks * rows, 768), t2_ref[i])
            out = part if out is None else out + part
        for b in range(blocks):
            y = iota((rows, 128), 0) - 1
            z = (iota((rows, 128), 1) + b * 128) // CH - 1
            ok = (z < pz + 1) & (y <= py) & ((y >= 0) | (iy > 0)) & ((y < py) | (iy < y_count - 1))
            ok = ok & ((z >= 0) | (iz > 0)) & ((z < pz) | (iz < z_count - 1))
            for p in range(3):
                s = (p * blocks + b) * rows
                a = gelu(out[s:s + rows] + bias_ref[1:2, 0:128])
                good = ok & (ix + p - 1 >= 0) & (ix + p - 1 < x_count)
                act2_ref[p, :, b * 128:(b + 1) * 128] = jnp.where(good, a, 0.0).astype(BF16)
        out = None
        for i in range(3):
            part = mm(act2_ref[i], t3_ref[i])
            out = part if out is None else out + part
        tail_ref[0:rows, :] = out
        score = tail_ref[0:py, :]
        for j in (1, 2):
            score = score + pltpu.roll(tail_ref[j:j + py, :], 128 - j * pz, 1)
        out_ref[0] = jnp.transpose(score)[0:pz, :] + bias_ref[2:3, 0:1]
    return kernel


def detector(pooled, edge, ids, weights, py, pz):
    counts = tuple(lax.axis_size(a) for a in ("gx", "gy", "gz"))
    half = pooled.shape[1]
    assert half == 128 and pz * CIN == half and pz * 3 <= 128
    rows = py + 4
    width = lanes_for((pz + 4) * CH)
    blocks = width // 128
    yr = both_sides(edge, "gy")
    tall = -(-(TOP + py + 3) // 16) * 16
    (plane,) = call(
        plane_kernel(py, counts[1]), [((tall, half), BF16)], ids, pooled, yr,
        scratch=[pltpu.VMEM((tall, half), F32)])
    shifts = []
    for s in (1, -1, 2, -2, 3, -3):
        if s % counts[0] and s % counts[0] not in shifts:
            shifts.append(s % counts[0])
    own = [plane] + [lax.ppermute(plane, "gx", ring("gx", s)) for s in shifts]
    matrices = call(
        weight_kernel,
        [((3, 6 * half, width), BF16), ((3, 768, 128), BF16), ((3, width, 128), BF16), ((8, width), F32)],
        *weights, plane)
    own[1], *matrices = lax.optimization_barrier((own[1], *matrices))
    other = [z_neighbour(v, "gz", False) for v in own]
    args = (ids, *own, *other, *matrices)
    (score,) = call(
        conv_kernel(py, counts, shifts), [((1, pz, py), F32)], *args,
        scratch=[
            pltpu.VMEM((7, tall, 2 * half), F32),
            pltpu.VMEM((7, rows, 6 * half), BF16),
            pltpu.VMEM((5, rows + 8, width + 128), F32),
            pltpu.VMEM((5, blocks, rows, 768), BF16),
            pltpu.VMEM((3, rows, width), BF16),
            pltpu.VMEM((rows + 8, 128), F32),
        ], mib=32)
    return jnp.swapaxes(score, 1, 2)


def solution(mesh):
    slab = P(("groups", "gx"), "gy", "gz")
    return jax.shard_map(
        body,
        mesh=mesh,
        in_specs=(slab, slab, slab, P(), P(), P(), P(), P(), P()),
        out_specs=(slab, slab, slab, slab),
        check_vma=False,
    )
```

```python
import functools

import jax
import jax.numpy as jnp
import numpy as np
from jax import lax
from jax.experimental import pallas as pl
from jax.experimental.pallas import tpu as pltpu
from jax.sharding import PartitionSpec as P

F32 = jnp.float32
BF16 = jnp.bfloat16
I16 = jnp.int16
WELL_HEIGHT = 1.0
STRAIN_COUPLING = 4.0
TIME_STEP = 0.01
DAMAGE_RATE = 0.8
ENERGY_CRITICAL = 0.02

OFF = 16
A_CODE = (0.0, 1.0)
B_CODE = (-1.1, 3.1)
SUM_LOW, SUM_SPAN = -1280.0, 4096.0

VMEM = pl.BlockSpec(memory_space=pltpu.VMEM)
HBM = pl.BlockSpec(memory_space=pltpu.HBM)


def to_code(x, code):
    low, span = code
    v = (x - low) * (65535.0 / span) - 32768.0
    return jnp.clip(jnp.round(v), -32768.0, 32767.0).astype(jnp.int32).astype(I16)


def from_code(q, code):
    low, span = code
    return q.astype(jnp.int32).astype(F32) * (span / 65535.0) + (low + 32768.0 * span / 65535.0)


def sum_digits(s):
    v = (s[0:2] - SUM_LOW) * (65536.0 / SUM_SPAN)
    high = jnp.floor(v)
    low = jnp.minimum(jnp.floor((v - high) * 65536.0), 65535.0)
    rows = jnp.concatenate([high, low, jnp.full((12, s.shape[1]), 32768.0, F32)]) - 32768.0
    return rows.astype(jnp.int32).astype(I16)


def from_digits(tile):
    v = tile.astype(jnp.int32).astype(F32) + 32768.0
    return (v[0:2] + v[2:4] * (1.0 / 65536.0)) * (SUM_SPAN / 65536.0) + SUM_LOW


def each(count, looped, body):
    def step(i, carry):
        body(i)
        return carry
    if looped:
        lax.fori_loop(0, count, step, 0)
    else:
        for i in range(count):
            body(i)


def by_label(labels, values):
    return jnp.where(labels == 0, values[0], jnp.where(labels == 1, values[1], values[2])).astype(F32)


FACTORS = (1.0, 0.3, 0.05)
ROOTS = tuple(float(np.sqrt(np.float32(v))) for v in FACTORS)


def call(kernel, outs, *args, in_specs=None, out_specs=None, scratch=(), mib=16):
    return pl.pallas_call(
        kernel,
        in_specs=in_specs or [VMEM] * len(args),
        out_specs=out_specs or [VMEM] * len(outs),
        out_shape=[jax.ShapeDtypeStruct(s, t) for s, t in outs],
        scratch_shapes=scratch,
        compiler_params=pltpu.CompilerParams(vmem_limit_bytes=mib * 1024 * 1024),
    )(*args)


def chunks(start, stop, size):
    return [(r, min(size, stop - r)) for r in range(start, stop, size)]


def fold(x):
    return x.reshape(x.shape[0] // 8, 8, x.shape[1]).sum(0)


def to_rows(top, bottom):
    return jnp.concatenate([jnp.sum(top, 0, keepdims=True), jnp.sum(bottom, 0, keepdims=True),
                            jnp.zeros((6, top.shape[1]), F32)])


def first_kernel(c_hbm, d_hbm, l_hbm, f_ref, amp_ref, lo_ref, hi_ref, sum_ref, le_ref, d_ref, l_ref, sems):
    nx, ny, nz = f_ref.shape
    order = [0, nx - 1] + list(range(1, nx - 1))
    copies = []
    for x in order:
        copies.append([pltpu.make_async_copy(src.at[x], dst.at[x], sems.at[k, x])
                       for k, (src, dst) in enumerate(((c_hbm, f_ref), (d_hbm, d_ref), (l_hbm, l_ref)))])
        for c in copies[-1]:
            c.start()
    top = jnp.zeros((8, nz), F32)
    bottom = jnp.zeros((8, nz), F32)
    for k, x in enumerate(order):
        for c in copies[k]:
            c.wait()
        le_ref[x, 0:16, :] = l_ref[x, 0:16, :]
        le_ref[x, 16:32, :] = l_ref[x, ny - 16:ny, :]
        for r, n in chunks(0, ny, 48):
            f = f_ref[x, r:r + n, :]
            a = by_label(l_ref[x, r:r + n, :], ROOTS) * (1.0 - d_ref[x, r:r + n, :])
            amp_ref[x, r:r + n, :] = a
            m = a * a
            top = top + fold(m * f)
            bottom = bottom + fold(m)
            for near, far, out in ((0, 1, lo_ref), (nx - 1, nx - 2, hi_ref)):
                if x == near:
                    out[r:r + n, :] = to_code(f, A_CODE)
                    out[2 * ny + r:2 * ny + r + n, :] = to_code(a, A_CODE)
                if x == far:
                    out[ny + r:ny + r + n, :] = to_code(f, A_CODE)
    s = to_rows(top, bottom)
    sum_ref[...] = s
    lo_ref[3 * ny:3 * ny + 16, :] = sum_digits(s)
    hi_ref[3 * ny:3 * ny + 16, :] = sum_digits(s)


def edge_rows(code, ride_x, with_amp):
    def kernel(*refs):
        f_ref = refs[0]
        amp_ref = refs[1] if with_amp else None
        lo_ref, hi_ref, s_ref, far_ref = refs[1 + with_amp:5 + with_amp]
        out_ref = refs[-1]
        nx, ny, nz = f_ref.shape
        low_rows = [from_code(r[0:16, :], code)[0:1] for r in (lo_ref, hi_ref)]
        high_rows = [from_code(r[ny - 16:ny, :], code)[15:16] for r in (lo_ref, hi_ref)]
        s = s_ref[...]
        if ride_x:
            s = s + far_ref[...]
        for side, first, second, beside in ((0, 0, 1, low_rows), (1, ny - 1, ny - 2, high_rows)):
            for x in range(nx):
                out_ref[side, 2 * x:2 * x + 1, :] = f_ref[x, first:first + 1, :]
                out_ref[side, 2 * x + 1:2 * x + 2, :] = f_ref[x, second:second + 1, :]
                if amp_ref is not None:
                    out_ref[side, 10 + x:11 + x, :] = amp_ref[x, first:first + 1, :]
            out_ref[side, 8:9, :] = beside[0]
            out_ref[side, 9:10, :] = beside[1]
            out_ref[side, 16:24, :] = s
            if ride_x:
                out_ref[side, 16:18, :] = (s[0:2] + from_digits(lo_ref[lo_ref.shape[0] - 16:, :])
                                           + from_digits(hi_ref[hi_ref.shape[0] - 16:, :]))
    return kernel


def group(lane, j, nz, first, count):
    return (lane - (32 * j + first)) % nz < count


def pack_z(code, ride_y, with_amp):
    def kernel(*refs):
        f_ref = refs[0]
        amp_ref = refs[1] if with_amp else None
        lo_ref, hi_ref, yr_ref, yp_ref, out_ref = refs[1 + with_amp:]
        nx, ny, nz = f_ref.shape
        end = OFF + ny
        lane = lax.broadcasted_iota(jnp.int32, (1, nz), 1)
        for k in range(out_ref.shape[0]):
            planes = [p for p in range(4 * k, 4 * k + 4) if p < nx + 2]

            def packed(f_of, a_of, ps):
                out = None
                for p in ps:
                    j = p % 4
                    f = f_of(p)
                    f = pltpu.roll(f, 32 * j, 1) if j else f
                    out = f if out is None else jnp.where(group(lane, j, nz, -2, 4), f, out)
                    a = a_of(p)
                    if a is not None:
                        out = jnp.where(group(lane, j, nz, 15, 2), pltpu.roll(a, 32 * j + 16, 1), out)
                return out

            for r, n in chunks(0, ny, 48):
                def f_of(p):
                    if p == 0:
                        return from_code(lo_ref[r:r + n, :], code)
                    if p == nx + 1:
                        return from_code(hi_ref[r:r + n, :], code)
                    return f_ref[p - 1, r:r + n, :]

                def a_of(p):
                    return amp_ref[p - 1, r:r + n, :] if with_amp and 1 <= p <= nx else None

                out_ref[k, OFF + r:OFF + r + n, :] = packed(f_of, a_of, planes)
            inner = [p for p in planes if 1 <= p <= nx]
            if inner:
                for side, near in ((1, OFF - 1), (0, end)):
                    out_ref[k, near:near + 1, :] = packed(
                        lambda p: yr_ref[side, 2 * (p - 1):2 * (p - 1) + 1, :], lambda p: None, inner)
        s = yp_ref[0, 16:24, :]
        out_ref[0, 0:8, :] = s + yr_ref[0, 16:24, :] if ride_y else s
    return kernel


def spread(spans, extra, size):
    return [v for a, b in spans for v in chunks(OFF + a - extra, OFF + b + extra, size)]


def fill(code, f_ref, lo_ref, hi_ref, yr_ref, zr_ref, pad_ref, ze_ref, spans):
    nx, ny, nz = f_ref.shape
    end = OFF + ny
    wide = [v for a, b in spans for v in chunks(max(a - 16, 0), min(b + 16, ny), 48)]
    for near, far, ref in ((1, 0, lo_ref), (nx + 2, nx + 3, hi_ref)):
        for r, n in wide:
            pad_ref[near, OFF + r:OFF + r + n, :] = from_code(ref[r:r + n, :], code)
            pad_ref[far, OFF + r:OFF + r + n, :] = from_code(ref[ny + r:ny + r + n, :], code)
    for p, k in ((1, 8), (nx + 2, 9)):
        pad_ref[p, OFF - 1:OFF, :] = yr_ref[1, k:k + 1, :]
        pad_ref[p, end:end + 1, :] = yr_ref[0, k:k + 1, :]
    for x in range(nx):
        for r, n in wide:
            pad_ref[x + 2, OFF + r:OFF + r + n, :] = f_ref[x, r:r + n, :]
        for side, near, far in ((1, OFF - 1, OFF - 2), (0, end, end + 1)):
            pad_ref[x + 2, near:near + 1, :] = yr_ref[side, 2 * x:2 * x + 1, :]
            pad_ref[x + 2, far:far + 1, :] = yr_ref[side, 2 * x + 1:2 * x + 2, :]
    for p in range(nx + 2):
        for r, n in spread(spans, 8, 32):
            e = zr_ref[p // 4, r:r + n, :]
            ze_ref[p, r:r + n, :] = pltpu.roll(e, nz - 32 * (p % 4), 1) if p % 4 else e


def weighted_mean(yp_ref, yr_ref, zr_ref, ride_y, ride_z):
    s = yp_ref[0, 16:24, :]
    if ride_y:
        s = s + yr_ref[0, 16:24, :]
    if ride_z:
        s = s + zr_ref[0, 0:8, :]
    return jnp.sum(s[0:1], keepdims=True) / jnp.sum(s[1:2], keepdims=True)


def worn(a, m, f, mean):
    e = f - mean
    loss = DAMAGE_RATE * 0.5 * STRAIN_COUPLING * (m * (e * e)) - DAMAGE_RATE * ENERGY_CRITICAL
    return a * (1.0 - jnp.maximum(loss, 0.0))


class Geometry:
    def __init__(self, nx, ny, nz):
        self.nx, self.ny, self.nz = nx, ny, nz
        self.lane = lax.broadcasted_iota(jnp.int32, (1, nz), 1)
        self.first = self.lane == 0
        self.last = self.lane == nz - 1

    def before(self, own, other):
        return pltpu.roll(jnp.where(self.last, other, own), 1, 1)

    def after(self, own, other):
        return pltpu.roll(jnp.where(self.first, other, own), self.nz - 1, 1)


def chem_of(f, m, around, mean):
    w = 2.0 * WELL_HEIGHT
    return ((2.0 * w * f - 3.0 * w) * f + (w + 6.0)) * f - around + STRAIN_COUPLING * (m * (f - mean))


def chemistry(g, pad_ref, mob_ref, mobe_ref, ze_ref, chem_ref, cheme_ref, mean, spans, looped=False):
    nx = g.nx

    @functools.partial(each, nx + 2, looped)
    def _(p):
        for r, n in spread(spans, 0, 48) if not looped and p in (0, nx + 1) else spread(spans, 8, 32):
            f = pad_ref[p + 1, r:r + n, :]
            e = ze_ref[p, r:r + n, :]
            around = (pad_ref[p, r:r + n, :] + pad_ref[p + 2, r:r + n, :]
                      + pad_ref[p + 1, r - 1:r - 1 + n, :] + pad_ref[p + 1, r + 1:r + 1 + n, :]
                      + g.before(f, e) + g.after(f, e))
            chem_ref[p, r:r + n, :] = chem_of(f, mob_ref[p, r:r + n, :], around, mean)

    @functools.partial(each, nx, looped)
    def _(x):
        p = x + 1
        for r, n in spread(spans, 0, 48):
            f = pad_ref[p + 1, r:r + n, :]
            e = ze_ref[p, r:r + n, :]
            around = (ze_ref[p - 1, r:r + n, :] + ze_ref[p + 1, r:r + n, :]
                      + ze_ref[p, r - 1:r - 1 + n, :] + ze_ref[p, r + 1:r + 1 + n, :]
                      + g.before(e, f) + g.after(e, f))
            cheme_ref[x, r - OFF:r - OFF + n, :] = chem_of(
                e, mobe_ref[x, r - OFF:r - OFF + n, :], around, mean)


def flux_of(g, x, r, n, mob_ref, mobe_ref, chem_ref, cheme_ref):
    p = x + 1
    m = mob_ref[p, r:r + n, :]
    q = chem_ref[p, r:r + n, :]
    me = mobe_ref[x, r - OFF:r - OFF + n, :]
    qe = cheme_ref[x, r - OFF:r - OFF + n, :]
    total = None
    for nm, nq in (
        (mob_ref[p - 1, r:r + n, :], chem_ref[p - 1, r:r + n, :]),
        (mob_ref[p + 1, r:r + n, :], chem_ref[p + 1, r:r + n, :]),
        (mob_ref[p, r - 1:r - 1 + n, :], chem_ref[p, r - 1:r - 1 + n, :]),
        (mob_ref[p, r + 1:r + 1 + n, :], chem_ref[p, r + 1:r + 1 + n, :]),
        (g.before(m, me), g.before(q, qe)),
        (g.after(m, me), g.after(q, qe)),
    ):
        term = (nm + m) * (nq - q)
        total = term if total is None else total + term
    return m, 0.5 * total


def pack_edges(values, lane, nz):
    out = values[0]
    for x, v in enumerate(values[1:], 1):
        out = jnp.where(group(lane, x, nz, -1, 2), pltpu.roll(v, 32 * x, 1), out)
    return out


def step_a(ride_y, ride_z):
    def kernel(f_ref, amp_ref, lo_ref, hi_ref, yr_ref, zr_ref, yp_ref,
               f2_ref, a2_ref, ae2_ref, lo_out, hi_out, sum_ref,
               pad_ref, ze_ref, mob_ref, mobe_ref, chem_ref, cheme_ref):
        nx, ny, nz = f2_ref.shape
        end = OFF + ny
        g = Geometry(nx, ny, nz)
        mean = weighted_mean(yp_ref, yr_ref, zr_ref, ride_y, ride_z)
        fill(A_CODE, f_ref, lo_ref, hi_ref, yr_ref, zr_ref, pad_ref, ze_ref, [(0, ny)])

        def wear(p, r, n, a):
            m = a * a
            mob_ref[p, r:r + n, :] = m
            a2_ref[p, r:r + n, :] = worn(a, m, pad_ref[p + 1, r:r + n, :], mean)

        for r, n in chunks(0, ny, 48):
            wear(0, OFF + r, n, from_code(lo_ref[2 * ny + r:2 * ny + r + n, :], A_CODE))
            wear(nx + 1, OFF + r, n, from_code(hi_ref[2 * ny + r:2 * ny + r + n, :], A_CODE))
            edges = []
            for x in range(nx):
                wear(x + 1, OFF + r, n, amp_ref[x, r:r + n, :])
                p = x + 1
                a = pltpu.roll(zr_ref[p // 4, OFF + r:OFF + r + n, :], nz - 32 * (p % 4) - 16, 1)
                m = a * a
                mobe_ref[x, r:r + n, :] = m
                edges.append(worn(a, m, ze_ref[p, OFF + r:OFF + r + n, :], mean))
            ae2_ref[r:r + n, :] = pack_edges(edges, g.lane, nz)
        for x in range(nx):
            wear(x + 1, OFF - 1, 1, yr_ref[1, 10 + x:11 + x, :])
            wear(x + 1, end, 1, yr_ref[0, 10 + x:11 + x, :])
        chemistry(g, pad_ref, mob_ref, mobe_ref, ze_ref, chem_ref, cheme_ref, mean, [(0, ny)])
        top = jnp.zeros((8, nz), F32)
        bottom = jnp.zeros((8, nz), F32)
        for x in range(nx):
            for r, n in chunks(OFF, end, 48):
                _, flux = flux_of(g, x, r, n, mob_ref, mobe_ref, chem_ref, cheme_ref)
                f = pad_ref[x + 2, r:r + n, :] + TIME_STEP * flux
                s = slice(r - OFF, r - OFF + n)
                f2_ref[x, s, :] = f
                a = a2_ref[x + 1, r:r + n, :]
                m = a * a
                top = top + fold(m * f)
                bottom = bottom + fold(m)
                for near, far, out in ((0, 1, lo_out), (nx - 1, nx - 2, hi_out)):
                    if x == near:
                        out[s, :] = to_code(f, B_CODE)
                    if x == far:
                        out[r - OFF + ny:r - OFF + ny + n, :] = to_code(f, B_CODE)
        s = to_rows(top, bottom)
        sum_ref[...] = s
        lo_out[2 * ny:2 * ny + 16, :] = sum_digits(s)
        hi_out[2 * ny:2 * ny + 16, :] = sum_digits(s)
    return kernel


def potentials_b(g, mean, a2_ref, ae2_ref, others, scratch, spans, looped):
    f_ref, lo_ref, hi_ref, yr_ref, zr_ref = others
    pad_ref, ze_ref, mob_ref, mobe_ref, chem_ref, cheme_ref = scratch
    nx, nz = g.nx, g.nz
    fill(B_CODE, f_ref, lo_ref, hi_ref, yr_ref, zr_ref, pad_ref, ze_ref, spans)

    @functools.partial(each, nx + 2, looped)
    def _(p):
        for r, n in spread(spans, 8, 32):
            a = a2_ref[p, r:r + n, :]
            mob_ref[p, r:r + n, :] = a * a

    for r, n in spread(spans, 0, 48):
        a = ae2_ref[r - OFF:r - OFF + n, :]
        a = a * a
        for x in range(nx):
            mobe_ref[x, r - OFF:r - OFF + n, :] = pltpu.roll(a, nz - 32 * x, 1) if x else a
    chemistry(g, pad_ref, mob_ref, mobe_ref, ze_ref, chem_ref, cheme_ref, mean, spans, looped)


def finish_b(g, mean, x, r, n, labels, a2_ref, scratch):
    pad_ref, ze_ref, mob_ref, mobe_ref, chem_ref, cheme_ref = scratch
    m, flux = flux_of(g, x, r, n, mob_ref, mobe_ref, chem_ref, cheme_ref)
    f0 = pad_ref[x + 2, r:r + n, :]
    f = f0 + TIME_STEP * flux
    a = worn(a2_ref[x + 1, r:r + n, :], m, f0, mean)
    dmg = 1.0 - a * by_label(labels, tuple(1.0 / v for v in ROOTS))
    return flux, (f, dmg, a * a, by_label(labels, FACTORS))


def pool_rows(scr_ref, count, nz):
    zin = lax.broadcasted_iota(jnp.int32, (nz, nz), 0)
    out = lax.broadcasted_iota(jnp.int32, (nz, nz), 1)
    total = jnp.zeros((count, nz), F32)
    for i in range(4):
        rows = (scr_ref[i, pl.ds(0, count, stride=4), :] + scr_ref[i, pl.ds(1, count, stride=4), :]
                + scr_ref[i, pl.ds(2, count, stride=4), :] + scr_ref[i, pl.ds(3, count, stride=4), :])
        pick = jnp.where((zin // 4 == out // 4) & (out % 4 == i), 1.0 / 64.0, 0.0).astype(F32)
        total = total + jnp.dot(rows, pick, precision=lax.Precision.HIGHEST, preferred_element_type=F32)
    return total


def edge_b(ride_y, ride_z):
    def kernel(f_ref, a2_ref, ae2_ref, lo_ref, hi_ref, yr_ref, zr_ref, yp_ref, l_ref, edge_ref, *rest):
        *scratch, pool_scr = rest
        nx, ny, nz = f_ref.shape
        spans = [(0, 16), (ny - 16, ny)]
        g = Geometry(nx, ny, nz)
        mean = weighted_mean(yp_ref, yr_ref, zr_ref, ride_y, ride_z)
        potentials_b(g, mean, a2_ref, ae2_ref, (f_ref, lo_ref, hi_ref, yr_ref, zr_ref), scratch, spans, False)
        for k, (a, b) in enumerate(spans):
            s = slice(16 * k, 16 * k + 16)
            pooled = [None] * 4
            for x in range(nx):
                _, values = finish_b(g, mean, x, OFF + a, 16, l_ref[x, s, :], a2_ref, scratch)
                pooled = [v if p is None else p + v for p, v in zip(pooled, values)]
            for i in range(4):
                pool_scr[i, s, :] = pooled[i]
        total = pool_rows(pool_scr, 8, nz)
        blank = jnp.zeros((13, nz), F32)
        edge_ref[0] = jnp.concatenate([total[0:3], blank]).astype(BF16)
        edge_ref[1] = jnp.concatenate([total[5:8], blank]).astype(BF16)
    return kernel


def step_b(ride_y, ride_z):
    def kernel(f_ref, a2_ref, ae2_ref, lo_ref, hi_ref, yr_ref, zr_ref, yp_ref, l_hbm,
               f3_hbm, dmg_hbm, flux_hbm, pool_ref, *rest):
        *scratch, pool_scr, l_ref, f3_ref, dmg_ref, flux_ref, l_sem, sems = rest
        nx, ny, nz = f_ref.shape
        labels_in = pltpu.make_async_copy(l_hbm, l_ref, l_sem)
        labels_in.start()
        g = Geometry(nx, ny, nz)
        mean = weighted_mean(yp_ref, yr_ref, zr_ref, ride_y, ride_z)
        potentials_b(g, mean, a2_ref, ae2_ref, (f_ref, lo_ref, hi_ref, yr_ref, zr_ref), scratch, [(0, ny)], True)
        labels_in.wait()
        outs = ((f3_ref, f3_hbm), (dmg_ref, dmg_hbm), (flux_ref, flux_hbm))

        def out_copy(i, x):
            return pltpu.make_async_copy(outs[i][0].at[x], outs[i][1].at[x], sems.at[i, x])

        pool_scr[...] = jnp.zeros(pool_scr.shape, F32)

        @functools.partial(each, nx, True)
        def _(x):
            for r, n in chunks(OFF, OFF + ny, 48):
                s = slice(r - OFF, r - OFF + n)
                flux, values = finish_b(g, mean, x, r, n, l_ref[x, s, :], a2_ref, scratch)
                f3_ref[x, s, :] = values[0]
                dmg_ref[x, s, :] = values[1]
                flux_ref[x, s, :] = flux
                for i in range(4):
                    pool_scr[i, s, :] = pool_scr[i, s, :] + values[i]
            for i in range(3):
                out_copy(i, x).start()

        pool_ref[...] = pool_rows(pool_scr, ny // 4, nz).astype(BF16)
        for x in range(nx):
            for i in range(3):
                out_copy(i, x).wait()
    return kernel


def ring(axis, shift):
    count = lax.axis_size(axis)
    return [(i, (i + shift) % count) for i in range(count)]


def pair_sum(s, axis):
    count = lax.axis_size(axis)
    if count & (count - 1):
        return lax.psum(s, axis)
    bit = 1
    while bit < count:
        s = s + lax.ppermute(s, axis, [(i, i ^ bit) for i in range(count)])
        bit *= 2
    return s


def both_sides(pay, axis):
    if lax.axis_size(axis) == 2:
        return lax.ppermute(pay, axis, ring(axis, 1))
    return jnp.stack([lax.ppermute(pay[0], axis, ring(axis, -1)), lax.ppermute(pay[1], axis, ring(axis, 1))])


def z_neighbour(pay, axis, packed=True):
    if lax.axis_size(axis) == 2:
        return lax.ppermute(pay, axis, ring(axis, 1))
    above = lax.ppermute(pay, axis, ring(axis, -1))
    below = lax.ppermute(pay, axis, ring(axis, 1))
    lane = lax.broadcasted_iota(jnp.int32, pay.shape, pay.ndim - 1)
    if packed:
        low = (lane % 32 < 8) | (lane % 32 == 16)
    else:
        low = lane < pay.shape[-1] // 2
    return jnp.where(low, above, below)


def x_sides(lo, hi):
    return lax.ppermute(hi, "gx", ring("gx", 1)), lax.ppermute(lo, "gx", ring("gx", -1))


def body(concentration, damage, labels, w_first, b_first, w_second, b_second, w_third, b_third):
    nx, ny, nz = concentration.shape
    rows = ny + 2 * OFF
    block = (nx, ny, nz)
    padded = (nx + 2, rows, nz)
    ride_x = lax.axis_size("gx") == 4
    ride_y = lax.axis_size("gy") == 2
    ride_z = lax.axis_size("gz") == 2
    packed = (-(-(nx + 2) // 4), rows, nz)
    assert nz == 128
    scratch = [pltpu.VMEM((nx + 4, rows, nz), F32), pltpu.VMEM(padded, F32), pltpu.VMEM(padded, F32),
               pltpu.VMEM(block, F32), pltpu.VMEM(padded, F32), pltpu.VMEM(block, F32)]

    def start(sums):
        if ride_x:
            return sums, lax.ppermute(sums, "gx", ring("gx", 2))
        sums = pair_sum(sums, "gx")
        for axis, ride in (("gy", ride_y), ("gz", ride_z)):
            if not ride:
                sums = pair_sum(sums, axis)
        return sums, sums

    concentration, damage, labels = (
        pltpu.with_memory_space_constraint(v, pltpu.HBM) for v in (concentration, damage, labels))
    tall = 3 * ny + 16
    f, amp, lo, hi, sums, edge_labels = call(
        first_kernel,
        [(block, F32), (block, F32), ((tall, nz), I16), ((tall, nz), I16), ((8, nz), F32),
         ((nx, 32, nz), jnp.int32)],
        concentration, damage, labels,
        in_specs=[HBM] * 3,
        scratch=[pltpu.VMEM(block, F32), pltpu.VMEM(block, jnp.int32), pltpu.SemaphoreType.DMA((3, nx))])
    weights = weight_rows(w_first, w_second, w_third)
    sums, far = start(sums)
    lo, hi = x_sides(lo, hi)
    (ypay,) = call(edge_rows(A_CODE, ride_x, True), [((2, 24, nz), F32)], f, amp, lo, hi, sums, far, *weights)
    yr = both_sides(ypay, "gy")
    (zpay,) = call(pack_z(A_CODE, ride_y, True), [(packed, F32)], f, amp, lo, hi, yr, ypay)
    zr = z_neighbour(zpay, "gz")
    tall = 2 * ny + 16
    f, a2, ae2, lo, hi, sums = call(
        step_a(ride_y, ride_z),
        [(block, F32), (padded, F32), ((ny, nz), F32), ((tall, nz), I16), ((tall, nz), I16), ((8, nz), F32)],
        f, amp, lo, hi, yr, zr, ypay, scratch=scratch)

    sums, far = start(sums)
    lo, hi = x_sides(lo, hi)
    (ypay,) = call(edge_rows(B_CODE, ride_x, False), [((2, 24, nz), F32)], f, lo, hi, sums, far)
    yr = both_sides(ypay, "gy")
    (zpay,) = call(pack_z(B_CODE, ride_y, False), [(packed, F32)], f, lo, hi, yr, ypay)
    zr = z_neighbour(zpay, "gz")
    last = (f, a2, ae2, lo, hi, yr, zr, ypay)
    (edge,) = call(
        edge_b(ride_y, ride_z), [((2, 16, nz), BF16)], *last, edge_labels,
        scratch=scratch + [pltpu.VMEM((4, 32, nz), F32)])
    fraction, damage_field, flux_sum, pooled = call(
        step_b(ride_y, ride_z),
        [(block, F32), (block, F32), (block, F32), ((ny // 4, nz), BF16)], *last, labels,
        in_specs=[VMEM] * 8 + [HBM], out_specs=[HBM] * 3 + [VMEM],
        scratch=scratch + [
            pltpu.VMEM((4, ny, nz), F32), pltpu.VMEM(block, jnp.int32),
            pltpu.VMEM(block, F32), pltpu.VMEM(block, F32), pltpu.VMEM(block, F32),
            pltpu.SemaphoreType.DMA, pltpu.SemaphoreType.DMA((3, nx))])
    ids = jnp.broadcast_to(jnp.stack([lax.axis_index(a) for a in ("gx", "gy", "gz")])[:, None], (3, nz))
    crack_score = detector(pooled, edge, ids, weights + (b_first[None], b_second[None], b_third[None]), ny // 4, nz // 4)
    return (fraction, damage_field, flux_sum, crack_score)


CH = 16
CIN = 4
TOP = 8


def iota(shape, dim):
    return lax.broadcasted_iota(jnp.int32, shape, dim)


def lanes_for(n):
    return -(-n // 128) * 128


def one_hot(mask):
    return jnp.where(mask, 1.0, 0.0).astype(BF16)


def mm(a, b):
    return jnp.dot(a, b, preferred_element_type=F32)


SHIFTS = tuple(k for k in range(-3, 10) if k % (16 // CIN) == 3)


def weight_kernel(w1_ref, w2_ref, w3_ref, b1_ref, b2_ref, b3_ref, plane_ref, t1_ref, t2_ref, t3_ref, bias_ref):
    n1 = bias_ref.shape[1]
    pz = 128 // CIN
    spread = one_hot(iota((CH, 128), 1) % CH == iota((CH, 128), 0))
    tile1 = mm(w1_ref[...], spread)
    tile2 = mm(w2_ref[...], spread)
    tile3 = mm(w3_ref[...], one_hot(iota((3, 128), 1) // pz == iota((3, 128), 0)))
    step1 = iota((16, 128), 0) // CIN - iota((16, 128), 1) // CH
    step2 = -(iota((16, 128), 1) // CH)
    step3 = -(iota((16, 128), 1) % pz)

    def tile(source, base, stride, step, shift):
        out = jnp.zeros((16, 128), F32)
        for l in range(3):
            k = base + stride * l
            out = jnp.where(step + shift == l, source[16 * k:16 * k + 16], out)
        return out.astype(BF16)

    zero = jnp.zeros((16, 128), BF16)
    bias_ref[...] = jnp.broadcast_to(b3_ref[...], bias_ref.shape)
    for i in range(3):
        for j in range(3):
            tap = 9 * i + 3 * j
            known = {k: tile(tile1, tap, 1, step1, k) for k in SHIFTS}
            places = [(j * 128 + rb * 16, rb * 16 // CIN) for rb in range(8)]
            places += [(384 + 32 * j, pz), (384 + (32 * j - 16) % 128, -16 // CIN)]
            for row, z_in in places:
                for cb in range(n1 // 128):
                    t1_ref[i, row:row + 16, cb * 128:(cb + 1) * 128] = known.get(z_in - cb * 8 + 3, zero)
            for rb in range(10):
                row = j * 128 + rb * 16 if rb < 8 else 384 + 32 * j + (rb - 8) * 16
                t2_ref[i, row:row + 16, :] = tile(tile2, tap, 1, step2, rb)
        for row in (464, 480):
            for cb in range(n1 // 128):
                t1_ref[i, row:row + 16, cb * 128:(cb + 1) * 128] = zero
        for row in (480, 496):
            t2_ref[i, row:row + 16, :] = zero
        for rb in range(t3_ref.shape[1] // 16):
            t3_ref[i, rb * 16:rb * 16 + 16, :] = tile(tile3, 3 * i, 1, step3, rb) if rb < pz + 2 else zero
    wide = one_hot(iota((CH, n1), 1) % CH == iota((CH, n1), 0)).astype(F32)
    for k, ref in ((0, b1_ref), (1, b2_ref)):
        bias_ref[k:k + 1, :] = jnp.dot(ref[...], wide, precision=lax.Precision.HIGHEST, preferred_element_type=F32)


def weight_rows(w_first, w_second, w_third):
    return (jnp.tile(jnp.swapaxes(w_first, 1, 2), (1, 16 // CIN, 1)).reshape(27 * 16, CH),
            jnp.swapaxes(w_second, 1, 2).reshape(27 * CH, CH),
            w_third.reshape(3, 3, 3, CH).transpose(0, 2, 3, 1).reshape(9 * CH, 3))


def gelu(x):
    return 0.5 * x * (1.0 + jnp.tanh(0.7978845608028654 * (x + 0.044715 * (x * x * x))))


def plane_kernel(py, y_count):
    def kernel(ids_ref, pool_ref, yr_ref, out_ref, scr_ref):
        iy = ids_ref[1:2, 0:1]
        scr_ref[...] = jnp.zeros(scr_ref.shape, F32)
        scr_ref[TOP:TOP + py, :] = pool_ref[0:py, :].astype(F32)
        below = yr_ref[1].astype(F32)[0:3]
        above = yr_ref[0].astype(F32)[0:3]
        scr_ref[TOP - 3:TOP, :] = jnp.where(iy > 0, below, 0.0)
        scr_ref[TOP + py:TOP + py + 3, :] = jnp.where(iy < y_count - 1, above, 0.0)
        out_ref[...] = scr_ref[...].astype(BF16)
    return kernel


def conv_kernel(py, counts, shifts):
    x_count, y_count, z_count = counts
    n = len(shifts)

    def kernel(*refs):
        ids_ref = refs[0]
        own = refs[1:2 + n]
        other = refs[2 + n:3 + 2 * n]
        t1_ref, t2_ref, t3_ref, bias_ref, out_ref = refs[3 + 2 * n:8 + 2 * n]
        in_ref, beside_ref, lhs1_ref, act1_ref, lhs2_ref, act2_ref, tail_ref = refs[8 + 2 * n:]
        ix, iy, iz = ids_ref[0:1, 0:1], ids_ref[1:2, 0:1], ids_ref[2:3, 0:1]
        half = own[0].shape[1]
        pz = half // CIN
        rows = py + 4
        z_row = iota((1, half), 1) // CIN
        z_ok = ((z_row < pz // 2) & (iz < z_count - 1)) | ((z_row >= pz // 2) & (iz > 0))
        for w in range(7):
            o = w - 3
            k = 0 if o == 0 else 1 + shifts.index((-o) % x_count) if (-o) % x_count in shifts else None
            if k is None:
                in_ref[w] = jnp.zeros(in_ref.shape[1:], F32)
                beside_ref[w] = jnp.zeros(in_ref.shape[1:], F32)
                continue
            inside = (ix + o >= 0) & (ix + o < x_count)
            in_ref[w] = jnp.where(inside, own[k][...].astype(F32), 0.0)
            beside_ref[w] = jnp.where(z_ok & inside, other[k][...].astype(F32), 0.0)
        lane = iota((1, 128), 1)

        def shared(parts, first, count):
            out = parts[0]
            for j in (1, 2):
                out = jnp.where(group(lane, j, 128, first, count), pltpu.roll(parts[j], 32 * j, 1), out)
            return out.astype(BF16)

        for w in range(7):
            starts = [TOP - 3 + j for j in range(3)]
            for j, r in enumerate(starts):
                lhs1_ref[w, :, j * 128:(j + 1) * 128] = in_ref[w, r:r + rows, :].astype(BF16)
            lhs1_ref[w, :, 384:512] = shared([beside_ref[w, r:r + rows, :] for r in starts], -3 * CIN, 6 * CIN)
        out = None
        for i in range(3):
            part = mm(lhs1_ref[i:i + 5].reshape(5 * rows, 512), t1_ref[i])
            out = part if out is None else out + part
        width = out.shape[1]
        y = iota((rows, width), 0) - 2
        z = iota((rows, width), 1) // CH - 2
        ok = (z < pz + 2) & ((y >= 0) | (iy > 0)) & ((y < py) | (iy < y_count - 1))
        ok = ok & ((z >= 0) | (iz > 0)) & ((z < pz) | (iz < z_count - 1))
        for p in range(5):
            a = gelu(out[p * rows:(p + 1) * rows] + bias_ref[0:1, :])
            good = ok & (ix + p - 2 >= 0) & (ix + p - 2 < x_count)
            act1_ref[p, 0:rows, 0:width] = jnp.where(good, a, 0.0)
            act1_ref[p, rows:, 0:width] = jnp.zeros((act1_ref.shape[1] - rows, width), F32)
            act1_ref[p, :, width:] = jnp.zeros((act1_ref.shape[1], act1_ref.shape[2] - width), F32)
        blocks = lhs2_ref.shape[1]
        for p in range(5):
            for b in range(blocks):
                for j in range(3):
                    lhs2_ref[p, b, :, j * 128:(j + 1) * 128] = (
                        act1_ref[p, j:j + rows, b * 128:(b + 1) * 128].astype(BF16))
                following = slice((b + 1) * 128, (b + 2) * 128)
                lhs2_ref[p, b, :, 384:512] = shared([act1_ref[p, j:j + rows, following] for j in range(3)], 0, 32)
        out = None
        for i in range(3):
            part = mm(lhs2_ref[i:i + 3].reshape(3 * blocks * rows, 512), t2_ref[i])
            out = part if out is None else out + part
        for b in range(blocks):
            y = iota((rows, 128), 0) - 1
            z = (iota((rows, 128), 1) + b * 128) // CH - 1
            ok = (z < pz + 1) & (y <= py) & ((y >= 0) | (iy > 0)) & ((y < py) | (iy < y_count - 1))
            ok = ok & ((z >= 0) | (iz > 0)) & ((z < pz) | (iz < z_count - 1))
            for p in range(3):
                s = (p * blocks + b) * rows
                a = gelu(out[s:s + rows] + bias_ref[1:2, 0:128])
                good = ok & (ix + p - 1 >= 0) & (ix + p - 1 < x_count)
                act2_ref[p, :, b * 128:(b + 1) * 128] = jnp.where(good, a, 0.0).astype(BF16)
        out = None
        for i in range(3):
            part = mm(act2_ref[i], t3_ref[i])
            out = part if out is None else out + part
        tail_ref[0:rows, :] = out
        score = tail_ref[0:py, :]
        for j in (1, 2):
            score = score + pltpu.roll(tail_ref[j:j + py, :], 128 - j * pz, 1)
        out_ref[0] = jnp.transpose(score)[0:pz, :] + bias_ref[2:3, 0:1]
    return kernel


def detector(pooled, edge, ids, weights, py, pz):
    counts = tuple(lax.axis_size(a) for a in ("gx", "gy", "gz"))
    half = pooled.shape[1]
    assert half == 128 and pz * CIN == half and pz * 3 <= 128
    rows = py + 4
    width = lanes_for((pz + 4) * CH)
    blocks = width // 128
    yr = both_sides(edge, "gy")
    tall = -(-(TOP + py + 3) // 16) * 16
    (plane,) = call(
        plane_kernel(py, counts[1]), [((tall, half), BF16)], ids, pooled, yr,
        scratch=[pltpu.VMEM((tall, half), F32)])
    shifts = []
    for s in (1, -1, 2, -2, 3, -3):
        if s % counts[0] and s % counts[0] not in shifts:
            shifts.append(s % counts[0])
    own = [plane] + [lax.ppermute(plane, "gx", ring("gx", s)) for s in shifts]
    matrices = call(
        weight_kernel,
        [((3, 512, width), BF16), ((3, 512, 128), BF16), ((3, width, 128), BF16), ((8, width), F32)],
        *weights, plane)
    own[1], *matrices = lax.optimization_barrier((own[1], *matrices))
    other = [z_neighbour(v, "gz", False) for v in own]
    args = (ids, *own, *other, *matrices)
    (score,) = call(
        conv_kernel(py, counts, shifts), [((1, pz, py), F32)], *args,
        scratch=[
            pltpu.VMEM((7, tall, half), F32),
            pltpu.VMEM((7, tall, half), F32),
            pltpu.VMEM((7, rows, 512), BF16),
            pltpu.VMEM((5, rows + 8, width + 128), F32),
            pltpu.VMEM((5, blocks, rows, 512), BF16),
            pltpu.VMEM((3, rows, width), BF16),
            pltpu.VMEM((rows + 8, 128), F32),
        ], mib=32)
    return jnp.swapaxes(score, 1, 2)


def solution(mesh):
    slab = P(("groups", "gx"), "gy", "gz")
    return jax.shard_map(
        body,
        mesh=mesh,
        in_specs=(slab, slab, slab, P(), P(), P(), P(), P(), P()),
        out_specs=(slab, slab, slab, slab),
        check_vma=False,
    )
```

```python
import functools

import jax
import jax.numpy as jnp
import numpy as np
from jax import lax
from jax.experimental import pallas as pl
from jax.experimental.pallas import tpu as pltpu
from jax.sharding import PartitionSpec as P

F32 = jnp.float32
BF16 = jnp.bfloat16
I16 = jnp.int16
WELL_HEIGHT = 1.0
STRAIN_COUPLING = 4.0
TIME_STEP = 0.01
DAMAGE_RATE = 0.8
ENERGY_CRITICAL = 0.02

OFF = 16
A_CODE = (0.0, 1.0)
B_CODE = (-1.1, 3.1)
SUM_LOW, SUM_SPAN = -1280.0, 4096.0

VMEM = pl.BlockSpec(memory_space=pltpu.VMEM)
HBM = pl.BlockSpec(memory_space=pltpu.HBM)


def to_code(x, code):
    low, span = code
    v = (x - low) * (65535.0 / span) - 32768.0
    return jnp.clip(jnp.round(v), -32768.0, 32767.0).astype(jnp.int32).astype(I16)


def from_code(q, code):
    low, span = code
    return q.astype(jnp.int32).astype(F32) * (span / 65535.0) + (low + 32768.0 * span / 65535.0)


def sum_digits(s):
    v = (s[0:2] - SUM_LOW) * (65536.0 / SUM_SPAN)
    high = jnp.floor(v)
    low = jnp.minimum(jnp.floor((v - high) * 65536.0), 65535.0)
    rows = jnp.concatenate([high, low, jnp.full((12, s.shape[1]), 32768.0, F32)]) - 32768.0
    return rows.astype(jnp.int32).astype(I16)


def from_digits(tile):
    v = tile.astype(jnp.int32).astype(F32) + 32768.0
    return (v[0:2] + v[2:4] * (1.0 / 65536.0)) * (SUM_SPAN / 65536.0) + SUM_LOW


def each(count, looped, body):
    def step(i, carry):
        body(i)
        return carry
    if looped:
        lax.fori_loop(0, count, step, 0)
    else:
        for i in range(count):
            body(i)


def by_label(labels, values):
    return jnp.where(labels == 0, values[0], jnp.where(labels == 1, values[1], values[2])).astype(F32)


FACTORS = (1.0, 0.3, 0.05)
ROOTS = tuple(float(np.sqrt(np.float32(v))) for v in FACTORS)


def call(kernel, outs, *args, in_specs=None, out_specs=None, scratch=(), mib=16):
    return pl.pallas_call(
        kernel,
        in_specs=in_specs or [VMEM] * len(args),
        out_specs=out_specs or [VMEM] * len(outs),
        out_shape=[jax.ShapeDtypeStruct(s, t) for s, t in outs],
        scratch_shapes=scratch,
        compiler_params=pltpu.CompilerParams(vmem_limit_bytes=mib * 1024 * 1024),
    )(*args)


def chunks(start, stop, size):
    return [(r, min(size, stop - r)) for r in range(start, stop, size)]


def fold(x):
    return x.reshape(x.shape[0] // 8, 8, x.shape[1]).sum(0)


def to_rows(top, bottom):
    return jnp.concatenate([jnp.sum(top, 0, keepdims=True), jnp.sum(bottom, 0, keepdims=True),
                            jnp.zeros((6, top.shape[1]), F32)])


def first_kernel(c_hbm, d_hbm, l_hbm, f_ref, amp_ref, lo_ref, hi_ref, sum_ref, le_ref, d_ref, l_ref, sems):
    nx, ny, nz = f_ref.shape
    order = [0, nx - 1] + list(range(1, nx - 1))
    copies = []
    for x in order:
        copies.append([pltpu.make_async_copy(src.at[x], dst.at[x], sems.at[k, x])
                       for k, (src, dst) in enumerate(((c_hbm, f_ref), (d_hbm, d_ref), (l_hbm, l_ref)))])
        for c in copies[-1]:
            c.start()
    top = jnp.zeros((8, nz), F32)
    bottom = jnp.zeros((8, nz), F32)
    for k, x in enumerate(order):
        for c in copies[k]:
            c.wait()
        le_ref[x, 0:16, :] = l_ref[x, 0:16, :]
        le_ref[x, 16:32, :] = l_ref[x, ny - 16:ny, :]
        for r, n in chunks(0, ny, 48):
            f = f_ref[x, r:r + n, :]
            a = by_label(l_ref[x, r:r + n, :], ROOTS) * (1.0 - d_ref[x, r:r + n, :])
            amp_ref[x, r:r + n, :] = a
            m = a * a
            top = top + fold(m * f)
            bottom = bottom + fold(m)
            for near, far, out in ((0, 1, lo_ref), (nx - 1, nx - 2, hi_ref)):
                if x == near:
                    out[r:r + n, :] = to_code(f, A_CODE)
                    out[2 * ny + r:2 * ny + r + n, :] = to_code(a, A_CODE)
                if x == far:
                    out[ny + r:ny + r + n, :] = to_code(f, A_CODE)
    s = to_rows(top, bottom)
    sum_ref[...] = s
    lo_ref[3 * ny:3 * ny + 16, :] = sum_digits(s)
    hi_ref[3 * ny:3 * ny + 16, :] = sum_digits(s)


def edge_rows(code, ride_x, with_amp):
    def kernel(*refs):
        f_ref = refs[0]
        amp_ref = refs[1] if with_amp else None
        lo_ref, hi_ref, s_ref, far_ref = refs[1 + with_amp:5 + with_amp]
        out_ref = refs[-1]
        nx, ny, nz = f_ref.shape
        low_rows = [from_code(r[0:16, :], code)[0:1] for r in (lo_ref, hi_ref)]
        high_rows = [from_code(r[ny - 16:ny, :], code)[15:16] for r in (lo_ref, hi_ref)]
        s = s_ref[...]
        if ride_x:
            s = s + far_ref[...]
        for side, first, second, beside in ((0, 0, 1, low_rows), (1, ny - 1, ny - 2, high_rows)):
            for x in range(nx):
                out_ref[side, 2 * x:2 * x + 1, :] = f_ref[x, first:first + 1, :]
                out_ref[side, 2 * x + 1:2 * x + 2, :] = f_ref[x, second:second + 1, :]
                if amp_ref is not None:
                    out_ref[side, 10 + x:11 + x, :] = amp_ref[x, first:first + 1, :]
            out_ref[side, 8:9, :] = beside[0]
            out_ref[side, 9:10, :] = beside[1]
            out_ref[side, 16:24, :] = s
            if ride_x:
                out_ref[side, 16:18, :] = (s[0:2] + from_digits(lo_ref[lo_ref.shape[0] - 16:, :])
                                           + from_digits(hi_ref[hi_ref.shape[0] - 16:, :]))
    return kernel


def group(lane, j, nz, first, count):
    return (lane - (32 * j + first)) % nz < count


def pack_z(code, ride_y, with_amp):
    def kernel(*refs):
        f_ref = refs[0]
        amp_ref = refs[1] if with_amp else None
        lo_ref, hi_ref, yr_ref, yp_ref, out_ref = refs[1 + with_amp:]
        nx, ny, nz = f_ref.shape
        end = OFF + ny
        lane = lax.broadcasted_iota(jnp.int32, (1, nz), 1)
        for k in range(out_ref.shape[0]):
            planes = [p for p in range(4 * k, 4 * k + 4) if p < nx + 2]

            def packed(f_of, a_of, ps):
                out = None
                for p in ps:
                    j = p % 4
                    f = f_of(p)
                    f = pltpu.roll(f, 32 * j, 1) if j else f
                    out = f if out is None else jnp.where(group(lane, j, nz, -2, 4), f, out)
                    a = a_of(p)
                    if a is not None:
                        out = jnp.where(group(lane, j, nz, 15, 2), pltpu.roll(a, 32 * j + 16, 1), out)
                return out

            for r, n in chunks(0, ny, 48):
                def f_of(p):
                    if p == 0:
                        return from_code(lo_ref[r:r + n, :], code)
                    if p == nx + 1:
                        return from_code(hi_ref[r:r + n, :], code)
                    return f_ref[p - 1, r:r + n, :]

                def a_of(p):
                    return amp_ref[p - 1, r:r + n, :] if with_amp and 1 <= p <= nx else None

                out_ref[k, OFF + r:OFF + r + n, :] = packed(f_of, a_of, planes)
            inner = [p for p in planes if 1 <= p <= nx]
            if inner:
                for side, near in ((1, OFF - 1), (0, end)):
                    out_ref[k, near:near + 1, :] = packed(
                        lambda p: yr_ref[side, 2 * (p - 1):2 * (p - 1) + 1, :], lambda p: None, inner)
        s = yp_ref[0, 16:24, :]
        out_ref[0, 0:8, :] = s + yr_ref[0, 16:24, :] if ride_y else s
    return kernel


def spread(spans, extra, size):
    return [v for a, b in spans for v in chunks(OFF + a - extra, OFF + b + extra, size)]


def fill(code, f_ref, lo_ref, hi_ref, yr_ref, zr_ref, pad_ref, ze_ref, spans):
    nx, ny, nz = f_ref.shape
    end = OFF + ny
    wide = [v for a, b in spans for v in chunks(max(a - 16, 0), min(b + 16, ny), 48)]
    for near, far, ref in ((1, 0, lo_ref), (nx + 2, nx + 3, hi_ref)):
        for r, n in wide:
            pad_ref[near, OFF + r:OFF + r + n, :] = from_code(ref[r:r + n, :], code)
            pad_ref[far, OFF + r:OFF + r + n, :] = from_code(ref[ny + r:ny + r + n, :], code)
    for p, k in ((1, 8), (nx + 2, 9)):
        pad_ref[p, OFF - 1:OFF, :] = yr_ref[1, k:k + 1, :]
        pad_ref[p, end:end + 1, :] = yr_ref[0, k:k + 1, :]
    for x in range(nx):
        for r, n in wide:
            pad_ref[x + 2, OFF + r:OFF + r + n, :] = f_ref[x, r:r + n, :]
        for side, near, far in ((1, OFF - 1, OFF - 2), (0, end, end + 1)):
            pad_ref[x + 2, near:near + 1, :] = yr_ref[side, 2 * x:2 * x + 1, :]
            pad_ref[x + 2, far:far + 1, :] = yr_ref[side, 2 * x + 1:2 * x + 2, :]
    for p in range(nx + 2):
        for r, n in spread(spans, 8, 32):
            e = zr_ref[p // 4, r:r + n, :]
            ze_ref[p, r:r + n, :] = pltpu.roll(e, nz - 32 * (p % 4), 1) if p % 4 else e


def weighted_mean(yp_ref, yr_ref, zr_ref, ride_y, ride_z):
    s = yp_ref[0, 16:24, :]
    if ride_y:
        s = s + yr_ref[0, 16:24, :]
    if ride_z:
        s = s + zr_ref[0, 0:8, :]
    return jnp.sum(s[0:1], keepdims=True) / jnp.sum(s[1:2], keepdims=True)


def worn(a, m, f, mean):
    e = f - mean
    loss = DAMAGE_RATE * 0.5 * STRAIN_COUPLING * (m * (e * e)) - DAMAGE_RATE * ENERGY_CRITICAL
    return a * (1.0 - jnp.maximum(loss, 0.0))


class Geometry:
    def __init__(self, nx, ny, nz):
        self.nx, self.ny, self.nz = nx, ny, nz
        self.lane = lax.broadcasted_iota(jnp.int32, (1, nz), 1)
        self.first = self.lane == 0
        self.last = self.lane == nz - 1

    def before(self, own, other):
        return pltpu.roll(jnp.where(self.last, other, own), 1, 1)

    def after(self, own, other):
        return pltpu.roll(jnp.where(self.first, other, own), self.nz - 1, 1)


def chem_of(f, m, around, mean):
    w = 2.0 * WELL_HEIGHT
    return ((2.0 * w * f - 3.0 * w) * f + (w + 6.0)) * f - around + STRAIN_COUPLING * (m * (f - mean))


def chemistry(g, pad_ref, mob_ref, mobe_ref, ze_ref, chem_ref, cheme_ref, mean, spans, looped=False):
    nx = g.nx

    @functools.partial(each, nx + 2, looped)
    def _(p):
        for r, n in spread(spans, 0, 48) if not looped and p in (0, nx + 1) else spread(spans, 8, 32):
            f = pad_ref[p + 1, r:r + n, :]
            e = ze_ref[p, r:r + n, :]
            around = (pad_ref[p, r:r + n, :] + pad_ref[p + 2, r:r + n, :]
                      + pad_ref[p + 1, r - 1:r - 1 + n, :] + pad_ref[p + 1, r + 1:r + 1 + n, :]
                      + g.before(f, e) + g.after(f, e))
            chem_ref[p, r:r + n, :] = chem_of(f, mob_ref[p, r:r + n, :], around, mean)

    @functools.partial(each, nx, looped)
    def _(x):
        p = x + 1
        for r, n in spread(spans, 0, 48):
            f = pad_ref[p + 1, r:r + n, :]
            e = ze_ref[p, r:r + n, :]
            around = (ze_ref[p - 1, r:r + n, :] + ze_ref[p + 1, r:r + n, :]
                      + ze_ref[p, r - 1:r - 1 + n, :] + ze_ref[p, r + 1:r + 1 + n, :]
                      + g.before(e, f) + g.after(e, f))
            cheme_ref[x, r - OFF:r - OFF + n, :] = chem_of(
                e, mobe_ref[x, r - OFF:r - OFF + n, :], around, mean)


def flux_of(g, x, r, n, mob_ref, mobe_ref, chem_ref, cheme_ref):
    p = x + 1
    m = mob_ref[p, r:r + n, :]
    q = chem_ref[p, r:r + n, :]
    me = mobe_ref[x, r - OFF:r - OFF + n, :]
    qe = cheme_ref[x, r - OFF:r - OFF + n, :]
    total = None
    for nm, nq in (
        (mob_ref[p - 1, r:r + n, :], chem_ref[p - 1, r:r + n, :]),
        (mob_ref[p + 1, r:r + n, :], chem_ref[p + 1, r:r + n, :]),
        (mob_ref[p, r - 1:r - 1 + n, :], chem_ref[p, r - 1:r - 1 + n, :]),
        (mob_ref[p, r + 1:r + 1 + n, :], chem_ref[p, r + 1:r + 1 + n, :]),
        (g.before(m, me), g.before(q, qe)),
        (g.after(m, me), g.after(q, qe)),
    ):
        term = (nm + m) * (nq - q)
        total = term if total is None else total + term
    return m, 0.5 * total


def pack_edges(values, lane, nz):
    out = values[0]
    for x, v in enumerate(values[1:], 1):
        out = jnp.where(group(lane, x, nz, -1, 2), pltpu.roll(v, 32 * x, 1), out)
    return out


def step_a(ride_y, ride_z):
    def kernel(f_ref, amp_ref, lo_ref, hi_ref, yr_ref, zr_ref, yp_ref,
               f2_ref, a2_ref, ae2_ref, lo_out, hi_out, sum_ref,
               pad_ref, ze_ref, mob_ref, mobe_ref, chem_ref, cheme_ref):
        nx, ny, nz = f2_ref.shape
        end = OFF + ny
        g = Geometry(nx, ny, nz)
        mean = weighted_mean(yp_ref, yr_ref, zr_ref, ride_y, ride_z)
        fill(A_CODE, f_ref, lo_ref, hi_ref, yr_ref, zr_ref, pad_ref, ze_ref, [(0, ny)])

        def wear(p, r, n, a):
            m = a * a
            mob_ref[p, r:r + n, :] = m
            a2_ref[p, r:r + n, :] = worn(a, m, pad_ref[p + 1, r:r + n, :], mean)

        for r, n in chunks(0, ny, 48):
            wear(0, OFF + r, n, from_code(lo_ref[2 * ny + r:2 * ny + r + n, :], A_CODE))
            wear(nx + 1, OFF + r, n, from_code(hi_ref[2 * ny + r:2 * ny + r + n, :], A_CODE))
            edges = []
            for x in range(nx):
                wear(x + 1, OFF + r, n, amp_ref[x, r:r + n, :])
                p = x + 1
                a = pltpu.roll(zr_ref[p // 4, OFF + r:OFF + r + n, :], nz - 32 * (p % 4) - 16, 1)
                m = a * a
                mobe_ref[x, r:r + n, :] = m
                edges.append(worn(a, m, ze_ref[p, OFF + r:OFF + r + n, :], mean))
            ae2_ref[r:r + n, :] = pack_edges(edges, g.lane, nz)
        for x in range(nx):
            wear(x + 1, OFF - 1, 1, yr_ref[1, 10 + x:11 + x, :])
            wear(x + 1, end, 1, yr_ref[0, 10 + x:11 + x, :])
        chemistry(g, pad_ref, mob_ref, mobe_ref, ze_ref, chem_ref, cheme_ref, mean, [(0, ny)])
        top = jnp.zeros((8, nz), F32)
        bottom = jnp.zeros((8, nz), F32)
        for x in range(nx):
            for r, n in chunks(OFF, end, 48):
                _, flux = flux_of(g, x, r, n, mob_ref, mobe_ref, chem_ref, cheme_ref)
                f = pad_ref[x + 2, r:r + n, :] + TIME_STEP * flux
                s = slice(r - OFF, r - OFF + n)
                f2_ref[x, s, :] = f
                a = a2_ref[x + 1, r:r + n, :]
                m = a * a
                top = top + fold(m * f)
                bottom = bottom + fold(m)
                for near, far, out in ((0, 1, lo_out), (nx - 1, nx - 2, hi_out)):
                    if x == near:
                        out[s, :] = to_code(f, B_CODE)
                    if x == far:
                        out[r - OFF + ny:r - OFF + ny + n, :] = to_code(f, B_CODE)
        s = to_rows(top, bottom)
        sum_ref[...] = s
        lo_out[2 * ny:2 * ny + 16, :] = sum_digits(s)
        hi_out[2 * ny:2 * ny + 16, :] = sum_digits(s)
    return kernel


def potentials_b(g, mean, a2_ref, ae2_ref, others, scratch, spans, looped):
    f_ref, lo_ref, hi_ref, yr_ref, zr_ref = others
    pad_ref, ze_ref, mob_ref, mobe_ref, chem_ref, cheme_ref = scratch
    nx, nz = g.nx, g.nz
    fill(B_CODE, f_ref, lo_ref, hi_ref, yr_ref, zr_ref, pad_ref, ze_ref, spans)

    @functools.partial(each, nx + 2, looped)
    def _(p):
        for r, n in spread(spans, 8, 32):
            a = a2_ref[p, r:r + n, :]
            mob_ref[p, r:r + n, :] = a * a

    for r, n in spread(spans, 0, 48):
        a = ae2_ref[r - OFF:r - OFF + n, :]
        a = a * a
        for x in range(nx):
            mobe_ref[x, r - OFF:r - OFF + n, :] = pltpu.roll(a, nz - 32 * x, 1) if x else a
    chemistry(g, pad_ref, mob_ref, mobe_ref, ze_ref, chem_ref, cheme_ref, mean, spans, looped)


def finish_b(g, mean, x, r, n, labels, a2_ref, scratch):
    pad_ref, ze_ref, mob_ref, mobe_ref, chem_ref, cheme_ref = scratch
    m, flux = flux_of(g, x, r, n, mob_ref, mobe_ref, chem_ref, cheme_ref)
    f0 = pad_ref[x + 2, r:r + n, :]
    f = f0 + TIME_STEP * flux
    a = worn(a2_ref[x + 1, r:r + n, :], m, f0, mean)
    dmg = 1.0 - a * by_label(labels, tuple(1.0 / v for v in ROOTS))
    return flux, (f, dmg, a * a, by_label(labels, FACTORS))


def pool_rows(scr_ref, count, nz):
    zin = lax.broadcasted_iota(jnp.int32, (nz, nz), 0)
    out = lax.broadcasted_iota(jnp.int32, (nz, nz), 1)
    total = jnp.zeros((count, nz), F32)
    for i in range(4):
        rows = (scr_ref[i, pl.ds(0, count, stride=4), :] + scr_ref[i, pl.ds(1, count, stride=4), :]
                + scr_ref[i, pl.ds(2, count, stride=4), :] + scr_ref[i, pl.ds(3, count, stride=4), :])
        pick = jnp.where((zin // 4 == out // 4) & (out % 4 == i), 1.0 / 64.0, 0.0).astype(F32)
        total = total + jnp.dot(rows, pick, precision=lax.Precision.HIGHEST, preferred_element_type=F32)
    return total


def edge_b(ride_y, ride_z):
    def kernel(f_ref, a2_ref, ae2_ref, lo_ref, hi_ref, yr_ref, zr_ref, yp_ref, l_ref, edge_ref, *rest):
        *scratch, pool_scr = rest
        nx, ny, nz = f_ref.shape
        spans = [(0, 16), (ny - 16, ny)]
        g = Geometry(nx, ny, nz)
        mean = weighted_mean(yp_ref, yr_ref, zr_ref, ride_y, ride_z)
        potentials_b(g, mean, a2_ref, ae2_ref, (f_ref, lo_ref, hi_ref, yr_ref, zr_ref), scratch, spans, False)
        for k, (a, b) in enumerate(spans):
            s = slice(16 * k, 16 * k + 16)
            pooled = [None] * 4
            for x in range(nx):
                _, values = finish_b(g, mean, x, OFF + a, 16, l_ref[x, s, :], a2_ref, scratch)
                pooled = [v if p is None else p + v for p, v in zip(pooled, values)]
            for i in range(4):
                pool_scr[i, s, :] = pooled[i]
        total = pool_rows(pool_scr, 8, nz)
        blank = jnp.zeros((13, nz), F32)
        edge_ref[0] = jnp.concatenate([total[0:3], blank]).astype(BF16)
        edge_ref[1] = jnp.concatenate([total[5:8], blank]).astype(BF16)
    return kernel


def step_b(ride_y, ride_z):
    def kernel(f_ref, a2_ref, ae2_ref, lo_ref, hi_ref, yr_ref, zr_ref, yp_ref, l_hbm,
               f3_hbm, dmg_hbm, flux_hbm, pool_ref, *rest):
        *scratch, pool_scr, l_ref, f3_ref, dmg_ref, flux_ref, l_sem, sems = rest
        nx, ny, nz = f_ref.shape
        labels_in = pltpu.make_async_copy(l_hbm, l_ref, l_sem)
        labels_in.start()
        g = Geometry(nx, ny, nz)
        mean = weighted_mean(yp_ref, yr_ref, zr_ref, ride_y, ride_z)
        potentials_b(g, mean, a2_ref, ae2_ref, (f_ref, lo_ref, hi_ref, yr_ref, zr_ref), scratch, [(0, ny)], True)
        labels_in.wait()
        outs = ((f3_ref, f3_hbm), (dmg_ref, dmg_hbm), (flux_ref, flux_hbm))

        def out_copy(i, x):
            return pltpu.make_async_copy(outs[i][0].at[x], outs[i][1].at[x], sems.at[i, x])

        pool_scr[...] = jnp.zeros(pool_scr.shape, F32)

        @functools.partial(each, nx, True)
        def _(x):
            for r, n in chunks(OFF, OFF + ny, 48):
                s = slice(r - OFF, r - OFF + n)
                flux, values = finish_b(g, mean, x, r, n, l_ref[x, s, :], a2_ref, scratch)
                f3_ref[x, s, :] = values[0]
                dmg_ref[x, s, :] = values[1]
                flux_ref[x, s, :] = flux
                for i in range(4):
                    pool_scr[i, s, :] = pool_scr[i, s, :] + values[i]
            for i in range(3):
                out_copy(i, x).start()

        pool_ref[...] = pool_rows(pool_scr, ny // 4, nz).astype(BF16)
        for x in range(nx):
            for i in range(3):
                out_copy(i, x).wait()
    return kernel


def ring(axis, shift):
    count = lax.axis_size(axis)
    return [(i, (i + shift) % count) for i in range(count)]


def pair_sum(s, axis):
    count = lax.axis_size(axis)
    if count & (count - 1):
        return lax.psum(s, axis)
    bit = 1
    while bit < count:
        s = s + lax.ppermute(s, axis, [(i, i ^ bit) for i in range(count)])
        bit *= 2
    return s


def both_sides(pay, axis):
    if lax.axis_size(axis) == 2:
        return lax.ppermute(pay, axis, ring(axis, 1))
    return jnp.stack([lax.ppermute(pay[0], axis, ring(axis, -1)), lax.ppermute(pay[1], axis, ring(axis, 1))])


def z_neighbour(pay, axis, packed=True):
    if lax.axis_size(axis) == 2:
        return lax.ppermute(pay, axis, ring(axis, 1))
    above = lax.ppermute(pay, axis, ring(axis, -1))
    below = lax.ppermute(pay, axis, ring(axis, 1))
    lane = lax.broadcasted_iota(jnp.int32, pay.shape, pay.ndim - 1)
    if packed:
        low = (lane % 32 < 8) | (lane % 32 == 16)
    else:
        low = lane < pay.shape[-1] // 2
    return jnp.where(low, above, below)


def x_sides(lo, hi):
    return lax.ppermute(hi, "gx", ring("gx", 1)), lax.ppermute(lo, "gx", ring("gx", -1))


def body(concentration, damage, labels, w_first, b_first, w_second, b_second, w_third, b_third):
    nx, ny, nz = concentration.shape
    rows = ny + 2 * OFF
    block = (nx, ny, nz)
    padded = (nx + 2, rows, nz)
    ride_x = lax.axis_size("gx") == 4
    ride_y = lax.axis_size("gy") == 2
    ride_z = lax.axis_size("gz") == 2
    packed = (-(-(nx + 2) // 4), rows, nz)
    assert nz == 128
    scratch = [pltpu.VMEM((nx + 4, rows, nz), F32), pltpu.VMEM(padded, F32), pltpu.VMEM(padded, F32),
               pltpu.VMEM(block, F32), pltpu.VMEM(padded, F32), pltpu.VMEM(block, F32)]

    def start(sums):
        if ride_x:
            return sums, lax.ppermute(sums, "gx", ring("gx", 2))
        sums = pair_sum(sums, "gx")
        for axis, ride in (("gy", ride_y), ("gz", ride_z)):
            if not ride:
                sums = pair_sum(sums, axis)
        return sums, sums

    concentration, damage, labels = (
        pltpu.with_memory_space_constraint(v, pltpu.HBM) for v in (concentration, damage, labels))
    tall = 3 * ny + 16
    f, amp, lo, hi, sums, edge_labels = call(
        first_kernel,
        [(block, F32), (block, F32), ((tall, nz), I16), ((tall, nz), I16), ((8, nz), F32),
         ((nx, 32, nz), jnp.int32)],
        concentration, damage, labels,
        in_specs=[HBM] * 3,
        scratch=[pltpu.VMEM(block, F32), pltpu.VMEM(block, jnp.int32), pltpu.SemaphoreType.DMA((3, nx))])
    weights = weight_rows(w_first, w_second, w_third) + (b_first[None], b_second[None], b_third[None])
    sums, far = start(sums)
    lo, hi = x_sides(lo, hi)
    (ypay,) = call(edge_rows(A_CODE, ride_x, True), [((2, 24, nz), F32)], f, amp, lo, hi, sums, far, *weights)
    yr = both_sides(ypay, "gy")
    (zpay,) = call(pack_z(A_CODE, ride_y, True), [(packed, F32)], f, amp, lo, hi, yr, ypay)
    zr = z_neighbour(zpay, "gz")
    tall = 2 * ny + 16
    f, a2, ae2, lo, hi, sums = call(
        step_a(ride_y, ride_z),
        [(block, F32), (padded, F32), ((ny, nz), F32), ((tall, nz), I16), ((tall, nz), I16), ((8, nz), F32)],
        f, amp, lo, hi, yr, zr, ypay, scratch=scratch)

    sums, far = start(sums)
    lo, hi = x_sides(lo, hi)
    (ypay,) = call(edge_rows(B_CODE, ride_x, False), [((2, 24, nz), F32)], f, lo, hi, sums, far)
    yr = both_sides(ypay, "gy")
    (zpay,) = call(pack_z(B_CODE, ride_y, False), [(packed, F32)], f, lo, hi, yr, ypay)
    zr = z_neighbour(zpay, "gz")
    last = (f, a2, ae2, lo, hi, yr, zr, ypay)
    (edge,) = call(
        edge_b(ride_y, ride_z), [((2, 16, nz), BF16)], *last, edge_labels,
        scratch=scratch + [pltpu.VMEM((4, 32, nz), F32)])
    fraction, damage_field, flux_sum, pooled = call(
        step_b(ride_y, ride_z),
        [(block, F32), (block, F32), (block, F32), ((ny // 4, nz), BF16)], *last, labels,
        in_specs=[VMEM] * 8 + [HBM], out_specs=[HBM] * 3 + [VMEM],
        scratch=scratch + [
            pltpu.VMEM((4, ny, nz), F32), pltpu.VMEM(block, jnp.int32),
            pltpu.VMEM(block, F32), pltpu.VMEM(block, F32), pltpu.VMEM(block, F32),
            pltpu.SemaphoreType.DMA, pltpu.SemaphoreType.DMA((3, nx))])
    ids = jnp.broadcast_to(jnp.stack([lax.axis_index(a) for a in ("gx", "gy", "gz")])[:, None], (3, nz))
    crack_score = detector(pooled, edge, ids, weights, ny // 4, nz // 4)
    return (fraction, damage_field, flux_sum, crack_score)


CH = 16
CIN = 4
TOP = 8


def iota(shape, dim):
    return lax.broadcasted_iota(jnp.int32, shape, dim)


def lanes_for(n):
    return -(-n // 128) * 128


def one_hot(mask):
    return jnp.where(mask, 1.0, 0.0).astype(BF16)


def mm(a, b):
    return jnp.dot(a, b, preferred_element_type=F32)


SHIFTS = tuple(k for k in range(-3, 10) if k % (16 // CIN) == 3)


def weight_kernel(w1_ref, w2_ref, w3_ref, b1_ref, b2_ref, b3_ref, plane_ref, t1_ref, t2_ref, t3_ref, bias_ref):
    n1 = bias_ref.shape[1]
    pz = 128 // CIN
    spread = one_hot(iota((CH, 128), 1) % CH == iota((CH, 128), 0))
    tile1 = mm(w1_ref[...], spread)
    tile2 = mm(w2_ref[...], spread)
    tile3 = mm(w3_ref[...], one_hot(iota((3, 128), 1) // pz == iota((3, 128), 0)))
    step1 = iota((16, 128), 0) // CIN - iota((16, 128), 1) // CH
    step2 = -(iota((16, 128), 1) // CH)
    step3 = -(iota((16, 128), 1) % pz)

    def tile(source, base, stride, step, shift):
        out = jnp.zeros((16, 128), F32)
        for l in range(3):
            k = base + stride * l
            out = jnp.where(step + shift == l, source[16 * k:16 * k + 16], out)
        return out.astype(BF16)

    zero = jnp.zeros((16, 128), BF16)
    bias_ref[...] = jnp.broadcast_to(b3_ref[...], bias_ref.shape)
    for i in range(3):
        for j in range(3):
            tap = 9 * i + 3 * j
            known = {k: tile(tile1, tap, 1, step1, k) for k in SHIFTS}
            places = [(j * 128 + rb * 16, rb * 16 // CIN) for rb in range(8)]
            places += [(384 + 32 * j, pz), (384 + (32 * j - 16) % 128, -16 // CIN)]
            for row, z_in in places:
                for cb in range(n1 // 128):
                    t1_ref[i, row:row + 16, cb * 128:(cb + 1) * 128] = known.get(z_in - cb * 8 + 3, zero)
            for rb in range(10):
                row = j * 128 + rb * 16 if rb < 8 else 384 + 32 * j + (rb - 8) * 16
                t2_ref[i, row:row + 16, :] = tile(tile2, tap, 1, step2, rb)
        for row in (464, 480):
            for cb in range(n1 // 128):
                t1_ref[i, row:row + 16, cb * 128:(cb + 1) * 128] = zero
        for row in (480, 496):
            t2_ref[i, row:row + 16, :] = zero
        for rb in range(t3_ref.shape[1] // 16):
            t3_ref[i, rb * 16:rb * 16 + 16, :] = tile(tile3, 3 * i, 1, step3, rb) if rb < pz + 2 else zero
    wide = one_hot(iota((CH, n1), 1) % CH == iota((CH, n1), 0)).astype(F32)
    for k, ref in ((0, b1_ref), (1, b2_ref)):
        bias_ref[k:k + 1, :] = jnp.dot(ref[...], wide, precision=lax.Precision.HIGHEST, preferred_element_type=F32)


def weight_rows(w_first, w_second, w_third):
    return (jnp.tile(jnp.swapaxes(w_first, 1, 2), (1, 16 // CIN, 1)).reshape(27 * 16, CH),
            jnp.swapaxes(w_second, 1, 2).reshape(27 * CH, CH),
            w_third.reshape(3, 3, 3, CH).transpose(0, 2, 3, 1).reshape(9 * CH, 3))


def gelu(x):
    return 0.5 * x * (1.0 + jnp.tanh(0.7978845608028654 * (x + 0.044715 * (x * x * x))))


def plane_kernel(py, y_count):
    def kernel(ids_ref, pool_ref, yr_ref, out_ref, scr_ref):
        iy = ids_ref[1:2, 0:1]
        scr_ref[...] = jnp.zeros(scr_ref.shape, F32)
        scr_ref[TOP:TOP + py, :] = pool_ref[0:py, :].astype(F32)
        below = yr_ref[1].astype(F32)[0:3]
        above = yr_ref[0].astype(F32)[0:3]
        scr_ref[TOP - 3:TOP, :] = jnp.where(iy > 0, below, 0.0)
        scr_ref[TOP + py:TOP + py + 3, :] = jnp.where(iy < y_count - 1, above, 0.0)
        out_ref[...] = scr_ref[...].astype(BF16)
    return kernel


def conv_kernel(py, counts, shifts):
    x_count, y_count, z_count = counts
    n = len(shifts)

    def kernel(*refs):
        ids_ref = refs[0]
        own = refs[1:2 + n]
        other = refs[2 + n:3 + 2 * n]
        t1_ref, t2_ref, t3_ref, bias_ref, out_ref = refs[3 + 2 * n:8 + 2 * n]
        in_ref, beside_ref, lhs1_ref, act1_ref, lhs2_ref, act2_ref, tail_ref = refs[8 + 2 * n:]
        ix, iy, iz = ids_ref[0:1, 0:1], ids_ref[1:2, 0:1], ids_ref[2:3, 0:1]
        half = own[0].shape[1]
        pz = half // CIN
        rows = py + 4
        z_row = iota((1, half), 1) // CIN
        z_ok = ((z_row < pz // 2) & (iz < z_count - 1)) | ((z_row >= pz // 2) & (iz > 0))
        for w in range(7):
            o = w - 3
            k = 0 if o == 0 else 1 + shifts.index((-o) % x_count) if (-o) % x_count in shifts else None
            if k is None:
                in_ref[w] = jnp.zeros(in_ref.shape[1:], F32)
                beside_ref[w] = jnp.zeros(in_ref.shape[1:], F32)
                continue
            inside = (ix + o >= 0) & (ix + o < x_count)
            in_ref[w] = jnp.where(inside, own[k][...].astype(F32), 0.0)
            beside_ref[w] = jnp.where(z_ok & inside, other[k][...].astype(F32), 0.0)
        lane = iota((1, 128), 1)

        def shared(parts, first, count):
            out = parts[0]
            for j in (1, 2):
                out = jnp.where(group(lane, j, 128, first, count), pltpu.roll(parts[j], 32 * j, 1), out)
            return out.astype(BF16)

        for w in range(7):
            starts = [TOP - 3 + j for j in range(3)]
            for j, r in enumerate(starts):
                lhs1_ref[w, :, j * 128:(j + 1) * 128] = in_ref[w, r:r + rows, :].astype(BF16)
            lhs1_ref[w, :, 384:512] = shared([beside_ref[w, r:r + rows, :] for r in starts], -3 * CIN, 6 * CIN)
        out = None
        for i in range(3):
            part = mm(lhs1_ref[i:i + 5].reshape(5 * rows, 512), t1_ref[i])
            out = part if out is None else out + part
        width = out.shape[1]
        y = iota((rows, width), 0) - 2
        z = iota((rows, width), 1) // CH - 2
        ok = (z < pz + 2) & ((y >= 0) | (iy > 0)) & ((y < py) | (iy < y_count - 1))
        ok = ok & ((z >= 0) | (iz > 0)) & ((z < pz) | (iz < z_count - 1))
        for p in range(5):
            a = gelu(out[p * rows:(p + 1) * rows] + bias_ref[0:1, :])
            good = ok & (ix + p - 2 >= 0) & (ix + p - 2 < x_count)
            act1_ref[p, 0:rows, 0:width] = jnp.where(good, a, 0.0)
            act1_ref[p, rows:, 0:width] = jnp.zeros((act1_ref.shape[1] - rows, width), F32)
            act1_ref[p, :, width:] = jnp.zeros((act1_ref.shape[1], act1_ref.shape[2] - width), F32)
        blocks = lhs2_ref.shape[1]
        for p in range(5):
            for b in range(blocks):
                for j in range(3):
                    lhs2_ref[p, b, :, j * 128:(j + 1) * 128] = (
                        act1_ref[p, j:j + rows, b * 128:(b + 1) * 128].astype(BF16))
                following = slice((b + 1) * 128, (b + 2) * 128)
                lhs2_ref[p, b, :, 384:512] = shared([act1_ref[p, j:j + rows, following] for j in range(3)], 0, 32)
        out = None
        for i in range(3):
            part = mm(lhs2_ref[i:i + 3].reshape(3 * blocks * rows, 512), t2_ref[i])
            out = part if out is None else out + part
        for b in range(blocks):
            y = iota((rows, 128), 0) - 1
            z = (iota((rows, 128), 1) + b * 128) // CH - 1
            ok = (z < pz + 1) & (y <= py) & ((y >= 0) | (iy > 0)) & ((y < py) | (iy < y_count - 1))
            ok = ok & ((z >= 0) | (iz > 0)) & ((z < pz) | (iz < z_count - 1))
            for p in range(3):
                s = (p * blocks + b) * rows
                a = gelu(out[s:s + rows] + bias_ref[1:2, 0:128])
                good = ok & (ix + p - 1 >= 0) & (ix + p - 1 < x_count)
                act2_ref[p, :, b * 128:(b + 1) * 128] = jnp.where(good, a, 0.0).astype(BF16)
        out = None
        for i in range(3):
            part = mm(act2_ref[i], t3_ref[i])
            out = part if out is None else out + part
        tail_ref[0:rows, :] = out
        score = tail_ref[0:py, :]
        for j in (1, 2):
            score = score + pltpu.roll(tail_ref[j:j + py, :], 128 - j * pz, 1)
        out_ref[0] = jnp.transpose(score)[0:pz, :] + bias_ref[2:3, 0:1]
    return kernel


def detector(pooled, edge, ids, weights, py, pz):
    counts = tuple(lax.axis_size(a) for a in ("gx", "gy", "gz"))
    half = pooled.shape[1]
    assert half == 128 and pz * CIN == half and pz * 3 <= 128
    rows = py + 4
    width = lanes_for((pz + 4) * CH)
    blocks = width // 128
    yr = both_sides(edge, "gy")
    tall = -(-(TOP + py + 3) // 16) * 16
    (plane,) = call(
        plane_kernel(py, counts[1]), [((tall, half), BF16)], ids, pooled, yr,
        scratch=[pltpu.VMEM((tall, half), F32)])
    shifts = []
    for s in (1, -1, 2, -2, 3, -3):
        if s % counts[0] and s % counts[0] not in shifts:
            shifts.append(s % counts[0])
    own = [plane] + [lax.ppermute(plane, "gx", ring("gx", s)) for s in shifts]
    matrices = call(
        weight_kernel,
        [((3, 512, width), BF16), ((3, 512, 128), BF16), ((3, width, 128), BF16), ((8, width), F32)],
        *weights, plane)
    own[-1], *matrices = lax.optimization_barrier((own[-1], *matrices))
    other = [z_neighbour(v, "gz", False) for v in own]
    args = (ids, *own, *other, *matrices)
    (score,) = call(
        conv_kernel(py, counts, shifts), [((1, pz, py), F32)], *args,
        scratch=[
            pltpu.VMEM((7, tall, half), F32),
            pltpu.VMEM((7, tall, half), F32),
            pltpu.VMEM((7, rows, 512), BF16),
            pltpu.VMEM((5, rows + 8, width + 128), F32),
            pltpu.VMEM((5, blocks, rows, 512), BF16),
            pltpu.VMEM((3, rows, width), BF16),
            pltpu.VMEM((rows + 8, 128), F32),
        ], mib=32)
    return jnp.swapaxes(score, 1, 2)


def solution(mesh):
    slab = P(("groups", "gx"), "gy", "gz")
    return jax.shard_map(
        body,
        mesh=mesh,
        in_specs=(slab, slab, slab, P(), P(), P(), P(), P(), P()),
        out_specs=(slab, slab, slab, slab),
        check_vma=False,
    )
```

```python
import functools

import jax
import jax.numpy as jnp
import numpy as np
from jax import lax
from jax.experimental import pallas as pl
from jax.experimental.pallas import tpu as pltpu
from jax.sharding import PartitionSpec as P

F32 = jnp.float32
BF16 = jnp.bfloat16
I16 = jnp.int16
WELL_HEIGHT = 1.0
STRAIN_COUPLING = 4.0
TIME_STEP = 0.01
DAMAGE_RATE = 0.8
ENERGY_CRITICAL = 0.02

OFF = 16
A_CODE = (0.0, 1.0)
B_CODE = (-1.1, 3.1)
SUM_LOW, SUM_SPAN = -1280.0, 4096.0

VMEM = pl.BlockSpec(memory_space=pltpu.VMEM)
HBM = pl.BlockSpec(memory_space=pltpu.HBM)


def to_code(x, code):
    low, span = code
    v = (x - low) * (65535.0 / span) - 32768.0
    return jnp.clip(jnp.round(v), -32768.0, 32767.0).astype(jnp.int32).astype(I16)


def from_code(q, code):
    low, span = code
    return q.astype(jnp.int32).astype(F32) * (span / 65535.0) + (low + 32768.0 * span / 65535.0)


def sum_digits(s):
    v = (s[0:2] - SUM_LOW) * (65536.0 / SUM_SPAN)
    high = jnp.floor(v)
    low = jnp.minimum(jnp.floor((v - high) * 65536.0), 65535.0)
    rows = jnp.concatenate([high, low, jnp.full((12, s.shape[1]), 32768.0, F32)]) - 32768.0
    return rows.astype(jnp.int32).astype(I16)


def from_digits(tile):
    v = tile.astype(jnp.int32).astype(F32) + 32768.0
    return (v[0:2] + v[2:4] * (1.0 / 65536.0)) * (SUM_SPAN / 65536.0) + SUM_LOW


def each(count, looped, body):
    def step(i, carry):
        body(i)
        return carry
    if looped:
        lax.fori_loop(0, count, step, 0)
    else:
        for i in range(count):
            body(i)


def by_label(labels, values):
    return jnp.where(labels == 0, values[0], jnp.where(labels == 1, values[1], values[2])).astype(F32)


FACTORS = (1.0, 0.3, 0.05)
ROOTS = tuple(float(np.sqrt(np.float32(v))) for v in FACTORS)


def call(kernel, outs, *args, in_specs=None, out_specs=None, scratch=(), mib=16):
    return pl.pallas_call(
        kernel,
        in_specs=in_specs or [VMEM] * len(args),
        out_specs=out_specs or [VMEM] * len(outs),
        out_shape=[jax.ShapeDtypeStruct(s, t) for s, t in outs],
        scratch_shapes=scratch,
        compiler_params=pltpu.CompilerParams(vmem_limit_bytes=mib * 1024 * 1024),
    )(*args)


def chunks(start, stop, size):
    return [(r, min(size, stop - r)) for r in range(start, stop, size)]


def fold(x):
    return x.reshape(x.shape[0] // 8, 8, x.shape[1]).sum(0)


def to_rows(top, bottom):
    return jnp.concatenate([jnp.sum(top, 0, keepdims=True), jnp.sum(bottom, 0, keepdims=True),
                            jnp.zeros((6, top.shape[1]), F32)])


def first_kernel(c_hbm, d_hbm, l_hbm, f_ref, amp_ref, lo_ref, hi_ref, sum_ref, le_ref, d_ref, l_ref, sems):
    nx, ny, nz = f_ref.shape
    order = [0, nx - 1] + list(range(1, nx - 1))
    copies = []
    for x in order:
        copies.append([pltpu.make_async_copy(src.at[x], dst.at[x], sems.at[k, x])
                       for k, (src, dst) in enumerate(((c_hbm, f_ref), (d_hbm, d_ref), (l_hbm, l_ref)))])
        for c in copies[-1]:
            c.start()
    top = jnp.zeros((8, nz), F32)
    bottom = jnp.zeros((8, nz), F32)
    for k, x in enumerate(order):
        for c in copies[k]:
            c.wait()
        le_ref[x, 0:16, :] = l_ref[x, 0:16, :]
        le_ref[x, 16:32, :] = l_ref[x, ny - 16:ny, :]
        for r, n in chunks(0, ny, 48):
            f = f_ref[x, r:r + n, :]
            a = by_label(l_ref[x, r:r + n, :], ROOTS) * (1.0 - d_ref[x, r:r + n, :])
            amp_ref[x, r:r + n, :] = a
            m = a * a
            top = top + fold(m * f)
            bottom = bottom + fold(m)
            for near, far, out in ((0, 1, lo_ref), (nx - 1, nx - 2, hi_ref)):
                if x == near:
                    out[r:r + n, :] = to_code(f, A_CODE)
                    out[2 * ny + r:2 * ny + r + n, :] = to_code(a, A_CODE)
                if x == far:
                    out[ny + r:ny + r + n, :] = to_code(f, A_CODE)
    s = to_rows(top, bottom)
    sum_ref[...] = s
    lo_ref[3 * ny:3 * ny + 16, :] = sum_digits(s)
    hi_ref[3 * ny:3 * ny + 16, :] = sum_digits(s)


def edge_rows(code, ride_x, with_amp):
    def kernel(*refs):
        f_ref = refs[0]
        amp_ref = refs[1] if with_amp else None
        lo_ref, hi_ref, s_ref, far_ref = refs[1 + with_amp:5 + with_amp]
        out_ref = refs[-1]
        nx, ny, nz = f_ref.shape
        low_rows = [from_code(r[0:16, :], code)[0:1] for r in (lo_ref, hi_ref)]
        high_rows = [from_code(r[ny - 16:ny, :], code)[15:16] for r in (lo_ref, hi_ref)]
        s = s_ref[...]
        if ride_x:
            s = s + far_ref[...]
        for side, first, second, beside in ((0, 0, 1, low_rows), (1, ny - 1, ny - 2, high_rows)):
            for x in range(nx):
                out_ref[side, 2 * x:2 * x + 1, :] = f_ref[x, first:first + 1, :]
                out_ref[side, 2 * x + 1:2 * x + 2, :] = f_ref[x, second:second + 1, :]
                if amp_ref is not None:
                    out_ref[side, 10 + x:11 + x, :] = amp_ref[x, first:first + 1, :]
            out_ref[side, 8:9, :] = beside[0]
            out_ref[side, 9:10, :] = beside[1]
            out_ref[side, 16:24, :] = s
            if ride_x:
                out_ref[side, 16:18, :] = (s[0:2] + from_digits(lo_ref[lo_ref.shape[0] - 16:, :])
                                           + from_digits(hi_ref[hi_ref.shape[0] - 16:, :]))
    return kernel


def group(lane, j, nz, first, count):
    return (lane - (32 * j + first)) % nz < count


def pack_z(code, ride_y, with_amp):
    def kernel(*refs):
        f_ref = refs[0]
        amp_ref = refs[1] if with_amp else None
        lo_ref, hi_ref, yr_ref, yp_ref, out_ref = refs[1 + with_amp:]
        nx, ny, nz = f_ref.shape
        end = OFF + ny
        lane = lax.broadcasted_iota(jnp.int32, (1, nz), 1)
        for k in range(out_ref.shape[0]):
            planes = [p for p in range(4 * k, 4 * k + 4) if p < nx + 2]

            def packed(f_of, a_of, ps):
                out = None
                for p in ps:
                    j = p % 4
                    f = f_of(p)
                    f = pltpu.roll(f, 32 * j, 1) if j else f
                    out = f if out is None else jnp.where(group(lane, j, nz, -2, 4), f, out)
                    a = a_of(p)
                    if a is not None:
                        out = jnp.where(group(lane, j, nz, 15, 2), pltpu.roll(a, 32 * j + 16, 1), out)
                return out

            for r, n in chunks(0, ny, 48):
                def f_of(p):
                    if p == 0:
                        return from_code(lo_ref[r:r + n, :], code)
                    if p == nx + 1:
                        return from_code(hi_ref[r:r + n, :], code)
                    return f_ref[p - 1, r:r + n, :]

                def a_of(p):
                    return amp_ref[p - 1, r:r + n, :] if with_amp and 1 <= p <= nx else None

                out_ref[k, OFF + r:OFF + r + n, :] = packed(f_of, a_of, planes)
            inner = [p for p in planes if 1 <= p <= nx]
            if inner:
                for side, near in ((1, OFF - 1), (0, end)):
                    out_ref[k, near:near + 1, :] = packed(
                        lambda p: yr_ref[side, 2 * (p - 1):2 * (p - 1) + 1, :], lambda p: None, inner)
        s = yp_ref[0, 16:24, :]
        out_ref[0, 0:8, :] = s + yr_ref[0, 16:24, :] if ride_y else s
    return kernel


def spread(spans, extra, size):
    return [v for a, b in spans for v in chunks(OFF + a - extra, OFF + b + extra, size)]


def fill(code, f_ref, lo_ref, hi_ref, yr_ref, zr_ref, pad_ref, ze_ref, spans):
    nx, ny, nz = f_ref.shape
    end = OFF + ny
    wide = [v for a, b in spans for v in chunks(max(a - 16, 0), min(b + 16, ny), 48)]
    for near, far, ref in ((1, 0, lo_ref), (nx + 2, nx + 3, hi_ref)):
        for r, n in wide:
            pad_ref[near, OFF + r:OFF + r + n, :] = from_code(ref[r:r + n, :], code)
            pad_ref[far, OFF + r:OFF + r + n, :] = from_code(ref[ny + r:ny + r + n, :], code)
    for p, k in ((1, 8), (nx + 2, 9)):
        pad_ref[p, OFF - 1:OFF, :] = yr_ref[1, k:k + 1, :]
        pad_ref[p, end:end + 1, :] = yr_ref[0, k:k + 1, :]
    for x in range(nx):
        for r, n in wide:
            pad_ref[x + 2, OFF + r:OFF + r + n, :] = f_ref[x, r:r + n, :]
        for side, near, far in ((1, OFF - 1, OFF - 2), (0, end, end + 1)):
            pad_ref[x + 2, near:near + 1, :] = yr_ref[side, 2 * x:2 * x + 1, :]
            pad_ref[x + 2, far:far + 1, :] = yr_ref[side, 2 * x + 1:2 * x + 2, :]
    for p in range(nx + 2):
        for r, n in spread(spans, 8, 32):
            e = zr_ref[p // 4, r:r + n, :]
            ze_ref[p, r:r + n, :] = pltpu.roll(e, nz - 32 * (p % 4), 1) if p % 4 else e


def weighted_mean(yp_ref, yr_ref, zr_ref, ride_y, ride_z):
    s = yp_ref[0, 16:24, :]
    if ride_y:
        s = s + yr_ref[0, 16:24, :]
    if ride_z:
        s = s + zr_ref[0, 0:8, :]
    return jnp.sum(s[0:1], keepdims=True) / jnp.sum(s[1:2], keepdims=True)


def worn(a, m, f, mean):
    e = f - mean
    loss = DAMAGE_RATE * 0.5 * STRAIN_COUPLING * (m * (e * e)) - DAMAGE_RATE * ENERGY_CRITICAL
    return a * (1.0 - jnp.maximum(loss, 0.0))


class Geometry:
    def __init__(self, nx, ny, nz):
        self.nx, self.ny, self.nz = nx, ny, nz
        self.lane = lax.broadcasted_iota(jnp.int32, (1, nz), 1)
        self.first = self.lane == 0
        self.last = self.lane == nz - 1

    def before(self, own, other):
        return pltpu.roll(jnp.where(self.last, other, own), 1, 1)

    def after(self, own, other):
        return pltpu.roll(jnp.where(self.first, other, own), self.nz - 1, 1)


def chem_of(f, m, around, mean):
    w = 2.0 * WELL_HEIGHT
    return ((2.0 * w * f - 3.0 * w) * f + (w + 6.0)) * f - around + STRAIN_COUPLING * (m * (f - mean))


def chemistry(g, pad_ref, mob_ref, mobe_ref, ze_ref, chem_ref, cheme_ref, mean, spans, looped=False):
    nx = g.nx

    @functools.partial(each, nx + 2, looped)
    def _(p):
        for r, n in spread(spans, 0, 48) if not looped and p in (0, nx + 1) else spread(spans, 8, 32):
            f = pad_ref[p + 1, r:r + n, :]
            e = ze_ref[p, r:r + n, :]
            around = (pad_ref[p, r:r + n, :] + pad_ref[p + 2, r:r + n, :]
                      + pad_ref[p + 1, r - 1:r - 1 + n, :] + pad_ref[p + 1, r + 1:r + 1 + n, :]
                      + g.before(f, e) + g.after(f, e))
            chem_ref[p, r:r + n, :] = chem_of(f, mob_ref[p, r:r + n, :], around, mean)

    @functools.partial(each, nx, looped)
    def _(x):
        p = x + 1
        for r, n in spread(spans, 0, 48):
            f = pad_ref[p + 1, r:r + n, :]
            e = ze_ref[p, r:r + n, :]
            around = (ze_ref[p - 1, r:r + n, :] + ze_ref[p + 1, r:r + n, :]
                      + ze_ref[p, r - 1:r - 1 + n, :] + ze_ref[p, r + 1:r + 1 + n, :]
                      + g.before(e, f) + g.after(e, f))
            cheme_ref[x, r - OFF:r - OFF + n, :] = chem_of(
                e, mobe_ref[x, r - OFF:r - OFF + n, :], around, mean)


def flux_of(g, x, r, n, mob_ref, mobe_ref, chem_ref, cheme_ref):
    p = x + 1
    m = mob_ref[p, r:r + n, :]
    q = chem_ref[p, r:r + n, :]
    me = mobe_ref[x, r - OFF:r - OFF + n, :]
    qe = cheme_ref[x, r - OFF:r - OFF + n, :]
    total = None
    for nm, nq in (
        (mob_ref[p - 1, r:r + n, :], chem_ref[p - 1, r:r + n, :]),
        (mob_ref[p + 1, r:r + n, :], chem_ref[p + 1, r:r + n, :]),
        (mob_ref[p, r - 1:r - 1 + n, :], chem_ref[p, r - 1:r - 1 + n, :]),
        (mob_ref[p, r + 1:r + 1 + n, :], chem_ref[p, r + 1:r + 1 + n, :]),
        (g.before(m, me), g.before(q, qe)),
        (g.after(m, me), g.after(q, qe)),
    ):
        term = (nm + m) * (nq - q)
        total = term if total is None else total + term
    return m, 0.5 * total


def pack_edges(values, lane, nz):
    out = values[0]
    for x, v in enumerate(values[1:], 1):
        out = jnp.where(group(lane, x, nz, -1, 2), pltpu.roll(v, 32 * x, 1), out)
    return out


def step_a(ride_y, ride_z):
    def kernel(f_ref, amp_ref, lo_ref, hi_ref, yr_ref, zr_ref, yp_ref,
               f2_ref, a2_ref, ae2_ref, lo_out, hi_out, sum_ref,
               pad_ref, ze_ref, mob_ref, mobe_ref, chem_ref, cheme_ref):
        nx, ny, nz = f2_ref.shape
        end = OFF + ny
        g = Geometry(nx, ny, nz)
        mean = weighted_mean(yp_ref, yr_ref, zr_ref, ride_y, ride_z)
        fill(A_CODE, f_ref, lo_ref, hi_ref, yr_ref, zr_ref, pad_ref, ze_ref, [(0, ny)])

        def wear(p, r, n, a):
            m = a * a
            mob_ref[p, r:r + n, :] = m
            a2_ref[p, r:r + n, :] = worn(a, m, pad_ref[p + 1, r:r + n, :], mean)

        for r, n in chunks(0, ny, 48):
            wear(0, OFF + r, n, from_code(lo_ref[2 * ny + r:2 * ny + r + n, :], A_CODE))
            wear(nx + 1, OFF + r, n, from_code(hi_ref[2 * ny + r:2 * ny + r + n, :], A_CODE))
            edges = []
            for x in range(nx):
                wear(x + 1, OFF + r, n, amp_ref[x, r:r + n, :])
                p = x + 1
                a = pltpu.roll(zr_ref[p // 4, OFF + r:OFF + r + n, :], nz - 32 * (p % 4) - 16, 1)
                m = a * a
                mobe_ref[x, r:r + n, :] = m
                edges.append(worn(a, m, ze_ref[p, OFF + r:OFF + r + n, :], mean))
            ae2_ref[r:r + n, :] = pack_edges(edges, g.lane, nz)
        for x in range(nx):
            wear(x + 1, OFF - 1, 1, yr_ref[1, 10 + x:11 + x, :])
            wear(x + 1, end, 1, yr_ref[0, 10 + x:11 + x, :])
        chemistry(g, pad_ref, mob_ref, mobe_ref, ze_ref, chem_ref, cheme_ref, mean, [(0, ny)])
        top = jnp.zeros((8, nz), F32)
        bottom = jnp.zeros((8, nz), F32)
        for x in range(nx):
            for r, n in chunks(OFF, end, 48):
                _, flux = flux_of(g, x, r, n, mob_ref, mobe_ref, chem_ref, cheme_ref)
                f = pad_ref[x + 2, r:r + n, :] + TIME_STEP * flux
                s = slice(r - OFF, r - OFF + n)
                f2_ref[x, s, :] = f
                a = a2_ref[x + 1, r:r + n, :]
                m = a * a
                top = top + fold(m * f)
                bottom = bottom + fold(m)
                for near, far, out in ((0, 1, lo_out), (nx - 1, nx - 2, hi_out)):
                    if x == near:
                        out[s, :] = to_code(f, B_CODE)
                    if x == far:
                        out[r - OFF + ny:r - OFF + ny + n, :] = to_code(f, B_CODE)
        s = to_rows(top, bottom)
        sum_ref[...] = s
        lo_out[2 * ny:2 * ny + 16, :] = sum_digits(s)
        hi_out[2 * ny:2 * ny + 16, :] = sum_digits(s)
    return kernel


def potentials_b(g, mean, a2_ref, ae2_ref, others, scratch, spans, looped):
    f_ref, lo_ref, hi_ref, yr_ref, zr_ref = others
    pad_ref, ze_ref, mob_ref, mobe_ref, chem_ref, cheme_ref = scratch
    nx, nz = g.nx, g.nz
    fill(B_CODE, f_ref, lo_ref, hi_ref, yr_ref, zr_ref, pad_ref, ze_ref, spans)

    @functools.partial(each, nx + 2, looped)
    def _(p):
        for r, n in spread(spans, 8, 32):
            a = a2_ref[p, r:r + n, :]
            mob_ref[p, r:r + n, :] = a * a

    for r, n in spread(spans, 0, 48):
        a = ae2_ref[r - OFF:r - OFF + n, :]
        a = a * a
        for x in range(nx):
            mobe_ref[x, r - OFF:r - OFF + n, :] = pltpu.roll(a, nz - 32 * x, 1) if x else a
    chemistry(g, pad_ref, mob_ref, mobe_ref, ze_ref, chem_ref, cheme_ref, mean, spans, looped)


def finish_b(g, mean, x, r, n, labels, a2_ref, scratch):
    pad_ref, ze_ref, mob_ref, mobe_ref, chem_ref, cheme_ref = scratch
    m, flux = flux_of(g, x, r, n, mob_ref, mobe_ref, chem_ref, cheme_ref)
    f0 = pad_ref[x + 2, r:r + n, :]
    f = f0 + TIME_STEP * flux
    a = worn(a2_ref[x + 1, r:r + n, :], m, f0, mean)
    dmg = 1.0 - a * by_label(labels, tuple(1.0 / v for v in ROOTS))
    return flux, (f, dmg, a * a, by_label(labels, FACTORS))


def pool_rows(scr_ref, count, nz):
    zin = lax.broadcasted_iota(jnp.int32, (nz, nz), 0)
    out = lax.broadcasted_iota(jnp.int32, (nz, nz), 1)
    total = jnp.zeros((count, nz), F32)
    for i in range(4):
        rows = (scr_ref[i, pl.ds(0, count, stride=4), :] + scr_ref[i, pl.ds(1, count, stride=4), :]
                + scr_ref[i, pl.ds(2, count, stride=4), :] + scr_ref[i, pl.ds(3, count, stride=4), :])
        pick = jnp.where((zin // 4 == out // 4) & (out % 4 == i), 1.0 / 64.0, 0.0).astype(F32)
        total = total + jnp.dot(rows, pick, precision=lax.Precision.HIGHEST, preferred_element_type=F32)
    return total


def edge_b(ride_y, ride_z):
    def kernel(f_ref, a2_ref, ae2_ref, lo_ref, hi_ref, yr_ref, zr_ref, yp_ref, l_ref, edge_ref, *rest):
        *scratch, pool_scr = rest
        nx, ny, nz = f_ref.shape
        spans = [(0, 16), (ny - 16, ny)]
        g = Geometry(nx, ny, nz)
        mean = weighted_mean(yp_ref, yr_ref, zr_ref, ride_y, ride_z)
        potentials_b(g, mean, a2_ref, ae2_ref, (f_ref, lo_ref, hi_ref, yr_ref, zr_ref), scratch, spans, False)
        for k, (a, b) in enumerate(spans):
            s = slice(16 * k, 16 * k + 16)
            pooled = [None] * 4
            for x in range(nx):
                _, values = finish_b(g, mean, x, OFF + a, 16, l_ref[x, s, :], a2_ref, scratch)
                pooled = [v if p is None else p + v for p, v in zip(pooled, values)]
            for i in range(4):
                pool_scr[i, s, :] = pooled[i]
        total = pool_rows(pool_scr, 8, nz)
        blank = jnp.zeros((13, nz), F32)
        edge_ref[0] = jnp.concatenate([total[0:3], blank]).astype(BF16)
        edge_ref[1] = jnp.concatenate([total[5:8], blank]).astype(BF16)
    return kernel


def step_b(ride_y, ride_z):
    def kernel(f_ref, a2_ref, ae2_ref, lo_ref, hi_ref, yr_ref, zr_ref, yp_ref, l_hbm,
               f3_hbm, dmg_hbm, flux_hbm, pool_ref, *rest):
        *scratch, pool_scr, l_ref, f3_ref, dmg_ref, flux_ref, l_sem, sems = rest
        nx, ny, nz = f_ref.shape
        labels_in = pltpu.make_async_copy(l_hbm, l_ref, l_sem)
        labels_in.start()
        g = Geometry(nx, ny, nz)
        mean = weighted_mean(yp_ref, yr_ref, zr_ref, ride_y, ride_z)
        potentials_b(g, mean, a2_ref, ae2_ref, (f_ref, lo_ref, hi_ref, yr_ref, zr_ref), scratch, [(0, ny)], True)
        labels_in.wait()
        outs = ((f3_ref, f3_hbm), (dmg_ref, dmg_hbm), (flux_ref, flux_hbm))

        def out_copy(i, x):
            return pltpu.make_async_copy(outs[i][0].at[x], outs[i][1].at[x], sems.at[i, x])

        pool_scr[...] = jnp.zeros(pool_scr.shape, F32)

        @functools.partial(each, nx, True)
        def _(x):
            for r, n in chunks(OFF, OFF + ny, 48):
                s = slice(r - OFF, r - OFF + n)
                flux, values = finish_b(g, mean, x, r, n, l_ref[x, s, :], a2_ref, scratch)
                f3_ref[x, s, :] = values[0]
                dmg_ref[x, s, :] = values[1]
                flux_ref[x, s, :] = flux
                for i in range(4):
                    pool_scr[i, s, :] = pool_scr[i, s, :] + values[i]
            for i in range(3):
                out_copy(i, x).start()

        pool_ref[...] = pool_rows(pool_scr, ny // 4, nz).astype(BF16)
        for x in range(nx):
            for i in range(3):
                out_copy(i, x).wait()
    return kernel


def ring(axis, shift):
    count = lax.axis_size(axis)
    return [(i, (i + shift) % count) for i in range(count)]


def pair_sum(s, axis):
    count = lax.axis_size(axis)
    if count & (count - 1):
        return lax.psum(s, axis)
    bit = 1
    while bit < count:
        s = s + lax.ppermute(s, axis, [(i, i ^ bit) for i in range(count)])
        bit *= 2
    return s


def both_sides(pay, axis):
    if lax.axis_size(axis) == 2:
        return lax.ppermute(pay, axis, ring(axis, 1))
    return jnp.stack([lax.ppermute(pay[0], axis, ring(axis, -1)), lax.ppermute(pay[1], axis, ring(axis, 1))])


def z_neighbour(pay, axis, packed=True):
    if lax.axis_size(axis) == 2:
        return lax.ppermute(pay, axis, ring(axis, 1))
    above = lax.ppermute(pay, axis, ring(axis, -1))
    below = lax.ppermute(pay, axis, ring(axis, 1))
    lane = lax.broadcasted_iota(jnp.int32, pay.shape, pay.ndim - 1)
    if packed:
        low = (lane % 32 < 8) | (lane % 32 == 16)
    else:
        low = lane < pay.shape[-1] // 2
    return jnp.where(low, above, below)


def x_sides(lo, hi):
    return lax.ppermute(hi, "gx", ring("gx", 1)), lax.ppermute(lo, "gx", ring("gx", -1))


def body(concentration, damage, labels, w_first, b_first, w_second, b_second, w_third, b_third):
    nx, ny, nz = concentration.shape
    rows = ny + 2 * OFF
    block = (nx, ny, nz)
    padded = (nx + 2, rows, nz)
    ride_x = lax.axis_size("gx") == 4
    ride_y = lax.axis_size("gy") == 2
    ride_z = lax.axis_size("gz") == 2
    packed = (-(-(nx + 2) // 4), rows, nz)
    assert nz == 128
    scratch = [pltpu.VMEM((nx + 4, rows, nz), F32), pltpu.VMEM(padded, F32), pltpu.VMEM(padded, F32),
               pltpu.VMEM(block, F32), pltpu.VMEM(padded, F32), pltpu.VMEM(block, F32)]

    def start(sums):
        if ride_x:
            return sums, lax.ppermute(sums, "gx", ring("gx", 2))
        sums = pair_sum(sums, "gx")
        for axis, ride in (("gy", ride_y), ("gz", ride_z)):
            if not ride:
                sums = pair_sum(sums, axis)
        return sums, sums

    concentration, damage, labels = (
        pltpu.with_memory_space_constraint(v, pltpu.HBM) for v in (concentration, damage, labels))
    tall = 3 * ny + 16
    f, amp, lo, hi, sums, edge_labels = call(
        first_kernel,
        [(block, F32), (block, F32), ((tall, nz), I16), ((tall, nz), I16), ((8, nz), F32),
         ((nx, 32, nz), jnp.int32)],
        concentration, damage, labels,
        in_specs=[HBM] * 3,
        scratch=[pltpu.VMEM(block, F32), pltpu.VMEM(block, jnp.int32), pltpu.SemaphoreType.DMA((3, nx))])
    weights = weight_rows(w_first, w_second, w_third) + (b_third[None],)
    sums, far = start(sums)
    lo, hi = x_sides(lo, hi)
    (ypay,) = call(edge_rows(A_CODE, ride_x, True), [((2, 24, nz), F32)], f, amp, lo, hi, sums, far, *weights)
    yr = both_sides(ypay, "gy")
    (zpay,) = call(pack_z(A_CODE, ride_y, True), [(packed, F32)], f, amp, lo, hi, yr, ypay)
    zr = z_neighbour(zpay, "gz")
    tall = 2 * ny + 16
    f, a2, ae2, lo, hi, sums = call(
        step_a(ride_y, ride_z),
        [(block, F32), (padded, F32), ((ny, nz), F32), ((tall, nz), I16), ((tall, nz), I16), ((8, nz), F32)],
        f, amp, lo, hi, yr, zr, ypay, scratch=scratch)

    sums, far = start(sums)
    lo, hi = x_sides(lo, hi)
    (ypay,) = call(edge_rows(B_CODE, ride_x, False), [((2, 24, nz), F32)], f, lo, hi, sums, far)
    yr = both_sides(ypay, "gy")
    (zpay,) = call(pack_z(B_CODE, ride_y, False), [(packed, F32)], f, lo, hi, yr, ypay)
    zr = z_neighbour(zpay, "gz")
    last = (f, a2, ae2, lo, hi, yr, zr, ypay)
    (edge,) = call(
        edge_b(ride_y, ride_z), [((2, 16, nz), BF16)], *last, edge_labels,
        scratch=scratch + [pltpu.VMEM((4, 32, nz), F32)])
    fraction, damage_field, flux_sum, pooled = call(
        step_b(ride_y, ride_z),
        [(block, F32), (block, F32), (block, F32), ((ny // 4, nz), BF16)], *last, labels,
        in_specs=[VMEM] * 8 + [HBM], out_specs=[HBM] * 3 + [VMEM],
        scratch=scratch + [
            pltpu.VMEM((4, ny, nz), F32), pltpu.VMEM(block, jnp.int32),
            pltpu.VMEM(block, F32), pltpu.VMEM(block, F32), pltpu.VMEM(block, F32),
            pltpu.SemaphoreType.DMA, pltpu.SemaphoreType.DMA((3, nx))])
    ids = jnp.broadcast_to(jnp.stack([lax.axis_index(a) for a in ("gx", "gy", "gz")])[:, None], (3, nz))
    crack_score = detector(pooled, edge, ids, weights + (b_first[None], b_second[None]), ny // 4, nz // 4)
    return (fraction, damage_field, flux_sum, crack_score)


CH = 16
CIN = 4
TOP = 8


def iota(shape, dim):
    return lax.broadcasted_iota(jnp.int32, shape, dim)


def lanes_for(n):
    return -(-n // 128) * 128


def one_hot(mask):
    return jnp.where(mask, 1.0, 0.0).astype(BF16)


def mm(a, b):
    return jnp.dot(a, b, preferred_element_type=F32)


SHIFTS = tuple(k for k in range(-3, 10) if k % (16 // CIN) == 3)


def weight_kernel(w1_ref, w2_ref, w3_ref, b3_ref, b1_ref, b2_ref, plane_ref, t1_ref, t2_ref, t3_ref, bias_ref):
    n1 = bias_ref.shape[1]
    pz = 128 // CIN
    spread = one_hot(iota((CH, 128), 1) % CH == iota((CH, 128), 0))
    tile1 = mm(w1_ref[...], spread)
    tile2 = mm(w2_ref[...], spread)
    tile3 = mm(w3_ref[...], one_hot(iota((3, 128), 1) // pz == iota((3, 128), 0)))
    step1 = iota((16, 128), 0) // CIN - iota((16, 128), 1) // CH
    step2 = -(iota((16, 128), 1) // CH)
    step3 = -(iota((16, 128), 1) % pz)

    def tile(source, base, stride, step, shift):
        out = jnp.zeros((16, 128), F32)
        for l in range(3):
            k = base + stride * l
            out = jnp.where(step + shift == l, source[16 * k:16 * k + 16], out)
        return out.astype(BF16)

    zero = jnp.zeros((16, 128), BF16)
    bias_ref[...] = jnp.broadcast_to(b3_ref[...], bias_ref.shape)
    for i in range(3):
        for j in range(3):
            tap = 9 * i + 3 * j
            known = {k: tile(tile1, tap, 1, step1, k) for k in SHIFTS}
            places = [(j * 128 + rb * 16, rb * 16 // CIN) for rb in range(8)]
            places += [(384 + 32 * j, pz), (384 + (32 * j - 16) % 128, -16 // CIN)]
            for row, z_in in places:
                for cb in range(n1 // 128):
                    t1_ref[i, row:row + 16, cb * 128:(cb + 1) * 128] = known.get(z_in - cb * 8 + 3, zero)
            for rb in range(10):
                row = j * 128 + rb * 16 if rb < 8 else 384 + 32 * j + (rb - 8) * 16
                t2_ref[i, row:row + 16, :] = tile(tile2, tap, 1, step2, rb)
        for row in (464, 480):
            for cb in range(n1 // 128):
                t1_ref[i, row:row + 16, cb * 128:(cb + 1) * 128] = zero
        for row in (480, 496):
            t2_ref[i, row:row + 16, :] = zero
        for rb in range(t3_ref.shape[1] // 16):
            t3_ref[i, rb * 16:rb * 16 + 16, :] = tile(tile3, 3 * i, 1, step3, rb) if rb < pz + 2 else zero
    wide = one_hot(iota((CH, n1), 1) % CH == iota((CH, n1), 0)).astype(F32)
    for k, ref in ((0, b1_ref), (1, b2_ref)):
        bias_ref[k:k + 1, :] = jnp.dot(ref[...], wide, precision=lax.Precision.HIGHEST, preferred_element_type=F32)


def weight_rows(w_first, w_second, w_third):
    return (jnp.tile(jnp.swapaxes(w_first, 1, 2), (1, 16 // CIN, 1)).reshape(27 * 16, CH),
            jnp.swapaxes(w_second, 1, 2).reshape(27 * CH, CH),
            w_third.reshape(3, 3, 3, CH).transpose(0, 2, 3, 1).reshape(9 * CH, 3))


def gelu(x):
    return 0.5 * x * (1.0 + jnp.tanh(0.7978845608028654 * (x + 0.044715 * (x * x * x))))


def plane_kernel(py, y_count):
    def kernel(ids_ref, pool_ref, yr_ref, out_ref, scr_ref):
        iy = ids_ref[1:2, 0:1]
        scr_ref[...] = jnp.zeros(scr_ref.shape, F32)
        scr_ref[TOP:TOP + py, :] = pool_ref[0:py, :].astype(F32)
        below = yr_ref[1].astype(F32)[0:3]
        above = yr_ref[0].astype(F32)[0:3]
        scr_ref[TOP - 3:TOP, :] = jnp.where(iy > 0, below, 0.0)
        scr_ref[TOP + py:TOP + py + 3, :] = jnp.where(iy < y_count - 1, above, 0.0)
        out_ref[...] = scr_ref[...].astype(BF16)
    return kernel


def conv_kernel(py, counts, shifts):
    x_count, y_count, z_count = counts
    n = len(shifts)

    def kernel(*refs):
        ids_ref = refs[0]
        own = refs[1:2 + n]
        other = refs[2 + n:3 + 2 * n]
        t1_ref, t2_ref, t3_ref, bias_ref, out_ref = refs[3 + 2 * n:8 + 2 * n]
        in_ref, beside_ref, lhs1_ref, act1_ref, lhs2_ref, act2_ref, tail_ref = refs[8 + 2 * n:]
        ix, iy, iz = ids_ref[0:1, 0:1], ids_ref[1:2, 0:1], ids_ref[2:3, 0:1]
        half = own[0].shape[1]
        pz = half // CIN
        rows = py + 4
        z_row = iota((1, half), 1) // CIN
        z_ok = ((z_row < pz // 2) & (iz < z_count - 1)) | ((z_row >= pz // 2) & (iz > 0))
        for w in range(7):
            o = w - 3
            k = 0 if o == 0 else 1 + shifts.index((-o) % x_count) if (-o) % x_count in shifts else None
            if k is None:
                in_ref[w] = jnp.zeros(in_ref.shape[1:], F32)
                beside_ref[w] = jnp.zeros(in_ref.shape[1:], F32)
                continue
            inside = (ix + o >= 0) & (ix + o < x_count)
            in_ref[w] = jnp.where(inside, own[k][...].astype(F32), 0.0)
            beside_ref[w] = jnp.where(z_ok & inside, other[k][...].astype(F32), 0.0)
        lane = iota((1, 128), 1)

        def shared(parts, first, count):
            out = parts[0]
            for j in (1, 2):
                out = jnp.where(group(lane, j, 128, first, count), pltpu.roll(parts[j], 32 * j, 1), out)
            return out.astype(BF16)

        for w in range(7):
            starts = [TOP - 3 + j for j in range(3)]
            for j, r in enumerate(starts):
                lhs1_ref[w, :, j * 128:(j + 1) * 128] = in_ref[w, r:r + rows, :].astype(BF16)
            lhs1_ref[w, :, 384:512] = shared([beside_ref[w, r:r + rows, :] for r in starts], -3 * CIN, 6 * CIN)
        out = None
        for i in range(3):
            part = mm(lhs1_ref[i:i + 5].reshape(5 * rows, 512), t1_ref[i])
            out = part if out is None else out + part
        width = out.shape[1]
        y = iota((rows, width), 0) - 2
        z = iota((rows, width), 1) // CH - 2
        ok = (z < pz + 2) & ((y >= 0) | (iy > 0)) & ((y < py) | (iy < y_count - 1))
        ok = ok & ((z >= 0) | (iz > 0)) & ((z < pz) | (iz < z_count - 1))
        for p in range(5):
            a = gelu(out[p * rows:(p + 1) * rows] + bias_ref[0:1, :])
            good = ok & (ix + p - 2 >= 0) & (ix + p - 2 < x_count)
            act1_ref[p, 0:rows, 0:width] = jnp.where(good, a, 0.0)
            act1_ref[p, rows:, 0:width] = jnp.zeros((act1_ref.shape[1] - rows, width), F32)
            act1_ref[p, :, width:] = jnp.zeros((act1_ref.shape[1], act1_ref.shape[2] - width), F32)
        blocks = lhs2_ref.shape[1]
        for p in range(5):
            for b in range(blocks):
                for j in range(3):
                    lhs2_ref[p, b, :, j * 128:(j + 1) * 128] = (
                        act1_ref[p, j:j + rows, b * 128:(b + 1) * 128].astype(BF16))
                following = slice((b + 1) * 128, (b + 2) * 128)
                lhs2_ref[p, b, :, 384:512] = shared([act1_ref[p, j:j + rows, following] for j in range(3)], 0, 32)
        out = None
        for i in range(3):
            part = mm(lhs2_ref[i:i + 3].reshape(3 * blocks * rows, 512), t2_ref[i])
            out = part if out is None else out + part
        for b in range(blocks):
            y = iota((rows, 128), 0) - 1
            z = (iota((rows, 128), 1) + b * 128) // CH - 1
            ok = (z < pz + 1) & (y <= py) & ((y >= 0) | (iy > 0)) & ((y < py) | (iy < y_count - 1))
            ok = ok & ((z >= 0) | (iz > 0)) & ((z < pz) | (iz < z_count - 1))
            for p in range(3):
                s = (p * blocks + b) * rows
                a = gelu(out[s:s + rows] + bias_ref[1:2, 0:128])
                good = ok & (ix + p - 1 >= 0) & (ix + p - 1 < x_count)
                act2_ref[p, :, b * 128:(b + 1) * 128] = jnp.where(good, a, 0.0).astype(BF16)
        out = None
        for i in range(3):
            part = mm(act2_ref[i], t3_ref[i])
            out = part if out is None else out + part
        tail_ref[0:rows, :] = out
        score = tail_ref[0:py, :]
        for j in (1, 2):
            score = score + pltpu.roll(tail_ref[j:j + py, :], 128 - j * pz, 1)
        out_ref[0] = jnp.transpose(score)[0:pz, :] + bias_ref[2:3, 0:1]
    return kernel


def detector(pooled, edge, ids, weights, py, pz):
    counts = tuple(lax.axis_size(a) for a in ("gx", "gy", "gz"))
    half = pooled.shape[1]
    assert half == 128 and pz * CIN == half and pz * 3 <= 128
    rows = py + 4
    width = lanes_for((pz + 4) * CH)
    blocks = width // 128
    yr = both_sides(edge, "gy")
    tall = -(-(TOP + py + 3) // 16) * 16
    (plane,) = call(
        plane_kernel(py, counts[1]), [((tall, half), BF16)], ids, pooled, yr,
        scratch=[pltpu.VMEM((tall, half), F32)])
    shifts = []
    for s in (1, -1, 2, -2, 3, -3):
        if s % counts[0] and s % counts[0] not in shifts:
            shifts.append(s % counts[0])
    own = [plane] + [lax.ppermute(plane, "gx", ring("gx", s)) for s in shifts]
    matrices = call(
        weight_kernel,
        [((3, 512, width), BF16), ((3, 512, 128), BF16), ((3, width, 128), BF16), ((8, width), F32)],
        *weights, plane)
    own[-1], *matrices = lax.optimization_barrier((own[-1], *matrices))
    other = [z_neighbour(v, "gz", False) for v in own]
    args = (ids, *own, *other, *matrices)
    (score,) = call(
        conv_kernel(py, counts, shifts), [((1, pz, py), F32)], *args,
        scratch=[
            pltpu.VMEM((7, tall, half), F32),
            pltpu.VMEM((7, tall, half), F32),
            pltpu.VMEM((7, rows, 512), BF16),
            pltpu.VMEM((5, rows + 8, width + 128), F32),
            pltpu.VMEM((5, blocks, rows, 512), BF16),
            pltpu.VMEM((3, rows, width), BF16),
            pltpu.VMEM((rows + 8, 128), F32),
        ], mib=32)
    return jnp.swapaxes(score, 1, 2)


def solution(mesh):
    slab = P(("groups", "gx"), "gy", "gz")
    return jax.shard_map(
        body,
        mesh=mesh,
        in_specs=(slab, slab, slab, P(), P(), P(), P(), P(), P()),
        out_specs=(slab, slab, slab, slab),
        check_vma=False,
    )
```

```python
import functools

import jax
import jax.numpy as jnp
import numpy as np
from jax import lax
from jax.experimental import pallas as pl
from jax.experimental.pallas import tpu as pltpu
from jax.sharding import PartitionSpec as P

F32 = jnp.float32
BF16 = jnp.bfloat16
I16 = jnp.int16
WELL_HEIGHT = 1.0
STRAIN_COUPLING = 4.0
TIME_STEP = 0.01
DAMAGE_RATE = 0.8
ENERGY_CRITICAL = 0.02

OFF = 16
A_CODE = (0.0, 1.0)
B_CODE = (-1.1, 3.1)
SUM_LOW, SUM_SPAN = -1280.0, 4096.0

VMEM = pl.BlockSpec(memory_space=pltpu.VMEM)
HBM = pl.BlockSpec(memory_space=pltpu.HBM)


def to_code(x, code):
    low, span = code
    v = (x - low) * (65535.0 / span) - 32768.0
    return jnp.clip(jnp.round(v), -32768.0, 32767.0).astype(jnp.int32).astype(I16)


def from_code(q, code):
    low, span = code
    return q.astype(jnp.int32).astype(F32) * (span / 65535.0) + (low + 32768.0 * span / 65535.0)


def sum_digits(s):
    v = (s[0:2] - SUM_LOW) * (65536.0 / SUM_SPAN)
    high = jnp.floor(v)
    low = jnp.minimum(jnp.floor((v - high) * 65536.0), 65535.0)
    rows = jnp.concatenate([high, low, jnp.full((12, s.shape[1]), 32768.0, F32)]) - 32768.0
    return rows.astype(jnp.int32).astype(I16)


def from_digits(tile):
    v = tile.astype(jnp.int32).astype(F32) + 32768.0
    return (v[0:2] + v[2:4] * (1.0 / 65536.0)) * (SUM_SPAN / 65536.0) + SUM_LOW


def each(count, looped, body):
    def step(i, carry):
        body(i)
        return carry
    if looped:
        lax.fori_loop(0, count, step, 0)
    else:
        for i in range(count):
            body(i)


def by_label(labels, values):
    return jnp.where(labels == 0, values[0], jnp.where(labels == 1, values[1], values[2])).astype(F32)


FACTORS = (1.0, 0.3, 0.05)
ROOTS = tuple(float(np.sqrt(np.float32(v))) for v in FACTORS)


def call(kernel, outs, *args, in_specs=None, out_specs=None, scratch=(), mib=16):
    return pl.pallas_call(
        kernel,
        in_specs=in_specs or [VMEM] * len(args),
        out_specs=out_specs or [VMEM] * len(outs),
        out_shape=[jax.ShapeDtypeStruct(s, t) for s, t in outs],
        scratch_shapes=scratch,
        compiler_params=pltpu.CompilerParams(vmem_limit_bytes=mib * 1024 * 1024),
    )(*args)


def chunks(start, stop, size):
    return [(r, min(size, stop - r)) for r in range(start, stop, size)]


def fold(x):
    return x.reshape(x.shape[0] // 8, 8, x.shape[1]).sum(0)


def to_rows(top, bottom):
    return jnp.concatenate([jnp.sum(top, 0, keepdims=True), jnp.sum(bottom, 0, keepdims=True),
                            jnp.zeros((6, top.shape[1]), F32)])


def first_kernel(c_hbm, d_hbm, l_hbm, f_ref, amp_ref, lo_ref, hi_ref, sum_ref, le_ref, d_ref, l_ref, sems):
    nx, ny, nz = f_ref.shape
    order = [0, nx - 1] + list(range(1, nx - 1))
    copies = []
    for x in order:
        copies.append([pltpu.make_async_copy(src.at[x], dst.at[x], sems.at[k, x])
                       for k, (src, dst) in enumerate(((c_hbm, f_ref), (d_hbm, d_ref), (l_hbm, l_ref)))])
        for c in copies[-1]:
            c.start()
    top = jnp.zeros((8, nz), F32)
    bottom = jnp.zeros((8, nz), F32)
    for k, x in enumerate(order):
        for c in copies[k]:
            c.wait()
        le_ref[x, 0:16, :] = l_ref[x, 0:16, :]
        le_ref[x, 16:32, :] = l_ref[x, ny - 16:ny, :]
        for r, n in chunks(0, ny, 48):
            f = f_ref[x, r:r + n, :]
            a = by_label(l_ref[x, r:r + n, :], ROOTS) * (1.0 - d_ref[x, r:r + n, :])
            amp_ref[x, r:r + n, :] = a
            m = a * a
            top = top + fold(m * f)
            bottom = bottom + fold(m)
            for near, far, out in ((0, 1, lo_ref), (nx - 1, nx - 2, hi_ref)):
                if x == near:
                    out[r:r + n, :] = to_code(f, A_CODE)
                    out[2 * ny + r:2 * ny + r + n, :] = to_code(a, A_CODE)
                if x == far:
                    out[ny + r:ny + r + n, :] = to_code(f, A_CODE)
    s = to_rows(top, bottom)
    sum_ref[...] = s
    lo_ref[3 * ny:3 * ny + 16, :] = sum_digits(s)
    hi_ref[3 * ny:3 * ny + 16, :] = sum_digits(s)


def edge_rows(code, ride_x, with_amp):
    def kernel(*refs):
        f_ref = refs[0]
        amp_ref = refs[1] if with_amp else None
        lo_ref, hi_ref, s_ref, far_ref = refs[1 + with_amp:5 + with_amp]
        out_ref = refs[-1]
        nx, ny, nz = f_ref.shape
        low_rows = [from_code(r[0:16, :], code)[0:1] for r in (lo_ref, hi_ref)]
        high_rows = [from_code(r[ny - 16:ny, :], code)[15:16] for r in (lo_ref, hi_ref)]
        s = s_ref[...]
        if ride_x:
            s = s + far_ref[...]
        for side, first, second, beside in ((0, 0, 1, low_rows), (1, ny - 1, ny - 2, high_rows)):
            for x in range(nx):
                out_ref[side, 2 * x:2 * x + 1, :] = f_ref[x, first:first + 1, :]
                out_ref[side, 2 * x + 1:2 * x + 2, :] = f_ref[x, second:second + 1, :]
                if amp_ref is not None:
                    out_ref[side, 10 + x:11 + x, :] = amp_ref[x, first:first + 1, :]
            out_ref[side, 8:9, :] = beside[0]
            out_ref[side, 9:10, :] = beside[1]
            out_ref[side, 16:24, :] = s
            if ride_x:
                out_ref[side, 16:18, :] = (s[0:2] + from_digits(lo_ref[lo_ref.shape[0] - 16:, :])
                                           + from_digits(hi_ref[hi_ref.shape[0] - 16:, :]))
    return kernel


def group(lane, j, nz, first, count):
    return (lane - (32 * j + first)) % nz < count


def pack_z(code, ride_y, with_amp):
    def kernel(*refs):
        f_ref = refs[0]
        amp_ref = refs[1] if with_amp else None
        lo_ref, hi_ref, yr_ref, yp_ref, out_ref = refs[1 + with_amp:]
        nx, ny, nz = f_ref.shape
        end = OFF + ny
        lane = lax.broadcasted_iota(jnp.int32, (1, nz), 1)
        for k in range(out_ref.shape[0]):
            planes = [p for p in range(4 * k, 4 * k + 4) if p < nx + 2]

            def packed(f_of, a_of, ps):
                out = None
                for p in ps:
                    j = p % 4
                    f = f_of(p)
                    f = pltpu.roll(f, 32 * j, 1) if j else f
                    out = f if out is None else jnp.where(group(lane, j, nz, -2, 4), f, out)
                    a = a_of(p)
                    if a is not None:
                        out = jnp.where(group(lane, j, nz, 15, 2), pltpu.roll(a, 32 * j + 16, 1), out)
                return out

            for r, n in chunks(0, ny, 48):
                def f_of(p):
                    if p == 0:
                        return from_code(lo_ref[r:r + n, :], code)
                    if p == nx + 1:
                        return from_code(hi_ref[r:r + n, :], code)
                    return f_ref[p - 1, r:r + n, :]

                def a_of(p):
                    return amp_ref[p - 1, r:r + n, :] if with_amp and 1 <= p <= nx else None

                out_ref[k, OFF + r:OFF + r + n, :] = packed(f_of, a_of, planes)
            inner = [p for p in planes if 1 <= p <= nx]
            if inner:
                for side, near in ((1, OFF - 1), (0, end)):
                    out_ref[k, near:near + 1, :] = packed(
                        lambda p: yr_ref[side, 2 * (p - 1):2 * (p - 1) + 1, :], lambda p: None, inner)
        s = yp_ref[0, 16:24, :]
        out_ref[0, 0:8, :] = s + yr_ref[0, 16:24, :] if ride_y else s
    return kernel


def spread(spans, extra, size):
    return [v for a, b in spans for v in chunks(OFF + a - extra, OFF + b + extra, size)]


def fill(code, f_ref, lo_ref, hi_ref, yr_ref, zr_ref, pad_ref, ze_ref, spans):
    nx, ny, nz = f_ref.shape
    end = OFF + ny
    wide = [v for a, b in spans for v in chunks(max(a - 16, 0), min(b + 16, ny), 48)]
    for near, far, ref in ((1, 0, lo_ref), (nx + 2, nx + 3, hi_ref)):
        for r, n in wide:
            pad_ref[near, OFF + r:OFF + r + n, :] = from_code(ref[r:r + n, :], code)
            pad_ref[far, OFF + r:OFF + r + n, :] = from_code(ref[ny + r:ny + r + n, :], code)
    for p, k in ((1, 8), (nx + 2, 9)):
        pad_ref[p, OFF - 1:OFF, :] = yr_ref[1, k:k + 1, :]
        pad_ref[p, end:end + 1, :] = yr_ref[0, k:k + 1, :]
    for x in range(nx):
        for r, n in wide:
            pad_ref[x + 2, OFF + r:OFF + r + n, :] = f_ref[x, r:r + n, :]
        for side, near, far in ((1, OFF - 1, OFF - 2), (0, end, end + 1)):
            pad_ref[x + 2, near:near + 1, :] = yr_ref[side, 2 * x:2 * x + 1, :]
            pad_ref[x + 2, far:far + 1, :] = yr_ref[side, 2 * x + 1:2 * x + 2, :]
    for p in range(nx + 2):
        for r, n in spread(spans, 8, 32):
            e = zr_ref[p // 4, r:r + n, :]
            ze_ref[p, r:r + n, :] = pltpu.roll(e, nz - 32 * (p % 4), 1) if p % 4 else e


def weighted_mean(yp_ref, yr_ref, zr_ref, ride_y, ride_z):
    s = yp_ref[0, 16:24, :]
    if ride_y:
        s = s + yr_ref[0, 16:24, :]
    if ride_z:
        s = s + zr_ref[0, 0:8, :]
    return jnp.sum(s[0:1], keepdims=True) / jnp.sum(s[1:2], keepdims=True)


def worn(a, m, f, mean):
    e = f - mean
    loss = DAMAGE_RATE * 0.5 * STRAIN_COUPLING * (m * (e * e)) - DAMAGE_RATE * ENERGY_CRITICAL
    return a * (1.0 - jnp.maximum(loss, 0.0))


class Geometry:
    def __init__(self, nx, ny, nz):
        self.nx, self.ny, self.nz = nx, ny, nz
        self.lane = lax.broadcasted_iota(jnp.int32, (1, nz), 1)
        self.first = self.lane == 0
        self.last = self.lane == nz - 1

    def before(self, own, other):
        return pltpu.roll(jnp.where(self.last, other, own), 1, 1)

    def after(self, own, other):
        return pltpu.roll(jnp.where(self.first, other, own), self.nz - 1, 1)


def chem_of(f, m, around, mean):
    w = 2.0 * WELL_HEIGHT
    return ((2.0 * w * f - 3.0 * w) * f + (w + 6.0)) * f - around + STRAIN_COUPLING * (m * (f - mean))


def chemistry(g, pad_ref, mob_ref, mobe_ref, ze_ref, chem_ref, cheme_ref, mean, spans, looped=False):
    nx = g.nx

    @functools.partial(each, nx + 2, looped)
    def _(p):
        for r, n in spread(spans, 0, 48) if not looped and p in (0, nx + 1) else spread(spans, 8, 32):
            f = pad_ref[p + 1, r:r + n, :]
            e = ze_ref[p, r:r + n, :]
            around = (pad_ref[p, r:r + n, :] + pad_ref[p + 2, r:r + n, :]
                      + pad_ref[p + 1, r - 1:r - 1 + n, :] + pad_ref[p + 1, r + 1:r + 1 + n, :]
                      + g.before(f, e) + g.after(f, e))
            chem_ref[p, r:r + n, :] = chem_of(f, mob_ref[p, r:r + n, :], around, mean)

    @functools.partial(each, nx, looped)
    def _(x):
        p = x + 1
        for r, n in spread(spans, 0, 48):
            f = pad_ref[p + 1, r:r + n, :]
            e = ze_ref[p, r:r + n, :]
            around = (ze_ref[p - 1, r:r + n, :] + ze_ref[p + 1, r:r + n, :]
                      + ze_ref[p, r - 1:r - 1 + n, :] + ze_ref[p, r + 1:r + 1 + n, :]
                      + g.before(e, f) + g.after(e, f))
            cheme_ref[x, r - OFF:r - OFF + n, :] = chem_of(
                e, mobe_ref[x, r - OFF:r - OFF + n, :], around, mean)


def flux_of(g, x, r, n, mob_ref, mobe_ref, chem_ref, cheme_ref):
    p = x + 1
    m = mob_ref[p, r:r + n, :]
    q = chem_ref[p, r:r + n, :]
    me = mobe_ref[x, r - OFF:r - OFF + n, :]
    qe = cheme_ref[x, r - OFF:r - OFF + n, :]
    total = None
    for nm, nq in (
        (mob_ref[p - 1, r:r + n, :], chem_ref[p - 1, r:r + n, :]),
        (mob_ref[p + 1, r:r + n, :], chem_ref[p + 1, r:r + n, :]),
        (mob_ref[p, r - 1:r - 1 + n, :], chem_ref[p, r - 1:r - 1 + n, :]),
        (mob_ref[p, r + 1:r + 1 + n, :], chem_ref[p, r + 1:r + 1 + n, :]),
        (g.before(m, me), g.before(q, qe)),
        (g.after(m, me), g.after(q, qe)),
    ):
        term = (nm + m) * (nq - q)
        total = term if total is None else total + term
    return m, 0.5 * total


def pack_edges(values, lane, nz):
    out = values[0]
    for x, v in enumerate(values[1:], 1):
        out = jnp.where(group(lane, x, nz, -1, 2), pltpu.roll(v, 32 * x, 1), out)
    return out


def step_a(ride_y, ride_z):
    def kernel(f_ref, amp_ref, lo_ref, hi_ref, yr_ref, zr_ref, yp_ref,
               f2_ref, a2_ref, ae2_ref, lo_out, hi_out, sum_ref,
               pad_ref, ze_ref, mob_ref, mobe_ref, chem_ref, cheme_ref):
        nx, ny, nz = f2_ref.shape
        end = OFF + ny
        g = Geometry(nx, ny, nz)
        mean = weighted_mean(yp_ref, yr_ref, zr_ref, ride_y, ride_z)
        fill(A_CODE, f_ref, lo_ref, hi_ref, yr_ref, zr_ref, pad_ref, ze_ref, [(0, ny)])

        def wear(p, r, n, a):
            m = a * a
            mob_ref[p, r:r + n, :] = m
            a2_ref[p, r:r + n, :] = worn(a, m, pad_ref[p + 1, r:r + n, :], mean)

        for r, n in chunks(0, ny, 48):
            wear(0, OFF + r, n, from_code(lo_ref[2 * ny + r:2 * ny + r + n, :], A_CODE))
            wear(nx + 1, OFF + r, n, from_code(hi_ref[2 * ny + r:2 * ny + r + n, :], A_CODE))
            edges = []
            for x in range(nx):
                wear(x + 1, OFF + r, n, amp_ref[x, r:r + n, :])
                p = x + 1
                a = pltpu.roll(zr_ref[p // 4, OFF + r:OFF + r + n, :], nz - 32 * (p % 4) - 16, 1)
                m = a * a
                mobe_ref[x, r:r + n, :] = m
                edges.append(worn(a, m, ze_ref[p, OFF + r:OFF + r + n, :], mean))
            ae2_ref[r:r + n, :] = pack_edges(edges, g.lane, nz)
        for x in range(nx):
            wear(x + 1, OFF - 1, 1, yr_ref[1, 10 + x:11 + x, :])
            wear(x + 1, end, 1, yr_ref[0, 10 + x:11 + x, :])
        chemistry(g, pad_ref, mob_ref, mobe_ref, ze_ref, chem_ref, cheme_ref, mean, [(0, ny)])
        top = jnp.zeros((8, nz), F32)
        bottom = jnp.zeros((8, nz), F32)
        for x in range(nx):
            for r, n in chunks(OFF, end, 48):
                _, flux = flux_of(g, x, r, n, mob_ref, mobe_ref, chem_ref, cheme_ref)
                f = pad_ref[x + 2, r:r + n, :] + TIME_STEP * flux
                s = slice(r - OFF, r - OFF + n)
                f2_ref[x, s, :] = f
                a = a2_ref[x + 1, r:r + n, :]
                m = a * a
                top = top + fold(m * f)
                bottom = bottom + fold(m)
                for near, far, out in ((0, 1, lo_out), (nx - 1, nx - 2, hi_out)):
                    if x == near:
                        out[s, :] = to_code(f, B_CODE)
                    if x == far:
                        out[r - OFF + ny:r - OFF + ny + n, :] = to_code(f, B_CODE)
        s = to_rows(top, bottom)
        sum_ref[...] = s
        lo_out[2 * ny:2 * ny + 16, :] = sum_digits(s)
        hi_out[2 * ny:2 * ny + 16, :] = sum_digits(s)
    return kernel


def potentials_b(g, mean, a2_ref, ae2_ref, others, scratch, spans, looped):
    f_ref, lo_ref, hi_ref, yr_ref, zr_ref = others
    pad_ref, ze_ref, mob_ref, mobe_ref, chem_ref, cheme_ref = scratch
    nx, nz = g.nx, g.nz
    fill(B_CODE, f_ref, lo_ref, hi_ref, yr_ref, zr_ref, pad_ref, ze_ref, spans)

    @functools.partial(each, nx + 2, looped)
    def _(p):
        for r, n in spread(spans, 8, 32):
            a = a2_ref[p, r:r + n, :]
            mob_ref[p, r:r + n, :] = a * a

    for r, n in spread(spans, 0, 48):
        a = ae2_ref[r - OFF:r - OFF + n, :]
        a = a * a
        for x in range(nx):
            mobe_ref[x, r - OFF:r - OFF + n, :] = pltpu.roll(a, nz - 32 * x, 1) if x else a
    chemistry(g, pad_ref, mob_ref, mobe_ref, ze_ref, chem_ref, cheme_ref, mean, spans, looped)


def finish_b(g, mean, x, r, n, labels, a2_ref, scratch):
    pad_ref, ze_ref, mob_ref, mobe_ref, chem_ref, cheme_ref = scratch
    m, flux = flux_of(g, x, r, n, mob_ref, mobe_ref, chem_ref, cheme_ref)
    f0 = pad_ref[x + 2, r:r + n, :]
    f = f0 + TIME_STEP * flux
    a = worn(a2_ref[x + 1, r:r + n, :], m, f0, mean)
    dmg = 1.0 - a * by_label(labels, tuple(1.0 / v for v in ROOTS))
    return flux, (f, dmg, a * a, by_label(labels, FACTORS))


def pool_rows(scr_ref, count, nz):
    k = lax.broadcasted_iota(jnp.int32, (4 * nz, nz), 0)
    out = lax.broadcasted_iota(jnp.int32, (4 * nz, nz), 1)
    pick = jnp.where((k % nz // 4 == out // 4) & (out % 4 == k // nz), 1.0 / 64.0, 0.0).astype(BF16)
    high, low = [], []
    for i in range(4):
        rows = (scr_ref[i, pl.ds(0, count, stride=4), :] + scr_ref[i, pl.ds(1, count, stride=4), :]
                + scr_ref[i, pl.ds(2, count, stride=4), :] + scr_ref[i, pl.ds(3, count, stride=4), :])
        high.append(rows.astype(BF16))
        low.append((rows - high[-1].astype(F32)).astype(BF16))
    return sum(jnp.dot(jnp.concatenate(v, axis=1), pick, preferred_element_type=F32) for v in (high, low))


def edge_b(ride_y, ride_z):
    def kernel(f_ref, a2_ref, ae2_ref, lo_ref, hi_ref, yr_ref, zr_ref, yp_ref, l_ref, edge_ref, *rest):
        *scratch, pool_scr = rest
        nx, ny, nz = f_ref.shape
        spans = [(0, 16), (ny - 16, ny)]
        g = Geometry(nx, ny, nz)
        mean = weighted_mean(yp_ref, yr_ref, zr_ref, ride_y, ride_z)
        potentials_b(g, mean, a2_ref, ae2_ref, (f_ref, lo_ref, hi_ref, yr_ref, zr_ref), scratch, spans, False)
        for k, (a, b) in enumerate(spans):
            s = slice(16 * k, 16 * k + 16)
            pooled = [None] * 4
            for x in range(nx):
                _, values = finish_b(g, mean, x, OFF + a, 16, l_ref[x, s, :], a2_ref, scratch)
                pooled = [v if p is None else p + v for p, v in zip(pooled, values)]
            for i in range(4):
                pool_scr[i, s, :] = pooled[i]
        total = pool_rows(pool_scr, 8, nz)
        blank = jnp.zeros((13, nz), F32)
        edge_ref[0] = jnp.concatenate([total[0:3], blank]).astype(BF16)
        edge_ref[1] = jnp.concatenate([total[5:8], blank]).astype(BF16)
    return kernel


def step_b(ride_y, ride_z):
    def kernel(f_ref, a2_ref, ae2_ref, lo_ref, hi_ref, yr_ref, zr_ref, yp_ref, l_hbm,
               f3_hbm, dmg_hbm, flux_hbm, pool_ref, *rest):
        *scratch, pool_scr, l_ref, f3_ref, dmg_ref, flux_ref, l_sem, sems = rest
        nx, ny, nz = f_ref.shape
        labels_in = pltpu.make_async_copy(l_hbm, l_ref, l_sem)
        labels_in.start()
        g = Geometry(nx, ny, nz)
        mean = weighted_mean(yp_ref, yr_ref, zr_ref, ride_y, ride_z)
        potentials_b(g, mean, a2_ref, ae2_ref, (f_ref, lo_ref, hi_ref, yr_ref, zr_ref), scratch, [(0, ny)], True)
        labels_in.wait()
        outs = ((f3_ref, f3_hbm), (dmg_ref, dmg_hbm), (flux_ref, flux_hbm))

        def out_copy(i, x):
            return pltpu.make_async_copy(outs[i][0].at[x], outs[i][1].at[x], sems.at[i, x])

        pool_scr[...] = jnp.zeros(pool_scr.shape, F32)

        @functools.partial(each, nx, True)
        def _(x):
            for r, n in chunks(OFF, OFF + ny, 48):
                s = slice(r - OFF, r - OFF + n)
                flux, values = finish_b(g, mean, x, r, n, l_ref[x, s, :], a2_ref, scratch)
                f3_ref[x, s, :] = values[0]
                dmg_ref[x, s, :] = values[1]
                flux_ref[x, s, :] = flux
                for i in range(4):
                    pool_scr[i, s, :] = pool_scr[i, s, :] + values[i]
            for i in range(3):
                out_copy(i, x).start()

        pool_ref[...] = pool_rows(pool_scr, ny // 4, nz).astype(BF16)
        for x in range(nx):
            for i in range(3):
                out_copy(i, x).wait()
    return kernel


def ring(axis, shift):
    count = lax.axis_size(axis)
    return [(i, (i + shift) % count) for i in range(count)]


def pair_sum(s, axis):
    count = lax.axis_size(axis)
    if count & (count - 1):
        return lax.psum(s, axis)
    bit = 1
    while bit < count:
        s = s + lax.ppermute(s, axis, [(i, i ^ bit) for i in range(count)])
        bit *= 2
    return s


def both_sides(pay, axis):
    if lax.axis_size(axis) == 2:
        return lax.ppermute(pay, axis, ring(axis, 1))
    return jnp.stack([lax.ppermute(pay[0], axis, ring(axis, -1)), lax.ppermute(pay[1], axis, ring(axis, 1))])


def z_neighbour(pay, axis, packed=True):
    if lax.axis_size(axis) == 2:
        return lax.ppermute(pay, axis, ring(axis, 1))
    above = lax.ppermute(pay, axis, ring(axis, -1))
    below = lax.ppermute(pay, axis, ring(axis, 1))
    lane = lax.broadcasted_iota(jnp.int32, pay.shape, pay.ndim - 1)
    if packed:
        low = (lane % 32 < 8) | (lane % 32 == 16)
    else:
        low = lane < pay.shape[-1] // 2
    return jnp.where(low, above, below)


def x_sides(lo, hi):
    return lax.ppermute(hi, "gx", ring("gx", 1)), lax.ppermute(lo, "gx", ring("gx", -1))


def body(concentration, damage, labels, w_first, b_first, w_second, b_second, w_third, b_third):
    nx, ny, nz = concentration.shape
    rows = ny + 2 * OFF
    block = (nx, ny, nz)
    padded = (nx + 2, rows, nz)
    ride_x = lax.axis_size("gx") == 4
    ride_y = lax.axis_size("gy") == 2
    ride_z = lax.axis_size("gz") == 2
    packed = (-(-(nx + 2) // 4), rows, nz)
    assert nz == 128
    scratch = [pltpu.VMEM((nx + 4, rows, nz), F32), pltpu.VMEM(padded, F32), pltpu.VMEM(padded, F32),
               pltpu.VMEM(block, F32), pltpu.VMEM(padded, F32), pltpu.VMEM(block, F32)]

    def start(sums):
        if ride_x:
            return sums, lax.ppermute(sums, "gx", ring("gx", 2))
        sums = pair_sum(sums, "gx")
        for axis, ride in (("gy", ride_y), ("gz", ride_z)):
            if not ride:
                sums = pair_sum(sums, axis)
        return sums, sums

    concentration, damage, labels = (
        pltpu.with_memory_space_constraint(v, pltpu.HBM) for v in (concentration, damage, labels))
    tall = 3 * ny + 16
    f, amp, lo, hi, sums, edge_labels = call(
        first_kernel,
        [(block, F32), (block, F32), ((tall, nz), I16), ((tall, nz), I16), ((8, nz), F32),
         ((nx, 32, nz), jnp.int32)],
        concentration, damage, labels,
        in_specs=[HBM] * 3,
        scratch=[pltpu.VMEM(block, F32), pltpu.VMEM(block, jnp.int32), pltpu.SemaphoreType.DMA((3, nx))])
    weights = weight_rows(w_first, w_second, w_third) + (b_third[None],)
    sums, far = start(sums)
    lo, hi = x_sides(lo, hi)
    (ypay,) = call(edge_rows(A_CODE, ride_x, True), [((2, 24, nz), F32)], f, amp, lo, hi, sums, far, *weights)
    yr = both_sides(ypay, "gy")
    (zpay,) = call(pack_z(A_CODE, ride_y, True), [(packed, F32)], f, amp, lo, hi, yr, ypay)
    zr = z_neighbour(zpay, "gz")
    tall = 2 * ny + 16
    f, a2, ae2, lo, hi, sums = call(
        step_a(ride_y, ride_z),
        [(block, F32), (padded, F32), ((ny, nz), F32), ((tall, nz), I16), ((tall, nz), I16), ((8, nz), F32)],
        f, amp, lo, hi, yr, zr, ypay, scratch=scratch)

    sums, far = start(sums)
    lo, hi = x_sides(lo, hi)
    (ypay,) = call(edge_rows(B_CODE, ride_x, False), [((2, 24, nz), F32)], f, lo, hi, sums, far)
    yr = both_sides(ypay, "gy")
    (zpay,) = call(pack_z(B_CODE, ride_y, False), [(packed, F32)], f, lo, hi, yr, ypay)
    zr = z_neighbour(zpay, "gz")
    last = (f, a2, ae2, lo, hi, yr, zr, ypay)
    (edge,) = call(
        edge_b(ride_y, ride_z), [((2, 16, nz), BF16)], *last, edge_labels,
        scratch=scratch + [pltpu.VMEM((4, 32, nz), F32)])
    fraction, damage_field, flux_sum, pooled = call(
        step_b(ride_y, ride_z),
        [(block, F32), (block, F32), (block, F32), ((ny // 4, nz), BF16)], *last, labels,
        in_specs=[VMEM] * 8 + [HBM], out_specs=[HBM] * 3 + [VMEM],
        scratch=scratch + [
            pltpu.VMEM((4, ny, nz), F32), pltpu.VMEM(block, jnp.int32),
            pltpu.VMEM(block, F32), pltpu.VMEM(block, F32), pltpu.VMEM(block, F32),
            pltpu.SemaphoreType.DMA, pltpu.SemaphoreType.DMA((3, nx))])
    ids = jnp.broadcast_to(jnp.stack([lax.axis_index(a) for a in ("gx", "gy", "gz")])[:, None], (3, nz))
    crack_score = detector(pooled, edge, ids, weights + (b_first[None], b_second[None]), ny // 4, nz // 4)
    return (fraction, damage_field, flux_sum, crack_score)


CH = 16
CIN = 4
TOP = 8


def iota(shape, dim):
    return lax.broadcasted_iota(jnp.int32, shape, dim)


def lanes_for(n):
    return -(-n // 128) * 128


def one_hot(mask):
    return jnp.where(mask, 1.0, 0.0).astype(BF16)


def mm(a, b):
    return jnp.dot(a, b, preferred_element_type=F32)


SHIFTS = tuple(k for k in range(-3, 10) if k % (16 // CIN) == 3)


def weight_kernel(w1_ref, w2_ref, w3_ref, b3_ref, b1_ref, b2_ref, plane_ref, t1_ref, t2_ref, t3_ref, bias_ref):
    n1 = bias_ref.shape[1]
    pz = 128 // CIN
    spread = one_hot(iota((CH, 128), 1) % CH == iota((CH, 128), 0))
    tile1 = mm(w1_ref[...], spread)
    tile2 = mm(w2_ref[...], spread)
    tile3 = mm(w3_ref[...], one_hot(iota((3, 128), 1) // pz == iota((3, 128), 0)))
    step1 = iota((16, 128), 0) // CIN - iota((16, 128), 1) // CH
    step2 = -(iota((16, 128), 1) // CH)
    step3 = -(iota((16, 128), 1) % pz)

    def tile(source, base, stride, step, shift):
        out = jnp.zeros((16, 128), F32)
        for l in range(3):
            k = base + stride * l
            out = jnp.where(step + shift == l, source[16 * k:16 * k + 16], out)
        return out.astype(BF16)

    zero = jnp.zeros((16, 128), BF16)
    bias_ref[...] = jnp.broadcast_to(b3_ref[...], bias_ref.shape)
    for i in range(3):
        for j in range(3):
            tap = 9 * i + 3 * j
            known = {k: tile(tile1, tap, 1, step1, k) for k in SHIFTS}
            places = [(j * 128 + rb * 16, rb * 16 // CIN) for rb in range(8)]
            places += [(384 + 32 * j, pz), (384 + (32 * j - 16) % 128, -16 // CIN)]
            for row, z_in in places:
                for cb in range(n1 // 128):
                    t1_ref[i, row:row + 16, cb * 128:(cb + 1) * 128] = known.get(z_in - cb * 8 + 3, zero)
            for rb in range(10):
                row = j * 128 + rb * 16 if rb < 8 else 384 + 32 * j + (rb - 8) * 16
                t2_ref[i, row:row + 16, :] = tile(tile2, tap, 1, step2, rb)
        for row in (464, 480):
            for cb in range(n1 // 128):
                t1_ref[i, row:row + 16, cb * 128:(cb + 1) * 128] = zero
        for row in (480, 496):
            t2_ref[i, row:row + 16, :] = zero
        for rb in range(t3_ref.shape[1] // 16):
            t3_ref[i, rb * 16:rb * 16 + 16, :] = tile(tile3, 3 * i, 1, step3, rb) if rb < pz + 2 else zero
    wide = one_hot(iota((CH, n1), 1) % CH == iota((CH, n1), 0)).astype(F32)
    for k, ref in ((0, b1_ref), (1, b2_ref)):
        bias_ref[k:k + 1, :] = jnp.dot(ref[...], wide, precision=lax.Precision.HIGHEST, preferred_element_type=F32)


def weight_rows(w_first, w_second, w_third):
    return (jnp.tile(jnp.swapaxes(w_first, 1, 2), (1, 16 // CIN, 1)).reshape(27 * 16, CH),
            jnp.swapaxes(w_second, 1, 2).reshape(27 * CH, CH),
            w_third.reshape(3, 3, 3, CH).transpose(0, 2, 3, 1).reshape(9 * CH, 3))


def gelu(x):
    return 0.5 * x * (1.0 + jnp.tanh(0.7978845608028654 * (x + 0.044715 * (x * x * x))))


def plane_kernel(py, y_count):
    def kernel(ids_ref, pool_ref, yr_ref, out_ref, scr_ref):
        iy = ids_ref[1:2, 0:1]
        scr_ref[...] = jnp.zeros(scr_ref.shape, F32)
        scr_ref[TOP:TOP + py, :] = pool_ref[0:py, :].astype(F32)
        below = yr_ref[1].astype(F32)[0:3]
        above = yr_ref[0].astype(F32)[0:3]
        scr_ref[TOP - 3:TOP, :] = jnp.where(iy > 0, below, 0.0)
        scr_ref[TOP + py:TOP + py + 3, :] = jnp.where(iy < y_count - 1, above, 0.0)
        out_ref[...] = scr_ref[...].astype(BF16)
    return kernel


def conv_kernel(py, counts, shifts):
    x_count, y_count, z_count = counts
    n = len(shifts)

    def kernel(*refs):
        ids_ref = refs[0]
        own = refs[1:2 + n]
        other = refs[2 + n:3 + 2 * n]
        t1_ref, t2_ref, t3_ref, bias_ref, out_ref = refs[3 + 2 * n:8 + 2 * n]
        in_ref, beside_ref, lhs1_ref, act1_ref, lhs2_ref, act2_ref, tail_ref = refs[8 + 2 * n:]
        ix, iy, iz = ids_ref[0:1, 0:1], ids_ref[1:2, 0:1], ids_ref[2:3, 0:1]
        half = own[0].shape[1]
        pz = half // CIN
        rows = py + 4
        z_row = iota((1, half), 1) // CIN
        z_ok = ((z_row < pz // 2) & (iz < z_count - 1)) | ((z_row >= pz // 2) & (iz > 0))
        for w in range(7):
            o = w - 3
            k = 0 if o == 0 else 1 + shifts.index((-o) % x_count) if (-o) % x_count in shifts else None
            if k is None:
                in_ref[w] = jnp.zeros(in_ref.shape[1:], F32)
                beside_ref[w] = jnp.zeros(in_ref.shape[1:], F32)
                continue
            inside = (ix + o >= 0) & (ix + o < x_count)
            in_ref[w] = jnp.where(inside, own[k][...].astype(F32), 0.0)
            beside_ref[w] = jnp.where(z_ok & inside, other[k][...].astype(F32), 0.0)
        lane = iota((1, 128), 1)

        def shared(parts, first, count):
            out = parts[0]
            for j in (1, 2):
                out = jnp.where(group(lane, j, 128, first, count), pltpu.roll(parts[j], 32 * j, 1), out)
            return out.astype(BF16)

        for w in range(7):
            starts = [TOP - 3 + j for j in range(3)]
            for j, r in enumerate(starts):
                lhs1_ref[w, :, j * 128:(j + 1) * 128] = in_ref[w, r:r + rows, :].astype(BF16)
            lhs1_ref[w, :, 384:512] = shared([beside_ref[w, r:r + rows, :] for r in starts], -3 * CIN, 6 * CIN)
        out = None
        for i in range(3):
            part = mm(lhs1_ref[i:i + 5].reshape(5 * rows, 512), t1_ref[i])
            out = part if out is None else out + part
        width = out.shape[1]
        y = iota((rows, width), 0) - 2
        z = iota((rows, width), 1) // CH - 2
        ok = (z < pz + 2) & ((y >= 0) | (iy > 0)) & ((y < py) | (iy < y_count - 1))
        ok = ok & ((z >= 0) | (iz > 0)) & ((z < pz) | (iz < z_count - 1))
        for p in range(5):
            a = gelu(out[p * rows:(p + 1) * rows] + bias_ref[0:1, :])
            good = ok & (ix + p - 2 >= 0) & (ix + p - 2 < x_count)
            act1_ref[p, 0:rows, 0:width] = jnp.where(good, a, 0.0)
            act1_ref[p, rows:, 0:width] = jnp.zeros((act1_ref.shape[1] - rows, width), F32)
            act1_ref[p, :, width:] = jnp.zeros((act1_ref.shape[1], act1_ref.shape[2] - width), F32)
        blocks = lhs2_ref.shape[1]
        for p in range(5):
            for b in range(blocks):
                for j in range(3):
                    lhs2_ref[p, b, :, j * 128:(j + 1) * 128] = (
                        act1_ref[p, j:j + rows, b * 128:(b + 1) * 128].astype(BF16))
                following = slice((b + 1) * 128, (b + 2) * 128)
                lhs2_ref[p, b, :, 384:512] = shared([act1_ref[p, j:j + rows, following] for j in range(3)], 0, 32)
        out = None
        for i in range(3):
            part = mm(lhs2_ref[i:i + 3].reshape(3 * blocks * rows, 512), t2_ref[i])
            out = part if out is None else out + part
        for b in range(blocks):
            y = iota((rows, 128), 0) - 1
            z = (iota((rows, 128), 1) + b * 128) // CH - 1
            ok = (z < pz + 1) & (y <= py) & ((y >= 0) | (iy > 0)) & ((y < py) | (iy < y_count - 1))
            ok = ok & ((z >= 0) | (iz > 0)) & ((z < pz) | (iz < z_count - 1))
            for p in range(3):
                s = (p * blocks + b) * rows
                a = gelu(out[s:s + rows] + bias_ref[1:2, 0:128])
                good = ok & (ix + p - 1 >= 0) & (ix + p - 1 < x_count)
                act2_ref[p, :, b * 128:(b + 1) * 128] = jnp.where(good, a, 0.0).astype(BF16)
        out = None
        for i in range(3):
            part = mm(act2_ref[i], t3_ref[i])
            out = part if out is None else out + part
        tail_ref[0:rows, :] = out
        score = tail_ref[0:py, :]
        for j in (1, 2):
            score = score + pltpu.roll(tail_ref[j:j + py, :], 128 - j * pz, 1)
        out_ref[0] = jnp.transpose(score)[0:pz, :] + bias_ref[2:3, 0:1]
    return kernel


def detector(pooled, edge, ids, weights, py, pz):
    counts = tuple(lax.axis_size(a) for a in ("gx", "gy", "gz"))
    half = pooled.shape[1]
    assert half == 128 and pz * CIN == half and pz * 3 <= 128
    rows = py + 4
    width = lanes_for((pz + 4) * CH)
    blocks = width // 128
    yr = both_sides(edge, "gy")
    tall = -(-(TOP + py + 3) // 16) * 16
    (plane,) = call(
        plane_kernel(py, counts[1]), [((tall, half), BF16)], ids, pooled, yr,
        scratch=[pltpu.VMEM((tall, half), F32)])
    shifts = []
    for s in (1, -1, 2, -2, 3, -3):
        if s % counts[0] and s % counts[0] not in shifts:
            shifts.append(s % counts[0])
    own = [plane] + [lax.ppermute(plane, "gx", ring("gx", s)) for s in shifts]
    matrices = call(
        weight_kernel,
        [((3, 512, width), BF16), ((3, 512, 128), BF16), ((3, width, 128), BF16), ((8, width), F32)],
        *weights, plane)
    own[-1], *matrices = lax.optimization_barrier((own[-1], *matrices))
    other = [z_neighbour(v, "gz", False) for v in own]
    args = (ids, *own, *other, *matrices)
    (score,) = call(
        conv_kernel(py, counts, shifts), [((1, pz, py), F32)], *args,
        scratch=[
            pltpu.VMEM((7, tall, half), F32),
            pltpu.VMEM((7, tall, half), F32),
            pltpu.VMEM((7, rows, 512), BF16),
            pltpu.VMEM((5, rows + 8, width + 128), F32),
            pltpu.VMEM((5, blocks, rows, 512), BF16),
            pltpu.VMEM((3, rows, width), BF16),
            pltpu.VMEM((rows + 8, 128), F32),
        ], mib=32)
    return jnp.swapaxes(score, 1, 2)


def solution(mesh):
    slab = P(("groups", "gx"), "gy", "gz")
    return jax.shard_map(
        body,
        mesh=mesh,
        in_specs=(slab, slab, slab, P(), P(), P(), P(), P(), P()),
        out_specs=(slab, slab, slab, slab),
        check_vma=False,
    )
```

```python
import functools

import jax
import jax.numpy as jnp
import numpy as np
from jax import lax
from jax.experimental import pallas as pl
from jax.experimental.pallas import tpu as pltpu
from jax.sharding import PartitionSpec as P

F32 = jnp.float32
BF16 = jnp.bfloat16
I16 = jnp.int16
WELL_HEIGHT = 1.0
STRAIN_COUPLING = 4.0
TIME_STEP = 0.01
DAMAGE_RATE = 0.8
ENERGY_CRITICAL = 0.02

OFF = 16
A_CODE = (0.0, 1.0)
B_CODE = (-1.1, 3.1)
SUM_LOW, SUM_SPAN = -1280.0, 4096.0

VMEM = pl.BlockSpec(memory_space=pltpu.VMEM)
HBM = pl.BlockSpec(memory_space=pltpu.HBM)


def to_code(x, code):
    low, span = code
    v = (x - low) * (65535.0 / span) - 32768.0
    return jnp.clip(jnp.round(v), -32768.0, 32767.0).astype(jnp.int32).astype(I16)


def from_code(q, code):
    low, span = code
    return q.astype(jnp.int32).astype(F32) * (span / 65535.0) + (low + 32768.0 * span / 65535.0)


def sum_digits(s):
    v = (s[0:2] - SUM_LOW) * (65536.0 / SUM_SPAN)
    high = jnp.floor(v)
    low = jnp.minimum(jnp.floor((v - high) * 65536.0), 65535.0)
    rows = jnp.concatenate([high, low, jnp.full((12, s.shape[1]), 32768.0, F32)]) - 32768.0
    return rows.astype(jnp.int32).astype(I16)


def from_digits(tile):
    v = tile.astype(jnp.int32).astype(F32) + 32768.0
    return (v[0:2] + v[2:4] * (1.0 / 65536.0)) * (SUM_SPAN / 65536.0) + SUM_LOW


def each(count, looped, body):
    def step(i, carry):
        body(i)
        return carry
    if looped:
        lax.fori_loop(0, count, step, 0)
    else:
        for i in range(count):
            body(i)


def by_label(labels, values):
    return jnp.where(labels == 0, values[0], jnp.where(labels == 1, values[1], values[2])).astype(F32)


FACTORS = (1.0, 0.3, 0.05)
ROOTS = tuple(float(np.sqrt(np.float32(v))) for v in FACTORS)


def call(kernel, outs, *args, in_specs=None, out_specs=None, scratch=(), mib=16):
    return pl.pallas_call(
        kernel,
        in_specs=in_specs or [VMEM] * len(args),
        out_specs=out_specs or [VMEM] * len(outs),
        out_shape=[jax.ShapeDtypeStruct(s, t) for s, t in outs],
        scratch_shapes=scratch,
        compiler_params=pltpu.CompilerParams(vmem_limit_bytes=mib * 1024 * 1024),
    )(*args)


def chunks(start, stop, size):
    return [(r, min(size, stop - r)) for r in range(start, stop, size)]


def fold(x):
    return x.reshape(x.shape[0] // 8, 8, x.shape[1]).sum(0)


def to_rows(top, bottom):
    return jnp.concatenate([jnp.sum(top, 0, keepdims=True), jnp.sum(bottom, 0, keepdims=True),
                            jnp.zeros((6, top.shape[1]), F32)])


def first_kernel(c_hbm, d_hbm, l_hbm, f_ref, amp_ref, lo_ref, hi_ref, sum_ref, le_ref, d_ref, l_ref, sems):
    nx, ny, nz = f_ref.shape
    order = [0, nx - 1] + list(range(1, nx - 1))
    copies = []
    for x in order:
        copies.append([pltpu.make_async_copy(src.at[x], dst.at[x], sems.at[k, x])
                       for k, (src, dst) in enumerate(((c_hbm, f_ref), (d_hbm, d_ref), (l_hbm, l_ref)))])
        for c in copies[-1]:
            c.start()
    top = jnp.zeros((8, nz), F32)
    bottom = jnp.zeros((8, nz), F32)
    for k, x in enumerate(order):
        for c in copies[k]:
            c.wait()
        le_ref[x, 0:16, :] = l_ref[x, 0:16, :]
        le_ref[x, 16:32, :] = l_ref[x, ny - 16:ny, :]
        for r, n in chunks(0, ny, 48):
            f = f_ref[x, r:r + n, :]
            a = by_label(l_ref[x, r:r + n, :], ROOTS) * (1.0 - d_ref[x, r:r + n, :])
            amp_ref[x, r:r + n, :] = a
            m = a * a
            top = top + fold(m * f)
            bottom = bottom + fold(m)
            for near, far, out in ((0, 1, lo_ref), (nx - 1, nx - 2, hi_ref)):
                if x == near:
                    out[r:r + n, :] = to_code(f, A_CODE)
                    out[2 * ny + r:2 * ny + r + n, :] = to_code(a, A_CODE)
                if x == far:
                    out[ny + r:ny + r + n, :] = to_code(f, A_CODE)
    s = to_rows(top, bottom)
    sum_ref[...] = s
    lo_ref[3 * ny:3 * ny + 16, :] = sum_digits(s)
    hi_ref[3 * ny:3 * ny + 16, :] = sum_digits(s)


def edge_rows(code, ride_x, with_amp):
    def kernel(*refs):
        f_ref = refs[0]
        amp_ref = refs[1] if with_amp else None
        lo_ref, hi_ref, s_ref, far_ref = refs[1 + with_amp:5 + with_amp]
        out_ref = refs[-1]
        nx, ny, nz = f_ref.shape
        low_rows = [from_code(r[0:16, :], code)[0:1] for r in (lo_ref, hi_ref)]
        high_rows = [from_code(r[ny - 16:ny, :], code)[15:16] for r in (lo_ref, hi_ref)]
        s = s_ref[...]
        if ride_x:
            s = s + far_ref[...]
        for side, first, second, beside in ((0, 0, 1, low_rows), (1, ny - 1, ny - 2, high_rows)):
            for x in range(nx):
                out_ref[side, 2 * x:2 * x + 1, :] = f_ref[x, first:first + 1, :]
                out_ref[side, 2 * x + 1:2 * x + 2, :] = f_ref[x, second:second + 1, :]
                if amp_ref is not None:
                    out_ref[side, 10 + x:11 + x, :] = amp_ref[x, first:first + 1, :]
            out_ref[side, 8:9, :] = beside[0]
            out_ref[side, 9:10, :] = beside[1]
            out_ref[side, 16:24, :] = s
            if ride_x:
                out_ref[side, 16:18, :] = (s[0:2] + from_digits(lo_ref[lo_ref.shape[0] - 16:, :])
                                           + from_digits(hi_ref[hi_ref.shape[0] - 16:, :]))
    return kernel


def group(lane, j, nz, first, count):
    return (lane - (32 * j + first)) % nz < count


def pack_z(code, ride_y, with_amp):
    def kernel(*refs):
        f_ref = refs[0]
        amp_ref = refs[1] if with_amp else None
        lo_ref, hi_ref, yr_ref, yp_ref, out_ref = refs[1 + with_amp:]
        nx, ny, nz = f_ref.shape
        end = OFF + ny
        lane = lax.broadcasted_iota(jnp.int32, (1, nz), 1)
        for k in range(out_ref.shape[0]):
            planes = [p for p in range(4 * k, 4 * k + 4) if p < nx + 2]

            def packed(f_of, a_of, ps):
                out = None
                for p in ps:
                    j = p % 4
                    f = f_of(p)
                    f = pltpu.roll(f, 32 * j, 1) if j else f
                    out = f if out is None else jnp.where(group(lane, j, nz, -2, 4), f, out)
                    a = a_of(p)
                    if a is not None:
                        out = jnp.where(group(lane, j, nz, 15, 2), pltpu.roll(a, 32 * j + 16, 1), out)
                return out

            for r, n in chunks(0, ny, 48):
                def f_of(p):
                    if p == 0:
                        return from_code(lo_ref[r:r + n, :], code)
                    if p == nx + 1:
                        return from_code(hi_ref[r:r + n, :], code)
                    return f_ref[p - 1, r:r + n, :]

                def a_of(p):
                    return amp_ref[p - 1, r:r + n, :] if with_amp and 1 <= p <= nx else None

                out_ref[k, OFF + r:OFF + r + n, :] = packed(f_of, a_of, planes)
            inner = [p for p in planes if 1 <= p <= nx]
            if inner:
                for side, near in ((1, OFF - 1), (0, end)):
                    out_ref[k, near:near + 1, :] = packed(
                        lambda p: yr_ref[side, 2 * (p - 1):2 * (p - 1) + 1, :], lambda p: None, inner)
        s = yp_ref[0, 16:24, :]
        out_ref[0, 0:8, :] = s + yr_ref[0, 16:24, :] if ride_y else s
    return kernel


def spread(spans, extra, size):
    return [v for a, b in spans for v in chunks(OFF + a - extra, OFF + b + extra, size)]


def fill(code, f_ref, lo_ref, hi_ref, yr_ref, zr_ref, pad_ref, ze_ref, spans):
    nx, ny, nz = f_ref.shape
    end = OFF + ny
    wide = [v for a, b in spans for v in chunks(max(a - 16, 0), min(b + 16, ny), 48)]
    for near, far, ref in ((1, 0, lo_ref), (nx + 2, nx + 3, hi_ref)):
        for r, n in wide:
            pad_ref[near, OFF + r:OFF + r + n, :] = from_code(ref[r:r + n, :], code)
            pad_ref[far, OFF + r:OFF + r + n, :] = from_code(ref[ny + r:ny + r + n, :], code)
    for p, k in ((1, 8), (nx + 2, 9)):
        pad_ref[p, OFF - 1:OFF, :] = yr_ref[1, k:k + 1, :]
        pad_ref[p, end:end + 1, :] = yr_ref[0, k:k + 1, :]
    for x in range(nx):
        for r, n in wide:
            pad_ref[x + 2, OFF + r:OFF + r + n, :] = f_ref[x, r:r + n, :]
        for side, near, far in ((1, OFF - 1, OFF - 2), (0, end, end + 1)):
            pad_ref[x + 2, near:near + 1, :] = yr_ref[side, 2 * x:2 * x + 1, :]
            pad_ref[x + 2, far:far + 1, :] = yr_ref[side, 2 * x + 1:2 * x + 2, :]
    for p in range(nx + 2):
        for r, n in spread(spans, 8, 32):
            e = zr_ref[p // 4, r:r + n, :]
            ze_ref[p, r:r + n, :] = pltpu.roll(e, nz - 32 * (p % 4), 1) if p % 4 else e


def weighted_mean(yp_ref, yr_ref, zr_ref, ride_y, ride_z):
    s = yp_ref[0, 16:24, :]
    if ride_y:
        s = s + yr_ref[0, 16:24, :]
    if ride_z:
        s = s + zr_ref[0, 0:8, :]
    return jnp.sum(s[0:1], keepdims=True) / jnp.sum(s[1:2], keepdims=True)


def worn(a, m, f, mean):
    e = f - mean
    loss = DAMAGE_RATE * 0.5 * STRAIN_COUPLING * (m * (e * e)) - DAMAGE_RATE * ENERGY_CRITICAL
    return a * (1.0 - jnp.maximum(loss, 0.0))


class Geometry:
    def __init__(self, nx, ny, nz):
        self.nx, self.ny, self.nz = nx, ny, nz
        self.lane = lax.broadcasted_iota(jnp.int32, (1, nz), 1)
        self.first = self.lane == 0
        self.last = self.lane == nz - 1

    def before(self, own, other):
        return pltpu.roll(jnp.where(self.last, other, own), 1, 1)

    def after(self, own, other):
        return pltpu.roll(jnp.where(self.first, other, own), self.nz - 1, 1)


def chem_of(f, m, around, mean):
    w = 2.0 * WELL_HEIGHT
    return ((2.0 * w * f - 3.0 * w) * f + (w + 6.0)) * f - around + STRAIN_COUPLING * (m * (f - mean))


def chemistry(g, pad_ref, mob_ref, mobe_ref, ze_ref, chem_ref, cheme_ref, mean, spans, looped=False):
    nx = g.nx

    @functools.partial(each, nx + 2, looped)
    def _(p):
        for r, n in spread(spans, 0, 48) if not looped and p in (0, nx + 1) else spread(spans, 8, 32):
            f = pad_ref[p + 1, r:r + n, :]
            e = ze_ref[p, r:r + n, :]
            around = (pad_ref[p, r:r + n, :] + pad_ref[p + 2, r:r + n, :]
                      + pad_ref[p + 1, r - 1:r - 1 + n, :] + pad_ref[p + 1, r + 1:r + 1 + n, :]
                      + g.before(f, e) + g.after(f, e))
            chem_ref[p, r:r + n, :] = chem_of(f, mob_ref[p, r:r + n, :], around, mean)

    @functools.partial(each, nx, looped)
    def _(x):
        p = x + 1
        for r, n in spread(spans, 0, 48):
            f = pad_ref[p + 1, r:r + n, :]
            e = ze_ref[p, r:r + n, :]
            around = (ze_ref[p - 1, r:r + n, :] + ze_ref[p + 1, r:r + n, :]
                      + ze_ref[p, r - 1:r - 1 + n, :] + ze_ref[p, r + 1:r + 1 + n, :]
                      + g.before(e, f) + g.after(e, f))
            cheme_ref[x, r - OFF:r - OFF + n, :] = chem_of(
                e, mobe_ref[x, r - OFF:r - OFF + n, :], around, mean)


def flux_of(g, x, r, n, mob_ref, mobe_ref, chem_ref, cheme_ref):
    p = x + 1
    m = mob_ref[p, r:r + n, :]
    q = chem_ref[p, r:r + n, :]
    me = mobe_ref[x, r - OFF:r - OFF + n, :]
    qe = cheme_ref[x, r - OFF:r - OFF + n, :]
    total = None
    for nm, nq in (
        (mob_ref[p - 1, r:r + n, :], chem_ref[p - 1, r:r + n, :]),
        (mob_ref[p + 1, r:r + n, :], chem_ref[p + 1, r:r + n, :]),
        (mob_ref[p, r - 1:r - 1 + n, :], chem_ref[p, r - 1:r - 1 + n, :]),
        (mob_ref[p, r + 1:r + 1 + n, :], chem_ref[p, r + 1:r + 1 + n, :]),
        (g.before(m, me), g.before(q, qe)),
        (g.after(m, me), g.after(q, qe)),
    ):
        term = (nm + m) * (nq - q)
        total = term if total is None else total + term
    return m, 0.5 * total


def pack_edges(values, lane, nz):
    out = values[0]
    for x, v in enumerate(values[1:], 1):
        out = jnp.where(group(lane, x, nz, -1, 2), pltpu.roll(v, 32 * x, 1), out)
    return out


def step_a(ride_y, ride_z):
    def kernel(f_ref, amp_ref, lo_ref, hi_ref, yr_ref, zr_ref, yp_ref,
               f2_ref, a2_ref, ae2_ref, lo_out, hi_out, sum_ref,
               pad_ref, ze_ref, mob_ref, mobe_ref, chem_ref, cheme_ref):
        nx, ny, nz = f2_ref.shape
        end = OFF + ny
        g = Geometry(nx, ny, nz)
        mean = weighted_mean(yp_ref, yr_ref, zr_ref, ride_y, ride_z)
        fill(A_CODE, f_ref, lo_ref, hi_ref, yr_ref, zr_ref, pad_ref, ze_ref, [(0, ny)])

        def wear(p, r, n, a):
            m = a * a
            mob_ref[p, r:r + n, :] = m
            a2_ref[p, r:r + n, :] = worn(a, m, pad_ref[p + 1, r:r + n, :], mean)

        for r, n in chunks(0, ny, 48):
            wear(0, OFF + r, n, from_code(lo_ref[2 * ny + r:2 * ny + r + n, :], A_CODE))
            wear(nx + 1, OFF + r, n, from_code(hi_ref[2 * ny + r:2 * ny + r + n, :], A_CODE))
            edges = []
            for x in range(nx):
                wear(x + 1, OFF + r, n, amp_ref[x, r:r + n, :])
                p = x + 1
                a = pltpu.roll(zr_ref[p // 4, OFF + r:OFF + r + n, :], nz - 32 * (p % 4) - 16, 1)
                m = a * a
                mobe_ref[x, r:r + n, :] = m
                edges.append(worn(a, m, ze_ref[p, OFF + r:OFF + r + n, :], mean))
            ae2_ref[r:r + n, :] = pack_edges(edges, g.lane, nz)
        for x in range(nx):
            wear(x + 1, OFF - 1, 1, yr_ref[1, 10 + x:11 + x, :])
            wear(x + 1, end, 1, yr_ref[0, 10 + x:11 + x, :])
        chemistry(g, pad_ref, mob_ref, mobe_ref, ze_ref, chem_ref, cheme_ref, mean, [(0, ny)])
        top = jnp.zeros((8, nz), F32)
        bottom = jnp.zeros((8, nz), F32)
        for x in range(nx):
            for r, n in chunks(OFF, end, 48):
                _, flux = flux_of(g, x, r, n, mob_ref, mobe_ref, chem_ref, cheme_ref)
                f = pad_ref[x + 2, r:r + n, :] + TIME_STEP * flux
                s = slice(r - OFF, r - OFF + n)
                f2_ref[x, s, :] = f
                a = a2_ref[x + 1, r:r + n, :]
                m = a * a
                top = top + fold(m * f)
                bottom = bottom + fold(m)
                for near, far, out in ((0, 1, lo_out), (nx - 1, nx - 2, hi_out)):
                    if x == near:
                        out[s, :] = to_code(f, B_CODE)
                    if x == far:
                        out[r - OFF + ny:r - OFF + ny + n, :] = to_code(f, B_CODE)
        s = to_rows(top, bottom)
        sum_ref[...] = s
        lo_out[2 * ny:2 * ny + 16, :] = sum_digits(s)
        hi_out[2 * ny:2 * ny + 16, :] = sum_digits(s)
    return kernel


def potentials_b(g, mean, a2_ref, ae2_ref, others, scratch, spans, looped):
    f_ref, lo_ref, hi_ref, yr_ref, zr_ref = others
    pad_ref, ze_ref, mob_ref, mobe_ref, chem_ref, cheme_ref = scratch
    nx, nz = g.nx, g.nz
    fill(B_CODE, f_ref, lo_ref, hi_ref, yr_ref, zr_ref, pad_ref, ze_ref, spans)

    @functools.partial(each, nx + 2, looped)
    def _(p):
        for r, n in spread(spans, 8, 32):
            a = a2_ref[p, r:r + n, :]
            mob_ref[p, r:r + n, :] = a * a

    for r, n in spread(spans, 0, 48):
        a = ae2_ref[r - OFF:r - OFF + n, :]
        a = a * a
        for x in range(nx):
            mobe_ref[x, r - OFF:r - OFF + n, :] = pltpu.roll(a, nz - 32 * x, 1) if x else a
    chemistry(g, pad_ref, mob_ref, mobe_ref, ze_ref, chem_ref, cheme_ref, mean, spans, looped)


def finish_b(g, mean, x, r, n, labels, a2_ref, scratch):
    pad_ref, ze_ref, mob_ref, mobe_ref, chem_ref, cheme_ref = scratch
    m, flux = flux_of(g, x, r, n, mob_ref, mobe_ref, chem_ref, cheme_ref)
    f0 = pad_ref[x + 2, r:r + n, :]
    f = f0 + TIME_STEP * flux
    a = worn(a2_ref[x + 1, r:r + n, :], m, f0, mean)
    dmg = 1.0 - a * by_label(labels, tuple(1.0 / v for v in ROOTS))
    return flux, (f, dmg, a * a, by_label(labels, FACTORS))


def pool_rows(scr_ref, count, nz):
    k = lax.broadcasted_iota(jnp.int32, (4 * nz, nz), 0)
    out = lax.broadcasted_iota(jnp.int32, (4 * nz, nz), 1)
    pick = jnp.where((k % nz // 4 == out // 4) & (out % 4 == k // nz), 1.0 / 64.0, 0.0).astype(BF16)
    high, low = [], []
    for i in range(4):
        rows = (scr_ref[i, pl.ds(0, count, stride=4), :] + scr_ref[i, pl.ds(1, count, stride=4), :]
                + scr_ref[i, pl.ds(2, count, stride=4), :] + scr_ref[i, pl.ds(3, count, stride=4), :])
        high.append(rows.astype(BF16))
        low.append((rows - high[-1].astype(F32)).astype(BF16))
    return sum(jnp.dot(jnp.concatenate(v, axis=1), pick, preferred_element_type=F32) for v in (high, low))


def edge_b(ride_y, ride_z):
    def kernel(f_ref, a2_ref, ae2_ref, lo_ref, hi_ref, yr_ref, zr_ref, yp_ref, l_ref, edge_ref, *rest):
        *scratch, pool_scr = rest
        nx, ny, nz = f_ref.shape
        spans = [(0, 16), (ny - 16, ny)]
        g = Geometry(nx, ny, nz)
        mean = weighted_mean(yp_ref, yr_ref, zr_ref, ride_y, ride_z)
        potentials_b(g, mean, a2_ref, ae2_ref, (f_ref, lo_ref, hi_ref, yr_ref, zr_ref), scratch, spans, False)
        for k, (a, b) in enumerate(spans):
            s = slice(16 * k, 16 * k + 16)
            pooled = [None] * 4
            for x in range(nx):
                _, values = finish_b(g, mean, x, OFF + a, 16, l_ref[x, s, :], a2_ref, scratch)
                pooled = [v if p is None else p + v for p, v in zip(pooled, values)]
            for i in range(4):
                pool_scr[i, s, :] = pooled[i]
        total = pool_rows(pool_scr, 8, nz)
        blank = jnp.zeros((13, nz), F32)
        edge_ref[0] = jnp.concatenate([total[0:3], blank]).astype(BF16)
        edge_ref[1] = jnp.concatenate([total[5:8], blank]).astype(BF16)
    return kernel


def step_b(ride_y, ride_z):
    def kernel(f_ref, a2_ref, ae2_ref, lo_ref, hi_ref, yr_ref, zr_ref, yp_ref, l_hbm,
               f3_hbm, dmg_hbm, flux_hbm, pool_ref, *rest):
        *scratch, pool_scr, l_ref, f3_ref, dmg_ref, flux_ref, l_sem, sems = rest
        nx, ny, nz = f_ref.shape
        labels_in = pltpu.make_async_copy(l_hbm, l_ref, l_sem)
        labels_in.start()
        g = Geometry(nx, ny, nz)
        mean = weighted_mean(yp_ref, yr_ref, zr_ref, ride_y, ride_z)
        potentials_b(g, mean, a2_ref, ae2_ref, (f_ref, lo_ref, hi_ref, yr_ref, zr_ref), scratch, [(0, ny)], True)
        labels_in.wait()
        copies = []
        for k, (r, n) in enumerate(chunks(OFF, OFF + ny, 48)):
            s = slice(r - OFF, r - OFF + n)
            pooled = [None] * 4
            for x in range(nx):
                flux, values = finish_b(g, mean, x, r, n, l_ref[x, s, :], a2_ref, scratch)
                f3_ref[x, s, :] = values[0]
                dmg_ref[x, s, :] = values[1]
                flux_ref[x, s, :] = flux
                pooled = [v if p is None else p + v for p, v in zip(pooled, values)]
            for i in range(4):
                pool_scr[i, s, :] = pooled[i]
            for i, (src, dst) in enumerate(((f3_ref, f3_hbm), (dmg_ref, dmg_hbm), (flux_ref, flux_hbm))):
                copies.append(pltpu.make_async_copy(src.at[:, s, :], dst.at[:, s, :], sems.at[i, k]))
                copies[-1].start()
        pool_ref[...] = pool_rows(pool_scr, ny // 4, nz).astype(BF16)
        for c in copies:
            c.wait()
    return kernel


def ring(axis, shift):
    count = lax.axis_size(axis)
    return [(i, (i + shift) % count) for i in range(count)]


def pair_sum(s, axis):
    count = lax.axis_size(axis)
    if count & (count - 1):
        return lax.psum(s, axis)
    bit = 1
    while bit < count:
        s = s + lax.ppermute(s, axis, [(i, i ^ bit) for i in range(count)])
        bit *= 2
    return s


def both_sides(pay, axis):
    if lax.axis_size(axis) == 2:
        return lax.ppermute(pay, axis, ring(axis, 1))
    return jnp.stack([lax.ppermute(pay[0], axis, ring(axis, -1)), lax.ppermute(pay[1], axis, ring(axis, 1))])


def z_neighbour(pay, axis, packed=True):
    if lax.axis_size(axis) == 2:
        return lax.ppermute(pay, axis, ring(axis, 1))
    above = lax.ppermute(pay, axis, ring(axis, -1))
    below = lax.ppermute(pay, axis, ring(axis, 1))
    lane = lax.broadcasted_iota(jnp.int32, pay.shape, pay.ndim - 1)
    if packed:
        low = (lane % 32 < 8) | (lane % 32 == 16)
    else:
        low = lane < pay.shape[-1] // 2
    return jnp.where(low, above, below)


def x_sides(lo, hi):
    return lax.ppermute(hi, "gx", ring("gx", 1)), lax.ppermute(lo, "gx", ring("gx", -1))


def body(concentration, damage, labels, w_first, b_first, w_second, b_second, w_third, b_third):
    nx, ny, nz = concentration.shape
    rows = ny + 2 * OFF
    block = (nx, ny, nz)
    padded = (nx + 2, rows, nz)
    ride_x = lax.axis_size("gx") == 4
    ride_y = lax.axis_size("gy") == 2
    ride_z = lax.axis_size("gz") == 2
    packed = (-(-(nx + 2) // 4), rows, nz)
    assert nz == 128
    scratch = [pltpu.VMEM((nx + 4, rows, nz), F32), pltpu.VMEM(padded, F32), pltpu.VMEM(padded, F32),
               pltpu.VMEM(block, F32), pltpu.VMEM(padded, F32), pltpu.VMEM(block, F32)]

    def start(sums):
        if ride_x:
            return sums, lax.ppermute(sums, "gx", ring("gx", 2))
        sums = pair_sum(sums, "gx")
        for axis, ride in (("gy", ride_y), ("gz", ride_z)):
            if not ride:
                sums = pair_sum(sums, axis)
        return sums, sums

    concentration, damage, labels = (
        pltpu.with_memory_space_constraint(v, pltpu.HBM) for v in (concentration, damage, labels))
    tall = 3 * ny + 16
    f, amp, lo, hi, sums, edge_labels = call(
        first_kernel,
        [(block, F32), (block, F32), ((tall, nz), I16), ((tall, nz), I16), ((8, nz), F32),
         ((nx, 32, nz), jnp.int32)],
        concentration, damage, labels,
        in_specs=[HBM] * 3,
        scratch=[pltpu.VMEM(block, F32), pltpu.VMEM(block, jnp.int32), pltpu.SemaphoreType.DMA((3, nx))])
    weights = weight_rows(w_first, w_second, w_third) + (b_third[None],)
    sums, far = start(sums)
    lo, hi = x_sides(lo, hi)
    (ypay,) = call(edge_rows(A_CODE, ride_x, True), [((2, 24, nz), F32)], f, amp, lo, hi, sums, far, *weights)
    yr = both_sides(ypay, "gy")
    (zpay,) = call(pack_z(A_CODE, ride_y, True), [(packed, F32)], f, amp, lo, hi, yr, ypay)
    zr = z_neighbour(zpay, "gz")
    tall = 2 * ny + 16
    f, a2, ae2, lo, hi, sums = call(
        step_a(ride_y, ride_z),
        [(block, F32), (padded, F32), ((ny, nz), F32), ((tall, nz), I16), ((tall, nz), I16), ((8, nz), F32)],
        f, amp, lo, hi, yr, zr, ypay, scratch=scratch)

    sums, far = start(sums)
    lo, hi = x_sides(lo, hi)
    (ypay,) = call(edge_rows(B_CODE, ride_x, False), [((2, 24, nz), F32)], f, lo, hi, sums, far)
    yr = both_sides(ypay, "gy")
    (zpay,) = call(pack_z(B_CODE, ride_y, False), [(packed, F32)], f, lo, hi, yr, ypay)
    zr = z_neighbour(zpay, "gz")
    last = (f, a2, ae2, lo, hi, yr, zr, ypay)
    (edge,) = call(
        edge_b(ride_y, ride_z), [((2, 16, nz), BF16)], *last, edge_labels,
        scratch=scratch + [pltpu.VMEM((4, 32, nz), F32)])
    fraction, damage_field, flux_sum, pooled = call(
        step_b(ride_y, ride_z),
        [(block, F32), (block, F32), (block, F32), ((ny // 4, nz), BF16)], *last, labels,
        in_specs=[VMEM] * 8 + [HBM], out_specs=[HBM] * 3 + [VMEM],
        scratch=scratch + [
            pltpu.VMEM((4, ny, nz), F32), pltpu.VMEM(block, jnp.int32),
            pltpu.VMEM(block, F32), pltpu.VMEM(block, F32), pltpu.VMEM(block, F32),
            pltpu.SemaphoreType.DMA, pltpu.SemaphoreType.DMA((3, len(chunks(OFF, OFF + ny, 48))))])
    ids = jnp.broadcast_to(jnp.stack([lax.axis_index(a) for a in ("gx", "gy", "gz")])[:, None], (3, nz))
    crack_score = detector(pooled, edge, ids, weights + (b_first[None], b_second[None]), ny // 4, nz // 4)
    return (fraction, damage_field, flux_sum, crack_score)


CH = 16
CIN = 4
TOP = 8


def iota(shape, dim):
    return lax.broadcasted_iota(jnp.int32, shape, dim)


def lanes_for(n):
    return -(-n // 128) * 128


def one_hot(mask):
    return jnp.where(mask, 1.0, 0.0).astype(BF16)


def mm(a, b):
    return jnp.dot(a, b, preferred_element_type=F32)


SHIFTS = tuple(k for k in range(-3, 10) if k % (16 // CIN) == 3)


def weight_kernel(w1_ref, w2_ref, w3_ref, b3_ref, b1_ref, b2_ref, plane_ref, t1_ref, t2_ref, t3_ref, bias_ref):
    n1 = bias_ref.shape[1]
    pz = 128 // CIN
    spread = one_hot(iota((CH, 128), 1) % CH == iota((CH, 128), 0))
    tile1 = mm(w1_ref[...], spread)
    tile2 = mm(w2_ref[...], spread)
    tile3 = mm(w3_ref[...], one_hot(iota((3, 128), 1) // pz == iota((3, 128), 0)))
    step1 = iota((16, 128), 0) // CIN - iota((16, 128), 1) // CH
    step2 = -(iota((16, 128), 1) // CH)
    step3 = -(iota((16, 128), 1) % pz)

    def tile(source, base, stride, step, shift):
        out = jnp.zeros((16, 128), F32)
        for l in range(3):
            k = base + stride * l
            out = jnp.where(step + shift == l, source[16 * k:16 * k + 16], out)
        return out.astype(BF16)

    zero = jnp.zeros((16, 128), BF16)
    bias_ref[...] = jnp.broadcast_to(b3_ref[...], bias_ref.shape)
    for i in range(3):
        for j in range(3):
            tap = 9 * i + 3 * j
            known = {k: tile(tile1, tap, 1, step1, k) for k in SHIFTS}
            places = [(j * 128 + rb * 16, rb * 16 // CIN) for rb in range(8)]
            places += [(384 + 32 * j, pz), (384 + (32 * j - 16) % 128, -16 // CIN)]
            for row, z_in in places:
                for cb in range(n1 // 128):
                    t1_ref[i, row:row + 16, cb * 128:(cb + 1) * 128] = known.get(z_in - cb * 8 + 3, zero)
            for rb in range(10):
                row = j * 128 + rb * 16 if rb < 8 else 384 + 32 * j + (rb - 8) * 16
                t2_ref[i, row:row + 16, :] = tile(tile2, tap, 1, step2, rb)
        for row in (464, 480):
            for cb in range(n1 // 128):
                t1_ref[i, row:row + 16, cb * 128:(cb + 1) * 128] = zero
        for row in (480, 496):
            t2_ref[i, row:row + 16, :] = zero
        for rb in range(t3_ref.shape[1] // 16):
            t3_ref[i, rb * 16:rb * 16 + 16, :] = tile(tile3, 3 * i, 1, step3, rb) if rb < pz + 2 else zero
    wide = one_hot(iota((CH, n1), 1) % CH == iota((CH, n1), 0)).astype(F32)
    for k, ref in ((0, b1_ref), (1, b2_ref)):
        bias_ref[k:k + 1, :] = jnp.dot(ref[...], wide, precision=lax.Precision.HIGHEST, preferred_element_type=F32)


def weight_rows(w_first, w_second, w_third):
    return (jnp.tile(jnp.swapaxes(w_first, 1, 2), (1, 16 // CIN, 1)).reshape(27 * 16, CH),
            jnp.swapaxes(w_second, 1, 2).reshape(27 * CH, CH),
            w_third.reshape(3, 3, 3, CH).transpose(0, 2, 3, 1).reshape(9 * CH, 3))


def gelu(x):
    return 0.5 * x * (1.0 + jnp.tanh(0.7978845608028654 * (x + 0.044715 * (x * x * x))))


def plane_kernel(py, y_count):
    def kernel(ids_ref, pool_ref, yr_ref, out_ref, scr_ref):
        iy = ids_ref[1:2, 0:1]
        scr_ref[...] = jnp.zeros(scr_ref.shape, F32)
        scr_ref[TOP:TOP + py, :] = pool_ref[0:py, :].astype(F32)
        below = yr_ref[1].astype(F32)[0:3]
        above = yr_ref[0].astype(F32)[0:3]
        scr_ref[TOP - 3:TOP, :] = jnp.where(iy > 0, below, 0.0)
        scr_ref[TOP + py:TOP + py + 3, :] = jnp.where(iy < y_count - 1, above, 0.0)
        out_ref[...] = scr_ref[...].astype(BF16)
    return kernel


def conv_kernel(py, counts, shifts):
    x_count, y_count, z_count = counts
    n = len(shifts)

    def kernel(*refs):
        ids_ref = refs[0]
        own = refs[1:2 + n]
        other = refs[2 + n:3 + 2 * n]
        t1_ref, t2_ref, t3_ref, bias_ref, out_ref = refs[3 + 2 * n:8 + 2 * n]
        in_ref, beside_ref, lhs1_ref, act1_ref, lhs2_ref, act2_ref, tail_ref = refs[8 + 2 * n:]
        ix, iy, iz = ids_ref[0:1, 0:1], ids_ref[1:2, 0:1], ids_ref[2:3, 0:1]
        half = own[0].shape[1]
        pz = half // CIN
        rows = py + 4
        z_row = iota((1, half), 1) // CIN
        z_ok = ((z_row < pz // 2) & (iz < z_count - 1)) | ((z_row >= pz // 2) & (iz > 0))
        for w in range(7):
            o = w - 3
            k = 0 if o == 0 else 1 + shifts.index((-o) % x_count) if (-o) % x_count in shifts else None
            if k is None:
                in_ref[w] = jnp.zeros(in_ref.shape[1:], F32)
                beside_ref[w] = jnp.zeros(in_ref.shape[1:], F32)
                continue
            inside = (ix + o >= 0) & (ix + o < x_count)
            in_ref[w] = jnp.where(inside, own[k][...].astype(F32), 0.0)
            beside_ref[w] = jnp.where(z_ok & inside, other[k][...].astype(F32), 0.0)
        lane = iota((1, 128), 1)

        def shared(parts, first, count):
            out = parts[0]
            for j in (1, 2):
                out = jnp.where(group(lane, j, 128, first, count), pltpu.roll(parts[j], 32 * j, 1), out)
            return out.astype(BF16)

        for w in range(7):
            starts = [TOP - 3 + j for j in range(3)]
            for j, r in enumerate(starts):
                lhs1_ref[w, :, j * 128:(j + 1) * 128] = in_ref[w, r:r + rows, :].astype(BF16)
            lhs1_ref[w, :, 384:512] = shared([beside_ref[w, r:r + rows, :] for r in starts], -3 * CIN, 6 * CIN)
        out = None
        for i in range(3):
            part = mm(lhs1_ref[i:i + 5].reshape(5 * rows, 512), t1_ref[i])
            out = part if out is None else out + part
        width = out.shape[1]
        y = iota((rows, width), 0) - 2
        z = iota((rows, width), 1) // CH - 2
        ok = (z < pz + 2) & ((y >= 0) | (iy > 0)) & ((y < py) | (iy < y_count - 1))
        ok = ok & ((z >= 0) | (iz > 0)) & ((z < pz) | (iz < z_count - 1))
        for p in range(5):
            a = gelu(out[p * rows:(p + 1) * rows] + bias_ref[0:1, :])
            good = ok & (ix + p - 2 >= 0) & (ix + p - 2 < x_count)
            act1_ref[p, 0:rows, 0:width] = jnp.where(good, a, 0.0)
            act1_ref[p, rows:, 0:width] = jnp.zeros((act1_ref.shape[1] - rows, width), F32)
            act1_ref[p, :, width:] = jnp.zeros((act1_ref.shape[1], act1_ref.shape[2] - width), F32)
        blocks = lhs2_ref.shape[1]
        for p in range(5):
            for b in range(blocks):
                for j in range(3):
                    lhs2_ref[p, b, :, j * 128:(j + 1) * 128] = (
                        act1_ref[p, j:j + rows, b * 128:(b + 1) * 128].astype(BF16))
                following = slice((b + 1) * 128, (b + 2) * 128)
                lhs2_ref[p, b, :, 384:512] = shared([act1_ref[p, j:j + rows, following] for j in range(3)], 0, 32)
        out = None
        for i in range(3):
            part = mm(lhs2_ref[i:i + 3].reshape(3 * blocks * rows, 512), t2_ref[i])
            out = part if out is None else out + part
        for b in range(blocks):
            y = iota((rows, 128), 0) - 1
            z = (iota((rows, 128), 1) + b * 128) // CH - 1
            ok = (z < pz + 1) & (y <= py) & ((y >= 0) | (iy > 0)) & ((y < py) | (iy < y_count - 1))
            ok = ok & ((z >= 0) | (iz > 0)) & ((z < pz) | (iz < z_count - 1))
            for p in range(3):
                s = (p * blocks + b) * rows
                a = gelu(out[s:s + rows] + bias_ref[1:2, 0:128])
                good = ok & (ix + p - 1 >= 0) & (ix + p - 1 < x_count)
                act2_ref[p, :, b * 128:(b + 1) * 128] = jnp.where(good, a, 0.0).astype(BF16)
        out = None
        for i in range(3):
            part = mm(act2_ref[i], t3_ref[i])
            out = part if out is None else out + part
        tail_ref[0:rows, :] = out
        score = tail_ref[0:py, :]
        for j in (1, 2):
            score = score + pltpu.roll(tail_ref[j:j + py, :], 128 - j * pz, 1)
        out_ref[0] = jnp.transpose(score)[0:pz, :] + bias_ref[2:3, 0:1]
    return kernel


def detector(pooled, edge, ids, weights, py, pz):
    counts = tuple(lax.axis_size(a) for a in ("gx", "gy", "gz"))
    half = pooled.shape[1]
    assert half == 128 and pz * CIN == half and pz * 3 <= 128
    rows = py + 4
    width = lanes_for((pz + 4) * CH)
    blocks = width // 128
    yr = both_sides(edge, "gy")
    tall = -(-(TOP + py + 3) // 16) * 16
    (plane,) = call(
        plane_kernel(py, counts[1]), [((tall, half), BF16)], ids, pooled, yr,
        scratch=[pltpu.VMEM((tall, half), F32)])
    shifts = []
    for s in (1, -1, 2, -2, 3, -3):
        if s % counts[0] and s % counts[0] not in shifts:
            shifts.append(s % counts[0])
    own = [plane] + [lax.ppermute(plane, "gx", ring("gx", s)) for s in shifts]
    matrices = call(
        weight_kernel,
        [((3, 512, width), BF16), ((3, 512, 128), BF16), ((3, width, 128), BF16), ((8, width), F32)],
        *weights, plane)
    own[-1], *matrices = lax.optimization_barrier((own[-1], *matrices))
    other = [z_neighbour(v, "gz", False) for v in own]
    args = (ids, *own, *other, *matrices)
    (score,) = call(
        conv_kernel(py, counts, shifts), [((1, pz, py), F32)], *args,
        scratch=[
            pltpu.VMEM((7, tall, half), F32),
            pltpu.VMEM((7, tall, half), F32),
            pltpu.VMEM((7, rows, 512), BF16),
            pltpu.VMEM((5, rows + 8, width + 128), F32),
            pltpu.VMEM((5, blocks, rows, 512), BF16),
            pltpu.VMEM((3, rows, width), BF16),
            pltpu.VMEM((rows + 8, 128), F32),
        ], mib=32)
    return jnp.swapaxes(score, 1, 2)


def solution(mesh):
    slab = P(("groups", "gx"), "gy", "gz")
    return jax.shard_map(
        body,
        mesh=mesh,
        in_specs=(slab, slab, slab, P(), P(), P(), P(), P(), P()),
        out_specs=(slab, slab, slab, slab),
        check_vma=False,
    )
```

```python
import functools

import jax
import jax.numpy as jnp
import numpy as np
from jax import lax
from jax.experimental import pallas as pl
from jax.experimental.pallas import tpu as pltpu
from jax.sharding import PartitionSpec as P

F32 = jnp.float32
BF16 = jnp.bfloat16
I16 = jnp.int16
WELL_HEIGHT = 1.0
STRAIN_COUPLING = 4.0
TIME_STEP = 0.01
DAMAGE_RATE = 0.8
ENERGY_CRITICAL = 0.02

OFF = 16
A_CODE = (0.0, 1.0)
B_CODE = (-1.1, 3.1)
SUM_LOW, SUM_SPAN = -1280.0, 4096.0

VMEM = pl.BlockSpec(memory_space=pltpu.VMEM)
HBM = pl.BlockSpec(memory_space=pltpu.HBM)


def to_code(x, code):
    low, span = code
    v = (x - low) * (65535.0 / span) - 32768.0
    return jnp.clip(jnp.round(v), -32768.0, 32767.0).astype(jnp.int32).astype(I16)


def from_code(q, code):
    low, span = code
    return q.astype(jnp.int32).astype(F32) * (span / 65535.0) + (low + 32768.0 * span / 65535.0)


def sum_digits(s):
    v = (s[0:2] - SUM_LOW) * (65536.0 / SUM_SPAN)
    high = jnp.floor(v)
    low = jnp.minimum(jnp.floor((v - high) * 65536.0), 65535.0)
    rows = jnp.concatenate([high, low, jnp.full((12, s.shape[1]), 32768.0, F32)]) - 32768.0
    return rows.astype(jnp.int32).astype(I16)


def from_digits(tile):
    v = tile.astype(jnp.int32).astype(F32) + 32768.0
    return (v[0:2] + v[2:4] * (1.0 / 65536.0)) * (SUM_SPAN / 65536.0) + SUM_LOW


def each(count, looped, body):
    def step(i, carry):
        body(i)
        return carry
    if looped:
        lax.fori_loop(0, count, step, 0)
    else:
        for i in range(count):
            body(i)


def by_label(labels, values):
    return jnp.where(labels == 0, values[0], jnp.where(labels == 1, values[1], values[2])).astype(F32)


FACTORS = (1.0, 0.3, 0.05)
ROOTS = tuple(float(np.sqrt(np.float32(v))) for v in FACTORS)


def call(kernel, outs, *args, in_specs=None, out_specs=None, scratch=(), mib=16):
    return pl.pallas_call(
        kernel,
        in_specs=in_specs or [VMEM] * len(args),
        out_specs=out_specs or [VMEM] * len(outs),
        out_shape=[jax.ShapeDtypeStruct(s, t) for s, t in outs],
        scratch_shapes=scratch,
        compiler_params=pltpu.CompilerParams(vmem_limit_bytes=mib * 1024 * 1024),
    )(*args)


def chunks(start, stop, size):
    return [(r, min(size, stop - r)) for r in range(start, stop, size)]


def fold(x):
    return x.reshape(x.shape[0] // 8, 8, x.shape[1]).sum(0)


def to_rows(top, bottom):
    return jnp.concatenate([jnp.sum(top, 0, keepdims=True), jnp.sum(bottom, 0, keepdims=True),
                            jnp.zeros((6, top.shape[1]), F32)])


def first_kernel(c_hbm, d_hbm, l_hbm, f_ref, amp_ref, lo_ref, hi_ref, sum_ref, le_ref, d_ref, l_ref, sems):
    nx, ny, nz = f_ref.shape
    order = [0, nx - 1] + list(range(1, nx - 1))
    copies = []
    for x in order:
        copies.append([pltpu.make_async_copy(src.at[x], dst.at[x], sems.at[k, x])
                       for k, (src, dst) in enumerate(((c_hbm, f_ref), (d_hbm, d_ref), (l_hbm, l_ref)))])
        for c in copies[-1]:
            c.start()
    top = jnp.zeros((8, nz), F32)
    bottom = jnp.zeros((8, nz), F32)
    for k, x in enumerate(order):
        for c in copies[k]:
            c.wait()
        le_ref[x, 0:16, :] = l_ref[x, 0:16, :]
        le_ref[x, 16:32, :] = l_ref[x, ny - 16:ny, :]
        for r, n in chunks(0, ny, 48):
            f = f_ref[x, r:r + n, :]
            a = by_label(l_ref[x, r:r + n, :], ROOTS) * (1.0 - d_ref[x, r:r + n, :])
            amp_ref[x, r:r + n, :] = a
            m = a * a
            top = top + fold(m * f)
            bottom = bottom + fold(m)
            for near, far, out in ((0, 1, lo_ref), (nx - 1, nx - 2, hi_ref)):
                if x == near:
                    out[r:r + n, :] = to_code(f, A_CODE)
                    out[2 * ny + r:2 * ny + r + n, :] = to_code(a, A_CODE)
                if x == far:
                    out[ny + r:ny + r + n, :] = to_code(f, A_CODE)
    s = to_rows(top, bottom)
    sum_ref[...] = s
    lo_ref[3 * ny:3 * ny + 16, :] = sum_digits(s)
    hi_ref[3 * ny:3 * ny + 16, :] = sum_digits(s)


def edge_rows(code, ride_x, with_amp):
    def kernel(*refs):
        f_ref = refs[0]
        amp_ref = refs[1] if with_amp else None
        lo_ref, hi_ref, s_ref, far_ref = refs[1 + with_amp:5 + with_amp]
        out_ref = refs[-1]
        nx, ny, nz = f_ref.shape
        low_rows = [from_code(r[0:16, :], code)[0:1] for r in (lo_ref, hi_ref)]
        high_rows = [from_code(r[ny - 16:ny, :], code)[15:16] for r in (lo_ref, hi_ref)]
        s = s_ref[...]
        if ride_x:
            s = s + far_ref[...]
        for side, first, second, beside in ((0, 0, 1, low_rows), (1, ny - 1, ny - 2, high_rows)):
            for x in range(nx):
                out_ref[side, 2 * x:2 * x + 1, :] = f_ref[x, first:first + 1, :]
                out_ref[side, 2 * x + 1:2 * x + 2, :] = f_ref[x, second:second + 1, :]
                if amp_ref is not None:
                    out_ref[side, 10 + x:11 + x, :] = amp_ref[x, first:first + 1, :]
            out_ref[side, 8:9, :] = beside[0]
            out_ref[side, 9:10, :] = beside[1]
            out_ref[side, 16:24, :] = s
            if ride_x:
                out_ref[side, 16:18, :] = (s[0:2] + from_digits(lo_ref[lo_ref.shape[0] - 16:, :])
                                           + from_digits(hi_ref[hi_ref.shape[0] - 16:, :]))
    return kernel


def group(lane, j, nz, first, count):
    return (lane - (32 * j + first)) % nz < count


def pack_z(code, ride_y, with_amp):
    def kernel(*refs):
        f_ref = refs[0]
        amp_ref = refs[1] if with_amp else None
        lo_ref, hi_ref, yr_ref, yp_ref, out_ref = refs[1 + with_amp:]
        nx, ny, nz = f_ref.shape
        end = OFF + ny
        lane = lax.broadcasted_iota(jnp.int32, (1, nz), 1)
        for k in range(out_ref.shape[0]):
            planes = [p for p in range(4 * k, 4 * k + 4) if p < nx + 2]

            def packed(f_of, a_of, ps):
                out = None
                for p in ps:
                    j = p % 4
                    f = f_of(p)
                    f = pltpu.roll(f, 32 * j, 1) if j else f
                    out = f if out is None else jnp.where(group(lane, j, nz, -2, 4), f, out)
                    a = a_of(p)
                    if a is not None:
                        out = jnp.where(group(lane, j, nz, 15, 2), pltpu.roll(a, 32 * j + 16, 1), out)
                return out

            for r, n in chunks(0, ny, 48):
                def f_of(p):
                    if p == 0:
                        return from_code(lo_ref[r:r + n, :], code)
                    if p == nx + 1:
                        return from_code(hi_ref[r:r + n, :], code)
                    return f_ref[p - 1, r:r + n, :]

                def a_of(p):
                    return amp_ref[p - 1, r:r + n, :] if with_amp and 1 <= p <= nx else None

                out_ref[k, OFF + r:OFF + r + n, :] = packed(f_of, a_of, planes)
            inner = [p for p in planes if 1 <= p <= nx]
            if inner:
                for side, near in ((1, OFF - 1), (0, end)):
                    out_ref[k, near:near + 1, :] = packed(
                        lambda p: yr_ref[side, 2 * (p - 1):2 * (p - 1) + 1, :], lambda p: None, inner)
        s = yp_ref[0, 16:24, :]
        out_ref[0, 0:8, :] = s + yr_ref[0, 16:24, :] if ride_y else s
    return kernel


def spread(spans, extra, size):
    return [v for a, b in spans for v in chunks(OFF + a - extra, OFF + b + extra, size)]


def fill(code, f_ref, lo_ref, hi_ref, yr_ref, zr_ref, pad_ref, ze_ref, spans):
    nx, ny, nz = f_ref.shape
    end = OFF + ny
    wide = [v for a, b in spans for v in chunks(max(a - 16, 0), min(b + 16, ny), 48)]
    for near, far, ref in ((1, 0, lo_ref), (nx + 2, nx + 3, hi_ref)):
        for r, n in wide:
            pad_ref[near, OFF + r:OFF + r + n, :] = from_code(ref[r:r + n, :], code)
            pad_ref[far, OFF + r:OFF + r + n, :] = from_code(ref[ny + r:ny + r + n, :], code)
    for p, k in ((1, 8), (nx + 2, 9)):
        pad_ref[p, OFF - 1:OFF, :] = yr_ref[1, k:k + 1, :]
        pad_ref[p, end:end + 1, :] = yr_ref[0, k:k + 1, :]
    for x in range(nx):
        for r, n in wide:
            pad_ref[x + 2, OFF + r:OFF + r + n, :] = f_ref[x, r:r + n, :]
        for side, near, far in ((1, OFF - 1, OFF - 2), (0, end, end + 1)):
            pad_ref[x + 2, near:near + 1, :] = yr_ref[side, 2 * x:2 * x + 1, :]
            pad_ref[x + 2, far:far + 1, :] = yr_ref[side, 2 * x + 1:2 * x + 2, :]
    for p in range(nx + 2):
        for r, n in spread(spans, 8, 32):
            e = zr_ref[p // 4, r:r + n, :]
            ze_ref[p, r:r + n, :] = pltpu.roll(e, nz - 32 * (p % 4), 1) if p % 4 else e


def weighted_mean(yp_ref, yr_ref, zr_ref, ride_y, ride_z):
    s = yp_ref[0, 16:24, :]
    if ride_y:
        s = s + yr_ref[0, 16:24, :]
    if ride_z:
        s = s + zr_ref[0, 0:8, :]
    return jnp.sum(s[0:1], keepdims=True) / jnp.sum(s[1:2], keepdims=True)


def worn(a, m, f, mean):
    e = f - mean
    loss = DAMAGE_RATE * 0.5 * STRAIN_COUPLING * (m * (e * e)) - DAMAGE_RATE * ENERGY_CRITICAL
    return a * (1.0 - jnp.maximum(loss, 0.0))


class Geometry:
    def __init__(self, nx, ny, nz):
        self.nx, self.ny, self.nz = nx, ny, nz
        self.lane = lax.broadcasted_iota(jnp.int32, (1, nz), 1)
        self.first = self.lane == 0
        self.last = self.lane == nz - 1

    def before(self, own, other):
        return pltpu.roll(jnp.where(self.last, other, own), 1, 1)

    def after(self, own, other):
        return pltpu.roll(jnp.where(self.first, other, own), self.nz - 1, 1)


def chem_of(f, m, around, mean):
    w = 2.0 * WELL_HEIGHT
    return ((2.0 * w * f - 3.0 * w) * f + (w + 6.0)) * f - around + STRAIN_COUPLING * (m * (f - mean))


def chemistry(g, pad_ref, mob_ref, mobe_ref, ze_ref, chem_ref, cheme_ref, mean, spans, looped=False):
    nx = g.nx

    @functools.partial(each, nx + 2, looped)
    def _(p):
        for r, n in spread(spans, 0, 48) if not looped and p in (0, nx + 1) else spread(spans, 8, 32):
            f = pad_ref[p + 1, r:r + n, :]
            e = ze_ref[p, r:r + n, :]
            around = (pad_ref[p, r:r + n, :] + pad_ref[p + 2, r:r + n, :]
                      + pad_ref[p + 1, r - 1:r - 1 + n, :] + pad_ref[p + 1, r + 1:r + 1 + n, :]
                      + g.before(f, e) + g.after(f, e))
            chem_ref[p, r:r + n, :] = chem_of(f, mob_ref[p, r:r + n, :], around, mean)

    @functools.partial(each, nx, looped)
    def _(x):
        p = x + 1
        for r, n in spread(spans, 0, 48):
            f = pad_ref[p + 1, r:r + n, :]
            e = ze_ref[p, r:r + n, :]
            around = (ze_ref[p - 1, r:r + n, :] + ze_ref[p + 1, r:r + n, :]
                      + ze_ref[p, r - 1:r - 1 + n, :] + ze_ref[p, r + 1:r + 1 + n, :]
                      + g.before(e, f) + g.after(e, f))
            cheme_ref[x, r - OFF:r - OFF + n, :] = chem_of(
                e, mobe_ref[x, r - OFF:r - OFF + n, :], around, mean)


def flux_of(g, x, r, n, mob_ref, mobe_ref, chem_ref, cheme_ref):
    p = x + 1
    m = mob_ref[p, r:r + n, :]
    q = chem_ref[p, r:r + n, :]
    me = mobe_ref[x, r - OFF:r - OFF + n, :]
    qe = cheme_ref[x, r - OFF:r - OFF + n, :]
    total = None
    for nm, nq in (
        (mob_ref[p - 1, r:r + n, :], chem_ref[p - 1, r:r + n, :]),
        (mob_ref[p + 1, r:r + n, :], chem_ref[p + 1, r:r + n, :]),
        (mob_ref[p, r - 1:r - 1 + n, :], chem_ref[p, r - 1:r - 1 + n, :]),
        (mob_ref[p, r + 1:r + 1 + n, :], chem_ref[p, r + 1:r + 1 + n, :]),
        (g.before(m, me), g.before(q, qe)),
        (g.after(m, me), g.after(q, qe)),
    ):
        term = (nm + m) * (nq - q)
        total = term if total is None else total + term
    return m, 0.5 * total


def pack_edges(values, lane, nz):
    out = values[0]
    for x, v in enumerate(values[1:], 1):
        out = jnp.where(group(lane, x, nz, -1, 2), pltpu.roll(v, 32 * x, 1), out)
    return out


def step_a(ride_y, ride_z):
    def kernel(f_ref, amp_ref, lo_ref, hi_ref, yr_ref, zr_ref, yp_ref,
               f2_ref, a2_ref, ae2_ref, lo_out, hi_out, sum_ref,
               pad_ref, ze_ref, mob_ref, mobe_ref, chem_ref, cheme_ref):
        nx, ny, nz = f2_ref.shape
        end = OFF + ny
        g = Geometry(nx, ny, nz)
        mean = weighted_mean(yp_ref, yr_ref, zr_ref, ride_y, ride_z)
        fill(A_CODE, f_ref, lo_ref, hi_ref, yr_ref, zr_ref, pad_ref, ze_ref, [(0, ny)])

        def wear(p, r, n, a):
            m = a * a
            mob_ref[p, r:r + n, :] = m
            a2_ref[p, r:r + n, :] = worn(a, m, pad_ref[p + 1, r:r + n, :], mean)

        for r, n in chunks(0, ny, 48):
            wear(0, OFF + r, n, from_code(lo_ref[2 * ny + r:2 * ny + r + n, :], A_CODE))
            wear(nx + 1, OFF + r, n, from_code(hi_ref[2 * ny + r:2 * ny + r + n, :], A_CODE))
            edges = []
            for x in range(nx):
                wear(x + 1, OFF + r, n, amp_ref[x, r:r + n, :])
                p = x + 1
                a = pltpu.roll(zr_ref[p // 4, OFF + r:OFF + r + n, :], nz - 32 * (p % 4) - 16, 1)
                m = a * a
                mobe_ref[x, r:r + n, :] = m
                edges.append(worn(a, m, ze_ref[p, OFF + r:OFF + r + n, :], mean))
            ae2_ref[r:r + n, :] = pack_edges(edges, g.lane, nz)
        for x in range(nx):
            wear(x + 1, OFF - 1, 1, yr_ref[1, 10 + x:11 + x, :])
            wear(x + 1, end, 1, yr_ref[0, 10 + x:11 + x, :])
        chemistry(g, pad_ref, mob_ref, mobe_ref, ze_ref, chem_ref, cheme_ref, mean, [(0, ny)])
        top = jnp.zeros((8, nz), F32)
        bottom = jnp.zeros((8, nz), F32)
        for x in range(nx):
            for r, n in chunks(OFF, end, 48):
                _, flux = flux_of(g, x, r, n, mob_ref, mobe_ref, chem_ref, cheme_ref)
                f = pad_ref[x + 2, r:r + n, :] + TIME_STEP * flux
                s = slice(r - OFF, r - OFF + n)
                f2_ref[x, s, :] = f
                a = a2_ref[x + 1, r:r + n, :]
                m = a * a
                top = top + fold(m * f)
                bottom = bottom + fold(m)
                for near, far, out in ((0, 1, lo_out), (nx - 1, nx - 2, hi_out)):
                    if x == near:
                        out[s, :] = to_code(f, B_CODE)
                    if x == far:
                        out[r - OFF + ny:r - OFF + ny + n, :] = to_code(f, B_CODE)
        s = to_rows(top, bottom)
        sum_ref[...] = s
        lo_out[2 * ny:2 * ny + 16, :] = sum_digits(s)
        hi_out[2 * ny:2 * ny + 16, :] = sum_digits(s)
    return kernel


def potentials_b(g, mean, a2_ref, ae2_ref, others, scratch, spans, looped):
    f_ref, lo_ref, hi_ref, yr_ref, zr_ref = others
    pad_ref, ze_ref, mob_ref, mobe_ref, chem_ref, cheme_ref = scratch
    nx, nz = g.nx, g.nz
    fill(B_CODE, f_ref, lo_ref, hi_ref, yr_ref, zr_ref, pad_ref, ze_ref, spans)

    @functools.partial(each, nx + 2, looped)
    def _(p):
        for r, n in spread(spans, 8, 32):
            a = a2_ref[p, r:r + n, :]
            mob_ref[p, r:r + n, :] = a * a

    for r, n in spread(spans, 0, 48):
        a = ae2_ref[r - OFF:r - OFF + n, :]
        a = a * a
        for x in range(nx):
            mobe_ref[x, r - OFF:r - OFF + n, :] = pltpu.roll(a, nz - 32 * x, 1) if x else a
    chemistry(g, pad_ref, mob_ref, mobe_ref, ze_ref, chem_ref, cheme_ref, mean, spans, looped)


def finish_b(g, mean, x, r, n, labels, a2_ref, scratch):
    pad_ref, ze_ref, mob_ref, mobe_ref, chem_ref, cheme_ref = scratch
    m, flux = flux_of(g, x, r, n, mob_ref, mobe_ref, chem_ref, cheme_ref)
    f0 = pad_ref[x + 2, r:r + n, :]
    f = f0 + TIME_STEP * flux
    a = worn(a2_ref[x + 1, r:r + n, :], m, f0, mean)
    dmg = 1.0 - a * by_label(labels, tuple(1.0 / v for v in ROOTS))
    return flux, (f, dmg, a * a, by_label(labels, FACTORS))


def pool_rows(scr_ref, count, nz):
    k = lax.broadcasted_iota(jnp.int32, (4 * nz, nz), 0)
    out = lax.broadcasted_iota(jnp.int32, (4 * nz, nz), 1)
    pick = jnp.where((k % nz // 4 == out // 4) & (out % 4 == k // nz), 1.0 / 64.0, 0.0).astype(BF16)
    high, low = [], []
    for i in range(4):
        rows = (scr_ref[i, pl.ds(0, count, stride=4), :] + scr_ref[i, pl.ds(1, count, stride=4), :]
                + scr_ref[i, pl.ds(2, count, stride=4), :] + scr_ref[i, pl.ds(3, count, stride=4), :])
        high.append(rows.astype(BF16))
        low.append((rows - high[-1].astype(F32)).astype(BF16))
    return sum(jnp.dot(jnp.concatenate(v, axis=1), pick, preferred_element_type=F32) for v in (high, low))


def edge_b(ride_y, ride_z):
    def kernel(f_ref, a2_ref, ae2_ref, lo_ref, hi_ref, yr_ref, zr_ref, yp_ref, l_ref, edge_ref, *rest):
        *scratch, pool_scr = rest
        nx, ny, nz = f_ref.shape
        spans = [(0, 16), (ny - 16, ny)]
        g = Geometry(nx, ny, nz)
        mean = weighted_mean(yp_ref, yr_ref, zr_ref, ride_y, ride_z)
        potentials_b(g, mean, a2_ref, ae2_ref, (f_ref, lo_ref, hi_ref, yr_ref, zr_ref), scratch, spans, False)
        for k, (a, b) in enumerate(spans):
            s = slice(16 * k, 16 * k + 16)
            pooled = [None] * 4
            for x in range(nx):
                _, values = finish_b(g, mean, x, OFF + a, 16, l_ref[x, s, :], a2_ref, scratch)
                pooled = [v if p is None else p + v for p, v in zip(pooled, values)]
            for i in range(4):
                pool_scr[i, s, :] = pooled[i]
        total = pool_rows(pool_scr, 8, nz)
        blank = jnp.zeros((13, nz), F32)
        edge_ref[0] = jnp.concatenate([total[0:3], blank]).astype(BF16)
        edge_ref[1] = jnp.concatenate([total[5:8], blank]).astype(BF16)
    return kernel


def step_b(ride_y, ride_z):
    def kernel(f_ref, a2_ref, ae2_ref, lo_ref, hi_ref, yr_ref, zr_ref, yp_ref, l_hbm,
               f3_ref, dmg_ref, flux_ref, pool_ref, *rest):
        *scratch, pool_scr, l_ref, l_sem = rest
        nx, ny, nz = f_ref.shape
        labels_in = pltpu.make_async_copy(l_hbm, l_ref, l_sem)
        labels_in.start()
        g = Geometry(nx, ny, nz)
        mean = weighted_mean(yp_ref, yr_ref, zr_ref, ride_y, ride_z)
        potentials_b(g, mean, a2_ref, ae2_ref, (f_ref, lo_ref, hi_ref, yr_ref, zr_ref), scratch, [(0, ny)], True)
        labels_in.wait()
        for r, n in chunks(OFF, OFF + ny, 48):
            s = slice(r - OFF, r - OFF + n)
            pooled = [None] * 4
            for x in range(nx):
                flux, values = finish_b(g, mean, x, r, n, l_ref[x, s, :], a2_ref, scratch)
                f3_ref[x, s, :] = values[0]
                dmg_ref[x, s, :] = values[1]
                flux_ref[x, s, :] = flux
                pooled = [v if p is None else p + v for p, v in zip(pooled, values)]
            for i in range(4):
                pool_scr[i, s, :] = pooled[i]
        pool_ref[...] = pool_rows(pool_scr, ny // 4, nz).astype(BF16)
    return kernel


def ring(axis, shift):
    count = lax.axis_size(axis)
    return [(i, (i + shift) % count) for i in range(count)]


def pair_sum(s, axis):
    count = lax.axis_size(axis)
    if count & (count - 1):
        return lax.psum(s, axis)
    bit = 1
    while bit < count:
        s = s + lax.ppermute(s, axis, [(i, i ^ bit) for i in range(count)])
        bit *= 2
    return s


def both_sides(pay, axis):
    if lax.axis_size(axis) == 2:
        return lax.ppermute(pay, axis, ring(axis, 1))
    return jnp.stack([lax.ppermute(pay[0], axis, ring(axis, -1)), lax.ppermute(pay[1], axis, ring(axis, 1))])


def z_neighbour(pay, axis, packed=True):
    if lax.axis_size(axis) == 2:
        return lax.ppermute(pay, axis, ring(axis, 1))
    above = lax.ppermute(pay, axis, ring(axis, -1))
    below = lax.ppermute(pay, axis, ring(axis, 1))
    lane = lax.broadcasted_iota(jnp.int32, pay.shape, pay.ndim - 1)
    if packed:
        low = (lane % 32 < 8) | (lane % 32 == 16)
    else:
        low = lane < pay.shape[-1] // 2
    return jnp.where(low, above, below)


def x_sides(lo, hi):
    return lax.ppermute(hi, "gx", ring("gx", 1)), lax.ppermute(lo, "gx", ring("gx", -1))


def body(concentration, damage, labels, w_first, b_first, w_second, b_second, w_third, b_third):
    nx, ny, nz = concentration.shape
    rows = ny + 2 * OFF
    block = (nx, ny, nz)
    padded = (nx + 2, rows, nz)
    ride_x = lax.axis_size("gx") == 4
    ride_y = lax.axis_size("gy") == 2
    ride_z = lax.axis_size("gz") == 2
    packed = (-(-(nx + 2) // 4), rows, nz)
    assert nz == 128
    scratch = [pltpu.VMEM((nx + 4, rows, nz), F32), pltpu.VMEM(padded, F32), pltpu.VMEM(padded, F32),
               pltpu.VMEM(block, F32), pltpu.VMEM(padded, F32), pltpu.VMEM(block, F32)]

    def start(sums):
        if ride_x:
            return sums, lax.ppermute(sums, "gx", ring("gx", 2))
        sums = pair_sum(sums, "gx")
        for axis, ride in (("gy", ride_y), ("gz", ride_z)):
            if not ride:
                sums = pair_sum(sums, axis)
        return sums, sums

    concentration, damage, labels = (
        pltpu.with_memory_space_constraint(v, pltpu.HBM) for v in (concentration, damage, labels))
    tall = 3 * ny + 16
    f, amp, lo, hi, sums, edge_labels = call(
        first_kernel,
        [(block, F32), (block, F32), ((tall, nz), I16), ((tall, nz), I16), ((8, nz), F32),
         ((nx, 32, nz), jnp.int32)],
        concentration, damage, labels,
        in_specs=[HBM] * 3,
        scratch=[pltpu.VMEM(block, F32), pltpu.VMEM(block, jnp.int32), pltpu.SemaphoreType.DMA((3, nx))])
    weights = weight_rows(w_first, w_second, w_third) + (b_third[None],)
    sums, far = start(sums)
    lo, hi = x_sides(lo, hi)
    (ypay,) = call(edge_rows(A_CODE, ride_x, True), [((2, 24, nz), F32)], f, amp, lo, hi, sums, far, *weights)
    yr = both_sides(ypay, "gy")
    (zpay,) = call(pack_z(A_CODE, ride_y, True), [(packed, F32)], f, amp, lo, hi, yr, ypay)
    zr = z_neighbour(zpay, "gz")
    tall = 2 * ny + 16
    f, a2, ae2, lo, hi, sums = call(
        step_a(ride_y, ride_z),
        [(block, F32), (padded, F32), ((ny, nz), F32), ((tall, nz), I16), ((tall, nz), I16), ((8, nz), F32)],
        f, amp, lo, hi, yr, zr, ypay, scratch=scratch)

    sums, far = start(sums)
    lo, hi = x_sides(lo, hi)
    (ypay,) = call(edge_rows(B_CODE, ride_x, False), [((2, 24, nz), F32)], f, lo, hi, sums, far)
    yr = both_sides(ypay, "gy")
    (zpay,) = call(pack_z(B_CODE, ride_y, False), [(packed, F32)], f, lo, hi, yr, ypay)
    zr = z_neighbour(zpay, "gz")
    last = (f, a2, ae2, lo, hi, yr, zr, ypay)
    (edge,) = call(
        edge_b(ride_y, ride_z), [((2, 16, nz), BF16)], *last, edge_labels,
        scratch=scratch + [pltpu.VMEM((4, 32, nz), F32)])
    fraction, damage_field, flux_sum, pooled = pl.pallas_call(
        step_b(ride_y, ride_z),
        in_specs=[VMEM] * 8 + [HBM],
        out_specs=[VMEM] * 4,
        out_shape=[pltpu.VMEM(block, F32)] * 3 + [jax.ShapeDtypeStruct((ny // 4, nz), BF16)],
        scratch_shapes=scratch + [
            pltpu.VMEM((4, ny, nz), F32), pltpu.VMEM(block, jnp.int32), pltpu.SemaphoreType.DMA],
        compiler_params=pltpu.CompilerParams(vmem_limit_bytes=16 * 1024 * 1024),
    )(*last, labels)
    ids = jnp.broadcast_to(jnp.stack([lax.axis_index(a) for a in ("gx", "gy", "gz")])[:, None], (3, nz))
    return detector(
        pooled, edge, ids, weights + (b_first[None], b_second[None]), (fraction, damage_field, flux_sum), ny // 4, nz // 4)


CH = 16
CIN = 4
TOP = 8


def iota(shape, dim):
    return lax.broadcasted_iota(jnp.int32, shape, dim)


def lanes_for(n):
    return -(-n // 128) * 128


def one_hot(mask):
    return jnp.where(mask, 1.0, 0.0).astype(BF16)


def mm(a, b):
    return jnp.dot(a, b, preferred_element_type=F32)


SHIFTS = tuple(k for k in range(-3, 10) if k % (16 // CIN) == 3)


def weight_kernel(w1_ref, w2_ref, w3_ref, b3_ref, b1_ref, b2_ref, plane_ref, t1_ref, t2_ref, t3_ref, bias_ref):
    n1 = bias_ref.shape[1]
    pz = 128 // CIN
    spread = one_hot(iota((CH, 128), 1) % CH == iota((CH, 128), 0))
    tile1 = mm(w1_ref[...], spread)
    tile2 = mm(w2_ref[...], spread)
    tile3 = mm(w3_ref[...], one_hot(iota((3, 128), 1) // pz == iota((3, 128), 0)))
    step1 = iota((16, 128), 0) // CIN - iota((16, 128), 1) // CH
    step2 = -(iota((16, 128), 1) // CH)
    step3 = -(iota((16, 128), 1) % pz)

    def tile(source, base, stride, step, shift):
        out = jnp.zeros((16, 128), F32)
        for l in range(3):
            k = base + stride * l
            out = jnp.where(step + shift == l, source[16 * k:16 * k + 16], out)
        return out.astype(BF16)

    zero = jnp.zeros((16, 128), BF16)
    bias_ref[...] = jnp.broadcast_to(b3_ref[...], bias_ref.shape)
    for i in range(3):
        for j in range(3):
            tap = 9 * i + 3 * j
            known = {k: tile(tile1, tap, 1, step1, k) for k in SHIFTS}
            places = [(j * 128 + rb * 16, rb * 16 // CIN) for rb in range(8)]
            places += [(384 + 32 * j, pz), (384 + (32 * j - 16) % 128, -16 // CIN)]
            for row, z_in in places:
                for cb in range(n1 // 128):
                    t1_ref[i, row:row + 16, cb * 128:(cb + 1) * 128] = known.get(z_in - cb * 8 + 3, zero)
            for rb in range(10):
                row = j * 128 + rb * 16 if rb < 8 else 384 + 32 * j + (rb - 8) * 16
                t2_ref[i, row:row + 16, :] = tile(tile2, tap, 1, step2, rb)
        for row in (464, 480):
            for cb in range(n1 // 128):
                t1_ref[i, row:row + 16, cb * 128:(cb + 1) * 128] = zero
        for row in (480, 496):
            t2_ref[i, row:row + 16, :] = zero
        for rb in range(t3_ref.shape[1] // 16):
            t3_ref[i, rb * 16:rb * 16 + 16, :] = tile(tile3, 3 * i, 1, step3, rb) if rb < pz + 2 else zero
    wide = one_hot(iota((CH, n1), 1) % CH == iota((CH, n1), 0)).astype(F32)
    for k, ref in ((0, b1_ref), (1, b2_ref)):
        bias_ref[k:k + 1, :] = jnp.dot(ref[...], wide, precision=lax.Precision.HIGHEST, preferred_element_type=F32)


def weight_rows(w_first, w_second, w_third):
    return (jnp.tile(jnp.swapaxes(w_first, 1, 2), (1, 16 // CIN, 1)).reshape(27 * 16, CH),
            jnp.swapaxes(w_second, 1, 2).reshape(27 * CH, CH),
            w_third.reshape(3, 3, 3, CH).transpose(0, 2, 3, 1).reshape(9 * CH, 3))


def gelu(x):
    return 0.5 * x * (1.0 + jnp.tanh(0.7978845608028654 * (x + 0.044715 * (x * x * x))))


def plane_kernel(py, y_count):
    def kernel(ids_ref, pool_ref, yr_ref, out_ref, scr_ref):
        iy = ids_ref[1:2, 0:1]
        scr_ref[...] = jnp.zeros(scr_ref.shape, F32)
        scr_ref[TOP:TOP + py, :] = pool_ref[0:py, :].astype(F32)
        below = yr_ref[1].astype(F32)[0:3]
        above = yr_ref[0].astype(F32)[0:3]
        scr_ref[TOP - 3:TOP, :] = jnp.where(iy > 0, below, 0.0)
        scr_ref[TOP + py:TOP + py + 3, :] = jnp.where(iy < y_count - 1, above, 0.0)
        out_ref[...] = scr_ref[...].astype(BF16)
    return kernel


def conv_kernel(py, counts, shifts):
    x_count, y_count, z_count = counts
    n = len(shifts)

    def kernel(*refs):
        ids_ref = refs[0]
        own = refs[1:2 + n]
        other = refs[2 + n:3 + 2 * n]
        t1_ref, t2_ref, t3_ref, bias_ref = refs[3 + 2 * n:7 + 2 * n]
        fields = refs[7 + 2 * n:10 + 2 * n]
        out_ref = refs[10 + 2 * n]
        fields_hbm = refs[11 + 2 * n:14 + 2 * n]
        in_ref, beside_ref, lhs1_ref, act1_ref, lhs2_ref, act2_ref, tail_ref, sems = refs[14 + 2 * n:]
        copies = [pltpu.make_async_copy(src, dst, sems.at[k]) for k, (src, dst) in enumerate(zip(fields, fields_hbm))]
        for c in copies:
            c.start()
        ix, iy, iz = ids_ref[0:1, 0:1], ids_ref[1:2, 0:1], ids_ref[2:3, 0:1]
        half = own[0].shape[1]
        pz = half // CIN
        rows = py + 4
        z_row = iota((1, half), 1) // CIN
        z_ok = ((z_row < pz // 2) & (iz < z_count - 1)) | ((z_row >= pz // 2) & (iz > 0))
        for w in range(7):
            o = w - 3
            k = 0 if o == 0 else 1 + shifts.index((-o) % x_count) if (-o) % x_count in shifts else None
            if k is None:
                in_ref[w] = jnp.zeros(in_ref.shape[1:], F32)
                beside_ref[w] = jnp.zeros(in_ref.shape[1:], F32)
                continue
            inside = (ix + o >= 0) & (ix + o < x_count)
            in_ref[w] = jnp.where(inside, own[k][...].astype(F32), 0.0)
            beside_ref[w] = jnp.where(z_ok & inside, other[k][...].astype(F32), 0.0)
        lane = iota((1, 128), 1)

        def shared(parts, first, count):
            out = parts[0]
            for j in (1, 2):
                out = jnp.where(group(lane, j, 128, first, count), pltpu.roll(parts[j], 32 * j, 1), out)
            return out.astype(BF16)

        for w in range(7):
            starts = [TOP - 3 + j for j in range(3)]
            for j, r in enumerate(starts):
                lhs1_ref[w, :, j * 128:(j + 1) * 128] = in_ref[w, r:r + rows, :].astype(BF16)
            lhs1_ref[w, :, 384:512] = shared([beside_ref[w, r:r + rows, :] for r in starts], -3 * CIN, 6 * CIN)
        out = None
        for i in range(3):
            part = mm(lhs1_ref[i:i + 5].reshape(5 * rows, 512), t1_ref[i])
            out = part if out is None else out + part
        width = out.shape[1]
        y = iota((rows, width), 0) - 2
        z = iota((rows, width), 1) // CH - 2
        ok = (z < pz + 2) & ((y >= 0) | (iy > 0)) & ((y < py) | (iy < y_count - 1))
        ok = ok & ((z >= 0) | (iz > 0)) & ((z < pz) | (iz < z_count - 1))
        for p in range(5):
            a = gelu(out[p * rows:(p + 1) * rows] + bias_ref[0:1, :])
            good = ok & (ix + p - 2 >= 0) & (ix + p - 2 < x_count)
            act1_ref[p, 0:rows, 0:width] = jnp.where(good, a, 0.0)
            act1_ref[p, rows:, 0:width] = jnp.zeros((act1_ref.shape[1] - rows, width), F32)
            act1_ref[p, :, width:] = jnp.zeros((act1_ref.shape[1], act1_ref.shape[2] - width), F32)
        blocks = lhs2_ref.shape[1]
        for p in range(5):
            for b in range(blocks):
                for j in range(3):
                    lhs2_ref[p, b, :, j * 128:(j + 1) * 128] = (
                        act1_ref[p, j:j + rows, b * 128:(b + 1) * 128].astype(BF16))
                following = slice((b + 1) * 128, (b + 2) * 128)
                lhs2_ref[p, b, :, 384:512] = shared([act1_ref[p, j:j + rows, following] for j in range(3)], 0, 32)
        out = None
        for i in range(3):
            part = mm(lhs2_ref[i:i + 3].reshape(3 * blocks * rows, 512), t2_ref[i])
            out = part if out is None else out + part
        for b in range(blocks):
            y = iota((rows, 128), 0) - 1
            z = (iota((rows, 128), 1) + b * 128) // CH - 1
            ok = (z < pz + 1) & (y <= py) & ((y >= 0) | (iy > 0)) & ((y < py) | (iy < y_count - 1))
            ok = ok & ((z >= 0) | (iz > 0)) & ((z < pz) | (iz < z_count - 1))
            for p in range(3):
                s = (p * blocks + b) * rows
                a = gelu(out[s:s + rows] + bias_ref[1:2, 0:128])
                good = ok & (ix + p - 1 >= 0) & (ix + p - 1 < x_count)
                act2_ref[p, :, b * 128:(b + 1) * 128] = jnp.where(good, a, 0.0).astype(BF16)
        out = None
        for i in range(3):
            part = mm(act2_ref[i], t3_ref[i])
            out = part if out is None else out + part
        tail_ref[0:rows, :] = out
        score = tail_ref[0:py, :]
        for j in (1, 2):
            score = score + pltpu.roll(tail_ref[j:j + py, :], 128 - j * pz, 1)
        out_ref[0] = jnp.transpose(score)[0:pz, :] + bias_ref[2:3, 0:1]
        for c in copies:
            c.wait()
    return kernel


def detector(pooled, edge, ids, weights, fields, py, pz):
    counts = tuple(lax.axis_size(a) for a in ("gx", "gy", "gz"))
    half = pooled.shape[1]
    assert half == 128 and pz * CIN == half and pz * 3 <= 128
    rows = py + 4
    width = lanes_for((pz + 4) * CH)
    blocks = width // 128
    yr = both_sides(edge, "gy")
    tall = -(-(TOP + py + 3) // 16) * 16
    (plane,) = call(
        plane_kernel(py, counts[1]), [((tall, half), BF16)], ids, pooled, yr,
        scratch=[pltpu.VMEM((tall, half), F32)])
    shifts = []
    for s in (1, -1, 2, -2, 3, -3):
        if s % counts[0] and s % counts[0] not in shifts:
            shifts.append(s % counts[0])
    own = [plane] + [lax.ppermute(plane, "gx", ring("gx", s)) for s in shifts]
    matrices = call(
        weight_kernel,
        [((3, 512, width), BF16), ((3, 512, 128), BF16), ((3, width, 128), BF16), ((8, width), F32)],
        *weights, plane)
    own[-1], *matrices = lax.optimization_barrier((own[-1], *matrices))
    other = [z_neighbour(v, "gz", False) for v in own]
    args = (ids, *own, *other, *matrices, *fields)
    score, *fields = call(
        conv_kernel(py, counts, shifts), [((1, pz, py), F32)] + [(v.shape, F32) for v in fields], *args,
        out_specs=[VMEM] + [HBM] * 3,
        scratch=[
            pltpu.VMEM((7, tall, half), F32),
            pltpu.VMEM((7, tall, half), F32),
            pltpu.VMEM((7, rows, 512), BF16),
            pltpu.VMEM((5, rows + 8, width + 128), F32),
            pltpu.VMEM((5, blocks, rows, 512), BF16),
            pltpu.VMEM((3, rows, width), BF16),
            pltpu.VMEM((rows + 8, 128), F32),
            pltpu.SemaphoreType.DMA((3,)),
        ], mib=32)
    return *fields, jnp.swapaxes(score, 1, 2)


def solution(mesh):
    slab = P(("groups", "gx"), "gy", "gz")
    return jax.shard_map(
        body,
        mesh=mesh,
        in_specs=(slab, slab, slab, P(), P(), P(), P(), P(), P()),
        out_specs=(slab, slab, slab, slab),
        check_vma=False,
    )
```

```python
import functools

import jax
import jax.numpy as jnp
import numpy as np
from jax import lax
from jax.experimental import pallas as pl
from jax.experimental.pallas import tpu as pltpu
from jax.sharding import PartitionSpec as P

F32 = jnp.float32
BF16 = jnp.bfloat16
I16 = jnp.int16
WELL_HEIGHT = 1.0
STRAIN_COUPLING = 4.0
TIME_STEP = 0.01
DAMAGE_RATE = 0.8
ENERGY_CRITICAL = 0.02

OFF = 16
A_CODE = (0.0, 1.0)
B_CODE = (-1.1, 3.1)
SUM_LOW, SUM_SPAN = -1280.0, 4096.0

VMEM = pl.BlockSpec(memory_space=pltpu.VMEM)
HBM = pl.BlockSpec(memory_space=pltpu.HBM)


def to_code(x, code):
    low, span = code
    v = (x - low) * (65535.0 / span) - 32768.0
    return jnp.clip(jnp.round(v), -32768.0, 32767.0).astype(jnp.int32).astype(I16)


def from_code(q, code):
    low, span = code
    return q.astype(jnp.int32).astype(F32) * (span / 65535.0) + (low + 32768.0 * span / 65535.0)


def sum_digits(s):
    v = (s[0:2] - SUM_LOW) * (65536.0 / SUM_SPAN)
    high = jnp.floor(v)
    low = jnp.minimum(jnp.floor((v - high) * 65536.0), 65535.0)
    rows = jnp.concatenate([high, low, jnp.full((12, s.shape[1]), 32768.0, F32)]) - 32768.0
    return rows.astype(jnp.int32).astype(I16)


def from_digits(tile):
    v = tile.astype(jnp.int32).astype(F32) + 32768.0
    return (v[0:2] + v[2:4] * (1.0 / 65536.0)) * (SUM_SPAN / 65536.0) + SUM_LOW


def each(count, looped, body):
    def step(i, carry):
        body(i)
        return carry
    if looped:
        lax.fori_loop(0, count, step, 0)
    else:
        for i in range(count):
            body(i)


def by_label(labels, values):
    return jnp.where(labels == 0, values[0], jnp.where(labels == 1, values[1], values[2])).astype(F32)


FACTORS = (1.0, 0.3, 0.05)
ROOTS = tuple(float(np.sqrt(np.float32(v))) for v in FACTORS)


def call(kernel, outs, *args, in_specs=None, out_specs=None, scratch=(), mib=16):
    return pl.pallas_call(
        kernel,
        in_specs=in_specs or [VMEM] * len(args),
        out_specs=out_specs or [VMEM] * len(outs),
        out_shape=[jax.ShapeDtypeStruct(s, t) for s, t in outs],
        scratch_shapes=scratch,
        compiler_params=pltpu.CompilerParams(vmem_limit_bytes=mib * 1024 * 1024),
    )(*args)


def chunks(start, stop, size):
    return [(r, min(size, stop - r)) for r in range(start, stop, size)]


def fold(x):
    return x.reshape(x.shape[0] // 8, 8, x.shape[1]).sum(0)


def to_rows(top, bottom):
    return jnp.concatenate([jnp.sum(top, 0, keepdims=True), jnp.sum(bottom, 0, keepdims=True),
                            jnp.zeros((6, top.shape[1]), F32)])


def first_kernel(c_hbm, d_hbm, l_hbm, f_ref, amp_ref, lo_ref, hi_ref, sum_ref, le_ref, d_ref, l_ref, sems):
    nx, ny, nz = f_ref.shape
    order = [0, nx - 1] + list(range(1, nx - 1))
    copies = []
    for x in order:
        copies.append([pltpu.make_async_copy(src.at[x], dst.at[x], sems.at[k, x])
                       for k, (src, dst) in enumerate(((c_hbm, f_ref), (d_hbm, d_ref), (l_hbm, l_ref)))])
        for c in copies[-1]:
            c.start()
    top = jnp.zeros((8, nz), F32)
    bottom = jnp.zeros((8, nz), F32)
    for k, x in enumerate(order):
        for c in copies[k]:
            c.wait()
        le_ref[x, 0:16, :] = l_ref[x, 0:16, :]
        le_ref[x, 16:32, :] = l_ref[x, ny - 16:ny, :]
        for r, n in chunks(0, ny, 48):
            f = f_ref[x, r:r + n, :]
            a = by_label(l_ref[x, r:r + n, :], ROOTS) * (1.0 - d_ref[x, r:r + n, :])
            amp_ref[x, r:r + n, :] = a
            m = a * a
            top = top + fold(m * f)
            bottom = bottom + fold(m)
            for near, far, out in ((0, 1, lo_ref), (nx - 1, nx - 2, hi_ref)):
                if x == near:
                    out[r:r + n, :] = to_code(f, A_CODE)
                    out[2 * ny + r:2 * ny + r + n, :] = to_code(a, A_CODE)
                if x == far:
                    out[ny + r:ny + r + n, :] = to_code(f, A_CODE)
    s = to_rows(top, bottom)
    sum_ref[...] = s
    lo_ref[3 * ny:3 * ny + 16, :] = sum_digits(s)
    hi_ref[3 * ny:3 * ny + 16, :] = sum_digits(s)


def edge_rows(code, ride_x, with_amp):
    def kernel(*refs):
        f_ref = refs[0]
        amp_ref = refs[1] if with_amp else None
        lo_ref, hi_ref, s_ref, far_ref = refs[1 + with_amp:5 + with_amp]
        out_ref = refs[-1]
        nx, ny, nz = f_ref.shape
        low_rows = [from_code(r[0:16, :], code)[0:1] for r in (lo_ref, hi_ref)]
        high_rows = [from_code(r[ny - 16:ny, :], code)[15:16] for r in (lo_ref, hi_ref)]
        s = s_ref[...]
        if ride_x:
            s = s + far_ref[...]
        for side, first, second, beside in ((0, 0, 1, low_rows), (1, ny - 1, ny - 2, high_rows)):
            for x in range(nx):
                out_ref[side, 2 * x:2 * x + 1, :] = f_ref[x, first:first + 1, :]
                out_ref[side, 2 * x + 1:2 * x + 2, :] = f_ref[x, second:second + 1, :]
                if amp_ref is not None:
                    out_ref[side, 10 + x:11 + x, :] = amp_ref[x, first:first + 1, :]
            out_ref[side, 8:9, :] = beside[0]
            out_ref[side, 9:10, :] = beside[1]
            out_ref[side, 16:24, :] = s
            if ride_x:
                out_ref[side, 16:18, :] = (s[0:2] + from_digits(lo_ref[lo_ref.shape[0] - 16:, :])
                                           + from_digits(hi_ref[hi_ref.shape[0] - 16:, :]))
    return kernel


def group(lane, j, nz, first, count):
    return (lane - (32 * j + first)) % nz < count


def pack_z(code, ride_y, with_amp):
    def kernel(*refs):
        f_ref = refs[0]
        amp_ref = refs[1] if with_amp else None
        lo_ref, hi_ref, yr_ref, yp_ref, out_ref = refs[1 + with_amp:]
        nx, ny, nz = f_ref.shape
        end = OFF + ny
        lane = lax.broadcasted_iota(jnp.int32, (1, nz), 1)
        for k in range(out_ref.shape[0]):
            planes = [p for p in range(4 * k, 4 * k + 4) if p < nx + 2]

            def packed(f_of, a_of, ps):
                out = None
                for p in ps:
                    j = p % 4
                    f = f_of(p)
                    f = pltpu.roll(f, 32 * j, 1) if j else f
                    out = f if out is None else jnp.where(group(lane, j, nz, -2, 4), f, out)
                    a = a_of(p)
                    if a is not None:
                        out = jnp.where(group(lane, j, nz, 15, 2), pltpu.roll(a, 32 * j + 16, 1), out)
                return out

            for r, n in chunks(0, ny, 48):
                def f_of(p):
                    if p == 0:
                        return from_code(lo_ref[r:r + n, :], code)
                    if p == nx + 1:
                        return from_code(hi_ref[r:r + n, :], code)
                    return f_ref[p - 1, r:r + n, :]

                def a_of(p):
                    return amp_ref[p - 1, r:r + n, :] if with_amp and 1 <= p <= nx else None

                out_ref[k, OFF + r:OFF + r + n, :] = packed(f_of, a_of, planes)
            inner = [p for p in planes if 1 <= p <= nx]
            if inner:
                for side, near in ((1, OFF - 1), (0, end)):
                    out_ref[k, near:near + 1, :] = packed(
                        lambda p: yr_ref[side, 2 * (p - 1):2 * (p - 1) + 1, :], lambda p: None, inner)
        s = yp_ref[0, 16:24, :]
        out_ref[0, 0:8, :] = s + yr_ref[0, 16:24, :] if ride_y else s
    return kernel


def spread(spans, extra, size):
    return [v for a, b in spans for v in chunks(OFF + a - extra, OFF + b + extra, size)]


def fill(code, f_ref, lo_ref, hi_ref, yr_ref, zr_ref, pad_ref, ze_ref, spans):
    nx, ny, nz = f_ref.shape
    end = OFF + ny
    wide = [v for a, b in spans for v in chunks(max(a - 16, 0), min(b + 16, ny), 48)]
    for near, far, ref in ((1, 0, lo_ref), (nx + 2, nx + 3, hi_ref)):
        for r, n in wide:
            pad_ref[near, OFF + r:OFF + r + n, :] = from_code(ref[r:r + n, :], code)
            pad_ref[far, OFF + r:OFF + r + n, :] = from_code(ref[ny + r:ny + r + n, :], code)
    for p, k in ((1, 8), (nx + 2, 9)):
        pad_ref[p, OFF - 1:OFF, :] = yr_ref[1, k:k + 1, :]
        pad_ref[p, end:end + 1, :] = yr_ref[0, k:k + 1, :]
    for x in range(nx):
        for r, n in wide:
            pad_ref[x + 2, OFF + r:OFF + r + n, :] = f_ref[x, r:r + n, :]
        for side, near, far in ((1, OFF - 1, OFF - 2), (0, end, end + 1)):
            pad_ref[x + 2, near:near + 1, :] = yr_ref[side, 2 * x:2 * x + 1, :]
            pad_ref[x + 2, far:far + 1, :] = yr_ref[side, 2 * x + 1:2 * x + 2, :]
    for p in range(nx + 2):
        for r, n in spread(spans, 8, 32):
            e = zr_ref[p // 4, r:r + n, :]
            ze_ref[p, r:r + n, :] = pltpu.roll(e, nz - 32 * (p % 4), 1) if p % 4 else e


def weighted_mean(yp_ref, yr_ref, zr_ref, ride_y, ride_z):
    s = yp_ref[0, 16:24, :]
    if ride_y:
        s = s + yr_ref[0, 16:24, :]
    if ride_z:
        s = s + zr_ref[0, 0:8, :]
    return jnp.sum(s[0:1], keepdims=True) / jnp.sum(s[1:2], keepdims=True)


def worn(a, m, f, mean):
    e = f - mean
    loss = DAMAGE_RATE * 0.5 * STRAIN_COUPLING * (m * (e * e)) - DAMAGE_RATE * ENERGY_CRITICAL
    return a * (1.0 - jnp.maximum(loss, 0.0))


class Geometry:
    def __init__(self, nx, ny, nz):
        self.nx, self.ny, self.nz = nx, ny, nz
        self.lane = lax.broadcasted_iota(jnp.int32, (1, nz), 1)
        self.first = self.lane == 0
        self.last = self.lane == nz - 1

    def before(self, own, other):
        return pltpu.roll(jnp.where(self.last, other, own), 1, 1)

    def after(self, own, other):
        return pltpu.roll(jnp.where(self.first, other, own), self.nz - 1, 1)


def chem_of(f, m, around, mean):
    w = 2.0 * WELL_HEIGHT
    return ((2.0 * w * f - 3.0 * w) * f + (w + 6.0)) * f - around + STRAIN_COUPLING * (m * (f - mean))


def chemistry(g, pad_ref, mob_ref, mobe_ref, ze_ref, chem_ref, cheme_ref, mean, spans, looped=False):
    nx = g.nx

    @functools.partial(each, nx + 2, looped)
    def _(p):
        for r, n in spread(spans, 0, 48) if not looped and p in (0, nx + 1) else spread(spans, 8, 32):
            f = pad_ref[p + 1, r:r + n, :]
            e = ze_ref[p, r:r + n, :]
            around = (pad_ref[p, r:r + n, :] + pad_ref[p + 2, r:r + n, :]
                      + pad_ref[p + 1, r - 1:r - 1 + n, :] + pad_ref[p + 1, r + 1:r + 1 + n, :]
                      + g.before(f, e) + g.after(f, e))
            chem_ref[p, r:r + n, :] = chem_of(f, mob_ref[p, r:r + n, :], around, mean)

    @functools.partial(each, nx, looped)
    def _(x):
        p = x + 1
        for r, n in spread(spans, 0, 48):
            f = pad_ref[p + 1, r:r + n, :]
            e = ze_ref[p, r:r + n, :]
            around = (ze_ref[p - 1, r:r + n, :] + ze_ref[p + 1, r:r + n, :]
                      + ze_ref[p, r - 1:r - 1 + n, :] + ze_ref[p, r + 1:r + 1 + n, :]
                      + g.before(e, f) + g.after(e, f))
            cheme_ref[x, r - OFF:r - OFF + n, :] = chem_of(
                e, mobe_ref[x, r - OFF:r - OFF + n, :], around, mean)


def flux_of(g, x, r, n, mob_ref, mobe_ref, chem_ref, cheme_ref):
    p = x + 1
    m = mob_ref[p, r:r + n, :]
    q = chem_ref[p, r:r + n, :]
    me = mobe_ref[x, r - OFF:r - OFF + n, :]
    qe = cheme_ref[x, r - OFF:r - OFF + n, :]
    total = None
    for nm, nq in (
        (mob_ref[p - 1, r:r + n, :], chem_ref[p - 1, r:r + n, :]),
        (mob_ref[p + 1, r:r + n, :], chem_ref[p + 1, r:r + n, :]),
        (mob_ref[p, r - 1:r - 1 + n, :], chem_ref[p, r - 1:r - 1 + n, :]),
        (mob_ref[p, r + 1:r + 1 + n, :], chem_ref[p, r + 1:r + 1 + n, :]),
        (g.before(m, me), g.before(q, qe)),
        (g.after(m, me), g.after(q, qe)),
    ):
        term = (nm + m) * (nq - q)
        total = term if total is None else total + term
    return m, 0.5 * total


def pack_edges(values, lane, nz):
    out = values[0]
    for x, v in enumerate(values[1:], 1):
        out = jnp.where(group(lane, x, nz, -1, 2), pltpu.roll(v, 32 * x, 1), out)
    return out


def step_a(ride_y, ride_z):
    def kernel(f_ref, amp_ref, lo_ref, hi_ref, yr_ref, zr_ref, yp_ref,
               f2_ref, a2_ref, ae2_ref, lo_out, hi_out, sum_ref,
               pad_ref, ze_ref, mob_ref, mobe_ref, chem_ref, cheme_ref):
        nx, ny, nz = f2_ref.shape
        end = OFF + ny
        g = Geometry(nx, ny, nz)
        mean = weighted_mean(yp_ref, yr_ref, zr_ref, ride_y, ride_z)
        fill(A_CODE, f_ref, lo_ref, hi_ref, yr_ref, zr_ref, pad_ref, ze_ref, [(0, ny)])

        def wear(p, r, n, a):
            m = a * a
            mob_ref[p, r:r + n, :] = m
            a2_ref[p, r:r + n, :] = worn(a, m, pad_ref[p + 1, r:r + n, :], mean)

        for r, n in chunks(0, ny, 48):
            wear(0, OFF + r, n, from_code(lo_ref[2 * ny + r:2 * ny + r + n, :], A_CODE))
            wear(nx + 1, OFF + r, n, from_code(hi_ref[2 * ny + r:2 * ny + r + n, :], A_CODE))
            edges = []
            for x in range(nx):
                wear(x + 1, OFF + r, n, amp_ref[x, r:r + n, :])
                p = x + 1
                a = pltpu.roll(zr_ref[p // 4, OFF + r:OFF + r + n, :], nz - 32 * (p % 4) - 16, 1)
                m = a * a
                mobe_ref[x, r:r + n, :] = m
                edges.append(worn(a, m, ze_ref[p, OFF + r:OFF + r + n, :], mean))
            ae2_ref[r:r + n, :] = pack_edges(edges, g.lane, nz)
        for x in range(nx):
            wear(x + 1, OFF - 1, 1, yr_ref[1, 10 + x:11 + x, :])
            wear(x + 1, end, 1, yr_ref[0, 10 + x:11 + x, :])
        chemistry(g, pad_ref, mob_ref, mobe_ref, ze_ref, chem_ref, cheme_ref, mean, [(0, ny)])
        top = jnp.zeros((8, nz), F32)
        bottom = jnp.zeros((8, nz), F32)
        for x in range(nx):
            for r, n in chunks(OFF, end, 48):
                _, flux = flux_of(g, x, r, n, mob_ref, mobe_ref, chem_ref, cheme_ref)
                f = pad_ref[x + 2, r:r + n, :] + TIME_STEP * flux
                s = slice(r - OFF, r - OFF + n)
                f2_ref[x, s, :] = f
                a = a2_ref[x + 1, r:r + n, :]
                m = a * a
                top = top + fold(m * f)
                bottom = bottom + fold(m)
                for near, far, out in ((0, 1, lo_out), (nx - 1, nx - 2, hi_out)):
                    if x == near:
                        out[s, :] = to_code(f, B_CODE)
                    if x == far:
                        out[r - OFF + ny:r - OFF + ny + n, :] = to_code(f, B_CODE)
        s = to_rows(top, bottom)
        sum_ref[...] = s
        lo_out[2 * ny:2 * ny + 16, :] = sum_digits(s)
        hi_out[2 * ny:2 * ny + 16, :] = sum_digits(s)
    return kernel


def potentials_b(g, mean, a2_ref, ae2_ref, others, scratch, spans, looped):
    f_ref, lo_ref, hi_ref, yr_ref, zr_ref = others
    pad_ref, ze_ref, mob_ref, mobe_ref, chem_ref, cheme_ref = scratch
    nx, nz = g.nx, g.nz
    fill(B_CODE, f_ref, lo_ref, hi_ref, yr_ref, zr_ref, pad_ref, ze_ref, spans)

    @functools.partial(each, nx + 2, looped)
    def _(p):
        for r, n in spread(spans, 8, 32):
            a = a2_ref[p, r:r + n, :]
            mob_ref[p, r:r + n, :] = a * a

    for r, n in spread(spans, 0, 48):
        a = ae2_ref[r - OFF:r - OFF + n, :]
        a = a * a
        for x in range(nx):
            mobe_ref[x, r - OFF:r - OFF + n, :] = pltpu.roll(a, nz - 32 * x, 1) if x else a
    chemistry(g, pad_ref, mob_ref, mobe_ref, ze_ref, chem_ref, cheme_ref, mean, spans, looped)


def finish_b(g, mean, x, r, n, labels, a2_ref, scratch):
    pad_ref, ze_ref, mob_ref, mobe_ref, chem_ref, cheme_ref = scratch
    m, flux = flux_of(g, x, r, n, mob_ref, mobe_ref, chem_ref, cheme_ref)
    f0 = pad_ref[x + 2, r:r + n, :]
    f = f0 + TIME_STEP * flux
    a = worn(a2_ref[x + 1, r:r + n, :], m, f0, mean)
    dmg = 1.0 - a * by_label(labels, tuple(1.0 / v for v in ROOTS))
    return flux, (f, dmg, a * a, by_label(labels, FACTORS))


def pool_rows(scr_ref, count, nz):
    k = lax.broadcasted_iota(jnp.int32, (4 * nz, nz), 0)
    out = lax.broadcasted_iota(jnp.int32, (4 * nz, nz), 1)
    pick = jnp.where((k % nz // 4 == out // 4) & (out % 4 == k // nz), 1.0 / 64.0, 0.0).astype(BF16)
    high, low = [], []
    for i in range(4):
        rows = (scr_ref[i, pl.ds(0, count, stride=4), :] + scr_ref[i, pl.ds(1, count, stride=4), :]
                + scr_ref[i, pl.ds(2, count, stride=4), :] + scr_ref[i, pl.ds(3, count, stride=4), :])
        high.append(rows.astype(BF16))
        low.append((rows - high[-1].astype(F32)).astype(BF16))
    return sum(jnp.dot(jnp.concatenate(v, axis=1), pick, preferred_element_type=F32) for v in (high, low))


def edge_b(ride_y, ride_z):
    def kernel(f_ref, a2_ref, ae2_ref, lo_ref, hi_ref, yr_ref, zr_ref, yp_ref, l_ref, edge_ref, *rest):
        *scratch, pool_scr = rest
        nx, ny, nz = f_ref.shape
        spans = [(0, 16), (ny - 16, ny)]
        g = Geometry(nx, ny, nz)
        mean = weighted_mean(yp_ref, yr_ref, zr_ref, ride_y, ride_z)
        potentials_b(g, mean, a2_ref, ae2_ref, (f_ref, lo_ref, hi_ref, yr_ref, zr_ref), scratch, spans, False)
        for k, (a, b) in enumerate(spans):
            s = slice(16 * k, 16 * k + 16)
            pooled = [None] * 4
            for x in range(nx):
                _, values = finish_b(g, mean, x, OFF + a, 16, l_ref[x, s, :], a2_ref, scratch)
                pooled = [v if p is None else p + v for p, v in zip(pooled, values)]
            for i in range(4):
                pool_scr[i, s, :] = pooled[i]
        total = pool_rows(pool_scr, 8, nz)
        blank = jnp.zeros((13, nz), F32)
        edge_ref[0] = jnp.concatenate([total[0:3], blank]).astype(BF16)
        edge_ref[1] = jnp.concatenate([total[5:8], blank]).astype(BF16)
    return kernel


def step_b(ride_y, ride_z):
    def kernel(f_ref, a2_ref, ae2_ref, lo_ref, hi_ref, yr_ref, zr_ref, yp_ref, l_hbm,
               f3_ref, dmg_ref, flux_ref, pool_ref, *rest):
        *scratch, pool_scr, l_ref, l_sem = rest
        nx, ny, nz = f_ref.shape
        labels_in = pltpu.make_async_copy(l_hbm, l_ref, l_sem)
        labels_in.start()
        g = Geometry(nx, ny, nz)
        mean = weighted_mean(yp_ref, yr_ref, zr_ref, ride_y, ride_z)
        potentials_b(g, mean, a2_ref, ae2_ref, (f_ref, lo_ref, hi_ref, yr_ref, zr_ref), scratch, [(0, ny)], True)
        labels_in.wait()
        for r, n in chunks(OFF, OFF + ny, 48):
            s = slice(r - OFF, r - OFF + n)
            pooled = [None] * 4
            for x in range(nx):
                flux, values = finish_b(g, mean, x, r, n, l_ref[x, s, :], a2_ref, scratch)
                f3_ref[x, s, :] = values[0]
                dmg_ref[x, s, :] = values[1]
                flux_ref[x, s, :] = flux
                pooled = [v if p is None else p + v for p, v in zip(pooled, values)]
            for i in range(4):
                pool_scr[i, s, :] = pooled[i]
        pool_ref[...] = pool_rows(pool_scr, ny // 4, nz).astype(BF16)
    return kernel


def ring(axis, shift):
    count = lax.axis_size(axis)
    return [(i, (i + shift) % count) for i in range(count)]


def pair_sum(s, axis):
    count = lax.axis_size(axis)
    if count & (count - 1):
        return lax.psum(s, axis)
    bit = 1
    while bit < count:
        s = s + lax.ppermute(s, axis, [(i, i ^ bit) for i in range(count)])
        bit *= 2
    return s


def both_sides(pay, axis):
    if lax.axis_size(axis) == 2:
        return lax.ppermute(pay, axis, ring(axis, 1))
    return jnp.stack([lax.ppermute(pay[0], axis, ring(axis, -1)), lax.ppermute(pay[1], axis, ring(axis, 1))])


def z_neighbour(pay, axis, packed=True):
    if lax.axis_size(axis) == 2:
        return lax.ppermute(pay, axis, ring(axis, 1))
    above = lax.ppermute(pay, axis, ring(axis, -1))
    below = lax.ppermute(pay, axis, ring(axis, 1))
    lane = lax.broadcasted_iota(jnp.int32, pay.shape, pay.ndim - 1)
    if packed:
        low = (lane % 32 < 8) | (lane % 32 == 16)
    else:
        low = lane < pay.shape[-1] // 2
    return jnp.where(low, above, below)


def x_sides(lo, hi):
    return lax.ppermute(hi, "gx", ring("gx", 1)), lax.ppermute(lo, "gx", ring("gx", -1))


def body(concentration, damage, labels, w_first, b_first, w_second, b_second, w_third, b_third):
    nx, ny, nz = concentration.shape
    rows = ny + 2 * OFF
    block = (nx, ny, nz)
    padded = (nx + 2, rows, nz)
    ride_x = lax.axis_size("gx") == 4
    ride_y = lax.axis_size("gy") == 2
    ride_z = lax.axis_size("gz") == 2
    packed = (-(-(nx + 2) // 4), rows, nz)
    assert nz == 128
    scratch = [pltpu.VMEM((nx + 4, rows, nz), F32), pltpu.VMEM(padded, F32), pltpu.VMEM(padded, F32),
               pltpu.VMEM(block, F32), pltpu.VMEM(padded, F32), pltpu.VMEM(block, F32)]

    def start(sums):
        if ride_x:
            return sums, lax.ppermute(sums, "gx", ring("gx", 2))
        sums = pair_sum(sums, "gx")
        for axis, ride in (("gy", ride_y), ("gz", ride_z)):
            if not ride:
                sums = pair_sum(sums, axis)
        return sums, sums

    concentration, damage, labels = (
        pltpu.with_memory_space_constraint(v, pltpu.HBM) for v in (concentration, damage, labels))
    tall = 3 * ny + 16
    f, amp, lo, hi, sums, edge_labels = call(
        first_kernel,
        [(block, F32), (block, F32), ((tall, nz), I16), ((tall, nz), I16), ((8, nz), F32),
         ((nx, 32, nz), jnp.int32)],
        concentration, damage, labels,
        in_specs=[HBM] * 3,
        scratch=[pltpu.VMEM(block, F32), pltpu.VMEM(block, jnp.int32), pltpu.SemaphoreType.DMA((3, nx))])
    weights = weight_rows(w_first, w_second, w_third) + (b_third[None],)
    sums, far = start(sums)
    lo, hi = x_sides(lo, hi)
    (ypay,) = call(edge_rows(A_CODE, ride_x, True), [((2, 24, nz), F32)], f, amp, lo, hi, sums, far, *weights)
    yr = both_sides(ypay, "gy")
    (zpay,) = call(pack_z(A_CODE, ride_y, True), [(packed, F32)], f, amp, lo, hi, yr, ypay)
    zr = z_neighbour(zpay, "gz")
    tall = 2 * ny + 16
    f, a2, ae2, lo, hi, sums = call(
        step_a(ride_y, ride_z),
        [(block, F32), (padded, F32), ((ny, nz), F32), ((tall, nz), I16), ((tall, nz), I16), ((8, nz), F32)],
        f, amp, lo, hi, yr, zr, ypay, scratch=scratch)

    sums, far = start(sums)
    lo, hi = x_sides(lo, hi)
    (ypay,) = call(edge_rows(B_CODE, ride_x, False), [((2, 24, nz), F32)], f, lo, hi, sums, far)
    yr = both_sides(ypay, "gy")
    (zpay,) = call(pack_z(B_CODE, ride_y, False), [(packed, F32)], f, lo, hi, yr, ypay)
    zr = z_neighbour(zpay, "gz")
    last = (f, a2, ae2, lo, hi, yr, zr, ypay)
    (edge,) = call(
        edge_b(ride_y, ride_z), [((2, 16, nz), BF16)], *last, edge_labels,
        scratch=scratch + [pltpu.VMEM((4, 32, nz), F32)])
    fraction, damage_field, flux_sum, pooled = pl.pallas_call(
        step_b(ride_y, ride_z),
        in_specs=[VMEM] * 8 + [HBM],
        out_specs=[VMEM] * 4,
        out_shape=[pltpu.VMEM(block, F32)] * 3 + [jax.ShapeDtypeStruct((ny // 4, nz), BF16)],
        scratch_shapes=scratch + [
            pltpu.VMEM((4, ny, nz), F32), pltpu.VMEM(block, jnp.int32), pltpu.SemaphoreType.DMA],
        compiler_params=pltpu.CompilerParams(vmem_limit_bytes=16 * 1024 * 1024),
    )(*last, labels)
    ids = jnp.broadcast_to(jnp.stack([lax.axis_index(a) for a in ("gx", "gy", "gz")])[:, None], (3, nz))
    return detector(
        pooled, edge, ids, weights + (b_first[None], b_second[None]), (fraction, damage_field, flux_sum), ny // 4, nz // 4)


CH = 16
CIN = 4
TOP = 8


def iota(shape, dim):
    return lax.broadcasted_iota(jnp.int32, shape, dim)


def lanes_for(n):
    return -(-n // 128) * 128


def one_hot(mask):
    return jnp.where(mask, 1.0, 0.0).astype(BF16)


def mm(a, b):
    return jnp.dot(a, b, preferred_element_type=F32)


SHIFTS = tuple(k for k in range(-3, 10) if k % (16 // CIN) == 3)


def weight_kernel(w1_ref, w2_ref, w3_ref, b3_ref, b1_ref, b2_ref, plane_ref, t1_ref, t2_ref, t3_ref, bias_ref):
    n1 = bias_ref.shape[1]
    pz = 128 // CIN
    spread = one_hot(iota((CH, 128), 1) % CH == iota((CH, 128), 0))
    tile1 = mm(w1_ref[...], spread)
    tile2 = mm(w2_ref[...], spread)
    tile3 = mm(w3_ref[...], one_hot(iota((3, 128), 1) // pz == iota((3, 128), 0)))
    step1 = iota((16, 128), 0) // CIN - iota((16, 128), 1) // CH
    step2 = -(iota((16, 128), 1) // CH)
    step3 = -(iota((16, 128), 1) % pz)

    def tile(source, base, stride, step, shift):
        out = jnp.zeros((16, 128), F32)
        for l in range(3):
            k = base + stride * l
            out = jnp.where(step + shift == l, source[16 * k:16 * k + 16], out)
        return out.astype(BF16)

    zero = jnp.zeros((16, 128), BF16)
    bias_ref[...] = jnp.broadcast_to(b3_ref[...], bias_ref.shape)
    for i in range(3):
        for j in range(3):
            tap = 9 * i + 3 * j
            known = {k: tile(tile1, tap, 1, step1, k) for k in SHIFTS}
            places = [(j * 128 + rb * 16, rb * 16 // CIN) for rb in range(8)]
            places += [(384 + 32 * j, pz), (384 + (32 * j - 16) % 128, -16 // CIN)]
            for row, z_in in places:
                for cb in range(n1 // 128):
                    t1_ref[i, row:row + 16, cb * 128:(cb + 1) * 128] = known.get(z_in - cb * 8 + 3, zero)
            for rb in range(10):
                row = j * 128 + rb * 16 if rb < 8 else 384 + 32 * j + (rb - 8) * 16
                t2_ref[i, row:row + 16, :] = tile(tile2, tap, 1, step2, rb)
        for row in (464, 480):
            for cb in range(n1 // 128):
                t1_ref[i, row:row + 16, cb * 128:(cb + 1) * 128] = zero
        for row in (480, 496):
            t2_ref[i, row:row + 16, :] = zero
        for rb in range(t3_ref.shape[1] // 16):
            t3_ref[i, rb * 16:rb * 16 + 16, :] = tile(tile3, 3 * i, 1, step3, rb) if rb < pz + 2 else zero
    wide = one_hot(iota((CH, n1), 1) % CH == iota((CH, n1), 0)).astype(F32)
    for k, ref in ((0, b1_ref), (1, b2_ref)):
        bias_ref[k:k + 1, :] = jnp.dot(ref[...], wide, precision=lax.Precision.HIGHEST, preferred_element_type=F32)


def weight_rows(w_first, w_second, w_third):
    return (jnp.tile(jnp.swapaxes(w_first, 1, 2), (1, 16 // CIN, 1)).reshape(27 * 16, CH),
            jnp.swapaxes(w_second, 1, 2).reshape(27 * CH, CH),
            w_third.reshape(3, 3, 3, CH).transpose(0, 2, 3, 1).reshape(9 * CH, 3))


def gelu(x):
    return 0.5 * x * (1.0 + jnp.tanh(0.7978845608028654 * (x + 0.044715 * (x * x * x))))


def plane_kernel(py, y_count):
    def kernel(ids_ref, pool_ref, yr_ref, out_ref, scr_ref):
        iy = ids_ref[1:2, 0:1]
        scr_ref[...] = jnp.zeros(scr_ref.shape, F32)
        scr_ref[TOP:TOP + py, :] = pool_ref[0:py, :].astype(F32)
        below = yr_ref[1].astype(F32)[0:3]
        above = yr_ref[0].astype(F32)[0:3]
        scr_ref[TOP - 3:TOP, :] = jnp.where(iy > 0, below, 0.0)
        scr_ref[TOP + py:TOP + py + 3, :] = jnp.where(iy < y_count - 1, above, 0.0)
        out_ref[...] = scr_ref[...].astype(BF16)
    return kernel


def conv_kernel(py, counts, shifts):
    x_count, y_count, z_count = counts
    n = len(shifts)

    def kernel(*refs):
        ids_ref = refs[0]
        own = refs[1:2 + n]
        other = refs[2 + n:3 + 2 * n]
        t1_ref, t2_ref, t3_ref, bias_ref = refs[3 + 2 * n:7 + 2 * n]
        fields = refs[7 + 2 * n:10 + 2 * n]
        out_ref = refs[10 + 2 * n]
        fields_hbm = refs[11 + 2 * n:14 + 2 * n]
        in_ref, beside_ref, lhs1_ref, act1_ref, lhs2_ref, act2_ref, tail_ref, sems = refs[14 + 2 * n:]
        copies = [pltpu.make_async_copy(src, dst, sems.at[k]) for k, (src, dst) in enumerate(zip(fields, fields_hbm))]
        for c in copies:
            c.start()
        ix, iy, iz = ids_ref[0:1, 0:1], ids_ref[1:2, 0:1], ids_ref[2:3, 0:1]
        half = own[0].shape[1]
        pz = half // CIN
        rows = py + 4
        z_row = iota((1, half), 1) // CIN
        z_ok = ((z_row < pz // 2) & (iz < z_count - 1)) | ((z_row >= pz // 2) & (iz > 0))
        for w in range(7):
            o = w - 3
            k = 0 if o == 0 else 1 + shifts.index((-o) % x_count) if (-o) % x_count in shifts else None
            if k is None:
                in_ref[w] = jnp.zeros(in_ref.shape[1:], F32)
                beside_ref[w] = jnp.zeros(in_ref.shape[1:], F32)
                continue
            inside = (ix + o >= 0) & (ix + o < x_count)
            in_ref[w] = jnp.where(inside, own[k][...].astype(F32), 0.0)
            beside_ref[w] = jnp.where(z_ok & inside, other[k][...].astype(F32), 0.0)
        lane = iota((1, 128), 1)

        def shared(parts, first, count):
            out = parts[0]
            for j in (1, 2):
                out = jnp.where(group(lane, j, 128, first, count), pltpu.roll(parts[j], 32 * j, 1), out)
            return out.astype(BF16)

        for w in range(7):
            starts = [TOP - 3 + j for j in range(3)]
            for j, r in enumerate(starts):
                lhs1_ref[w, :, j * 128:(j + 1) * 128] = in_ref[w, r:r + rows, :].astype(BF16)
            lhs1_ref[w, :, 384:512] = shared([beside_ref[w, r:r + rows, :] for r in starts], -3 * CIN, 6 * CIN)
        out = None
        for i in range(3):
            part = mm(lhs1_ref[i:i + 5].reshape(5 * rows, 512), t1_ref[i])
            out = part if out is None else out + part
        width = out.shape[1]
        y = iota((rows, width), 0) - 2
        z = iota((rows, width), 1) // CH - 2
        ok = (z < pz + 2) & ((y >= 0) | (iy > 0)) & ((y < py) | (iy < y_count - 1))
        ok = ok & ((z >= 0) | (iz > 0)) & ((z < pz) | (iz < z_count - 1))
        for p in range(5):
            a = gelu(out[p * rows:(p + 1) * rows] + bias_ref[0:1, :])
            good = ok & (ix + p - 2 >= 0) & (ix + p - 2 < x_count)
            act1_ref[p, 0:rows, 0:width] = jnp.where(good, a, 0.0)
            act1_ref[p, rows:, 0:width] = jnp.zeros((act1_ref.shape[1] - rows, width), F32)
            act1_ref[p, :, width:] = jnp.zeros((act1_ref.shape[1], act1_ref.shape[2] - width), F32)
        blocks = lhs2_ref.shape[1]
        for p in range(5):
            for b in range(blocks):
                for j in range(3):
                    lhs2_ref[p, b, :, j * 128:(j + 1) * 128] = (
                        act1_ref[p, j:j + rows, b * 128:(b + 1) * 128].astype(BF16))
                following = slice((b + 1) * 128, (b + 2) * 128)
                lhs2_ref[p, b, :, 384:512] = shared([act1_ref[p, j:j + rows, following] for j in range(3)], 0, 32)
        out = None
        for i in range(3):
            part = mm(lhs2_ref[i:i + 3].reshape(3 * blocks * rows, 512), t2_ref[i])
            out = part if out is None else out + part
        for b in range(blocks):
            y = iota((rows, 128), 0) - 1
            z = (iota((rows, 128), 1) + b * 128) // CH - 1
            ok = (z < pz + 1) & (y <= py) & ((y >= 0) | (iy > 0)) & ((y < py) | (iy < y_count - 1))
            ok = ok & ((z >= 0) | (iz > 0)) & ((z < pz) | (iz < z_count - 1))
            for p in range(3):
                s = (p * blocks + b) * rows
                a = gelu(out[s:s + rows] + bias_ref[1:2, 0:128])
                good = ok & (ix + p - 1 >= 0) & (ix + p - 1 < x_count)
                act2_ref[p, :, b * 128:(b + 1) * 128] = jnp.where(good, a, 0.0).astype(BF16)
        out = None
        for i in range(3):
            part = mm(act2_ref[i], t3_ref[i])
            out = part if out is None else out + part
        tail_ref[0:rows, :] = out
        score = tail_ref[0:py, :]
        for j in (1, 2):
            score = score + pltpu.roll(tail_ref[j:j + py, :], 128 - j * pz, 1)
        out_ref[0] = jnp.transpose(score)[0:pz, :] + bias_ref[2:3, 0:1]
        for c in copies:
            c.wait()
    return kernel


def detector(pooled, edge, ids, weights, fields, py, pz):
    counts = tuple(lax.axis_size(a) for a in ("gx", "gy", "gz"))
    half = pooled.shape[1]
    assert half == 128 and pz * CIN == half and pz * 3 <= 128
    rows = py + 4
    width = lanes_for((pz + 4) * CH)
    blocks = width // 128
    yr = both_sides(edge, "gy")
    tall = -(-(TOP + py + 3) // 16) * 16
    (plane,) = call(
        plane_kernel(py, counts[1]), [((tall, half), BF16)], ids, pooled, yr,
        scratch=[pltpu.VMEM((tall, half), F32)])
    shifts = []
    for s in (-1, 1, 2, -2, 3, -3):
        if s % counts[0] and s % counts[0] not in shifts:
            shifts.append(s % counts[0])
    own = [plane] + [lax.ppermute(plane, "gx", ring("gx", s)) for s in shifts]
    matrices = call(
        weight_kernel,
        [((3, 512, width), BF16), ((3, 512, 128), BF16), ((3, width, 128), BF16), ((8, width), F32)],
        *weights, plane)
    own[-1], *matrices = lax.optimization_barrier((own[-1], *matrices))
    other = [z_neighbour(v, "gz", False) for v in own]
    args = (ids, *own, *other, *matrices, *fields)
    score, *fields = call(
        conv_kernel(py, counts, shifts), [((1, pz, py), F32)] + [(v.shape, F32) for v in fields], *args,
        out_specs=[VMEM] + [HBM] * 3,
        scratch=[
            pltpu.VMEM((7, tall, half), F32),
            pltpu.VMEM((7, tall, half), F32),
            pltpu.VMEM((7, rows, 512), BF16),
            pltpu.VMEM((5, rows + 8, width + 128), F32),
            pltpu.VMEM((5, blocks, rows, 512), BF16),
            pltpu.VMEM((3, rows, width), BF16),
            pltpu.VMEM((rows + 8, 128), F32),
            pltpu.SemaphoreType.DMA((3,)),
        ], mib=32)
    return *fields, jnp.swapaxes(score, 1, 2)


def solution(mesh):
    slab = P(("groups", "gx"), "gy", "gz")
    return jax.shard_map(
        body,
        mesh=mesh,
        in_specs=(slab, slab, slab, P(), P(), P(), P(), P(), P()),
        out_specs=(slab, slab, slab, slab),
        check_vma=False,
    )
```

```python
import functools

import jax
import jax.numpy as jnp
import numpy as np
from jax import lax
from jax.experimental import pallas as pl
from jax.experimental.pallas import tpu as pltpu
from jax.sharding import PartitionSpec as P

F32 = jnp.float32
BF16 = jnp.bfloat16
I16 = jnp.int16
WELL_HEIGHT = 1.0
STRAIN_COUPLING = 4.0
TIME_STEP = 0.01
DAMAGE_RATE = 0.8
ENERGY_CRITICAL = 0.02

OFF = 16
A_CODE = (0.0, 1.0)
B_CODE = (-1.1, 3.1)
SUM_LOW, SUM_SPAN = -1280.0, 4096.0

VMEM = pl.BlockSpec(memory_space=pltpu.VMEM)
HBM = pl.BlockSpec(memory_space=pltpu.HBM)


def to_code(x, code):
    low, span = code
    v = (x - low) * (65535.0 / span) - 32768.0
    return jnp.clip(jnp.round(v), -32768.0, 32767.0).astype(jnp.int32).astype(I16)


def from_code(q, code):
    low, span = code
    return q.astype(jnp.int32).astype(F32) * (span / 65535.0) + (low + 32768.0 * span / 65535.0)


def sum_digits(s):
    v = (s[0:2] - SUM_LOW) * (65536.0 / SUM_SPAN)
    high = jnp.floor(v)
    low = jnp.minimum(jnp.floor((v - high) * 65536.0), 65535.0)
    rows = jnp.concatenate([high, low, jnp.full((12, s.shape[1]), 32768.0, F32)]) - 32768.0
    return rows.astype(jnp.int32).astype(I16)


def from_digits(tile):
    v = tile.astype(jnp.int32).astype(F32) + 32768.0
    return (v[0:2] + v[2:4] * (1.0 / 65536.0)) * (SUM_SPAN / 65536.0) + SUM_LOW


def each(count, looped, body):
    def step(i, carry):
        body(i)
        return carry
    if looped:
        lax.fori_loop(0, count, step, 0)
    else:
        for i in range(count):
            body(i)


def by_label(labels, values):
    return jnp.where(labels == 0, values[0], jnp.where(labels == 1, values[1], values[2])).astype(F32)


FACTORS = (1.0, 0.3, 0.05)
ROOTS = tuple(float(np.sqrt(np.float32(v))) for v in FACTORS)


def call(kernel, outs, *args, in_specs=None, out_specs=None, scratch=(), mib=16):
    return pl.pallas_call(
        kernel,
        in_specs=in_specs or [VMEM] * len(args),
        out_specs=out_specs or [VMEM] * len(outs),
        out_shape=[jax.ShapeDtypeStruct(s, t) for s, t in outs],
        scratch_shapes=scratch,
        compiler_params=pltpu.CompilerParams(vmem_limit_bytes=mib * 1024 * 1024),
    )(*args)


def chunks(start, stop, size):
    return [(r, min(size, stop - r)) for r in range(start, stop, size)]


def fold(x):
    return x.reshape(x.shape[0] // 8, 8, x.shape[1]).sum(0)


def to_rows(top, bottom):
    return jnp.concatenate([jnp.sum(top, 0, keepdims=True), jnp.sum(bottom, 0, keepdims=True),
                            jnp.zeros((6, top.shape[1]), F32)])


def first_kernel(c_hbm, d_hbm, l_hbm, f_ref, amp_ref, lo_ref, hi_ref, sum_ref, le_ref, d_ref, l_ref, sems):
    nx, ny, nz = f_ref.shape
    order = [0, nx - 1] + list(range(1, nx - 1))
    copies = []
    for x in order:
        copies.append([pltpu.make_async_copy(src.at[x], dst.at[x], sems.at[k, x])
                       for k, (src, dst) in enumerate(((c_hbm, f_ref), (d_hbm, d_ref), (l_hbm, l_ref)))])
        for c in copies[-1]:
            c.start()
    top = jnp.zeros((8, nz), F32)
    bottom = jnp.zeros((8, nz), F32)
    for k, x in enumerate(order):
        for c in copies[k]:
            c.wait()
        le_ref[x, 0:16, :] = l_ref[x, 0:16, :]
        le_ref[x, 16:32, :] = l_ref[x, ny - 16:ny, :]
        for r, n in chunks(0, ny, 48):
            f = f_ref[x, r:r + n, :]
            a = by_label(l_ref[x, r:r + n, :], ROOTS) * (1.0 - d_ref[x, r:r + n, :])
            amp_ref[x, r:r + n, :] = a
            m = a * a
            top = top + fold(m * f)
            bottom = bottom + fold(m)
            for near, far, out in ((0, 1, lo_ref), (nx - 1, nx - 2, hi_ref)):
                if x == near:
                    out[r:r + n, :] = to_code(f, A_CODE)
                    out[2 * ny + r:2 * ny + r + n, :] = to_code(a, A_CODE)
                if x == far:
                    out[ny + r:ny + r + n, :] = to_code(f, A_CODE)
    s = to_rows(top, bottom)
    sum_ref[...] = s
    lo_ref[3 * ny:3 * ny + 16, :] = sum_digits(s)
    hi_ref[3 * ny:3 * ny + 16, :] = sum_digits(s)


def edge_rows(code, ride_x, with_amp):
    def kernel(*refs):
        f_ref = refs[0]
        amp_ref = refs[1] if with_amp else None
        lo_ref, hi_ref, s_ref, far_ref = refs[1 + with_amp:5 + with_amp]
        out_ref = refs[-1]
        nx, ny, nz = f_ref.shape
        low_rows = [from_code(r[0:16, :], code)[0:1] for r in (lo_ref, hi_ref)]
        high_rows = [from_code(r[ny - 16:ny, :], code)[15:16] for r in (lo_ref, hi_ref)]
        s = s_ref[...]
        if ride_x:
            s = s + far_ref[...]
        for side, first, second, beside in ((0, 0, 1, low_rows), (1, ny - 1, ny - 2, high_rows)):
            for x in range(nx):
                out_ref[side, 2 * x:2 * x + 1, :] = f_ref[x, first:first + 1, :]
                out_ref[side, 2 * x + 1:2 * x + 2, :] = f_ref[x, second:second + 1, :]
                if amp_ref is not None:
                    out_ref[side, 10 + x:11 + x, :] = amp_ref[x, first:first + 1, :]
            out_ref[side, 8:9, :] = beside[0]
            out_ref[side, 9:10, :] = beside[1]
            out_ref[side, 16:24, :] = s
            if ride_x:
                out_ref[side, 16:18, :] = (s[0:2] + from_digits(lo_ref[lo_ref.shape[0] - 16:, :])
                                           + from_digits(hi_ref[hi_ref.shape[0] - 16:, :]))
    return kernel


def group(lane, j, nz, first, count):
    return (lane - (32 * j + first)) % nz < count


def pack_z(code, ride_y, with_amp):
    def kernel(*refs):
        f_ref = refs[0]
        amp_ref = refs[1] if with_amp else None
        lo_ref, hi_ref, yr_ref, yp_ref, out_ref = refs[1 + with_amp:]
        nx, ny, nz = f_ref.shape
        end = OFF + ny
        lane = lax.broadcasted_iota(jnp.int32, (1, nz), 1)
        for k in range(out_ref.shape[0]):
            planes = [p for p in range(4 * k, 4 * k + 4) if p < nx + 2]

            def packed(f_of, a_of, ps):
                out = None
                for p in ps:
                    j = p % 4
                    f = f_of(p)
                    f = pltpu.roll(f, 32 * j, 1) if j else f
                    out = f if out is None else jnp.where(group(lane, j, nz, -2, 4), f, out)
                    a = a_of(p)
                    if a is not None:
                        out = jnp.where(group(lane, j, nz, 15, 2), pltpu.roll(a, 32 * j + 16, 1), out)
                return out

            for r, n in chunks(0, ny, 48):
                def f_of(p):
                    if p == 0:
                        return from_code(lo_ref[r:r + n, :], code)
                    if p == nx + 1:
                        return from_code(hi_ref[r:r + n, :], code)
                    return f_ref[p - 1, r:r + n, :]

                def a_of(p):
                    return amp_ref[p - 1, r:r + n, :] if with_amp and 1 <= p <= nx else None

                out_ref[k, OFF + r:OFF + r + n, :] = packed(f_of, a_of, planes)
            inner = [p for p in planes if 1 <= p <= nx]
            if inner:
                for side, near in ((1, OFF - 1), (0, end)):
                    out_ref[k, near:near + 1, :] = packed(
                        lambda p: yr_ref[side, 2 * (p - 1):2 * (p - 1) + 1, :], lambda p: None, inner)
        s = yp_ref[0, 16:24, :]
        out_ref[0, 0:8, :] = s + yr_ref[0, 16:24, :] if ride_y else s
    return kernel


def spread(spans, extra, size):
    return [v for a, b in spans for v in chunks(OFF + a - extra, OFF + b + extra, size)]


def fill(code, f_ref, lo_ref, hi_ref, yr_ref, zr_ref, pad_ref, ze_ref, spans):
    nx, ny, nz = f_ref.shape
    end = OFF + ny
    wide = [v for a, b in spans for v in chunks(max(a - 16, 0), min(b + 16, ny), 48)]
    for near, far, ref in ((1, 0, lo_ref), (nx + 2, nx + 3, hi_ref)):
        for r, n in wide:
            pad_ref[near, OFF + r:OFF + r + n, :] = from_code(ref[r:r + n, :], code)
            pad_ref[far, OFF + r:OFF + r + n, :] = from_code(ref[ny + r:ny + r + n, :], code)
    for p, k in ((1, 8), (nx + 2, 9)):
        pad_ref[p, OFF - 1:OFF, :] = yr_ref[1, k:k + 1, :]
        pad_ref[p, end:end + 1, :] = yr_ref[0, k:k + 1, :]
    for x in range(nx):
        for r, n in wide:
            pad_ref[x + 2, OFF + r:OFF + r + n, :] = f_ref[x, r:r + n, :]
        for side, near, far in ((1, OFF - 1, OFF - 2), (0, end, end + 1)):
            pad_ref[x + 2, near:near + 1, :] = yr_ref[side, 2 * x:2 * x + 1, :]
            pad_ref[x + 2, far:far + 1, :] = yr_ref[side, 2 * x + 1:2 * x + 2, :]
    for p in range(nx + 2):
        for r, n in spread(spans, 8, 32):
            e = zr_ref[p // 4, r:r + n, :]
            ze_ref[p, r:r + n, :] = pltpu.roll(e, nz - 32 * (p % 4), 1) if p % 4 else e


def weighted_mean(yp_ref, yr_ref, zr_ref, ride_y, ride_z):
    s = yp_ref[0, 16:24, :]
    if ride_y:
        s = s + yr_ref[0, 16:24, :]
    if ride_z:
        s = s + zr_ref[0, 0:8, :]
    return jnp.sum(s[0:1], keepdims=True) / jnp.sum(s[1:2], keepdims=True)


def worn(a, m, f, mean):
    e = f - mean
    loss = DAMAGE_RATE * 0.5 * STRAIN_COUPLING * (m * (e * e)) - DAMAGE_RATE * ENERGY_CRITICAL
    return a * (1.0 - jnp.maximum(loss, 0.0))


class Geometry:
    def __init__(self, nx, ny, nz):
        self.nx, self.ny, self.nz = nx, ny, nz
        self.lane = lax.broadcasted_iota(jnp.int32, (1, nz), 1)
        self.first = self.lane == 0
        self.last = self.lane == nz - 1

    def before(self, own, other):
        return pltpu.roll(jnp.where(self.last, other, own), 1, 1)

    def after(self, own, other):
        return pltpu.roll(jnp.where(self.first, other, own), self.nz - 1, 1)


def chem_of(f, m, around, mean):
    w = 2.0 * WELL_HEIGHT
    return ((2.0 * w * f - 3.0 * w) * f + (w + 6.0)) * f - around + STRAIN_COUPLING * (m * (f - mean))


def chemistry(g, pad_ref, mob_ref, mobe_ref, ze_ref, chem_ref, cheme_ref, mean, spans, looped=False):
    nx = g.nx

    @functools.partial(each, nx + 2, looped)
    def _(p):
        for r, n in spread(spans, 0, 48) if not looped and p in (0, nx + 1) else spread(spans, 8, 32):
            f = pad_ref[p + 1, r:r + n, :]
            e = ze_ref[p, r:r + n, :]
            around = (pad_ref[p, r:r + n, :] + pad_ref[p + 2, r:r + n, :]
                      + pad_ref[p + 1, r - 1:r - 1 + n, :] + pad_ref[p + 1, r + 1:r + 1 + n, :]
                      + g.before(f, e) + g.after(f, e))
            chem_ref[p, r:r + n, :] = chem_of(f, mob_ref[p, r:r + n, :], around, mean)

    @functools.partial(each, nx, looped)
    def _(x):
        p = x + 1
        for r, n in spread(spans, 0, 48):
            f = pad_ref[p + 1, r:r + n, :]
            e = ze_ref[p, r:r + n, :]
            around = (ze_ref[p - 1, r:r + n, :] + ze_ref[p + 1, r:r + n, :]
                      + ze_ref[p, r - 1:r - 1 + n, :] + ze_ref[p, r + 1:r + 1 + n, :]
                      + g.before(e, f) + g.after(e, f))
            cheme_ref[x, r - OFF:r - OFF + n, :] = chem_of(
                e, mobe_ref[x, r - OFF:r - OFF + n, :], around, mean)


def flux_of(g, x, r, n, mob_ref, mobe_ref, chem_ref, cheme_ref):
    p = x + 1
    m = mob_ref[p, r:r + n, :]
    q = chem_ref[p, r:r + n, :]
    me = mobe_ref[x, r - OFF:r - OFF + n, :]
    qe = cheme_ref[x, r - OFF:r - OFF + n, :]
    total = None
    for nm, nq in (
        (mob_ref[p - 1, r:r + n, :], chem_ref[p - 1, r:r + n, :]),
        (mob_ref[p + 1, r:r + n, :], chem_ref[p + 1, r:r + n, :]),
        (mob_ref[p, r - 1:r - 1 + n, :], chem_ref[p, r - 1:r - 1 + n, :]),
        (mob_ref[p, r + 1:r + 1 + n, :], chem_ref[p, r + 1:r + 1 + n, :]),
        (g.before(m, me), g.before(q, qe)),
        (g.after(m, me), g.after(q, qe)),
    ):
        term = (nm + m) * (nq - q)
        total = term if total is None else total + term
    return m, 0.5 * total


def pack_edges(values, lane, nz):
    out = values[0]
    for x, v in enumerate(values[1:], 1):
        out = jnp.where(group(lane, x, nz, -1, 2), pltpu.roll(v, 32 * x, 1), out)
    return out


def step_a(ride_y, ride_z):
    def kernel(f_ref, amp_ref, lo_ref, hi_ref, yr_ref, zr_ref, yp_ref,
               f2_ref, a2_ref, ae2_ref, lo_out, hi_out, sum_ref,
               pad_ref, ze_ref, mob_ref, mobe_ref, chem_ref, cheme_ref):
        nx, ny, nz = f2_ref.shape
        end = OFF + ny
        g = Geometry(nx, ny, nz)
        mean = weighted_mean(yp_ref, yr_ref, zr_ref, ride_y, ride_z)
        fill(A_CODE, f_ref, lo_ref, hi_ref, yr_ref, zr_ref, pad_ref, ze_ref, [(0, ny)])

        def wear(p, r, n, a):
            m = a * a
            mob_ref[p, r:r + n, :] = m
            a2_ref[p, r:r + n, :] = worn(a, m, pad_ref[p + 1, r:r + n, :], mean)

        for r, n in chunks(0, ny, 48):
            wear(0, OFF + r, n, from_code(lo_ref[2 * ny + r:2 * ny + r + n, :], A_CODE))
            wear(nx + 1, OFF + r, n, from_code(hi_ref[2 * ny + r:2 * ny + r + n, :], A_CODE))
            edges = []
            for x in range(nx):
                wear(x + 1, OFF + r, n, amp_ref[x, r:r + n, :])
                p = x + 1
                a = pltpu.roll(zr_ref[p // 4, OFF + r:OFF + r + n, :], nz - 32 * (p % 4) - 16, 1)
                m = a * a
                mobe_ref[x, r:r + n, :] = m
                edges.append(worn(a, m, ze_ref[p, OFF + r:OFF + r + n, :], mean))
            ae2_ref[r:r + n, :] = pack_edges(edges, g.lane, nz)
        for x in range(nx):
            wear(x + 1, OFF - 1, 1, yr_ref[1, 10 + x:11 + x, :])
            wear(x + 1, end, 1, yr_ref[0, 10 + x:11 + x, :])
        chemistry(g, pad_ref, mob_ref, mobe_ref, ze_ref, chem_ref, cheme_ref, mean, [(0, ny)])
        top = jnp.zeros((8, nz), F32)
        bottom = jnp.zeros((8, nz), F32)
        for x in range(nx):
            for r, n in chunks(OFF, end, 48):
                _, flux = flux_of(g, x, r, n, mob_ref, mobe_ref, chem_ref, cheme_ref)
                f = pad_ref[x + 2, r:r + n, :] + TIME_STEP * flux
                s = slice(r - OFF, r - OFF + n)
                f2_ref[x, s, :] = f
                a = a2_ref[x + 1, r:r + n, :]
                m = a * a
                top = top + fold(m * f)
                bottom = bottom + fold(m)
                for near, far, out in ((0, 1, lo_out), (nx - 1, nx - 2, hi_out)):
                    if x == near:
                        out[s, :] = to_code(f, B_CODE)
                    if x == far:
                        out[r - OFF + ny:r - OFF + ny + n, :] = to_code(f, B_CODE)
        s = to_rows(top, bottom)
        sum_ref[...] = s
        lo_out[2 * ny:2 * ny + 16, :] = sum_digits(s)
        hi_out[2 * ny:2 * ny + 16, :] = sum_digits(s)
    return kernel


def potentials_b(g, mean, a2_ref, ae2_ref, others, scratch, spans, looped):
    f_ref, lo_ref, hi_ref, yr_ref, zr_ref = others
    pad_ref, ze_ref, mob_ref, mobe_ref, chem_ref, cheme_ref = scratch
    nx, nz = g.nx, g.nz
    fill(B_CODE, f_ref, lo_ref, hi_ref, yr_ref, zr_ref, pad_ref, ze_ref, spans)

    @functools.partial(each, nx + 2, looped)
    def _(p):
        for r, n in spread(spans, 8, 32):
            a = a2_ref[p, r:r + n, :]
            mob_ref[p, r:r + n, :] = a * a

    for r, n in spread(spans, 0, 48):
        a = ae2_ref[r - OFF:r - OFF + n, :]
        a = a * a
        for x in range(nx):
            mobe_ref[x, r - OFF:r - OFF + n, :] = pltpu.roll(a, nz - 32 * x, 1) if x else a
    chemistry(g, pad_ref, mob_ref, mobe_ref, ze_ref, chem_ref, cheme_ref, mean, spans, looped)


def finish_b(g, mean, x, r, n, labels, a2_ref, scratch):
    pad_ref, ze_ref, mob_ref, mobe_ref, chem_ref, cheme_ref = scratch
    m, flux = flux_of(g, x, r, n, mob_ref, mobe_ref, chem_ref, cheme_ref)
    f0 = pad_ref[x + 2, r:r + n, :]
    f = f0 + TIME_STEP * flux
    a = worn(a2_ref[x + 1, r:r + n, :], m, f0, mean)
    dmg = 1.0 - a * by_label(labels, tuple(1.0 / v for v in ROOTS))
    return flux, (f, dmg, a * a, by_label(labels, FACTORS))


def pool_rows(scr_ref, count, nz):
    k = lax.broadcasted_iota(jnp.int32, (4 * nz, nz), 0)
    out = lax.broadcasted_iota(jnp.int32, (4 * nz, nz), 1)
    pick = jnp.where((k % nz // 4 == out // 4) & (out % 4 == k // nz), 1.0 / 64.0, 0.0).astype(BF16)
    high, low = [], []
    for i in range(4):
        rows = (scr_ref[i, pl.ds(0, count, stride=4), :] + scr_ref[i, pl.ds(1, count, stride=4), :]
                + scr_ref[i, pl.ds(2, count, stride=4), :] + scr_ref[i, pl.ds(3, count, stride=4), :])
        high.append(rows.astype(BF16))
        low.append((rows - high[-1].astype(F32)).astype(BF16))
    return sum(jnp.dot(jnp.concatenate(v, axis=1), pick, preferred_element_type=F32) for v in (high, low))


def edge_b(ride_y, ride_z):
    def kernel(f_ref, a2_ref, ae2_ref, lo_ref, hi_ref, yr_ref, zr_ref, yp_ref, l_ref, edge_ref, *rest):
        *scratch, pool_scr = rest
        nx, ny, nz = f_ref.shape
        spans = [(0, 16), (ny - 16, ny)]
        g = Geometry(nx, ny, nz)
        mean = weighted_mean(yp_ref, yr_ref, zr_ref, ride_y, ride_z)
        potentials_b(g, mean, a2_ref, ae2_ref, (f_ref, lo_ref, hi_ref, yr_ref, zr_ref), scratch, spans, False)
        for k, (a, b) in enumerate(spans):
            s = slice(16 * k, 16 * k + 16)
            pooled = [None] * 4
            for x in range(nx):
                _, values = finish_b(g, mean, x, OFF + a, 16, l_ref[x, s, :], a2_ref, scratch)
                pooled = [v if p is None else p + v for p, v in zip(pooled, values)]
            for i in range(4):
                pool_scr[i, s, :] = pooled[i]
        total = pool_rows(pool_scr, 8, nz)
        blank = jnp.zeros((13, nz), F32)
        edge_ref[0] = jnp.concatenate([total[0:3], blank]).astype(BF16)
        edge_ref[1] = jnp.concatenate([total[5:8], blank]).astype(BF16)
    return kernel


def step_b(ride_y, ride_z):
    def kernel(f_ref, a2_ref, ae2_ref, lo_ref, hi_ref, yr_ref, zr_ref, yp_ref, l_hbm,
               f3_ref, dmg_ref, flux_ref, pool_ref, *rest):
        *scratch, pool_scr, l_ref, l_sem = rest
        nx, ny, nz = f_ref.shape
        labels_in = pltpu.make_async_copy(l_hbm, l_ref, l_sem)
        labels_in.start()
        g = Geometry(nx, ny, nz)
        mean = weighted_mean(yp_ref, yr_ref, zr_ref, ride_y, ride_z)
        potentials_b(g, mean, a2_ref, ae2_ref, (f_ref, lo_ref, hi_ref, yr_ref, zr_ref), scratch, [(0, ny)], False)
        labels_in.wait()
        for r, n in chunks(OFF, OFF + ny, 48):
            s = slice(r - OFF, r - OFF + n)
            pooled = [None] * 4
            for x in range(nx):
                flux, values = finish_b(g, mean, x, r, n, l_ref[x, s, :], a2_ref, scratch)
                f3_ref[x, s, :] = values[0]
                dmg_ref[x, s, :] = values[1]
                flux_ref[x, s, :] = flux
                pooled = [v if p is None else p + v for p, v in zip(pooled, values)]
            for i in range(4):
                pool_scr[i, s, :] = pooled[i]
        pool_ref[...] = pool_rows(pool_scr, ny // 4, nz).astype(BF16)
    return kernel


def ring(axis, shift):
    count = lax.axis_size(axis)
    return [(i, (i + shift) % count) for i in range(count)]


def pair_sum(s, axis):
    count = lax.axis_size(axis)
    if count & (count - 1):
        return lax.psum(s, axis)
    bit = 1
    while bit < count:
        s = s + lax.ppermute(s, axis, [(i, i ^ bit) for i in range(count)])
        bit *= 2
    return s


def both_sides(pay, axis):
    if lax.axis_size(axis) == 2:
        return lax.ppermute(pay, axis, ring(axis, 1))
    return jnp.stack([lax.ppermute(pay[0], axis, ring(axis, -1)), lax.ppermute(pay[1], axis, ring(axis, 1))])


def z_neighbour(pay, axis, packed=True):
    if lax.axis_size(axis) == 2:
        return lax.ppermute(pay, axis, ring(axis, 1))
    above = lax.ppermute(pay, axis, ring(axis, -1))
    below = lax.ppermute(pay, axis, ring(axis, 1))
    lane = lax.broadcasted_iota(jnp.int32, pay.shape, pay.ndim - 1)
    if packed:
        low = (lane % 32 < 8) | (lane % 32 == 16)
    else:
        low = lane < pay.shape[-1] // 2
    return jnp.where(low, above, below)


def x_sides(lo, hi):
    return lax.ppermute(hi, "gx", ring("gx", 1)), lax.ppermute(lo, "gx", ring("gx", -1))


def body(concentration, damage, labels, w_first, b_first, w_second, b_second, w_third, b_third):
    nx, ny, nz = concentration.shape
    rows = ny + 2 * OFF
    block = (nx, ny, nz)
    padded = (nx + 2, rows, nz)
    ride_x = lax.axis_size("gx") == 4
    ride_y = lax.axis_size("gy") == 2
    ride_z = lax.axis_size("gz") == 2
    packed = (-(-(nx + 2) // 4), rows, nz)
    assert nz == 128
    scratch = [pltpu.VMEM((nx + 4, rows, nz), F32), pltpu.VMEM(padded, F32), pltpu.VMEM(padded, F32),
               pltpu.VMEM(block, F32), pltpu.VMEM(padded, F32), pltpu.VMEM(block, F32)]

    def start(sums):
        if ride_x:
            return sums, lax.ppermute(sums, "gx", ring("gx", 2))
        sums = pair_sum(sums, "gx")
        for axis, ride in (("gy", ride_y), ("gz", ride_z)):
            if not ride:
                sums = pair_sum(sums, axis)
        return sums, sums

    concentration, damage, labels = (
        pltpu.with_memory_space_constraint(v, pltpu.HBM) for v in (concentration, damage, labels))
    tall = 3 * ny + 16
    f, amp, lo, hi, sums, edge_labels = call(
        first_kernel,
        [(block, F32), (block, F32), ((tall, nz), I16), ((tall, nz), I16), ((8, nz), F32),
         ((nx, 32, nz), jnp.int32)],
        concentration, damage, labels,
        in_specs=[HBM] * 3,
        scratch=[pltpu.VMEM(block, F32), pltpu.VMEM(block, jnp.int32), pltpu.SemaphoreType.DMA((3, nx))])
    weights = weight_rows(w_first, w_second, w_third) + (b_third[None],)
    sums, far = start(sums)
    lo, hi = x_sides(lo, hi)
    (ypay,) = call(edge_rows(A_CODE, ride_x, True), [((2, 24, nz), F32)], f, amp, lo, hi, sums, far, *weights)
    yr = both_sides(ypay, "gy")
    (zpay,) = call(pack_z(A_CODE, ride_y, True), [(packed, F32)], f, amp, lo, hi, yr, ypay)
    zr = z_neighbour(zpay, "gz")
    tall = 2 * ny + 16
    f, a2, ae2, lo, hi, sums = call(
        step_a(ride_y, ride_z),
        [(block, F32), (padded, F32), ((ny, nz), F32), ((tall, nz), I16), ((tall, nz), I16), ((8, nz), F32)],
        f, amp, lo, hi, yr, zr, ypay, scratch=scratch)

    sums, far = start(sums)
    lo, hi = x_sides(lo, hi)
    (ypay,) = call(edge_rows(B_CODE, ride_x, False), [((2, 24, nz), F32)], f, lo, hi, sums, far)
    yr = both_sides(ypay, "gy")
    (zpay,) = call(pack_z(B_CODE, ride_y, False), [(packed, F32)], f, lo, hi, yr, ypay)
    zr = z_neighbour(zpay, "gz")
    last = (f, a2, ae2, lo, hi, yr, zr, ypay)
    (edge,) = call(
        edge_b(ride_y, ride_z), [((2, 16, nz), BF16)], *last, edge_labels,
        scratch=scratch + [pltpu.VMEM((4, 32, nz), F32)])
    fraction, damage_field, flux_sum, pooled = pl.pallas_call(
        step_b(ride_y, ride_z),
        in_specs=[VMEM] * 8 + [HBM],
        out_specs=[VMEM] * 4,
        out_shape=[pltpu.VMEM(block, F32)] * 3 + [jax.ShapeDtypeStruct((ny // 4, nz), BF16)],
        scratch_shapes=scratch + [
            pltpu.VMEM((4, ny, nz), F32), pltpu.VMEM(block, jnp.int32), pltpu.SemaphoreType.DMA],
        compiler_params=pltpu.CompilerParams(vmem_limit_bytes=16 * 1024 * 1024),
    )(*last, labels)
    ids = jnp.broadcast_to(jnp.stack([lax.axis_index(a) for a in ("gx", "gy", "gz")])[:, None], (3, nz))
    return detector(
        pooled, edge, ids, weights + (b_first[None], b_second[None]), (fraction, damage_field, flux_sum), ny // 4, nz // 4)


CH = 16
CIN = 4
TOP = 8


def iota(shape, dim):
    return lax.broadcasted_iota(jnp.int32, shape, dim)


def lanes_for(n):
    return -(-n // 128) * 128


def one_hot(mask):
    return jnp.where(mask, 1.0, 0.0).astype(BF16)


def mm(a, b):
    return jnp.dot(a, b, preferred_element_type=F32)


SHIFTS = tuple(k for k in range(-3, 10) if k % (16 // CIN) == 3)


def weight_kernel(w1_ref, w2_ref, w3_ref, b3_ref, b1_ref, b2_ref, plane_ref, t1_ref, t2_ref, t3_ref, bias_ref):
    n1 = bias_ref.shape[1]
    pz = 128 // CIN
    spread = one_hot(iota((CH, 128), 1) % CH == iota((CH, 128), 0))
    tile1 = mm(w1_ref[...], spread)
    tile2 = mm(w2_ref[...], spread)
    tile3 = mm(w3_ref[...], one_hot(iota((3, 128), 1) // pz == iota((3, 128), 0)))
    step1 = iota((16, 128), 0) // CIN - iota((16, 128), 1) // CH
    step2 = -(iota((16, 128), 1) // CH)
    step3 = -(iota((16, 128), 1) % pz)

    def tile(source, base, stride, step, shift):
        out = jnp.zeros((16, 128), F32)
        for l in range(3):
            k = base + stride * l
            out = jnp.where(step + shift == l, source[16 * k:16 * k + 16], out)
        return out.astype(BF16)

    zero = jnp.zeros((16, 128), BF16)
    bias_ref[...] = jnp.broadcast_to(b3_ref[...], bias_ref.shape)
    for i in range(3):
        for j in range(3):
            tap = 9 * i + 3 * j
            known = {k: tile(tile1, tap, 1, step1, k) for k in SHIFTS}
            places = [(j * 128 + rb * 16, rb * 16 // CIN) for rb in range(8)]
            places += [(384 + 32 * j, pz), (384 + (32 * j - 16) % 128, -16 // CIN)]
            for row, z_in in places:
                for cb in range(n1 // 128):
                    t1_ref[i, row:row + 16, cb * 128:(cb + 1) * 128] = known.get(z_in - cb * 8 + 3, zero)
            for rb in range(10):
                row = j * 128 + rb * 16 if rb < 8 else 384 + 32 * j + (rb - 8) * 16
                t2_ref[i, row:row + 16, :] = tile(tile2, tap, 1, step2, rb)
        for row in (464, 480):
            for cb in range(n1 // 128):
                t1_ref[i, row:row + 16, cb * 128:(cb + 1) * 128] = zero
        for row in (480, 496):
            t2_ref[i, row:row + 16, :] = zero
        for rb in range(t3_ref.shape[1] // 16):
            t3_ref[i, rb * 16:rb * 16 + 16, :] = tile(tile3, 3 * i, 1, step3, rb) if rb < pz + 2 else zero
    wide = one_hot(iota((CH, n1), 1) % CH == iota((CH, n1), 0)).astype(F32)
    for k, ref in ((0, b1_ref), (1, b2_ref)):
        bias_ref[k:k + 1, :] = jnp.dot(ref[...], wide, precision=lax.Precision.HIGHEST, preferred_element_type=F32)


def weight_rows(w_first, w_second, w_third):
    return (jnp.tile(jnp.swapaxes(w_first, 1, 2), (1, 16 // CIN, 1)).reshape(27 * 16, CH),
            jnp.swapaxes(w_second, 1, 2).reshape(27 * CH, CH),
            w_third.reshape(3, 3, 3, CH).transpose(0, 2, 3, 1).reshape(9 * CH, 3))


def gelu(x):
    return 0.5 * x * (1.0 + jnp.tanh(0.7978845608028654 * (x + 0.044715 * (x * x * x))))


def plane_kernel(py, y_count):
    def kernel(ids_ref, pool_ref, yr_ref, out_ref, scr_ref):
        iy = ids_ref[1:2, 0:1]
        scr_ref[...] = jnp.zeros(scr_ref.shape, F32)
        scr_ref[TOP:TOP + py, :] = pool_ref[0:py, :].astype(F32)
        below = yr_ref[1].astype(F32)[0:3]
        above = yr_ref[0].astype(F32)[0:3]
        scr_ref[TOP - 3:TOP, :] = jnp.where(iy > 0, below, 0.0)
        scr_ref[TOP + py:TOP + py + 3, :] = jnp.where(iy < y_count - 1, above, 0.0)
        out_ref[...] = scr_ref[...].astype(BF16)
    return kernel


def conv_kernel(py, counts, shifts):
    x_count, y_count, z_count = counts
    n = len(shifts)

    def kernel(*refs):
        ids_ref = refs[0]
        own = refs[1:2 + n]
        other = refs[2 + n:3 + 2 * n]
        t1_ref, t2_ref, t3_ref, bias_ref = refs[3 + 2 * n:7 + 2 * n]
        fields = refs[7 + 2 * n:10 + 2 * n]
        out_ref = refs[10 + 2 * n]
        fields_hbm = refs[11 + 2 * n:14 + 2 * n]
        in_ref, beside_ref, lhs1_ref, act1_ref, lhs2_ref, act2_ref, tail_ref, sems = refs[14 + 2 * n:]
        copies = [pltpu.make_async_copy(src, dst, sems.at[k]) for k, (src, dst) in enumerate(zip(fields, fields_hbm))]
        for c in copies:
            c.start()
        ix, iy, iz = ids_ref[0:1, 0:1], ids_ref[1:2, 0:1], ids_ref[2:3, 0:1]
        half = own[0].shape[1]
        pz = half // CIN
        rows = py + 4
        z_row = iota((1, half), 1) // CIN
        z_ok = ((z_row < pz // 2) & (iz < z_count - 1)) | ((z_row >= pz // 2) & (iz > 0))
        for w in range(7):
            o = w - 3
            k = 0 if o == 0 else 1 + shifts.index((-o) % x_count) if (-o) % x_count in shifts else None
            if k is None:
                in_ref[w] = jnp.zeros(in_ref.shape[1:], F32)
                beside_ref[w] = jnp.zeros(in_ref.shape[1:], F32)
                continue
            inside = (ix + o >= 0) & (ix + o < x_count)
            in_ref[w] = jnp.where(inside, own[k][...].astype(F32), 0.0)
            beside_ref[w] = jnp.where(z_ok & inside, other[k][...].astype(F32), 0.0)
        lane = iota((1, 128), 1)

        def shared(parts, first, count):
            out = parts[0]
            for j in (1, 2):
                out = jnp.where(group(lane, j, 128, first, count), pltpu.roll(parts[j], 32 * j, 1), out)
            return out.astype(BF16)

        for w in range(7):
            starts = [TOP - 3 + j for j in range(3)]
            for j, r in enumerate(starts):
                lhs1_ref[w, :, j * 128:(j + 1) * 128] = in_ref[w, r:r + rows, :].astype(BF16)
            lhs1_ref[w, :, 384:512] = shared([beside_ref[w, r:r + rows, :] for r in starts], -3 * CIN, 6 * CIN)
        out = None
        for i in range(3):
            part = mm(lhs1_ref[i:i + 5].reshape(5 * rows, 512), t1_ref[i])
            out = part if out is None else out + part
        width = out.shape[1]
        y = iota((rows, width), 0) - 2
        z = iota((rows, width), 1) // CH - 2
        ok = (z < pz + 2) & ((y >= 0) | (iy > 0)) & ((y < py) | (iy < y_count - 1))
        ok = ok & ((z >= 0) | (iz > 0)) & ((z < pz) | (iz < z_count - 1))
        for p in range(5):
            a = gelu(out[p * rows:(p + 1) * rows] + bias_ref[0:1, :])
            good = ok & (ix + p - 2 >= 0) & (ix + p - 2 < x_count)
            act1_ref[p, 0:rows, 0:width] = jnp.where(good, a, 0.0)
            act1_ref[p, rows:, 0:width] = jnp.zeros((act1_ref.shape[1] - rows, width), F32)
            act1_ref[p, :, width:] = jnp.zeros((act1_ref.shape[1], act1_ref.shape[2] - width), F32)
        blocks = lhs2_ref.shape[1]
        for p in range(5):
            for b in range(blocks):
                for j in range(3):
                    lhs2_ref[p, b, :, j * 128:(j + 1) * 128] = (
                        act1_ref[p, j:j + rows, b * 128:(b + 1) * 128].astype(BF16))
                following = slice((b + 1) * 128, (b + 2) * 128)
                lhs2_ref[p, b, :, 384:512] = shared([act1_ref[p, j:j + rows, following] for j in range(3)], 0, 32)
        out = None
        for i in range(3):
            part = mm(lhs2_ref[i:i + 3].reshape(3 * blocks * rows, 512), t2_ref[i])
            out = part if out is None else out + part
        for b in range(blocks):
            y = iota((rows, 128), 0) - 1
            z = (iota((rows, 128), 1) + b * 128) // CH - 1
            ok = (z < pz + 1) & (y <= py) & ((y >= 0) | (iy > 0)) & ((y < py) | (iy < y_count - 1))
            ok = ok & ((z >= 0) | (iz > 0)) & ((z < pz) | (iz < z_count - 1))
            for p in range(3):
                s = (p * blocks + b) * rows
                a = gelu(out[s:s + rows] + bias_ref[1:2, 0:128])
                good = ok & (ix + p - 1 >= 0) & (ix + p - 1 < x_count)
                act2_ref[p, :, b * 128:(b + 1) * 128] = jnp.where(good, a, 0.0).astype(BF16)
        out = None
        for i in range(3):
            part = mm(act2_ref[i], t3_ref[i])
            out = part if out is None else out + part
        tail_ref[0:rows, :] = out
        score = tail_ref[0:py, :]
        for j in (1, 2):
            score = score + pltpu.roll(tail_ref[j:j + py, :], 128 - j * pz, 1)
        out_ref[0] = jnp.transpose(score)[0:pz, :] + bias_ref[2:3, 0:1]
        for c in copies:
            c.wait()
    return kernel


def detector(pooled, edge, ids, weights, fields, py, pz):
    counts = tuple(lax.axis_size(a) for a in ("gx", "gy", "gz"))
    half = pooled.shape[1]
    assert half == 128 and pz * CIN == half and pz * 3 <= 128
    rows = py + 4
    width = lanes_for((pz + 4) * CH)
    blocks = width // 128
    yr = both_sides(edge, "gy")
    tall = -(-(TOP + py + 3) // 16) * 16
    (plane,) = call(
        plane_kernel(py, counts[1]), [((tall, half), BF16)], ids, pooled, yr,
        scratch=[pltpu.VMEM((tall, half), F32)])
    shifts = []
    for s in (-1, 1, 2, -2, 3, -3):
        if s % counts[0] and s % counts[0] not in shifts:
            shifts.append(s % counts[0])
    own = [plane] + [lax.ppermute(plane, "gx", ring("gx", s)) for s in shifts]
    matrices = call(
        weight_kernel,
        [((3, 512, width), BF16), ((3, 512, 128), BF16), ((3, width, 128), BF16), ((8, width), F32)],
        *weights, plane)
    own[-1], *matrices = lax.optimization_barrier((own[-1], *matrices))
    other = [z_neighbour(v, "gz", False) for v in own]
    args = (ids, *own, *other, *matrices, *fields)
    score, *fields = call(
        conv_kernel(py, counts, shifts), [((1, pz, py), F32)] + [(v.shape, F32) for v in fields], *args,
        out_specs=[VMEM] + [HBM] * 3,
        scratch=[
            pltpu.VMEM((7, tall, half), F32),
            pltpu.VMEM((7, tall, half), F32),
            pltpu.VMEM((7, rows, 512), BF16),
            pltpu.VMEM((5, rows + 8, width + 128), F32),
            pltpu.VMEM((5, blocks, rows, 512), BF16),
            pltpu.VMEM((3, rows, width), BF16),
            pltpu.VMEM((rows + 8, 128), F32),
            pltpu.SemaphoreType.DMA((3,)),
        ], mib=32)
    return *fields, jnp.swapaxes(score, 1, 2)


def solution(mesh):
    slab = P(("groups", "gx"), "gy", "gz")
    return jax.shard_map(
        body,
        mesh=mesh,
        in_specs=(slab, slab, slab, P(), P(), P(), P(), P(), P()),
        out_specs=(slab, slab, slab, slab),
        check_vma=False,
    )
```
